256 devices in a mesh: section: 2 (over y_hi), sx: 16 (over z, core), sy: 8 (over y_lo, x).
Axes of the slice: x: 4, y: 4 (y_hi: 2, y_lo: 2; y = y_hi * 2 + y_lo), z: 8, core: 2. Of those that a mesh axis runs over, the one named last changes fastest.
Arguments:
- previous: float32 [16, 256, 1024], P(None, 'sx', 'sy'), may hold values from -3 to 3
- sections: float32 [4, 16, 256, 1024], P('section', None, 'sx', 'sy'), may hold values from -3 to 3
- diffusivity: float32 [16, 256, 1024], P(None, 'sx', 'sy'), may hold values from 0.3 to 3
- reaction: float32 [16, 256, 1024], P(None, 'sx', 'sy'), may hold values from 0.2 to 2
Outputs:
- updated: float32 [4, 16, 256, 1024], P('section', None, 'sx', 'sy')
The draws below stay inside these ranges and needn't reach their ends.
All inputs are finite; a program needn't handle non-finite values.
Results may differ from the reference program's by a relative error of at most 0.0003.
Values sent between devices are 32-bit elements; how exact they have to be, the bound alone decides.
No kernel may reach another device: no remote copies, remote signals or barrier semaphores. Data moves between devices by JAX's collectives and lax.ppermute only.
A program may use at most 64 MiB of HBM per device.

```python
import math
import jax
import jax.numpy as jnp

NZ = 16
SECTIONS = 4
ITERS = 4
NX = 256
NY = 1024


def level_of(rng, shape, split, least, high):
    factor_of, own = 1.0, jax.random.fold_in(rng, 6)
    for axis_at, shards_of in split:
        draws = jnp.exp(jax.random.uniform(jax.random.fold_in(own, axis_at), (shards_of,), jnp.float32, least / len(split), high / len(split)))
        factor_of = factor_of * jnp.repeat(draws, shape[axis_at] // shards_of).reshape([-1 if axis == axis_at else 1 for axis in range(len(shape))])
    return factor_of


def scatter_about(own_key, extent, scale, most, pieces=(), held_as=jnp.bfloat16):
    entries = jax.random.normal(own_key, extent, jnp.float32) * scale
    if len(pieces) > 0:
        entries = level_of(own_key, extent, pieces, -0.22, 0.18) * entries
    return jnp.clip(entries, min=-most, max=most).astype(held_as)


def setup_inputs(seed: int = 0) -> dict:
    key_of = jax.random.split(jax.random.key(seed), 5)
    previous = scatter_about(key_of[0], (NZ, NX, NY), 0.8, 3.0, ((1, 16), (2, 8)), jnp.float32)
    sections = scatter_about(key_of[1], (SECTIONS, NZ, NX, NY), 1.0, 3.0, ((0, 2), (2, 16), (3, 8)), jnp.float32)
    diffusivity = jnp.clip(jnp.exp(math.log(3.0) - 2.3025851 * jax.random.uniform(key_of[2], (NZ, NX, NY), jnp.float32) ** level_of(key_of[2], (NZ, NX, NY), ((1, 16), (2, 8)), -0.2, 0.2)), 0.3, 3.0)
    reaction = jnp.clip(jnp.exp(math.log(2.0) - 2.3025851 * jax.random.uniform(key_of[3], (NZ, NX, NY), jnp.float32) ** level_of(key_of[3], (NZ, NX, NY), ((1, 16), (2, 8)), -0.2, 0.2)), 0.2, 2.0)
    return dict(previous=previous, sections=sections, diffusivity=diffusivity, reaction=reaction)


step_size = 1.0
tiny_value = 1e-6


def invert_table(matrix):
    order_n = len(matrix)
    augmented = [list(matrix[r]) + [1.0 if c == r else 0.0 for c in range(order_n)] for r in range(order_n)]
    for col in range(order_n):
        pivot_row = max(range(col, order_n), key=lambda r: abs(augmented[r][col]))
        augmented[col], augmented[pivot_row] = augmented[pivot_row], augmented[col]
        leading = augmented[col][col]
        augmented[col] = [v / leading for v in augmented[col]]
        for r in range(order_n):
            if r != col:
                factor = augmented[r][col]
                augmented[r] = [a - factor * b for a, b in zip(augmented[r], augmented[col])]
    return [row_values[order_n:] for row_values in augmented]


def table_product(left, right):
    return [[sum(left[i][k] * right[k][j] for k in range(len(right))) for j in range(len(right[0]))] for i in range(len(left))]


def pair_add(first, second):
    return (first[0] + second[0], first[1] + second[1])


def pair_sub(first, second):
    return (first[0] - second[0], first[1] - second[1])


def pair_mul(first, second):
    return (first[0] * second[0] - first[1] * second[1], first[0] * second[1] + first[1] * second[0])


def pair_div(first, second):
    scale_sq = second[0] * second[0] + second[1] * second[1]
    return ((first[0] * second[0] + first[1] * second[1]) / scale_sq, (first[1] * second[0] - first[0] * second[1]) / scale_sq)


def quartic_value(point):
    return (((210.0 * point - 480.0) * point + 360.0) * point - 96.0) * point + 6.0


def bisect_root(lower, upper):
    for count in range(200):
        middle = 0.5 * (lower + upper)
        if (quartic_value(lower) < 0.0) == (quartic_value(middle) < 0.0):
            lower = middle
        else:
            upper = middle
    return 0.5 * (lower + upper)


def radau_tables():
    abscissae = []
    grid_steps = 4000
    for m in range(grid_steps):
        lower = 0.999 * m / grid_steps
        upper = 0.999 * (m + 1) / grid_steps
        if (quartic_value(lower) < 0.0) != (quartic_value(upper) < 0.0):
            abscissae.append(bisect_root(lower, upper))
    abscissae.append(1.0)
    vander = [[abscissae[j] ** k for k in range(4)] for j in range(4)]
    moments = [[abscissae[i] ** (k + 1) / (k + 1) for k in range(4)] for i in range(4)]
    tableau = table_product(moments, invert_table(vander))
    inverse = invert_table(tableau)
    running = [list(row_values) for row_values in inverse]
    coeffs = []
    for k in range(1, 5):
        trace_value = sum(running[i][i] for i in range(4))
        coeffs.append(-trace_value / k)
        shifted_table = [[running[i][j] + (coeffs[-1] if i == j else 0.0) for j in range(4)] for i in range(4)]
        running = table_product(inverse, shifted_table)
    start_point = (0.4, 0.9)
    estimates = [(1.0, 0.0)]
    for k in range(3):
        estimates.append(pair_mul(estimates[-1], start_point))
    for count in range(500):
        for i in range(4):
            value = (1.0, 0.0)
            for coef_value in coeffs:
                value = pair_add(pair_mul(value, estimates[i]), (coef_value, 0.0))
            denom = (1.0, 0.0)
            for j in range(4):
                if j != i:
                    denom = pair_mul(denom, pair_sub(estimates[i], estimates[j]))
            estimates[i] = pair_sub(estimates[i], pair_div(value, denom))
    chosen = [m for m in range(4) if estimates[m][1] > 0.0]
    ranking = sorted(chosen, key=lambda m: -estimates[m][1])
    columns = []
    pairs = []
    for m in ranking:
        eigen_pair = estimates[m]
        system = [[(inverse[i][j] - (eigen_pair[0] if i == j else 0.0), -(eigen_pair[1] if i == j else 0.0)) for j in range(4)] for i in range(3)]
        rows_left = [[system[i][j] for j in range(3)] + [(-system[i][3][0], -system[i][3][1])] for i in range(3)]
        for col in range(3):
            pivot_row = max(range(col, 3), key=lambda r: rows_left[r][col][0] ** 2 + rows_left[r][col][1] ** 2)
            rows_left[col], rows_left[pivot_row] = rows_left[pivot_row], rows_left[col]
            leading = rows_left[col][col]
            rows_left[col] = [pair_div(v, leading) for v in rows_left[col]]
            for r in range(3):
                if r != col:
                    factor = rows_left[r][col]
                    rows_left[r] = [pair_sub(a, pair_mul(factor, b)) for a, b in zip(rows_left[r], rows_left[col])]
        vector = [rows_left[i][3] for i in range(3)] + [(1.0, 0.0)]
        columns.append([v[0] for v in vector])
        columns.append([v[1] for v in vector])
        pairs.append((eigen_pair[0], eigen_pair[1]))
    eigen_basis = [[columns[j][i] for j in range(4)] for i in range(4)]
    basis_inverse = invert_table(eigen_basis)
    return tableau, inverse, eigen_basis, basis_inverse, pairs


def center(padded):
    return padded[..., 1:-1, 1:-1, 1:-1]


def shifted(padded, member):
    if member == 0:
        return padded[..., 2:, 1:-1, 1:-1]
    if member == 1:
        return padded[..., :-2, 1:-1, 1:-1]
    if member == 2:
        return padded[..., 1:-1, 2:, 1:-1]
    if member == 3:
        return padded[..., 1:-1, :-2, 1:-1]
    if member == 4:
        return padded[..., 1:-1, 1:-1, 2:]
    return padded[..., 1:-1, 1:-1, :-2]


def face_terms(padded):
    middle = center(padded)
    return [0.5 * (middle + shifted(padded, m)) for m in range(6)]


def face_total(faces):
    total = faces[0]
    for m in range(1, 6):
        total = total + faces[m]
    return total


def neighbour_sum(faces, padded):
    total = faces[0] * shifted(padded, 0)
    for m in range(1, 6):
        total = total + faces[m] * shifted(padded, m)
    return total


def pad_cells(field, width):
    return jnp.pad(field, [(0, 0)] * (field.ndim - 3) + [(width, width)] * 3)


def apply_inverse(diag_real, coupling, determinant, vector):
    first = (diag_real * vector[0] - coupling * vector[1]) / determinant
    second = (coupling * vector[0] + diag_real * vector[1]) / determinant
    return jnp.stack([first, second])


def apply_block(diag_real, coupling, vector):
    return jnp.stack([diag_real * vector[0] + coupling * vector[1], diag_real * vector[1] - coupling * vector[0]])


def combine(coef, fields):
    total = coef[:, 0][:, None, None, None] * fields[0][None]
    for column in range(1, fields.shape[0]):
        total = total + coef[:, column][:, None, None, None] * fields[column][None]
    return total


def reference(previous, sections, diffusivity, reaction):
    tableau, inverse, eigen_basis, basis_inverse, pairs = radau_tables()
    flux_rows = jnp.asarray(basis_inverse, jnp.float32)
    shift_table = table_product(basis_inverse, inverse)
    shift_rows = jnp.asarray([[v / step_size for v in row_values] for row_values in shift_table], jnp.float32)
    section_coef = diffusivity * (1.0 + 0.5 * jnp.tanh(sections))
    section_faces = face_terms(pad_cells(section_coef, 1))
    section_flux = neighbour_sum(section_faces, pad_cells(sections, 1)) - face_total(section_faces) * sections
    section_flux = section_flux + reaction * sections * (1.0 - sections * sections)
    increment = sections - previous
    rhs = combine(flux_rows, section_flux) - combine(shift_rows, increment)
    frozen_coef = diffusivity * (1.0 + 0.5 * jnp.tanh(previous))
    faces = face_terms(pad_cells(frozen_coef, 1))
    react_slope = reaction * (1.0 - 3.0 * previous * previous)
    base_diag = face_total(faces) - react_slope
    solutions = []
    for eigen_block in range(2):
        real_part, imag_part = pairs[eigen_block]
        diag_real = real_part / step_size + base_diag
        coupling = imag_part / step_size
        determinant = diag_real * diag_real + coupling * coupling
        residue = rhs[2 * eigen_block:2 * eigen_block + 2]
        correction = jnp.zeros_like(residue)
        for sweep in range(ITERS):
            scaled = apply_inverse(diag_real, coupling, determinant, residue)
            search = scaled + apply_inverse(diag_real, coupling, determinant, neighbour_sum(faces, pad_cells(scaled, 1)))
            image = apply_block(diag_real, coupling, search) - neighbour_sum(faces, pad_cells(search, 1))
            step_length = jnp.sum(image * residue) / (jnp.sum(image * image) + tiny_value)
            correction = correction + step_length * search
            residue = residue - step_length * image
        solutions.append(correction)
    gathered = jnp.concatenate(solutions, 0)
    return sections + combine(jnp.asarray(eigen_basis, jnp.float32), gathered)
```

```python
import jax
import jax.numpy as jnp
from jax import lax
from jax.sharding import PartitionSpec as P

ITERS = 4


step_size = 1.0
tiny_value = 1e-06


def extended(cells, sides, width):
    for axis, dim in sides:
        count = lax.axis_size(axis)
        ends = count - 1
        head = lax.slice_in_dim(cells, 0, width, axis=dim)
        tail = lax.slice_in_dim(cells, cells.shape[dim] - width, cells.shape[dim], axis=dim)
        cells = jnp.concatenate(
            [
                lax.ppermute(tail, axis, [(i, (i + 1) % count) for i in range(ends)]),
                cells,
                lax.ppermute(head, axis, [((i + 1) % count, i) for i in range(ends)]),
            ],
            axis=dim,
        )
    return cells


def invert_table(matrix):
    order_n = len(matrix)
    augmented = [
        list(matrix[r]) + [1.0 if c == r else 0.0 for c in range(order_n)] for r in range(order_n)
    ]
    for col in range(order_n):
        pivot_row = max(range(col, order_n), key=lambda r: abs(augmented[r][col]))
        augmented[col], augmented[pivot_row] = (augmented[pivot_row], augmented[col])
        leading = augmented[col][col]
        augmented[col] = [v / leading for v in augmented[col]]
        for r in range(order_n):
            if r != col:
                factor = augmented[r][col]
                augmented[r] = [a - factor * b for a, b in zip(augmented[r], augmented[col])]
    return [row_values[order_n:] for row_values in augmented]


def table_product(left, right):
    return [
        [sum((left[i][k] * right[k][j] for k in range(len(right)))) for j in range(len(right[0]))]
        for i in range(len(left))
    ]


def pair_add(first, second):
    return (first[0] + second[0], first[1] + second[1])


def pair_sub(first, second):
    return (first[0] - second[0], first[1] - second[1])


def pair_mul(first, second):
    return (
        first[0] * second[0] - first[1] * second[1],
        first[0] * second[1] + first[1] * second[0],
    )


def pair_div(first, second):
    scale_sq = second[0] * second[0] + second[1] * second[1]
    return (
        (first[0] * second[0] + first[1] * second[1]) / scale_sq,
        (first[1] * second[0] - first[0] * second[1]) / scale_sq,
    )


def quartic_value(point):
    return (((210.0 * point - 480.0) * point + 360.0) * point - 96.0) * point + 6.0


def bisect_root(lower, upper):
    for count in range(200):
        middle = 0.5 * (lower + upper)
        if (quartic_value(lower) < 0.0) == (quartic_value(middle) < 0.0):
            lower = middle
        else:
            upper = middle
    return 0.5 * (lower + upper)


def radau_tables():
    abscissae = []
    grid_steps = 4000
    for m in range(grid_steps):
        lower = 0.999 * m / grid_steps
        upper = 0.999 * (m + 1) / grid_steps
        if (quartic_value(lower) < 0.0) != (quartic_value(upper) < 0.0):
            abscissae.append(bisect_root(lower, upper))
    abscissae.append(1.0)
    vander = [[abscissae[j] ** k for k in range(4)] for j in range(4)]
    moments = [[abscissae[i] ** (k + 1) / (k + 1) for k in range(4)] for i in range(4)]
    tableau = table_product(moments, invert_table(vander))
    inverse = invert_table(tableau)
    running = [list(row_values) for row_values in inverse]
    coeffs = []
    for k in range(1, 5):
        trace_value = sum((running[i][i] for i in range(4)))
        coeffs.append(-trace_value / k)
        shifted_table = [
            [running[i][j] + (coeffs[-1] if i == j else 0.0) for j in range(4)] for i in range(4)
        ]
        running = table_product(inverse, shifted_table)
    start_point = (0.4, 0.9)
    estimates = [(1.0, 0.0)]
    for k in range(3):
        estimates.append(pair_mul(estimates[-1], start_point))
    for count in range(500):
        for i in range(4):
            value = (1.0, 0.0)
            for coef_value in coeffs:
                value = pair_add(pair_mul(value, estimates[i]), (coef_value, 0.0))
            denom = (1.0, 0.0)
            for j in range(4):
                if j != i:
                    denom = pair_mul(denom, pair_sub(estimates[i], estimates[j]))
            estimates[i] = pair_sub(estimates[i], pair_div(value, denom))
    chosen = [m for m in range(4) if estimates[m][1] > 0.0]
    ranking = sorted(chosen, key=lambda m: -estimates[m][1])
    columns = []
    pairs = []
    for m in ranking:
        eigen_pair = estimates[m]
        system = [
            [
                (
                    inverse[i][j] - (eigen_pair[0] if i == j else 0.0),
                    -(eigen_pair[1] if i == j else 0.0),
                )
                for j in range(4)
            ]
            for i in range(3)
        ]
        rows_left = [
            [system[i][j] for j in range(3)] + [(-system[i][3][0], -system[i][3][1])]
            for i in range(3)
        ]
        for col in range(3):
            pivot_row = max(
                range(col, 3), key=lambda r: rows_left[r][col][0] ** 2 + rows_left[r][col][1] ** 2
            )
            rows_left[col], rows_left[pivot_row] = (rows_left[pivot_row], rows_left[col])
            leading = rows_left[col][col]
            rows_left[col] = [pair_div(v, leading) for v in rows_left[col]]
            for r in range(3):
                if r != col:
                    factor = rows_left[r][col]
                    rows_left[r] = [
                        pair_sub(a, pair_mul(factor, b))
                        for a, b in zip(rows_left[r], rows_left[col])
                    ]
        vector = [rows_left[i][3] for i in range(3)] + [(1.0, 0.0)]
        columns.append([v[0] for v in vector])
        columns.append([v[1] for v in vector])
        pairs.append((eigen_pair[0], eigen_pair[1]))
    eigen_basis = [[columns[j][i] for j in range(4)] for i in range(4)]
    basis_inverse = invert_table(eigen_basis)
    return (tableau, inverse, eigen_basis, basis_inverse, pairs)


def center(padded):
    return padded[..., 1:-1, 1:-1, 1:-1]


def shifted(padded, member):
    if member == 0:
        return padded[..., 2:, 1:-1, 1:-1]
    if member == 1:
        return padded[..., :-2, 1:-1, 1:-1]
    if member == 2:
        return padded[..., 1:-1, 2:, 1:-1]
    if member == 3:
        return padded[..., 1:-1, :-2, 1:-1]
    if member == 4:
        return padded[..., 1:-1, 1:-1, 2:]
    return padded[..., 1:-1, 1:-1, :-2]


def face_terms(padded):
    middle = center(padded)
    return [0.5 * (middle + shifted(padded, m)) for m in range(6)]


def face_total(faces):
    total = faces[0]
    for m in range(1, 6):
        total = total + faces[m]
    return total


def neighbour_sum(faces, padded):
    total = faces[0] * shifted(padded, 0)
    for m in range(1, 6):
        total = total + faces[m] * shifted(padded, m)
    return total


def pad_depth(field, width):
    return jnp.pad(field, [(0, 0)] * (field.ndim - 3) + [(width, width), (0, 0), (0, 0)])


def trim_cells(field, width):
    if width == 0:
        return field
    return field[..., width:-width, width:-width, width:-width]


def apply_inverse(diag_real, coupling, determinant, vector):
    first = (diag_real * vector[0] - coupling * vector[1]) / determinant
    second = (coupling * vector[0] + diag_real * vector[1]) / determinant
    return jnp.stack([first, second])


def apply_block(diag_real, coupling, vector):
    return jnp.stack(
        [diag_real * vector[0] + coupling * vector[1], diag_real * vector[1] - coupling * vector[0]]
    )


def combine(coef, fields):
    total = coef[:, 0][:, None, None, None] * fields[0][None]
    for column in range(1, fields.shape[0]):
        total = total + coef[:, column][:, None, None, None] * fields[column][None]
    return total


SHIFTS = (0.0, 0.9, 0.45, 0.7)
HALO = 9


def gram_pairs():
    return [(i, j) for i in range(ITERS + 1) for j in range(i, ITERS + 1)]


def step_weights(gram):
    table = {}
    for at, (i, j) in enumerate(gram_pairs()):
        table[i, j] = table[j, i] = gram[at]
    size = ITERS + 1
    one = jnp.ones_like(gram[0])
    zero = jnp.zeros_like(one)
    coef = [one] + [zero] * (size - 1)
    weight = [zero] * ITERS
    step = one
    for k in range(ITERS):
        moved = [zero] * size
        for j in range(k + 1):
            moved[j + 1] = moved[j + 1] + coef[j]
            moved[j] = moved[j] + SHIFTS[j] * coef[j]
        image = [coef[j] - moved[j] for j in range(size)]
        num, den, bound = zero, zero, zero
        for i in range(k + 2):
            for j in range(k + 2):
                term = image[i] * table[i, j]
                den = den + term * image[j]
                bound = bound + jnp.abs(term * image[j])
                num = num + term * coef[j]
        step = jnp.where(den > bound * 6e-8, num / (jnp.maximum(den, 0.0) + tiny_value), step)
        for j in range(k + 1):
            weight[j] = weight[j] + step * coef[j]
        coef = [coef[j] - step * image[j] for j in range(size)]
    return weight


def body(previous, sections, diffusivity, reaction):
    tableau, inverse, eigen_basis, basis_inverse, pairs = radau_tables()
    flux_rows = jnp.asarray(basis_inverse, jnp.float32)
    shift_table = table_product(basis_inverse, inverse)
    shift_rows = jnp.asarray(
        [[v / step_size for v in row_values] for row_values in shift_table], jnp.float32
    )
    basis_rows = jnp.asarray(eigen_basis, jnp.float32)
    own = lax.axis_index("section")
    every = lax.all_gather(sections, "section", axis=0, tiled=True)
    fields = jnp.concatenate([every, previous[None], diffusivity[None], reaction[None]], 0)
    fields = pad_depth(extended(fields, (("sy", 3), ("sx", 2)), HALO), 1)
    values, prev, diff, react = fields[:4], fields[4], fields[5], fields[6]
    coefs = diff * (1.0 + 0.5 * jnp.tanh(values))
    faces = face_terms(coefs)
    inner = center(values)
    flux = neighbour_sum(faces, values) - face_total(faces) * inner
    flux = flux + center(react) * inner * (1.0 - inner * inner)
    rhs = combine(flux_rows, flux) - combine(shift_rows, inner - center(prev))
    frozen = diff * (1.0 + 0.5 * jnp.tanh(prev))
    faces = face_terms(frozen)
    base = face_total(faces) - center(react * (1.0 - 3.0 * prev * prev))
    inside = center(diff) > 0.0
    extra = HALO - 1

    def crop(a, cut):
        return a[..., :, cut : a.shape[-2] - cut, cut : a.shape[-1] - cut] if cut else a

    sums, grams = [], []
    for block in range(2):
        real, imag = pairs[block]
        diag = real / step_size + base
        imag = imag / step_size
        det = diag * diag + imag * imag
        alpha = jnp.where(inside, diag / det, 0.0)
        beta = jnp.where(inside, imag / det, 0.0)

        def scale(v, cut):
            a, b = crop(alpha, cut), crop(beta, cut)
            return jnp.stack([a * v[0] - b * v[1], b * v[0] + a * v[1]])

        def spread(y, cut):
            cropped = [crop(face, cut + 1) for face in faces]
            return neighbour_sum(cropped, pad_depth(y, 1))

        vector = rhs[2 * block : 2 * block + 2]
        basis = [crop(vector, extra)]
        for j in range(ITERS):
            cut = 2 * j
            first = scale(vector, cut)
            half = spread(first, cut)
            second = scale(half, cut + 1)
            sums.append(crop(first, extra - cut) + crop(second, extra - cut - 1))
            vector = spread(second, cut + 1) - SHIFTS[j] * crop(vector, 2)
            basis.append(crop(vector, extra - cut - 2))
        grams += [jnp.sum(basis[i] * basis[j]) for i, j in gram_pairs()]
    part = jnp.zeros((1, 128), jnp.float32).at[0, : len(grams)].set(jnp.stack(grams))
    peers = lax.axis_size("sx") * lax.axis_size("sy")
    total = lax.all_to_all(jnp.broadcast_to(part[None], (peers, 1, 128)), ("sx", "sy"), 0, 0)
    total = jnp.sum(total, 0)[0]
    count = len(gram_pairs())
    weights = step_weights([jnp.stack([total[at], total[count + at]]) for at in range(count)])
    correction = jnp.concatenate(
        [sum(weights[j][b] * sums[ITERS * b + j] for j in range(ITERS)) for b in range(2)], 0
    )
    own_basis = lax.dynamic_slice(basis_rows, (2 * own, 0), (2, 4))
    return sections + combine(own_basis, correction)


def solution(mesh):
    in_specs = (
        P(None, "sx", "sy"),
        P("section", None, "sx", "sy"),
        P(None, "sx", "sy"),
        P(None, "sx", "sy"),
    )
    out_specs = P("section", None, "sx", "sy")
    return jax.shard_map(body, mesh=mesh, in_specs=in_specs, out_specs=out_specs, check_vma=False)
```

```python
import functools

import jax
import jax.numpy as jnp
from jax import lax
from jax.experimental import pallas as pl
from jax.experimental.pallas import tpu as pltpu
from jax.sharding import PartitionSpec as P

ITERS = 4
SHIFTS = (0.0, 0.9, 0.45, 0.7)
EDGE = 9
LANES = 128
SIZE = ITERS + 1
PAIRS = [(i, j) for i in range(SIZE) for j in range(i, SIZE)]
VMEM_LIMIT = 58 * 1024 * 1024


step_size = 1.0
tiny_value = 1e-06


def invert_table(matrix):
    order_n = len(matrix)
    augmented = [
        list(matrix[r]) + [1.0 if c == r else 0.0 for c in range(order_n)] for r in range(order_n)
    ]
    for col in range(order_n):
        pivot_row = max(range(col, order_n), key=lambda r: abs(augmented[r][col]))
        augmented[col], augmented[pivot_row] = (augmented[pivot_row], augmented[col])
        leading = augmented[col][col]
        augmented[col] = [v / leading for v in augmented[col]]
        for r in range(order_n):
            if r != col:
                factor = augmented[r][col]
                augmented[r] = [a - factor * b for a, b in zip(augmented[r], augmented[col])]
    return [row_values[order_n:] for row_values in augmented]


def table_product(left, right):
    return [
        [sum((left[i][k] * right[k][j] for k in range(len(right)))) for j in range(len(right[0]))]
        for i in range(len(left))
    ]


def pair_add(first, second):
    return (first[0] + second[0], first[1] + second[1])


def pair_sub(first, second):
    return (first[0] - second[0], first[1] - second[1])


def pair_mul(first, second):
    return (
        first[0] * second[0] - first[1] * second[1],
        first[0] * second[1] + first[1] * second[0],
    )


def pair_div(first, second):
    scale_sq = second[0] * second[0] + second[1] * second[1]
    return (
        (first[0] * second[0] + first[1] * second[1]) / scale_sq,
        (first[1] * second[0] - first[0] * second[1]) / scale_sq,
    )


def quartic_value(point):
    return (((210.0 * point - 480.0) * point + 360.0) * point - 96.0) * point + 6.0


def bisect_root(lower, upper):
    for count in range(200):
        middle = 0.5 * (lower + upper)
        if (quartic_value(lower) < 0.0) == (quartic_value(middle) < 0.0):
            lower = middle
        else:
            upper = middle
    return 0.5 * (lower + upper)


def radau_tables():
    abscissae = []
    grid_steps = 4000
    for m in range(grid_steps):
        lower = 0.999 * m / grid_steps
        upper = 0.999 * (m + 1) / grid_steps
        if (quartic_value(lower) < 0.0) != (quartic_value(upper) < 0.0):
            abscissae.append(bisect_root(lower, upper))
    abscissae.append(1.0)
    vander = [[abscissae[j] ** k for k in range(4)] for j in range(4)]
    moments = [[abscissae[i] ** (k + 1) / (k + 1) for k in range(4)] for i in range(4)]
    tableau = table_product(moments, invert_table(vander))
    inverse = invert_table(tableau)
    running = [list(row_values) for row_values in inverse]
    coeffs = []
    for k in range(1, 5):
        trace_value = sum((running[i][i] for i in range(4)))
        coeffs.append(-trace_value / k)
        shifted_table = [
            [running[i][j] + (coeffs[-1] if i == j else 0.0) for j in range(4)] for i in range(4)
        ]
        running = table_product(inverse, shifted_table)
    start_point = (0.4, 0.9)
    estimates = [(1.0, 0.0)]
    for k in range(3):
        estimates.append(pair_mul(estimates[-1], start_point))
    for count in range(500):
        for i in range(4):
            value = (1.0, 0.0)
            for coef_value in coeffs:
                value = pair_add(pair_mul(value, estimates[i]), (coef_value, 0.0))
            denom = (1.0, 0.0)
            for j in range(4):
                if j != i:
                    denom = pair_mul(denom, pair_sub(estimates[i], estimates[j]))
            estimates[i] = pair_sub(estimates[i], pair_div(value, denom))
    chosen = [m for m in range(4) if estimates[m][1] > 0.0]
    ranking = sorted(chosen, key=lambda m: -estimates[m][1])
    columns = []
    pairs = []
    for m in ranking:
        eigen_pair = estimates[m]
        system = [
            [
                (
                    inverse[i][j] - (eigen_pair[0] if i == j else 0.0),
                    -(eigen_pair[1] if i == j else 0.0),
                )
                for j in range(4)
            ]
            for i in range(3)
        ]
        rows_left = [
            [system[i][j] for j in range(3)] + [(-system[i][3][0], -system[i][3][1])]
            for i in range(3)
        ]
        for col in range(3):
            pivot_row = max(
                range(col, 3), key=lambda r: rows_left[r][col][0] ** 2 + rows_left[r][col][1] ** 2
            )
            rows_left[col], rows_left[pivot_row] = (rows_left[pivot_row], rows_left[col])
            leading = rows_left[col][col]
            rows_left[col] = [pair_div(v, leading) for v in rows_left[col]]
            for r in range(3):
                if r != col:
                    factor = rows_left[r][col]
                    rows_left[r] = [
                        pair_sub(a, pair_mul(factor, b))
                        for a, b in zip(rows_left[r], rows_left[col])
                    ]
        vector = [rows_left[i][3] for i in range(3)] + [(1.0, 0.0)]
        columns.append([v[0] for v in vector])
        columns.append([v[1] for v in vector])
        pairs.append((eigen_pair[0], eigen_pair[1]))
    eigen_basis = [[columns[j][i] for j in range(4)] for i in range(4)]
    basis_inverse = invert_table(eigen_basis)
    return (tableau, inverse, eigen_basis, basis_inverse, pairs)


def constants():
    tableau, inverse, eigen_basis, basis_inverse, pairs = radau_tables()
    shift_table = table_product(basis_inverse, inverse)
    shift_rows = [[v / step_size for v in row_values] for row_values in shift_table]
    pairs = [(p[0] / step_size, p[1] / step_size) for p in pairs]
    return eigen_basis, basis_inverse, shift_rows, pairs


def lane_ids(rows):
    return lax.broadcasted_iota(jnp.int32, (rows, LANES), 1)


def turn(cells, amount):
    return pltpu.roll(cells, amount % LANES, cells.ndim - 1)


def edges_kernel(own_ref, prev_ref, diff_ref, react_ref, low_ref, high_ref):
    nz, nx = prev_ref.shape[0], prev_ref.shape[1]
    lanes = lane_ids(nx)
    for z in range(nz // 2):
        low = jnp.zeros((nx, LANES), jnp.float32)
        high = low
        for part in range(2):
            plane = z + part * (nz // 2)
            cells = [own_ref[0, plane], own_ref[1, plane], prev_ref[plane], diff_ref[plane], react_ref[plane]]
            for f, cell in enumerate(cells):
                at = part * 64 + f * EDGE
                here = (lanes >= at) & (lanes < at + EDGE)
                low = jnp.where(here, turn(cell, at), low)
                high = jnp.where(here, turn(cell, at + EDGE), high)
        low_ref[z] = low
        high_ref[z] = high


def rows_kernel(own_ref, other_ref, prev_ref, diff_ref, react_ref, own_left_ref, own_right_ref, other_left_ref, other_right_ref, side_ref, low_ref, high_ref):
    nz, nx = prev_ref.shape[0], prev_ref.shape[1]
    lanes = lane_ids(nx)
    half = nz // 2
    for z in range(nz):
        part, plane = divmod(z, half)
        side = jnp.zeros((nx, LANES), jnp.float32)
        for f in range(7):
            source = (0, 1, 0, 1, 2, 3, 4)[f]
            refs = (other_left_ref, other_right_ref) if f in (2, 3) else (own_left_ref, own_right_ref)
            for right in range(2):
                at = f * 2 * EDGE + right * EDGE
                here = (lanes >= at) & (lanes < at + EDGE)
                side = jnp.where(here, turn(refs[right][plane], at - part * 64 - source * EDGE), side)
        side_ref[z] = side
        cells = [own_ref[0, z], own_ref[1, z], other_ref[0, z], other_ref[1, z], prev_ref[z], diff_ref[z], react_ref[z], side]
        for f, cell in enumerate(cells):
            low_ref[z, 8 * f : 8 * f + 8] = cell[0:8]
            low_ref[z, 64 + f : 65 + f] = cell[8:9]
            high_ref[z, 8 * f : 8 * f + 8] = cell[nx - 8 : nx]
            high_ref[z, 64 + f : 65 + f] = cell[nx - 9 : nx - 8]


ROWS = 48
FIRST, LAST = 8, 40
OWN = slice(16, 32)
WORK = slice(FIRST, LAST)
BEFORE = slice(FIRST - 1, LAST - 1)
AFTER = slice(FIRST + 1, LAST + 1)


def main_kernel(consts, own_ref, other_ref, prev_ref, diff_ref, react_ref, side_ref, from_low_ref, from_high_ref,
                part_ref, sums_ref, val, kap, frozen, slope, rea, prv, fx, fym, fyp, fz, alpha, beta, vec, ya, yb, keep, table):
    eigen_basis, basis_inverse, shift_rows, pairs = consts
    nz, nx = prev_ref.shape[0], prev_ref.shape[1]
    section = lax.axis_index("section")
    lanes = lane_ids(ROWS)
    zero_plane = jnp.zeros((ROWS, LANES), jnp.float32)

    def merged(pair):
        keep_left = lane_ids(pair[0].shape[0]) < 64
        return jnp.where(keep_left, turn(pair[0], -EDGE), turn(pair[1], EDGE))

    for a in range(2):
        for edge in (0, nz + 1):
            frozen[a, edge] = zero_plane
            for f in range(4):
                val[f, a, edge] = zero_plane
                kap[f, a, edge] = zero_plane
                ya[f, a, edge] = zero_plane
                yb[f, a, edge] = zero_plane

    def assemble(z, carry):
        side = side_ref[z]
        low, high = from_low_ref[z], from_high_ref[z]

        def column(main, f):
            tile = lambda t: jnp.broadcast_to(t, (8, LANES))
            if f == 7:
                body = main
            else:
                body = main
            return jnp.concatenate(
                [tile(low[64 + f : 65 + f]), low[8 * f : 8 * f + 8], body, high[8 * f : 8 * f + 8], tile(high[64 + f : 65 + f])], 0
            )

        sides = column(side, 7)

        def split(main, f):
            cells = column(main, f)
            at = 2 * EDGE * f
            left = jnp.where(lanes < EDGE, turn(sides, -at), turn(cells, EDGE))
            right = jnp.where(lanes >= LANES - EDGE, turn(sides, LANES - 2 * EDGE - at), turn(cells, -EDGE))
            return left, right

        diffs = split(diff_ref[z], 5)
        prevs = split(prev_ref[z], 4)
        reacts = split(react_ref[z], 6)
        for a in range(2):
            frozen[a, z + 1] = diffs[a] * (0.5 + 0.25 * jnp.tanh(prevs[a]))
            slope[a, z] = (reacts[a] * (1.0 - 3.0 * prevs[a] * prevs[a]))[WORK]
            rea[a, z] = reacts[a][WORK]
            prv[a, z] = prevs[a][WORK]
            inside = jnp.where(diffs[a] > 0.0, 1.0, 0.0)
            alpha[0, a, z] = inside[WORK]
        for f in range(4):
            main = own_ref[f, z] if f < 2 else other_ref[f - 2, z]
            values = split(main, f)
            for a in range(2):
                val[f, a, z + 1] = values[a]
                kap[f, a, z + 1] = diffs[a] * (0.5 + 0.25 * jnp.tanh(values[a]))
        return carry

    lax.fori_loop(0, nz, assemble, 0)

    def pick(matrix, m, j):
        first, second = matrix[m][j], matrix[m][(j + 2) % 4]
        return jnp.where(section == 0, jnp.float32(first), jnp.float32(second))

    q_rows = [[pick(basis_inverse, m, j) for j in range(4)] for m in range(4)]
    c_rows = [[pick(shift_rows, m, j) for j in range(4)] for m in range(4)]

    def prepare(z, carry):
        starts = []
        for a in range(2):
            mid = frozen[a, z + 1, WORK]
            f_xm = mid + frozen[a, z + 1, BEFORE]
            f_xp = mid + frozen[a, z + 1, AFTER]
            f_ym = mid + turn(mid, 1)
            f_yp = mid + turn(mid, -1)
            f_zm = mid + frozen[a, z, WORK]
            f_zp = mid + frozen[a, z + 2, WORK]
            fx[0, a, z] = f_xm
            fx[1, a, z] = f_xp
            fym[a, z] = f_ym
            fyp[a, z] = f_yp
            fz[0, a, z] = f_zm
            fz[1, a, z] = f_zp
            base = ((f_xm + f_xp) + (f_ym + f_yp)) + (f_zm + f_zp) - slope[a, z]
            inside = alpha[0, a, z]
            for b in range(2):
                real, imag = pairs[b]
                diag = base + real
                scale = inside / (diag * diag + imag * imag)
                alpha[b, a, z] = diag * scale
                beta[b, a, z] = imag * scale
            prev = prv[a, z]
            react = rea[a, z]
            rhs = [None] * 4
            for j in range(4):
                v = val[j, a, z + 1, WORK]
                k = kap[j, a, z + 1, WORK]
                flux = react * v * (1.0 - v * v)
                flux = flux + (k + kap[j, a, z + 1, BEFORE]) * (val[j, a, z + 1, BEFORE] - v)
                flux = flux + (k + kap[j, a, z + 1, AFTER]) * (val[j, a, z + 1, AFTER] - v)
                flux = flux + (k + turn(k, 1)) * (turn(v, 1) - v)
                flux = flux + (k + turn(k, -1)) * (turn(v, -1) - v)
                flux = flux + (k + kap[j, a, z, WORK]) * (val[j, a, z, WORK] - v)
                flux = flux + (k + kap[j, a, z + 2, WORK]) * (val[j, a, z + 2, WORK] - v)
                grown = v - prev
                for m in range(4):
                    term = q_rows[m][j] * flux - c_rows[m][j] * grown
                    rhs[m] = term if j == 0 else rhs[m] + term
            for m in range(4):
                vec[m, a, z] = rhs[m]
            for b in range(2):
                al, be = alpha[b, a, z], beta[b, a, z]
                ya[2 * b, a, z + 1, WORK] = al * rhs[2 * b] - be * rhs[2 * b + 1]
                ya[2 * b + 1, a, z + 1, WORK] = be * rhs[2 * b] + al * rhs[2 * b + 1]
            starts.append([r[8:24] for r in rhs])
        for m in range(4):
            keep[0, m, z] = merged([starts[0][m], starts[1][m]])
        for a in range(2):
            for m in range(4):
                for ref in (ya, yb):
                    ref[m, a, z + 1, 0:FIRST] = jnp.zeros((FIRST, LANES), jnp.float32)
                    ref[m, a, z + 1, LAST:ROWS] = jnp.zeros((ROWS - LAST, LANES), jnp.float32)
        return carry

    lax.fori_loop(0, nz, prepare, 0)

    def spread(ref, m, a, z, rows=WORK):
        lo, hi = rows.start, rows.stop
        cut = slice(lo - FIRST, hi - FIRST)
        mid = ref[m, a, z + 1, lo:hi]
        total = fx[0, a, z, cut] * ref[m, a, z + 1, lo - 1 : hi - 1]
        total = total + fx[1, a, z, cut] * ref[m, a, z + 1, lo + 1 : hi + 1]
        total = total + fym[a, z, cut] * turn(mid, 1)
        total = total + fyp[a, z, cut] * turn(mid, -1)
        total = total + fz[0, a, z, cut] * ref[m, a, z, lo:hi]
        return total + fz[1, a, z, cut] * ref[m, a, z + 2, lo:hi]

    for j in range(ITERS):

        def odd(z, carry, j=j):
            done = [[None] * 4, [None] * 4]
            for a in range(2):
                for b in range(2):
                    t0 = spread(ya, 2 * b, a, z)
                    t1 = spread(ya, 2 * b + 1, a, z)
                    al, be = alpha[b, a, z], beta[b, a, z]
                    y0 = al * t0 - be * t1
                    y1 = be * t0 + al * t1
                    yb[2 * b, a, z + 1, WORK] = y0
                    yb[2 * b + 1, a, z + 1, WORK] = y1
                    done[a][2 * b] = ya[2 * b, a, z + 1, OWN] + y0[8:24]
                    done[a][2 * b + 1] = ya[2 * b + 1, a, z + 1, OWN] + y1[8:24]
            for m in range(4):
                sums_ref[j, m, z] = merged([done[0][m], done[1][m]])
            return carry

        def even(z, carry, j=j):
            last = j == ITERS - 1
            done = [[None] * 4, [None] * 4]
            rows = OWN if last else WORK
            cut = slice(rows.start - FIRST, rows.stop - FIRST)
            for a in range(2):
                for b in range(2):
                    new = []
                    for m in (2 * b, 2 * b + 1):
                        v = spread(yb, m, a, z, rows)
                        if SHIFTS[j]:
                            v = v - SHIFTS[j] * vec[m, a, z, cut]
                        new.append(v)
                        done[a][m] = v if last else v[8:24]
                    if not last:
                        al, be = alpha[b, a, z], beta[b, a, z]
                        vec[2 * b, a, z] = new[0]
                        vec[2 * b + 1, a, z] = new[1]
                        ya[2 * b, a, z + 1, WORK] = al * new[0] - be * new[1]
                        ya[2 * b + 1, a, z + 1, WORK] = be * new[0] + al * new[1]
            for m in range(4):
                keep[j + 1, m, z] = merged([done[0][m], done[1][m]])
            return carry

        lax.fori_loop(0, nz, odd, 0)
        lax.fori_loop(0, nz, even, 0)

    table[...] = jnp.zeros((LANES, LANES), jnp.float32)
    for b in range(2):

        def dots(z, carry):
            out = list(carry)
            for m in (2 * b, 2 * b + 1):
                for r in range(0, nx, 8):
                    cells = [keep[i, m, z, r : r + 8] for i in range(SIZE)]
                    for at, (i, j) in enumerate(PAIRS):
                        out[at] = out[at] + cells[i] * cells[j]
            return tuple(out)

        zero = jnp.zeros((8, LANES), jnp.float32)
        out = lax.fori_loop(0, nz, dots, tuple(zero for _ in PAIRS))
        for at in range(len(PAIRS)):
            table[b * len(PAIRS) + at : b * len(PAIRS) + at + 1] = jnp.sum(out[at], axis=0, keepdims=True)
    total = jnp.sum(table[...].T, axis=0, keepdims=True)
    part_ref[...] = jnp.broadcast_to(total, part_ref.shape)


def step_weights(gram):
    table = {}
    for at, (i, j) in enumerate(PAIRS):
        table[i, j] = table[j, i] = gram[at]
    coef = [jnp.ones_like(gram[0])]
    weight = []
    step = coef[0]
    for k in range(ITERS):
        moved = [SHIFTS[j] * coef[j] for j in range(k + 1)] + [jnp.zeros_like(step)]
        for j in range(k + 1):
            moved[j + 1] = moved[j + 1] + coef[j]
        coef = coef + [jnp.zeros_like(step)]
        image = [coef[j] - moved[j] for j in range(k + 2)]
        num, den, bound = 0.0, 0.0, 0.0
        for i in range(k + 2):
            row, size = 0.0, 0.0
            for j in range(k + 2):
                term = table[i, j] * image[j]
                row = row + term
                size = size + jnp.abs(term)
            num = num + row * coef[i]
            den = den + row * image[i]
            bound = bound + size * jnp.abs(image[i])
        step = jnp.where(den > bound * 6e-8, num / (jnp.maximum(den, 0.0) + tiny_value), step)
        weight = weight + [jnp.zeros_like(step)]
        for j in range(k + 1):
            weight[j] = weight[j] + step * coef[j]
        coef = [coef[j] - step * image[j] for j in range(k + 2)]
    return weight


def finish_kernel(consts, total_ref, sums_ref, own_ref, out_ref):
    eigen_basis = consts[0]
    nz, nx = own_ref.shape[1], own_ref.shape[2]
    section = lax.axis_index("section")
    total = jnp.sum(total_ref[...], axis=0, keepdims=True)
    count = len(PAIRS)
    weights = []
    for b in range(2):
        gram = [jnp.broadcast_to(total[:, b * count + at : b * count + at + 1], (1, LANES)) for at in range(count)]
        weights.append(step_weights(gram))
    basis = [
        [jnp.where(section == 0, jnp.float32(eigen_basis[r][m]), jnp.float32(eigen_basis[2 + r][m])) for m in range(4)]
        for r in range(2)
    ]

    def combine(z, carry):
        outs = [own_ref[0, z], own_ref[1, z]]
        for m in range(4):
            field = 0.0
            for j in range(ITERS):
                field = field + weights[m // 2][j] * sums_ref[j, m, z]
            outs = [outs[r] + basis[r][m] * field for r in range(2)]
        out_ref[0, z] = outs[0]
        out_ref[1, z] = outs[1]
        return carry

    lax.fori_loop(0, nz, combine, 0)


def call(kernel, outs, scratch=(), flops=1_000_000, name=None):
    many = isinstance(outs, list)
    shapes = [jax.ShapeDtypeStruct(o, jnp.float32) for o in (outs if many else [outs])]

    def run(*args):
        moved = 4 * sum(int(a.size) for a in args) + 4 * sum(int(functools.reduce(lambda p, q: p * q, s.shape, 1)) for s in shapes)
        return pl.pallas_call(
            kernel,
            out_shape=shapes if many else shapes[0],
            in_specs=[pl.BlockSpec(memory_space=pltpu.VMEM)] * len(args),
            out_specs=[pl.BlockSpec(memory_space=pltpu.VMEM)] * len(shapes) if many else pl.BlockSpec(memory_space=pltpu.VMEM),
            scratch_shapes=[pltpu.VMEM(s, jnp.float32) for s in scratch],
            compiler_params=pltpu.CompilerParams(vmem_limit_bytes=VMEM_LIMIT),
            cost_estimate=pl.CostEstimate(flops=flops, bytes_accessed=moved, transcendentals=0),
            name=name,
        )(*args)

    return run


def neighbours(count, step):
    return [(i, i + step) for i in range(count) if 0 <= i + step < count]


def crossed(count, step):
    return [
        (s * count + i, (1 - s) * count + i + step) for s in range(2) for i in range(count) if 0 <= i + step < count
    ]


def body(previous, sections, diffusivity, reaction):
    consts = constants()
    nz, nx, ny = previous.shape
    columns, rows = lax.axis_size("sy"), lax.axis_size("sx")
    other = lax.ppermute(sections, "section", [(0, 1), (1, 0)])
    edge = (nz // 2, nx, ny)
    low, high = call(edges_kernel, [edge, edge], name="edges")(sections, previous, diffusivity, reaction)
    own_left = lax.ppermute(high, "sy", neighbours(columns, 1))
    own_right = lax.ppermute(low, "sy", neighbours(columns, -1))
    other_left = lax.ppermute(high, ("section", "sy"), crossed(columns, 1))
    other_right = lax.ppermute(low, ("section", "sy"), crossed(columns, -1))
    side, low_rows, high_rows = call(rows_kernel, [(nz, nx, ny), (nz, 72, ny), (nz, 72, ny)], name="rows")(
        sections, other, previous, diffusivity, reaction, own_left, own_right, other_left, other_right
    )
    from_low = lax.ppermute(high_rows, "sx", neighbours(rows, 1))
    from_high = lax.ppermute(low_rows, "sx", neighbours(rows, -1))
    peers = columns * rows
    padded, work = (2, nz + 2, ROWS, ny), (2, nz, LAST - FIRST, ny)
    scratch = [
        (4,) + padded, (4,) + padded, padded, work, work, work,
        (2,) + work, work, work, (2,) + work, (2,) + work, (2,) + work,
        (4,) + work, (4,) + padded, (4,) + padded, (SIZE, 4, nz, nx, ny), (LANES, LANES),
    ]
    part, sums = call(
        functools.partial(main_kernel, consts), [(peers, LANES), (ITERS, 4, nz, nx, ny)], scratch, 50_000_000, name="main"
    )(sections, other, previous, diffusivity, reaction, side, from_low, from_high)
    total = lax.all_to_all(part.reshape(peers, 1, LANES), ("sx", "sy"), 0, 0).reshape(peers, LANES)
    return call(functools.partial(finish_kernel, consts), sections.shape, name="finish")(total, sums, sections)


def solution(mesh):
    in_specs = (
        P(None, "sx", "sy"),
        P("section", None, "sx", "sy"),
        P(None, "sx", "sy"),
        P(None, "sx", "sy"),
    )
    out_specs = P("section", None, "sx", "sy")
    return jax.shard_map(body, mesh=mesh, in_specs=in_specs, out_specs=out_specs, check_vma=False)
```

```python
import functools

import jax
import jax.numpy as jnp
from jax import lax
from jax.experimental import pallas as pl
from jax.experimental.pallas import tpu as pltpu
from jax.sharding import PartitionSpec as P

ITERS = 4
SHIFTS = (0.0, 0.9, 0.45, 0.7)
EDGE = 9
LANES = 128
SIZE = ITERS + 1
PAIRS = [(i, j) for i in range(SIZE) for j in range(i, SIZE)]
PREPARE_UNROLL = 1
STEP_UNROLL = 2
VMEM_LIMIT = 58 * 1024 * 1024


step_size = 1.0
tiny_value = 1e-06


def invert_table(matrix):
    order_n = len(matrix)
    augmented = [
        list(matrix[r]) + [1.0 if c == r else 0.0 for c in range(order_n)] for r in range(order_n)
    ]
    for col in range(order_n):
        pivot_row = max(range(col, order_n), key=lambda r: abs(augmented[r][col]))
        augmented[col], augmented[pivot_row] = (augmented[pivot_row], augmented[col])
        leading = augmented[col][col]
        augmented[col] = [v / leading for v in augmented[col]]
        for r in range(order_n):
            if r != col:
                factor = augmented[r][col]
                augmented[r] = [a - factor * b for a, b in zip(augmented[r], augmented[col])]
    return [row_values[order_n:] for row_values in augmented]


def table_product(left, right):
    return [
        [sum((left[i][k] * right[k][j] for k in range(len(right)))) for j in range(len(right[0]))]
        for i in range(len(left))
    ]


def pair_add(first, second):
    return (first[0] + second[0], first[1] + second[1])


def pair_sub(first, second):
    return (first[0] - second[0], first[1] - second[1])


def pair_mul(first, second):
    return (
        first[0] * second[0] - first[1] * second[1],
        first[0] * second[1] + first[1] * second[0],
    )


def pair_div(first, second):
    scale_sq = second[0] * second[0] + second[1] * second[1]
    return (
        (first[0] * second[0] + first[1] * second[1]) / scale_sq,
        (first[1] * second[0] - first[0] * second[1]) / scale_sq,
    )


def quartic_value(point):
    return (((210.0 * point - 480.0) * point + 360.0) * point - 96.0) * point + 6.0


def bisect_root(lower, upper):
    for count in range(200):
        middle = 0.5 * (lower + upper)
        if (quartic_value(lower) < 0.0) == (quartic_value(middle) < 0.0):
            lower = middle
        else:
            upper = middle
    return 0.5 * (lower + upper)


def radau_tables():
    abscissae = []
    grid_steps = 4000
    for m in range(grid_steps):
        lower = 0.999 * m / grid_steps
        upper = 0.999 * (m + 1) / grid_steps
        if (quartic_value(lower) < 0.0) != (quartic_value(upper) < 0.0):
            abscissae.append(bisect_root(lower, upper))
    abscissae.append(1.0)
    vander = [[abscissae[j] ** k for k in range(4)] for j in range(4)]
    moments = [[abscissae[i] ** (k + 1) / (k + 1) for k in range(4)] for i in range(4)]
    tableau = table_product(moments, invert_table(vander))
    inverse = invert_table(tableau)
    running = [list(row_values) for row_values in inverse]
    coeffs = []
    for k in range(1, 5):
        trace_value = sum((running[i][i] for i in range(4)))
        coeffs.append(-trace_value / k)
        shifted_table = [
            [running[i][j] + (coeffs[-1] if i == j else 0.0) for j in range(4)] for i in range(4)
        ]
        running = table_product(inverse, shifted_table)
    start_point = (0.4, 0.9)
    estimates = [(1.0, 0.0)]
    for k in range(3):
        estimates.append(pair_mul(estimates[-1], start_point))
    for count in range(500):
        for i in range(4):
            value = (1.0, 0.0)
            for coef_value in coeffs:
                value = pair_add(pair_mul(value, estimates[i]), (coef_value, 0.0))
            denom = (1.0, 0.0)
            for j in range(4):
                if j != i:
                    denom = pair_mul(denom, pair_sub(estimates[i], estimates[j]))
            estimates[i] = pair_sub(estimates[i], pair_div(value, denom))
    chosen = [m for m in range(4) if estimates[m][1] > 0.0]
    ranking = sorted(chosen, key=lambda m: -estimates[m][1])
    columns = []
    pairs = []
    for m in ranking:
        eigen_pair = estimates[m]
        system = [
            [
                (
                    inverse[i][j] - (eigen_pair[0] if i == j else 0.0),
                    -(eigen_pair[1] if i == j else 0.0),
                )
                for j in range(4)
            ]
            for i in range(3)
        ]
        rows_left = [
            [system[i][j] for j in range(3)] + [(-system[i][3][0], -system[i][3][1])]
            for i in range(3)
        ]
        for col in range(3):
            pivot_row = max(
                range(col, 3), key=lambda r: rows_left[r][col][0] ** 2 + rows_left[r][col][1] ** 2
            )
            rows_left[col], rows_left[pivot_row] = (rows_left[pivot_row], rows_left[col])
            leading = rows_left[col][col]
            rows_left[col] = [pair_div(v, leading) for v in rows_left[col]]
            for r in range(3):
                if r != col:
                    factor = rows_left[r][col]
                    rows_left[r] = [
                        pair_sub(a, pair_mul(factor, b))
                        for a, b in zip(rows_left[r], rows_left[col])
                    ]
        vector = [rows_left[i][3] for i in range(3)] + [(1.0, 0.0)]
        columns.append([v[0] for v in vector])
        columns.append([v[1] for v in vector])
        pairs.append((eigen_pair[0], eigen_pair[1]))
    eigen_basis = [[columns[j][i] for j in range(4)] for i in range(4)]
    basis_inverse = invert_table(eigen_basis)
    return (tableau, inverse, eigen_basis, basis_inverse, pairs)


def constants():
    tableau, inverse, eigen_basis, basis_inverse, pairs = radau_tables()
    shift_table = table_product(basis_inverse, inverse)
    shift_rows = [[v / step_size for v in row_values] for row_values in shift_table]
    pairs = [(p[0] / step_size, p[1] / step_size) for p in pairs]
    return eigen_basis, basis_inverse, shift_rows, pairs


def lane_ids(rows):
    return lax.broadcasted_iota(jnp.int32, (rows, LANES), 1)


def turn(cells, amount):
    return pltpu.roll(cells, amount % LANES, cells.ndim - 1)


def half_mask(rows, section):
    return (lane_ids(rows) < LANES // 2) == (section == 0)


def edges_kernel(own_ref, prev_ref, diff_ref, react_ref, same_ref, cross_ref):
    nz, nx = prev_ref.shape[0], prev_ref.shape[1]
    lanes = lane_ids(nx)
    first = lax.axis_index("section") == 0
    high, low = LANES - EDGE, 0
    same_from = jnp.where(first, high, low)
    cross_from = jnp.where(first, low, high)

    def pack(ref, start, slot, fields):
        parts = LANES // slot
        planes = nz // parts
        for z in range(planes):
            tile = jnp.zeros((nx, LANES), jnp.float32)
            for part in range(parts):
                for f, load in enumerate(fields):
                    at = part * slot + f * EDGE
                    moved = pltpu.roll(load(part * planes + z), lax.rem(at + LANES - start, LANES), 1)
                    tile = jnp.where((lanes >= at) & (lanes < at + EDGE), moved, tile)
            ref[z] = tile

    sections = [lambda z: own_ref[0, z], lambda z: own_ref[1, z]]
    others = [lambda z: prev_ref[z], lambda z: diff_ref[z], lambda z: react_ref[z]]
    pack(same_ref, same_from, 64, sections + others)
    pack(cross_ref, cross_from, 32, sections)


def rows_kernel(own_ref, other_ref, prev_ref, diff_ref, react_ref, same_ref, cross_ref, ring_ref, low_ref, high_ref):
    nz, nx = prev_ref.shape[0], prev_ref.shape[1]
    lanes = lane_ids(nx)
    first = lax.axis_index("section") == 0
    to = jnp.where(first, LANES - EDGE, 0)
    border = (lanes >= to) & (lanes < to + EDGE)

    def unpack(ref, slot, f, z):
        planes = nz // (LANES // slot)
        part, plane = divmod(z, planes)
        at = part * slot + f * EDGE
        return pltpu.roll(ref[plane], lax.rem(to + LANES - at, LANES), 1)

    for z in range(nz):
        cells = [own_ref[0, z], own_ref[1, z], other_ref[0, z], other_ref[1, z], prev_ref[z], diff_ref[z], react_ref[z]]
        for f, cell in enumerate(cells):
            side = unpack(cross_ref, 32, f - 2, z) if f in (2, 3) else unpack(same_ref, 64, (0, 1, 0, 0, 2, 3, 4)[f], z)
            cell = jnp.where(border, side, cell)
            ring_ref[f, z] = cell
            low_ref[z, 8 * f : 8 * f + 8] = cell[0:8]
            low_ref[z, 56 + f : 57 + f] = cell[8:9]
            high_ref[z, 8 * f : 8 * f + 8] = cell[nx - 8 : nx]
            high_ref[z, 56 + f : 57 + f] = cell[nx - 9 : nx - 8]
        low_ref[z, 63:64] = jnp.zeros((1, LANES), jnp.float32)
        high_ref[z, 63:64] = jnp.zeros((1, LANES), jnp.float32)


ROWS = 48
FIRST, LAST = 8, 40
OWN = slice(16, 32)
WORK = slice(FIRST, LAST)
BEFORE = slice(FIRST - 1, LAST - 1)
AFTER = slice(FIRST + 1, LAST + 1)


def each_plane(count, unroll, work):
    def group(i, carry):
        for u in range(unroll):
            work(i * unroll + u)
        return carry

    lax.fori_loop(0, count // unroll, group, 0)


def main_kernel(consts, ring_ref, from_low_ref, from_high_ref, part_ref, sums_ref,
                val, kap, frozen, fx, fy, fz, alpha, beta, vec, ya, yb, table):
    eigen_basis, basis_inverse, shift_rows, pairs = consts
    nz = ring_ref.shape[1]
    section = lax.axis_index("section")
    zero_plane = jnp.zeros((ROWS, LANES), jnp.float32)
    zero_rows = jnp.zeros((FIRST, LANES), jnp.float32)

    for edge in (0, nz + 1):
        frozen[edge] = zero_plane
        for f in range(4):
            for ref in (val, kap, ya, yb):
                ref[f, edge] = zero_plane

    def column(f, z):
        tile = lambda t: jnp.broadcast_to(t, (8, LANES))
        low, high = from_low_ref, from_high_ref
        return jnp.concatenate(
            [tile(low[z, 56 + f : 57 + f]), low[z, 8 * f : 8 * f + 8], ring_ref[f, z], high[z, 8 * f : 8 * f + 8], tile(high[z, 56 + f : 57 + f])], 0
        )

    def assemble(z):
        diff = column(5, z)
        frozen[z + 1] = diff * (0.5 + 0.25 * jnp.tanh(column(4, z)))
        for f in range(4):
            value = column(f, z)
            val[f, z + 1] = value
            kap[f, z + 1] = diff * (0.5 + 0.25 * jnp.tanh(value))
            for ref in (ya, yb):
                ref[f, z + 1, 0:FIRST] = zero_rows
                ref[f, z + 1, LAST:ROWS] = zero_rows

    each_plane(nz, 1, assemble)

    def pick(matrix, m, j):
        return jnp.where(section == 0, jnp.float32(matrix[m][j]), jnp.float32(matrix[m][(j + 2) % 4]))

    q_rows = [[pick(basis_inverse, m, j) for j in range(4)] for m in range(4)]
    c_rows = [[pick(shift_rows, m, j) for j in range(4)] for m in range(4)]

    def prepare(z):
        def middle(f):
            return jnp.concatenate([from_low_ref[z, 8 * f : 8 * f + 8], ring_ref[f, z], from_high_ref[z, 8 * f : 8 * f + 8]], 0)

        mid = frozen[z + 1, WORK]
        faces = [
            mid + frozen[z + 1, BEFORE], mid + frozen[z + 1, AFTER], mid + turn(mid, 1), mid + turn(mid, -1),
            mid + frozen[z, WORK], mid + frozen[z + 2, WORK],
        ]
        for at, ref in enumerate((fx, fy, fz)):
            ref[0, z] = faces[2 * at]
            ref[1, z] = faces[2 * at + 1]
        prev, react = middle(4), middle(6)
        base = ((faces[0] + faces[1]) + (faces[2] + faces[3])) + (faces[4] + faces[5]) - react * (1.0 - 3.0 * prev * prev)
        inside = jnp.where(middle(5) > 0.0, 1.0, 0.0)
        scaled = []
        for b in range(2):
            real, imag = pairs[b]
            diag = base + real
            scale = inside / (diag * diag + imag * imag)
            scaled.append((diag * scale, imag * scale))
            alpha[b, z], beta[b, z] = scaled[b]
        rhs = [None] * 4
        for j in range(4):
            v = val[j, z + 1, WORK]
            k = kap[j, z + 1, WORK]
            flux = react * v * (1.0 - v * v)
            flux = flux + (k + kap[j, z + 1, BEFORE]) * (val[j, z + 1, BEFORE] - v)
            flux = flux + (k + kap[j, z + 1, AFTER]) * (val[j, z + 1, AFTER] - v)
            flux = flux + (k + turn(k, 1)) * (turn(v, 1) - v)
            flux = flux + (k + turn(k, -1)) * (turn(v, -1) - v)
            flux = flux + (k + kap[j, z, WORK]) * (val[j, z, WORK] - v)
            flux = flux + (k + kap[j, z + 2, WORK]) * (val[j, z + 2, WORK] - v)
            grown = v - prev
            for m in range(4):
                term = q_rows[m][j] * flux - c_rows[m][j] * grown
                rhs[m] = term if j == 0 else rhs[m] + term
        for m in range(4):
            vec[0, m, z] = rhs[m]
        for b in range(2):
            al, be = scaled[b]
            ya[2 * b, z + 1, WORK] = al * rhs[2 * b] - be * rhs[2 * b + 1]
            ya[2 * b + 1, z + 1, WORK] = be * rhs[2 * b] + al * rhs[2 * b + 1]

    each_plane(nz, PREPARE_UNROLL, prepare)

    def spread(ref, m, z, rows=WORK):
        lo, hi = rows.start, rows.stop
        cut = slice(lo - FIRST, hi - FIRST)
        mid = ref[m, z + 1, lo:hi]
        in_y = fy[0, z, cut] * turn(mid, 1) + fy[1, z, cut] * turn(mid, -1)
        in_x = fx[0, z, cut] * ref[m, z + 1, lo - 1 : hi - 1] + fx[1, z, cut] * ref[m, z + 1, lo + 1 : hi + 1]
        in_z = fz[0, z, cut] * ref[m, z, lo:hi] + fz[1, z, cut] * ref[m, z + 2, lo:hi]
        return (in_x + in_z) + in_y

    for j in range(ITERS):

        def odd(z, j=j):
            for b in range(2):
                t0 = spread(ya, 2 * b, z)
                t1 = spread(ya, 2 * b + 1, z)
                al, be = alpha[b, z], beta[b, z]
                y0 = al * t0 - be * t1
                y1 = be * t0 + al * t1
                yb[2 * b, z + 1, WORK] = y0
                yb[2 * b + 1, z + 1, WORK] = y1
                sums_ref[j, 2 * b, z] = ya[2 * b, z + 1, OWN] + y0[8:24]
                sums_ref[j, 2 * b + 1, z] = ya[2 * b + 1, z + 1, OWN] + y1[8:24]

        def even(z, j=j):
            last = j == ITERS - 1
            rows = OWN if last else WORK
            cut = slice(rows.start - FIRST, rows.stop - FIRST)
            for b in range(2):
                new = []
                for m in (2 * b, 2 * b + 1):
                    v = spread(yb, m, z, rows)
                    if SHIFTS[j]:
                        v = v - SHIFTS[j] * vec[j, m, z, cut]
                    vec[j + 1, m, z, cut] = v
                    new.append(v)
                if not last:
                    al, be = alpha[b, z], beta[b, z]
                    ya[2 * b, z + 1, WORK] = al * new[0] - be * new[1]
                    ya[2 * b + 1, z + 1, WORK] = be * new[0] + al * new[1]

        each_plane(nz, STEP_UNROLL, odd)
        each_plane(nz, STEP_UNROLL, even)

    table[...] = jnp.zeros((LANES, LANES), jnp.float32)
    mine = half_mask(8, section)
    for b in range(2):

        def dots(z, carry):
            out = list(carry)
            for m in (2 * b, 2 * b + 1):
                for r in (8, 16):
                    cells = [vec[i, m, z, r : r + 8] for i in range(SIZE)]
                    for at, (i, j) in enumerate(PAIRS):
                        out[at] = out[at] + cells[i] * cells[j]
            return tuple(out)

        zero = jnp.zeros((8, LANES), jnp.float32)
        out = lax.fori_loop(0, nz, dots, tuple(zero for _ in PAIRS))
        for at in range(len(PAIRS)):
            row = jnp.sum(jnp.where(mine, out[at], 0.0), axis=0, keepdims=True)
            table[b * len(PAIRS) + at : b * len(PAIRS) + at + 1] = row
    total = jnp.sum(table[...].T, axis=0, keepdims=True)
    part_ref[...] = jnp.broadcast_to(total, part_ref.shape)


def step_weights(gram):
    table = {}
    for at, (i, j) in enumerate(PAIRS):
        table[i, j] = table[j, i] = gram[at]
    coef = [jnp.ones_like(gram[0])]
    weight = []
    step = coef[0]
    for k in range(ITERS):
        moved = [SHIFTS[j] * coef[j] for j in range(k + 1)] + [jnp.zeros_like(step)]
        for j in range(k + 1):
            moved[j + 1] = moved[j + 1] + coef[j]
        coef = coef + [jnp.zeros_like(step)]
        image = [coef[j] - moved[j] for j in range(k + 2)]
        num, den, bound = 0.0, 0.0, 0.0
        for i in range(k + 2):
            row, size = 0.0, 0.0
            for j in range(k + 2):
                term = table[i, j] * image[j]
                row = row + term
                size = size + jnp.abs(term)
            num = num + row * coef[i]
            den = den + row * image[i]
            bound = bound + size * jnp.abs(image[i])
        step = jnp.where(den > bound * 6e-8, num / (jnp.maximum(den, 0.0) + tiny_value), step)
        weight = weight + [jnp.zeros_like(step)]
        for j in range(k + 1):
            weight[j] = weight[j] + step * coef[j]
        coef = [coef[j] - step * image[j] for j in range(k + 2)]
    return weight


def finish_kernel(consts, total_ref, sums_ref, ring_ref, mine_ref, send_ref):
    eigen_basis = consts[0]
    nz, nx = mine_ref.shape[1], mine_ref.shape[2]
    section = lax.axis_index("section")
    total = jnp.sum(total_ref[...], axis=0, keepdims=True)
    count = len(PAIRS)
    weights = []
    for b in range(2):
        gram = [jnp.broadcast_to(total[:, b * count + at : b * count + at + 1], (1, LANES)) for at in range(count)]
        weights.append(step_weights(gram))
    basis = [
        [jnp.where(section == 0, jnp.float32(eigen_basis[r][m]), jnp.float32(eigen_basis[(r + 2) % 4][m])) for m in range(4)]
        for r in range(4)
    ]
    mine = half_mask(nx, section)

    def combine(z):
        outs = [ring_ref[r, z] for r in range(4)]
        for m in range(4):
            field = weights[m // 2][0] * sums_ref[0, m, z]
            for j in range(1, ITERS):
                field = field + weights[m // 2][j] * sums_ref[j, m, z]
            outs = [outs[r] + basis[r][m] * field for r in range(4)]
        mine_ref[0, z] = outs[0]
        mine_ref[1, z] = outs[1]
        send_ref[z] = jnp.where(mine, outs[2], turn(outs[3], LANES // 2))

    each_plane(nz, 2, combine)


def join_kernel(mine_ref, other_ref, out_ref):
    nz, nx = mine_ref.shape[1], mine_ref.shape[2]
    mine = half_mask(nx, lax.axis_index("section"))
    for z in range(nz):
        other = other_ref[z]
        out_ref[0, z] = jnp.where(mine, mine_ref[0, z], other)
        out_ref[1, z] = jnp.where(mine, mine_ref[1, z], turn(other, LANES // 2))


def call(kernel, outs, scratch=(), flops=1_000_000, name=None):
    many = isinstance(outs, list)
    shapes = [jax.ShapeDtypeStruct(o, jnp.float32) for o in (outs if many else [outs])]

    def run(*args):
        moved = 4 * sum(int(a.size) for a in args) + 4 * sum(int(functools.reduce(lambda p, q: p * q, s.shape, 1)) for s in shapes)
        return pl.pallas_call(
            kernel,
            out_shape=shapes if many else shapes[0],
            in_specs=[pl.BlockSpec(memory_space=pltpu.VMEM)] * len(args),
            out_specs=[pl.BlockSpec(memory_space=pltpu.VMEM)] * len(shapes) if many else pl.BlockSpec(memory_space=pltpu.VMEM),
            scratch_shapes=[pltpu.VMEM(s, jnp.float32) for s in scratch],
            compiler_params=pltpu.CompilerParams(vmem_limit_bytes=VMEM_LIMIT),
            cost_estimate=pl.CostEstimate(flops=flops, bytes_accessed=moved, transcendentals=0),
            name=name,
        )(*args)

    return run


def beside(count, cross):
    pairs = []
    for s in range(2):
        to = 1 - s if cross else s
        step = 1 if to == 0 else -1
        for i in range(count):
            if 0 <= i + step < count:
                pairs.append((s * count + i, to * count + i + step))
    return pairs


def neighbours(count, step):
    return [(i, i + step) for i in range(count) if 0 <= i + step < count]


def body(previous, sections, diffusivity, reaction):
    consts = constants()
    nz, nx, ny = previous.shape
    columns, rows = lax.axis_size("sy"), lax.axis_size("sx")
    swap = [(0, 1), (1, 0)]
    other = lax.ppermute(sections, "section", swap)
    same, cross = call(edges_kernel, [(nz // 2, nx, ny), (nz // 4, nx, ny)], name="edges")(sections, previous, diffusivity, reaction)
    same = lax.ppermute(same, ("section", "sy"), beside(columns, False))
    cross = lax.ppermute(cross, ("section", "sy"), beside(columns, True))
    ring, low_rows, high_rows = call(rows_kernel, [(7, nz, nx, ny), (nz, 64, ny), (nz, 64, ny)], name="rows")(
        sections, other, previous, diffusivity, reaction, same, cross
    )
    from_low = lax.ppermute(high_rows, "sx", neighbours(rows, 1))
    from_high = lax.ppermute(low_rows, "sx", neighbours(rows, -1))
    peers = 2 * columns * rows
    padded, work = (nz + 2, ROWS, ny), (nz, LAST - FIRST, ny)
    scratch = [
        (4,) + padded, (4,) + padded, padded, (2,) + work, (2,) + work, (2,) + work, (2,) + work, (2,) + work,
        (SIZE, 4) + work, (4,) + padded, (4,) + padded, (LANES, LANES),
    ]
    part, sums = call(
        functools.partial(main_kernel, consts), [(peers, LANES), (ITERS, 4, nz, nx, ny)], scratch, 50_000_000, name="main"
    )(ring, from_low, from_high)
    total = lax.all_to_all(part.reshape(peers, 1, LANES), ("section", "sx", "sy"), 0, 0).reshape(peers, LANES)
    mine, send = call(functools.partial(finish_kernel, consts), [sections.shape, previous.shape], name="finish")(total, sums, ring)
    got = lax.ppermute(send, "section", swap)
    return call(join_kernel, sections.shape, name="join")(mine, got)


def solution(mesh):
    in_specs = (
        P(None, "sx", "sy"),
        P("section", None, "sx", "sy"),
        P(None, "sx", "sy"),
        P(None, "sx", "sy"),
    )
    out_specs = P("section", None, "sx", "sy")
    return jax.shard_map(body, mesh=mesh, in_specs=in_specs, out_specs=out_specs, check_vma=False)
```

```python
import functools

import jax
import jax.numpy as jnp
from jax import lax
from jax.experimental import pallas as pl
from jax.experimental.pallas import tpu as pltpu
from jax.sharding import PartitionSpec as P

ITERS = 4
SHIFTS = (0.0, 0.9, 0.45, 0.7)
EDGE = 9
LANES = 128
SIZE = ITERS + 1
PAIRS = [(i, j) for i in range(SIZE) for j in range(i, SIZE)]
PREPARE_UNROLL = 2
STEP_UNROLL = 8
VMEM_LIMIT = 58 * 1024 * 1024


step_size = 1.0
tiny_value = 1e-06


def invert_table(matrix):
    order_n = len(matrix)
    augmented = [
        list(matrix[r]) + [1.0 if c == r else 0.0 for c in range(order_n)] for r in range(order_n)
    ]
    for col in range(order_n):
        pivot_row = max(range(col, order_n), key=lambda r: abs(augmented[r][col]))
        augmented[col], augmented[pivot_row] = (augmented[pivot_row], augmented[col])
        leading = augmented[col][col]
        augmented[col] = [v / leading for v in augmented[col]]
        for r in range(order_n):
            if r != col:
                factor = augmented[r][col]
                augmented[r] = [a - factor * b for a, b in zip(augmented[r], augmented[col])]
    return [row_values[order_n:] for row_values in augmented]


def table_product(left, right):
    return [
        [sum((left[i][k] * right[k][j] for k in range(len(right)))) for j in range(len(right[0]))]
        for i in range(len(left))
    ]


def pair_add(first, second):
    return (first[0] + second[0], first[1] + second[1])


def pair_sub(first, second):
    return (first[0] - second[0], first[1] - second[1])


def pair_mul(first, second):
    return (
        first[0] * second[0] - first[1] * second[1],
        first[0] * second[1] + first[1] * second[0],
    )


def pair_div(first, second):
    scale_sq = second[0] * second[0] + second[1] * second[1]
    return (
        (first[0] * second[0] + first[1] * second[1]) / scale_sq,
        (first[1] * second[0] - first[0] * second[1]) / scale_sq,
    )


def quartic_value(point):
    return (((210.0 * point - 480.0) * point + 360.0) * point - 96.0) * point + 6.0


def bisect_root(lower, upper):
    for count in range(200):
        middle = 0.5 * (lower + upper)
        if (quartic_value(lower) < 0.0) == (quartic_value(middle) < 0.0):
            lower = middle
        else:
            upper = middle
    return 0.5 * (lower + upper)


def radau_tables():
    abscissae = []
    grid_steps = 4000
    for m in range(grid_steps):
        lower = 0.999 * m / grid_steps
        upper = 0.999 * (m + 1) / grid_steps
        if (quartic_value(lower) < 0.0) != (quartic_value(upper) < 0.0):
            abscissae.append(bisect_root(lower, upper))
    abscissae.append(1.0)
    vander = [[abscissae[j] ** k for k in range(4)] for j in range(4)]
    moments = [[abscissae[i] ** (k + 1) / (k + 1) for k in range(4)] for i in range(4)]
    tableau = table_product(moments, invert_table(vander))
    inverse = invert_table(tableau)
    running = [list(row_values) for row_values in inverse]
    coeffs = []
    for k in range(1, 5):
        trace_value = sum((running[i][i] for i in range(4)))
        coeffs.append(-trace_value / k)
        shifted_table = [
            [running[i][j] + (coeffs[-1] if i == j else 0.0) for j in range(4)] for i in range(4)
        ]
        running = table_product(inverse, shifted_table)
    start_point = (0.4, 0.9)
    estimates = [(1.0, 0.0)]
    for k in range(3):
        estimates.append(pair_mul(estimates[-1], start_point))
    for count in range(500):
        for i in range(4):
            value = (1.0, 0.0)
            for coef_value in coeffs:
                value = pair_add(pair_mul(value, estimates[i]), (coef_value, 0.0))
            denom = (1.0, 0.0)
            for j in range(4):
                if j != i:
                    denom = pair_mul(denom, pair_sub(estimates[i], estimates[j]))
            estimates[i] = pair_sub(estimates[i], pair_div(value, denom))
    chosen = [m for m in range(4) if estimates[m][1] > 0.0]
    ranking = sorted(chosen, key=lambda m: -estimates[m][1])
    columns = []
    pairs = []
    for m in ranking:
        eigen_pair = estimates[m]
        system = [
            [
                (
                    inverse[i][j] - (eigen_pair[0] if i == j else 0.0),
                    -(eigen_pair[1] if i == j else 0.0),
                )
                for j in range(4)
            ]
            for i in range(3)
        ]
        rows_left = [
            [system[i][j] for j in range(3)] + [(-system[i][3][0], -system[i][3][1])]
            for i in range(3)
        ]
        for col in range(3):
            pivot_row = max(
                range(col, 3), key=lambda r: rows_left[r][col][0] ** 2 + rows_left[r][col][1] ** 2
            )
            rows_left[col], rows_left[pivot_row] = (rows_left[pivot_row], rows_left[col])
            leading = rows_left[col][col]
            rows_left[col] = [pair_div(v, leading) for v in rows_left[col]]
            for r in range(3):
                if r != col:
                    factor = rows_left[r][col]
                    rows_left[r] = [
                        pair_sub(a, pair_mul(factor, b))
                        for a, b in zip(rows_left[r], rows_left[col])
                    ]
        vector = [rows_left[i][3] for i in range(3)] + [(1.0, 0.0)]
        columns.append([v[0] for v in vector])
        columns.append([v[1] for v in vector])
        pairs.append((eigen_pair[0], eigen_pair[1]))
    eigen_basis = [[columns[j][i] for j in range(4)] for i in range(4)]
    basis_inverse = invert_table(eigen_basis)
    return (tableau, inverse, eigen_basis, basis_inverse, pairs)


def constants():
    tableau, inverse, eigen_basis, basis_inverse, pairs = radau_tables()
    shift_table = table_product(basis_inverse, inverse)
    shift_rows = [[v / step_size for v in row_values] for row_values in shift_table]
    pairs = [(p[0] / step_size, p[1] / step_size) for p in pairs]
    return eigen_basis, basis_inverse, shift_rows, pairs


def lane_ids(rows):
    return lax.broadcasted_iota(jnp.int32, (rows, LANES), 1)


def turn(cells, amount):
    return pltpu.roll(cells, amount % LANES, cells.ndim - 1)


def half_mask(rows, section):
    return (lane_ids(rows) < LANES // 2) == (section == 0)


MINE = (0, 1, 4, 5, 6)


def border_start():
    first = lax.axis_index("section") == 0
    high, low = LANES - EDGE, 0
    return jnp.where(first, high, low)


def pack_border(tile, cell, field, part, lanes, start):
    at = part * 64 + field * EDGE
    moved = pltpu.roll(cell, lax.rem(at + LANES - start, LANES), 1)
    return jnp.where((lanes >= at) & (lanes < at + EDGE), moved, tile)


def pack_rows(low_ref, high_ref, cells, z, nx):
    count = len(cells)
    for f, cell in enumerate(cells):
        low_ref[z, 8 * f : 8 * f + 8] = cell[0:8]
        low_ref[z, 8 * count + f : 8 * count + f + 1] = cell[8:9]
        high_ref[z, 8 * f : 8 * f + 8] = cell[nx - 8 : nx]
        high_ref[z, 8 * count + f : 8 * count + f + 1] = cell[nx - 9 : nx - 8]
    rest = low_ref.shape[1] - 9 * count
    for ref in (low_ref, high_ref):
        ref[z, 9 * count :] = jnp.zeros((rest, LANES), jnp.float32)


def own_kernel(own_ref, prev_ref, diff_ref, react_ref, border_ref, low_ref, high_ref):
    nz, nx = prev_ref.shape[0], prev_ref.shape[1]
    lanes = lane_ids(nx)
    start = border_start()
    half = nz // 2
    for plane in range(half):
        tile = jnp.zeros((nx, LANES), jnp.float32)
        for part in range(2):
            z = part * half + plane
            cells = [own_ref[0, z], own_ref[1, z], prev_ref[z], diff_ref[z], react_ref[z]]
            for f, cell in zip(MINE, cells):
                tile = pack_border(tile, cell, f, part, lanes, start)
            pack_rows(low_ref, high_ref, cells, z, nx)
        border_ref[plane] = tile


def other_kernel(other_ref, partial_ref, border_ref, low_ref, high_ref):
    nz, nx = other_ref.shape[1], other_ref.shape[2]
    lanes = lane_ids(nx)
    start = border_start()
    half = nz // 2
    for plane in range(half):
        tile = partial_ref[plane]
        for part in range(2):
            z = part * half + plane
            cells = [other_ref[0, z], other_ref[1, z]]
            for f, cell in enumerate(cells):
                tile = pack_border(tile, cell, 2 + f, part, lanes, start)
            pack_rows(low_ref, high_ref, cells, z, nx)
        border_ref[plane] = tile


ROWS = 48
FIRST, LAST = 8, 40
OWN = slice(16, 32)
WORK = slice(FIRST, LAST)
BEFORE = slice(FIRST - 1, LAST - 1)
AFTER = slice(FIRST + 1, LAST + 1)


def each_plane(count, unroll, work):
    def group(i, carry):
        for u in range(unroll):
            work(i * unroll + u)
        return carry

    lax.fori_loop(0, count // unroll, group, 0)


def main_kernel(consts, own_ref, other_ref, prev_ref, diff_ref, react_ref, own_low_ref, own_high_ref, other_low_ref, other_high_ref,
                border_ref, corner_low_ref, corner_high_ref, part_ref, sums_ref,
                val, kap, frozen, prv, rea, dif, fx, fy, fz, alpha, beta, vec, ya, yb, table):
    eigen_basis, basis_inverse, shift_rows, pairs = consts
    nz, nx = prev_ref.shape[0], prev_ref.shape[1]
    section = lax.axis_index("section")
    zero_plane = jnp.zeros((ROWS, LANES), jnp.float32)
    zero_rows = jnp.zeros((FIRST, LANES), jnp.float32)
    start = border_start()
    lanes = lane_ids(ROWS)
    edge = (lanes >= start) & (lanes < start + EDGE)
    tile = lambda t: jnp.broadcast_to(t, (8, LANES))

    for at in (0, nz + 1):
        frozen[at] = zero_plane
        for f in range(4):
            for ref in (val, kap, ya, yb):
                ref[f, at] = zero_plane

    def assemble(plane):
        sides = jnp.concatenate(
            [
                tile(corner_low_ref[plane, nx - 9 : nx - 8]), corner_low_ref[plane, nx - 8 : nx], border_ref[plane],
                corner_high_ref[plane, 0:8], tile(corner_high_ref[plane, 8:9]),
            ],
            0,
        )
        for part in range(2):
            z = part * (nz // 2) + plane

            def column(f):
                if f in (2, 3):
                    low, high, slot, count, mid = other_low_ref, other_high_ref, f - 2, 2, other_ref[f - 2, z]
                else:
                    slot, count = MINE.index(f), len(MINE)
                    low, high = own_low_ref, own_high_ref
                    mid = (own_ref[0, z], own_ref[1, z], prev_ref[z], diff_ref[z], react_ref[z])[slot]
                ninth = 8 * count + slot
                cells = jnp.concatenate(
                    [tile(low[z, ninth : ninth + 1]), low[z, 8 * slot : 8 * slot + 8], mid, high[z, 8 * slot : 8 * slot + 8], tile(high[z, ninth : ninth + 1])], 0
                )
                at = part * 64 + f * EDGE
                return jnp.where(edge, pltpu.roll(sides, lax.rem(start + LANES - at, LANES), 1), cells)

            diff, prev, react = column(5), column(4), column(6)
            frozen[z + 1] = diff * (0.5 + 0.25 * jnp.tanh(prev))
            prv[z] = prev[WORK]
            rea[z] = react[WORK]
            dif[z] = diff[WORK]
            for f in range(4):
                value = column(f)
                val[f, z + 1] = value
                kap[f, z + 1] = diff * (0.5 + 0.25 * jnp.tanh(value))
                for ref in (ya, yb):
                    ref[f, z + 1, 0:FIRST] = zero_rows
                    ref[f, z + 1, LAST:ROWS] = zero_rows

    each_plane(nz // 2, 1, assemble)

    def pick(matrix, m, j):
        return jnp.where(section == 0, jnp.float32(matrix[m][j]), jnp.float32(matrix[m][(j + 2) % 4]))

    q_rows = [[pick(basis_inverse, m, j) for j in range(4)] for m in range(4)]
    c_rows = [[pick(shift_rows, m, j) for j in range(4)] for m in range(4)]

    def prepare(z):
        mid = frozen[z + 1, WORK]
        faces = [
            mid + frozen[z + 1, BEFORE], mid + frozen[z + 1, AFTER], mid + turn(mid, 1), mid + turn(mid, -1),
            mid + frozen[z, WORK], mid + frozen[z + 2, WORK],
        ]
        for at, ref in enumerate((fx, fy, fz)):
            ref[0, z] = faces[2 * at]
            ref[1, z] = faces[2 * at + 1]
        prev, react = prv[z], rea[z]
        base = ((faces[0] + faces[1]) + (faces[2] + faces[3])) + (faces[4] + faces[5]) - react * (1.0 - 3.0 * prev * prev)
        inside = jnp.where(dif[z] > 0.0, 1.0, 0.0)
        scaled = []
        for b in range(2):
            real, imag = pairs[b]
            diag = base + real
            scale = inside / (diag * diag + imag * imag)
            scaled.append((diag * scale, imag * scale))
            alpha[b, z], beta[b, z] = scaled[b]
        rhs = [None] * 4
        for j in range(4):
            v = val[j, z + 1, WORK]
            k = kap[j, z + 1, WORK]
            flux = react * v * (1.0 - v * v)
            flux = flux + (k + kap[j, z + 1, BEFORE]) * (val[j, z + 1, BEFORE] - v)
            flux = flux + (k + kap[j, z + 1, AFTER]) * (val[j, z + 1, AFTER] - v)
            flux = flux + (k + turn(k, 1)) * (turn(v, 1) - v)
            flux = flux + (k + turn(k, -1)) * (turn(v, -1) - v)
            flux = flux + (k + kap[j, z, WORK]) * (val[j, z, WORK] - v)
            flux = flux + (k + kap[j, z + 2, WORK]) * (val[j, z + 2, WORK] - v)
            grown = v - prev
            for m in range(4):
                term = q_rows[m][j] * flux - c_rows[m][j] * grown
                rhs[m] = term if j == 0 else rhs[m] + term
        for m in range(4):
            vec[0, m, z] = rhs[m]
        for b in range(2):
            al, be = scaled[b]
            ya[2 * b, z + 1, WORK] = al * rhs[2 * b] - be * rhs[2 * b + 1]
            ya[2 * b + 1, z + 1, WORK] = be * rhs[2 * b] + al * rhs[2 * b + 1]

    each_plane(nz, PREPARE_UNROLL, prepare)

    def spread(ref, m, z, rows=WORK):
        lo, hi = rows.start, rows.stop
        cut = slice(lo - FIRST, hi - FIRST)
        mid = ref[m, z + 1, lo:hi]
        in_y = fy[0, z, cut] * turn(mid, 1) + fy[1, z, cut] * turn(mid, -1)
        in_x = fx[0, z, cut] * ref[m, z + 1, lo - 1 : hi - 1] + fx[1, z, cut] * ref[m, z + 1, lo + 1 : hi + 1]
        in_z = fz[0, z, cut] * ref[m, z, lo:hi] + fz[1, z, cut] * ref[m, z + 2, lo:hi]
        return (in_x + in_z) + in_y

    for j in range(ITERS):

        def odd(z, j=j):
            for b in range(2):
                t0 = spread(ya, 2 * b, z)
                t1 = spread(ya, 2 * b + 1, z)
                al, be = alpha[b, z], beta[b, z]
                y0 = al * t0 - be * t1
                y1 = be * t0 + al * t1
                yb[2 * b, z + 1, WORK] = y0
                yb[2 * b + 1, z + 1, WORK] = y1
                sums_ref[j, 2 * b, z] = ya[2 * b, z + 1, OWN] + y0[8:24]
                sums_ref[j, 2 * b + 1, z] = ya[2 * b + 1, z + 1, OWN] + y1[8:24]

        def even(z, j=j):
            last = j == ITERS - 1
            rows = OWN if last else WORK
            cut = slice(rows.start - FIRST, rows.stop - FIRST)
            for b in range(2):
                new = []
                for m in (2 * b, 2 * b + 1):
                    v = spread(yb, m, z, rows)
                    if SHIFTS[j]:
                        v = v - SHIFTS[j] * vec[j, m, z, cut]
                    vec[j + 1, m, z, cut] = v
                    new.append(v)
                if not last:
                    al, be = alpha[b, z], beta[b, z]
                    ya[2 * b, z + 1, WORK] = al * new[0] - be * new[1]
                    ya[2 * b + 1, z + 1, WORK] = be * new[0] + al * new[1]

        each_plane(nz, STEP_UNROLL, odd)
        each_plane(nz, STEP_UNROLL, even)

    table[...] = jnp.zeros((LANES, LANES), jnp.float32)
    mine = half_mask(8, section)
    for b in range(2):

        def dots(z, carry):
            out = list(carry)
            for m in (2 * b, 2 * b + 1):
                for r in (8, 16):
                    cells = [vec[i, m, z, r : r + 8] for i in range(SIZE)]
                    for at, (i, j) in enumerate(PAIRS):
                        out[at] = out[at] + cells[i] * cells[j]
            return tuple(out)

        zero = jnp.zeros((8, LANES), jnp.float32)
        out = lax.fori_loop(0, nz, dots, tuple(zero for _ in PAIRS))
        for at in range(len(PAIRS)):
            row = jnp.sum(jnp.where(mine, out[at], 0.0), axis=0, keepdims=True)
            table[b * len(PAIRS) + at : b * len(PAIRS) + at + 1] = row
    total = jnp.sum(table[...].T, axis=0, keepdims=True)
    part_ref[...] = jnp.broadcast_to(total, part_ref.shape)


def step_weights(gram):
    table = {}
    for at, (i, j) in enumerate(PAIRS):
        table[i, j] = table[j, i] = gram[at]
    coef = [jnp.ones_like(gram[0])]
    weight = []
    step = coef[0]
    for k in range(ITERS):
        moved = [SHIFTS[j] * coef[j] for j in range(k + 1)] + [jnp.zeros_like(step)]
        for j in range(k + 1):
            moved[j + 1] = moved[j + 1] + coef[j]
        coef = coef + [jnp.zeros_like(step)]
        image = [coef[j] - moved[j] for j in range(k + 2)]
        num, den, bound = 0.0, 0.0, 0.0
        for i in range(k + 2):
            row, size = 0.0, 0.0
            for j in range(k + 2):
                term = table[i, j] * image[j]
                row = row + term
                size = size + jnp.abs(term)
            num = num + row * coef[i]
            den = den + row * image[i]
            bound = bound + size * jnp.abs(image[i])
        step = jnp.where(den > bound * 6e-8, num / (jnp.maximum(den, 0.0) + tiny_value), step)
        weight = weight + [jnp.zeros_like(step)]
        for j in range(k + 1):
            weight[j] = weight[j] + step * coef[j]
        coef = [coef[j] - step * image[j] for j in range(k + 2)]
    return weight


def send_kernel(consts, total_ref, sums_ref, other_ref, send_ref, weight_ref):
    eigen_basis = consts[0]
    nz, nx = other_ref.shape[1], other_ref.shape[2]
    section = lax.axis_index("section")
    total = jnp.sum(total_ref[...], axis=0, keepdims=True)
    count = len(PAIRS)
    weights = []
    for b in range(2):
        gram = [jnp.broadcast_to(total[:, b * count + at : b * count + at + 1], (1, LANES)) for at in range(count)]
        weights.append(step_weights(gram))
    for b in range(2):
        for j in range(ITERS):
            weight_ref[b * ITERS + j : b * ITERS + j + 1] = weights[b][j]
    basis = [
        [jnp.where(section == 0, jnp.float32(eigen_basis[2 + r][m]), jnp.float32(eigen_basis[r][m])) for m in range(4)]
        for r in range(2)
    ]
    mine = half_mask(nx, section)

    def combine(z):
        outs = [other_ref[r, z] for r in range(2)]
        for m in range(4):
            field = weights[m // 2][0] * sums_ref[0, m, z]
            for j in range(1, ITERS):
                field = field + weights[m // 2][j] * sums_ref[j, m, z]
            outs = [outs[r] + basis[r][m] * field for r in range(2)]
        send_ref[z] = jnp.where(mine, outs[0], turn(outs[1], LANES // 2))

    each_plane(nz, 4, combine)


def mine_kernel(consts, weight_ref, sums_ref, own_ref, mine_ref):
    eigen_basis = consts[0]
    nz = own_ref.shape[1]
    section = lax.axis_index("section")
    weights = [[weight_ref[b * ITERS + j : b * ITERS + j + 1] for j in range(ITERS)] for b in range(2)]
    basis = [
        [jnp.where(section == 0, jnp.float32(eigen_basis[r][m]), jnp.float32(eigen_basis[2 + r][m])) for m in range(4)]
        for r in range(2)
    ]

    def combine(z):
        outs = [own_ref[r, z] for r in range(2)]
        for m in range(4):
            field = weights[m // 2][0] * sums_ref[0, m, z]
            for j in range(1, ITERS):
                field = field + weights[m // 2][j] * sums_ref[j, m, z]
            outs = [outs[r] + basis[r][m] * field for r in range(2)]
        mine_ref[0, z] = outs[0]
        mine_ref[1, z] = outs[1]

    each_plane(nz, 4, combine)


def join_kernel(mine_ref, other_ref, out_ref):
    nz, nx = mine_ref.shape[1], mine_ref.shape[2]
    mine = half_mask(nx, lax.axis_index("section"))
    for z in range(nz):
        other = other_ref[z]
        out_ref[0, z] = jnp.where(mine, mine_ref[0, z], other)
        out_ref[1, z] = jnp.where(mine, mine_ref[1, z], turn(other, LANES // 2))


def call(kernel, outs, scratch=(), flops=1_000_000, name=None):
    many = isinstance(outs, list)
    shapes = [jax.ShapeDtypeStruct(o, jnp.float32) for o in (outs if many else [outs])]

    def run(*args):
        moved = 4 * sum(int(a.size) for a in args) + 4 * sum(int(functools.reduce(lambda p, q: p * q, s.shape, 1)) for s in shapes)
        return pl.pallas_call(
            kernel,
            out_shape=shapes if many else shapes[0],
            in_specs=[pl.BlockSpec(memory_space=pltpu.VMEM)] * len(args),
            out_specs=[pl.BlockSpec(memory_space=pltpu.VMEM)] * len(shapes) if many else pl.BlockSpec(memory_space=pltpu.VMEM),
            scratch_shapes=[pltpu.VMEM(s, jnp.float32) for s in scratch],
            compiler_params=pltpu.CompilerParams(vmem_limit_bytes=VMEM_LIMIT),
            cost_estimate=pl.CostEstimate(flops=flops, bytes_accessed=moved, transcendentals=0),
            name=name,
        )(*args)

    return run


def grid_pairs(columns, rows, x_step, y_out):
    pairs = []
    for s in range(2):
        y_step = (1 - 2 * s) if y_out else 0
        for x in range(rows):
            for y in range(columns):
                if 0 <= x + x_step < rows and 0 <= y + y_step < columns:
                    pairs.append(((s * rows + x) * columns + y, (s * rows + x + x_step) * columns + y + y_step))
    return pairs


def body(previous, sections, diffusivity, reaction):
    consts = constants()
    nz, nx, ny = previous.shape
    columns, rows = lax.axis_size("sy"), lax.axis_size("sx")
    axes = ("section", "sx", "sy")
    swap = [(0, 1), (1, 0)]
    send = lambda a, x_step, y_out: lax.ppermute(a, axes, grid_pairs(columns, rows, x_step, y_out))
    other = lax.ppermute(sections, "section", swap)
    partial, low, high = call(own_kernel, [(nz // 2, nx, ny), (nz, 48, ny), (nz, 48, ny)], name="own")(
        sections, previous, diffusivity, reaction
    )
    own_low, own_high = send(high, 1, False), send(low, -1, False)
    other, own_low, own_high = lax.optimization_barrier((other, own_low, own_high))
    border, low, high = call(other_kernel, [(nz // 2, nx, ny), (nz, 24, ny), (nz, 24, ny)], name="other")(other, partial)
    other_low, other_high = send(high, 1, False), send(low, -1, False)
    side = send(border, 0, True)
    corner_low, corner_high = send(border, 1, True), send(border, -1, True)
    peers = 2 * columns * rows
    padded, work = (nz + 2, ROWS, ny), (nz, LAST - FIRST, ny)
    scratch = [
        (4,) + padded, (4,) + padded, padded, work, work, work, (2,) + work, (2,) + work, (2,) + work, (2,) + work, (2,) + work,
        (SIZE, 4) + work, (4,) + padded, (4,) + padded, (LANES, LANES),
    ]
    part, sums = call(
        functools.partial(main_kernel, consts), [(peers, LANES), (ITERS, 4, nz, nx, ny)], scratch, 50_000_000, name="main"
    )(sections, other, previous, diffusivity, reaction, own_low, own_high, other_low, other_high, side, corner_low, corner_high)
    total = lax.all_to_all(part.reshape(peers, 1, LANES), axes, 0, 0).reshape(peers, LANES)
    half, weight = call(functools.partial(send_kernel, consts), [previous.shape, (2 * ITERS, LANES)], name="send")(total, sums, other)
    got = lax.ppermute(half, "section", swap)
    mine = call(functools.partial(mine_kernel, consts), sections.shape, name="mine")(weight, sums, sections)
    return call(join_kernel, sections.shape, name="join")(mine, got)


def solution(mesh):
    in_specs = (
        P(None, "sx", "sy"),
        P("section", None, "sx", "sy"),
        P(None, "sx", "sy"),
        P(None, "sx", "sy"),
    )
    out_specs = P("section", None, "sx", "sy")
    return jax.shard_map(body, mesh=mesh, in_specs=in_specs, out_specs=out_specs, check_vma=False)
```

```python
import functools

import jax
import jax.numpy as jnp
from jax import lax
from jax.experimental import pallas as pl
from jax.experimental.pallas import tpu as pltpu
from jax.sharding import PartitionSpec as P

ITERS = 4
SHIFTS = (0.0, 0.9, 0.45, 0.7)
EDGE = 9
LANES = 128
SIZE = ITERS + 1
PAIRS = [(i, j) for i in range(SIZE) for j in range(i, SIZE)]
PREPARE_UNROLL = 2
STEP_UNROLL = 8


step_size = 1.0
tiny_value = 1e-06


def invert_table(matrix):
    order_n = len(matrix)
    augmented = [
        list(matrix[r]) + [1.0 if c == r else 0.0 for c in range(order_n)] for r in range(order_n)
    ]
    for col in range(order_n):
        pivot_row = max(range(col, order_n), key=lambda r: abs(augmented[r][col]))
        augmented[col], augmented[pivot_row] = (augmented[pivot_row], augmented[col])
        leading = augmented[col][col]
        augmented[col] = [v / leading for v in augmented[col]]
        for r in range(order_n):
            if r != col:
                factor = augmented[r][col]
                augmented[r] = [a - factor * b for a, b in zip(augmented[r], augmented[col])]
    return [row_values[order_n:] for row_values in augmented]


def table_product(left, right):
    return [
        [sum((left[i][k] * right[k][j] for k in range(len(right)))) for j in range(len(right[0]))]
        for i in range(len(left))
    ]


def pair_add(first, second):
    return (first[0] + second[0], first[1] + second[1])


def pair_sub(first, second):
    return (first[0] - second[0], first[1] - second[1])


def pair_mul(first, second):
    return (
        first[0] * second[0] - first[1] * second[1],
        first[0] * second[1] + first[1] * second[0],
    )


def pair_div(first, second):
    scale_sq = second[0] * second[0] + second[1] * second[1]
    return (
        (first[0] * second[0] + first[1] * second[1]) / scale_sq,
        (first[1] * second[0] - first[0] * second[1]) / scale_sq,
    )


def quartic_value(point):
    return (((210.0 * point - 480.0) * point + 360.0) * point - 96.0) * point + 6.0


def bisect_root(lower, upper):
    for count in range(200):
        middle = 0.5 * (lower + upper)
        if (quartic_value(lower) < 0.0) == (quartic_value(middle) < 0.0):
            lower = middle
        else:
            upper = middle
    return 0.5 * (lower + upper)


def radau_tables():
    abscissae = []
    grid_steps = 4000
    for m in range(grid_steps):
        lower = 0.999 * m / grid_steps
        upper = 0.999 * (m + 1) / grid_steps
        if (quartic_value(lower) < 0.0) != (quartic_value(upper) < 0.0):
            abscissae.append(bisect_root(lower, upper))
    abscissae.append(1.0)
    vander = [[abscissae[j] ** k for k in range(4)] for j in range(4)]
    moments = [[abscissae[i] ** (k + 1) / (k + 1) for k in range(4)] for i in range(4)]
    tableau = table_product(moments, invert_table(vander))
    inverse = invert_table(tableau)
    running = [list(row_values) for row_values in inverse]
    coeffs = []
    for k in range(1, 5):
        trace_value = sum((running[i][i] for i in range(4)))
        coeffs.append(-trace_value / k)
        shifted_table = [
            [running[i][j] + (coeffs[-1] if i == j else 0.0) for j in range(4)] for i in range(4)
        ]
        running = table_product(inverse, shifted_table)
    start_point = (0.4, 0.9)
    estimates = [(1.0, 0.0)]
    for k in range(3):
        estimates.append(pair_mul(estimates[-1], start_point))
    for count in range(500):
        for i in range(4):
            value = (1.0, 0.0)
            for coef_value in coeffs:
                value = pair_add(pair_mul(value, estimates[i]), (coef_value, 0.0))
            denom = (1.0, 0.0)
            for j in range(4):
                if j != i:
                    denom = pair_mul(denom, pair_sub(estimates[i], estimates[j]))
            estimates[i] = pair_sub(estimates[i], pair_div(value, denom))
    chosen = [m for m in range(4) if estimates[m][1] > 0.0]
    ranking = sorted(chosen, key=lambda m: -estimates[m][1])
    columns = []
    pairs = []
    for m in ranking:
        eigen_pair = estimates[m]
        system = [
            [
                (
                    inverse[i][j] - (eigen_pair[0] if i == j else 0.0),
                    -(eigen_pair[1] if i == j else 0.0),
                )
                for j in range(4)
            ]
            for i in range(3)
        ]
        rows_left = [
            [system[i][j] for j in range(3)] + [(-system[i][3][0], -system[i][3][1])]
            for i in range(3)
        ]
        for col in range(3):
            pivot_row = max(
                range(col, 3), key=lambda r: rows_left[r][col][0] ** 2 + rows_left[r][col][1] ** 2
            )
            rows_left[col], rows_left[pivot_row] = (rows_left[pivot_row], rows_left[col])
            leading = rows_left[col][col]
            rows_left[col] = [pair_div(v, leading) for v in rows_left[col]]
            for r in range(3):
                if r != col:
                    factor = rows_left[r][col]
                    rows_left[r] = [
                        pair_sub(a, pair_mul(factor, b))
                        for a, b in zip(rows_left[r], rows_left[col])
                    ]
        vector = [rows_left[i][3] for i in range(3)] + [(1.0, 0.0)]
        columns.append([v[0] for v in vector])
        columns.append([v[1] for v in vector])
        pairs.append((eigen_pair[0], eigen_pair[1]))
    eigen_basis = [[columns[j][i] for j in range(4)] for i in range(4)]
    basis_inverse = invert_table(eigen_basis)
    return (tableau, inverse, eigen_basis, basis_inverse, pairs)


def constants():
    tableau, inverse, eigen_basis, basis_inverse, pairs = radau_tables()
    shift_table = table_product(basis_inverse, inverse)
    shift_rows = [[v / step_size for v in row_values] for row_values in shift_table]
    pairs = [(p[0] / step_size, p[1] / step_size) for p in pairs]
    return eigen_basis, basis_inverse, shift_rows, pairs


def lane_ids(rows):
    return lax.broadcasted_iota(jnp.int32, (rows, LANES), 1)


def turn(cells, amount):
    return pltpu.roll(cells, amount % LANES, cells.ndim - 1)


def left_half():
    return lax.rem(lax.axis_index("section") + lax.axis_index("sy"), 2) == 1


def half_mask(rows):
    return (lane_ids(rows) < LANES // 2) == left_half()


ORDER = (0, 1, 4, 5, 6, 2, 3)
TALL = 16
PARTS = 4


def border_start():
    return jnp.where(left_half(), LANES - EDGE, 0)


def leaving_start():
    return jnp.where(left_half(), 0, LANES - EDGE)


def on_even_row():
    return lax.rem(lax.axis_index("sx"), 2) == 0


def pack(border_ref, near_ref, far_ref, load, fields, first_slot, partial):
    nz = 2 * border_ref.shape[0]
    nx = border_ref.shape[1]
    lanes = lane_ids(nx)
    start = leaving_start()
    even = on_even_row()

    def plane_pair(plane):
        tile = partial(plane)
        for part in range(2):
            z = part * (nz // 2) + plane
            for slot, f in enumerate(fields, first_slot):
                cell = load(f, z)
                at = part * 64 + f * EDGE
                moved = pltpu.roll(cell, lax.rem(at + LANES - start, LANES), 1)
                tile = jnp.where((lanes >= at) & (lanes < at + EDGE), moved, tile)
                entry, row = divmod(8 * slot, TALL)
                last, ninth = divmod(56 + slot, TALL)
                near_ref[z * PARTS + entry, row : row + 8] = jnp.where(even, cell[nx - 8 : nx], cell[0:8])
                far_ref[z * PARTS + entry, row : row + 8] = jnp.where(even, cell[0:8], cell[nx - 8 : nx])
                near_ref[z * PARTS + last, ninth : ninth + 1] = jnp.where(even, cell[nx - 9 : nx - 8], cell[8:9])
                far_ref[z * PARTS + last, ninth : ninth + 1] = jnp.where(even, cell[8:9], cell[nx - 9 : nx - 8])
        border_ref[plane] = tile

    each_plane(nz // 2, 4, plane_pair)


def own_kernel(own_ref, prev_ref, diff_ref, react_ref, border_ref, near_ref, far_ref):
    nx = prev_ref.shape[1]
    refs = {4: prev_ref, 5: diff_ref, 6: react_ref}
    load = lambda f, z: own_ref[f, z] if f < 2 else refs[f][z]
    pack(border_ref, near_ref, far_ref, load, ORDER[:5], 0, lambda plane: jnp.zeros((nx, LANES), jnp.float32))


def other_kernel(other_ref, own_border_ref, own_near_ref, own_far_ref, border_ref, near_ref, far_ref):
    near_ref[...] = own_near_ref[...]
    far_ref[...] = own_far_ref[...]
    pack(border_ref, near_ref, far_ref, lambda f, z: other_ref[f - 2, z], ORDER[5:], 5, lambda plane: own_border_ref[plane])


ROWS = 48
FIRST, LAST = 8, 40
OWN = slice(16, 32)
WORK = slice(FIRST, LAST)
BEFORE = slice(FIRST - 1, LAST - 1)
AFTER = slice(FIRST + 1, LAST + 1)


def each_plane(count, unroll, work):
    def group(i, carry):
        for u in range(unroll):
            work(i * unroll + u)
        return carry

    lax.fori_loop(0, count // unroll, group, 0)


def main_kernel(consts, own_ref, other_ref, prev_ref, diff_ref, react_ref, border_ref, near_ref, far_ref, part_ref, sums_ref,
                val, kap, frozen, prv, rea, dif, fx, fy, fz, alpha, beta, vec, ya, yb, table):
    eigen_basis, basis_inverse, shift_rows, pairs = consts
    nz, nx = prev_ref.shape[0], prev_ref.shape[1]
    section = lax.axis_index("section")
    zero_plane = jnp.zeros((ROWS, LANES), jnp.float32)
    zero_rows = jnp.zeros((FIRST, LANES), jnp.float32)
    start = border_start()
    even = on_even_row()
    lanes = lane_ids(ROWS)
    edge = (lanes >= start) & (lanes < start + EDGE)
    tile = lambda t: jnp.broadcast_to(t, (8, LANES))

    for at in (0, nz + 1):
        frozen[at] = zero_plane
        for f in range(4):
            for ref in (val, kap, ya, yb):
                ref[f, at] = zero_plane

    def both(entry, row, count):
        near, far = near_ref[entry, row : row + count], far_ref[entry, row : row + count]
        return jnp.where(even, far, near), jnp.where(even, near, far)

    def assemble(plane):
        at = nz * PARTS + plane
        low = jnp.where(even, far_ref[at], near_ref[at])
        high = jnp.where(even, near_ref[at], far_ref[at])
        sides = jnp.concatenate([tile(low[nx - 9 : nx - 8]), low[nx - 8 : nx], border_ref[plane], high[0:8], tile(high[8:9])], 0)
        for part in range(2):
            z = part * (nz // 2) + plane

            def column(f):
                slot = ORDER.index(f)
                mid = (own_ref[0, z], own_ref[1, z], prev_ref[z], diff_ref[z], react_ref[z], other_ref[0, z], other_ref[1, z])[slot]
                entry, row = divmod(8 * slot, TALL)
                low, high = both(z * PARTS + entry, row, 8)
                entry, row = divmod(56 + slot, TALL)
                low_end, high_end = both(z * PARTS + entry, row, 1)
                cells = jnp.concatenate([tile(low_end), low, mid, high, tile(high_end)], 0)
                at = part * 64 + f * EDGE
                return jnp.where(edge, pltpu.roll(sides, lax.rem(start + LANES - at, LANES), 1), cells)

            diff, prev, react = column(5), column(4), column(6)
            frozen[z + 1] = diff * (0.5 + 0.25 * jnp.tanh(prev))
            prv[z] = prev[WORK]
            rea[z] = react[WORK]
            dif[z] = diff[WORK]
            for f in range(4):
                value = column(f)
                val[f, z + 1] = value
                kap[f, z + 1] = diff * (0.5 + 0.25 * jnp.tanh(value))
                for ref in (ya, yb):
                    ref[f, z + 1, 0:FIRST] = zero_rows
                    ref[f, z + 1, LAST:ROWS] = zero_rows

    each_plane(nz // 2, 1, assemble)

    def pick(matrix, m, j):
        return jnp.where(section == 0, jnp.float32(matrix[m][j]), jnp.float32(matrix[m][(j + 2) % 4]))

    q_rows = [[pick(basis_inverse, m, j) for j in range(4)] for m in range(4)]
    c_rows = [[pick(shift_rows, m, j) for j in range(4)] for m in range(4)]

    def prepare(z):
        mid = frozen[z + 1, WORK]
        faces = [
            mid + frozen[z + 1, BEFORE], mid + frozen[z + 1, AFTER], mid + turn(mid, 1), mid + turn(mid, -1),
            mid + frozen[z, WORK], mid + frozen[z + 2, WORK],
        ]
        for at, ref in enumerate((fx, fy, fz)):
            ref[0, z] = faces[2 * at]
            ref[1, z] = faces[2 * at + 1]
        prev, react = prv[z], rea[z]
        base = ((faces[0] + faces[1]) + (faces[2] + faces[3])) + (faces[4] + faces[5]) - react * (1.0 - 3.0 * prev * prev)
        inside = jnp.where(dif[z] > 0.0, 1.0, 0.0)
        scaled = []
        for b in range(2):
            real, imag = pairs[b]
            diag = base + real
            scale = inside / (diag * diag + imag * imag)
            scaled.append((diag * scale, imag * scale))
            alpha[b, z], beta[b, z] = scaled[b]
        rhs = [None] * 4
        for j in range(4):
            v = val[j, z + 1, WORK]
            k = kap[j, z + 1, WORK]
            flux = react * v * (1.0 - v * v)
            flux = flux + (k + kap[j, z + 1, BEFORE]) * (val[j, z + 1, BEFORE] - v)
            flux = flux + (k + kap[j, z + 1, AFTER]) * (val[j, z + 1, AFTER] - v)
            flux = flux + (k + turn(k, 1)) * (turn(v, 1) - v)
            flux = flux + (k + turn(k, -1)) * (turn(v, -1) - v)
            flux = flux + (k + kap[j, z, WORK]) * (val[j, z, WORK] - v)
            flux = flux + (k + kap[j, z + 2, WORK]) * (val[j, z + 2, WORK] - v)
            grown = v - prev
            for m in range(4):
                term = q_rows[m][j] * flux - c_rows[m][j] * grown
                rhs[m] = term if j == 0 else rhs[m] + term
        for m in range(4):
            vec[0, m, z] = rhs[m]
        for b in range(2):
            al, be = scaled[b]
            ya[2 * b, z + 1, WORK] = al * rhs[2 * b] - be * rhs[2 * b + 1]
            ya[2 * b + 1, z + 1, WORK] = be * rhs[2 * b] + al * rhs[2 * b + 1]

    each_plane(nz, PREPARE_UNROLL, prepare)

    def spread(ref, m, z, rows=WORK):
        lo, hi = rows.start, rows.stop
        cut = slice(lo - FIRST, hi - FIRST)
        mid = ref[m, z + 1, lo:hi]
        in_y = fy[0, z, cut] * turn(mid, 1) + fy[1, z, cut] * turn(mid, -1)
        in_x = fx[0, z, cut] * ref[m, z + 1, lo - 1 : hi - 1] + fx[1, z, cut] * ref[m, z + 1, lo + 1 : hi + 1]
        in_z = fz[0, z, cut] * ref[m, z, lo:hi] + fz[1, z, cut] * ref[m, z + 2, lo:hi]
        return (in_x + in_z) + in_y

    for j in range(ITERS):

        def odd(z, j=j):
            for b in range(2):
                t0 = spread(ya, 2 * b, z)
                t1 = spread(ya, 2 * b + 1, z)
                al, be = alpha[b, z], beta[b, z]
                y0 = al * t0 - be * t1
                y1 = be * t0 + al * t1
                yb[2 * b, z + 1, WORK] = y0
                yb[2 * b + 1, z + 1, WORK] = y1
                sums_ref[j, 2 * b, z] = ya[2 * b, z + 1, OWN] + y0[8:24]
                sums_ref[j, 2 * b + 1, z] = ya[2 * b + 1, z + 1, OWN] + y1[8:24]

        def even(z, j=j):
            last = j == ITERS - 1
            rows = OWN if last else WORK
            cut = slice(rows.start - FIRST, rows.stop - FIRST)
            for b in range(2):
                new = []
                for m in (2 * b, 2 * b + 1):
                    v = spread(yb, m, z, rows)
                    if SHIFTS[j]:
                        v = v - SHIFTS[j] * vec[j, m, z, cut]
                    vec[j + 1, m, z, cut] = v
                    new.append(v)
                if not last:
                    al, be = alpha[b, z], beta[b, z]
                    ya[2 * b, z + 1, WORK] = al * new[0] - be * new[1]
                    ya[2 * b + 1, z + 1, WORK] = be * new[0] + al * new[1]

        each_plane(nz, STEP_UNROLL, odd)
        each_plane(nz, STEP_UNROLL, even)

    table[...] = jnp.zeros((LANES, LANES), jnp.float32)
    mine = half_mask(8)
    for b in range(2):

        def dots(z, carry):
            out = list(carry)
            for m in (2 * b, 2 * b + 1):
                for r in (8, 16):
                    cells = [vec[i, m, z, r : r + 8] for i in range(SIZE)]
                    for at, (i, j) in enumerate(PAIRS):
                        out[at] = out[at] + cells[i] * cells[j]
            return tuple(out)

        zero = jnp.zeros((8, LANES), jnp.float32)
        out = lax.fori_loop(0, nz, dots, tuple(zero for _ in PAIRS))
        for at in range(len(PAIRS)):
            row = jnp.sum(jnp.where(mine, out[at], 0.0), axis=0, keepdims=True)
            table[b * len(PAIRS) + at : b * len(PAIRS) + at + 1] = row
    total = jnp.sum(table[...].T, axis=0, keepdims=True)
    part_ref[...] = jnp.broadcast_to(total, part_ref.shape)


def step_weights(gram):
    table = {}
    for at, (i, j) in enumerate(PAIRS):
        table[i, j] = table[j, i] = gram[at]
    coef = [jnp.ones_like(gram[0])]
    weight = []
    step = coef[0]
    for k in range(ITERS):
        moved = [SHIFTS[j] * coef[j] for j in range(k + 1)] + [jnp.zeros_like(step)]
        for j in range(k + 1):
            moved[j + 1] = moved[j + 1] + coef[j]
        coef = coef + [jnp.zeros_like(step)]
        image = [coef[j] - moved[j] for j in range(k + 2)]
        num, den, bound = 0.0, 0.0, 0.0
        for i in range(k + 2):
            row, size = 0.0, 0.0
            for j in range(k + 2):
                term = table[i, j] * image[j]
                row = row + term
                size = size + jnp.abs(term)
            num = num + row * coef[i]
            den = den + row * image[i]
            bound = bound + size * jnp.abs(image[i])
        step = jnp.where(den > bound * 6e-8, num / (jnp.maximum(den, 0.0) + tiny_value), step)
        weight = weight + [jnp.zeros_like(step)]
        for j in range(k + 1):
            weight[j] = weight[j] + step * coef[j]
        coef = [coef[j] - step * image[j] for j in range(k + 2)]
    return weight


def send_kernel(consts, total_ref, sums_ref, other_ref, send_ref, weight_ref):
    eigen_basis = consts[0]
    nz, nx = other_ref.shape[1], other_ref.shape[2]
    section = lax.axis_index("section")
    total = jnp.sum(total_ref[...], axis=0, keepdims=True)
    count = len(PAIRS)
    weights = []
    for b in range(2):
        gram = [jnp.broadcast_to(total[:, b * count + at : b * count + at + 1], (1, LANES)) for at in range(count)]
        weights.append(step_weights(gram))
    for b in range(2):
        for j in range(ITERS):
            weight_ref[b * ITERS + j : b * ITERS + j + 1] = weights[b][j]
    basis = [
        [jnp.where(section == 0, jnp.float32(eigen_basis[2 + r][m]), jnp.float32(eigen_basis[r][m])) for m in range(4)]
        for r in range(2)
    ]
    mine = half_mask(nx)

    def combine(z):
        outs = [other_ref[r, z] for r in range(2)]
        for m in range(4):
            field = weights[m // 2][0] * sums_ref[0, m, z]
            for j in range(1, ITERS):
                field = field + weights[m // 2][j] * sums_ref[j, m, z]
            outs = [outs[r] + basis[r][m] * field for r in range(2)]
        send_ref[z] = jnp.where(mine, outs[0], turn(outs[1], LANES // 2))

    each_plane(nz, 4, combine)


def mine_kernel(consts, weight_ref, sums_ref, own_ref, mine_ref):
    eigen_basis = consts[0]
    nz = own_ref.shape[1]
    section = lax.axis_index("section")
    weights = [[weight_ref[b * ITERS + j : b * ITERS + j + 1] for j in range(ITERS)] for b in range(2)]
    basis = [
        [jnp.where(section == 0, jnp.float32(eigen_basis[r][m]), jnp.float32(eigen_basis[2 + r][m])) for m in range(4)]
        for r in range(2)
    ]

    def combine(z):
        outs = [own_ref[r, z] for r in range(2)]
        for m in range(4):
            field = weights[m // 2][0] * sums_ref[0, m, z]
            for j in range(1, ITERS):
                field = field + weights[m // 2][j] * sums_ref[j, m, z]
            outs = [outs[r] + basis[r][m] * field for r in range(2)]
        mine_ref[0, z] = outs[0]
        mine_ref[1, z] = outs[1]

    each_plane(nz, 4, combine)


def join_kernel(mine_ref, other_ref, out_ref):
    nz, nx = mine_ref.shape[1], mine_ref.shape[2]
    mine = half_mask(nx)
    for z in range(nz):
        other = other_ref[z]
        out_ref[0, z] = jnp.where(mine, mine_ref[0, z], other)
        out_ref[1, z] = jnp.where(mine, mine_ref[1, z], turn(other, LANES // 2))


def call(kernel, outs, scratch=(), flops=1_000_000, name=None, limit=12):
    many = isinstance(outs, list)
    shapes = [jax.ShapeDtypeStruct(o, jnp.float32) for o in (outs if many else [outs])]

    def run(*args):
        moved = 4 * sum(int(a.size) for a in args) + 4 * sum(int(functools.reduce(lambda p, q: p * q, s.shape, 1)) for s in shapes)
        return pl.pallas_call(
            kernel,
            out_shape=shapes if many else shapes[0],
            in_specs=[pl.BlockSpec(memory_space=pltpu.VMEM)] * len(args),
            out_specs=[pl.BlockSpec(memory_space=pltpu.VMEM)] * len(shapes) if many else pl.BlockSpec(memory_space=pltpu.VMEM),
            scratch_shapes=[pltpu.VMEM(s, jnp.float32) for s in scratch],
            compiler_params=pltpu.CompilerParams(vmem_limit_bytes=limit * 1024 * 1024),
            cost_estimate=pl.CostEstimate(flops=flops, bytes_accessed=moved, transcendentals=0),
            name=name,
        )(*args)

    return run


def swaps(count, start):
    return [pair for i in range(start, count - 1, 2) for pair in ((i, i + 1), (i + 1, i))]


def body(previous, sections, diffusivity, reaction):
    consts = constants()
    nz, nx, ny = previous.shape
    columns, rows = lax.axis_size("sy"), lax.axis_size("sx")
    axes = ("section", "sx", "sy")
    partner = [(0, 1), (1, 0)]
    other = lax.ppermute(sections, "section", partner)
    shapes = [(nz // 2, nx, ny), (nz * PARTS + nz // 2, TALL, ny), (nz * PARTS + nz // 2, TALL, ny)]
    packed = call(own_kernel, shapes, name="own")(sections, previous, diffusivity, reaction)
    border, near, far = call(other_kernel, shapes, name="other")(other, *packed)
    edges = [(s * columns + a, s * columns + b) for s in range(2) for a, b in swaps(columns, s)]
    border = lax.ppermute(border, ("section", "sy"), edges)
    near = lax.dynamic_update_slice(near, border, (nz * PARTS, 0, 0))
    far = lax.dynamic_update_slice(far, border, (nz * PARTS, 0, 0))
    far = lax.ppermute(far, "sx", swaps(rows, 1))
    near = lax.ppermute(near, "sx", swaps(rows, 0))
    peers = 2 * columns * rows
    padded, work = (nz + 2, ROWS, ny), (nz, LAST - FIRST, ny)
    scratch = [
        (4,) + padded, (4,) + padded, padded, work, work, work, (2,) + work, (2,) + work, (2,) + work, (2,) + work, (2,) + work,
        (SIZE, 4) + work, (4,) + padded, (4,) + padded, (LANES, LANES),
    ]
    part, sums = call(
        functools.partial(main_kernel, consts), [(peers, LANES), (ITERS, 4, nz, nx, ny)], scratch, 50_000_000, "main", 26
    )(sections, other, previous, diffusivity, reaction, border, near, far)
    total = lax.all_to_all(part.reshape(peers, 1, LANES), axes, 0, 0).reshape(peers, LANES)
    half, weight = call(functools.partial(send_kernel, consts), [previous.shape, (2 * ITERS, LANES)], name="send")(total, sums, other)
    got = lax.ppermute(half, "section", partner)
    mine = call(functools.partial(mine_kernel, consts), sections.shape, name="mine")(weight, sums, sections)
    return call(join_kernel, sections.shape, name="join")(mine, got)


def solution(mesh):
    in_specs = (
        P(None, "sx", "sy"),
        P("section", None, "sx", "sy"),
        P(None, "sx", "sy"),
        P(None, "sx", "sy"),
    )
    out_specs = P("section", None, "sx", "sy")
    return jax.shard_map(body, mesh=mesh, in_specs=in_specs, out_specs=out_specs, check_vma=False)
```

```python
import functools

import jax
import jax.numpy as jnp
from jax import lax
from jax.experimental import pallas as pl
from jax.experimental.pallas import tpu as pltpu
from jax.sharding import PartitionSpec as P

ITERS = 4
SHIFTS = (0.0, 0.9, 0.45, 0.7)
EDGE = 9
LANES = 128
SIZE = ITERS + 1
PAIRS = [(i, j) for i in range(SIZE) for j in range(i, SIZE)]
PREPARE_UNROLL = 2
STEP_UNROLL = 8


step_size = 1.0
tiny_value = 1e-06


def invert_table(matrix):
    order_n = len(matrix)
    augmented = [
        list(matrix[r]) + [1.0 if c == r else 0.0 for c in range(order_n)] for r in range(order_n)
    ]
    for col in range(order_n):
        pivot_row = max(range(col, order_n), key=lambda r: abs(augmented[r][col]))
        augmented[col], augmented[pivot_row] = (augmented[pivot_row], augmented[col])
        leading = augmented[col][col]
        augmented[col] = [v / leading for v in augmented[col]]
        for r in range(order_n):
            if r != col:
                factor = augmented[r][col]
                augmented[r] = [a - factor * b for a, b in zip(augmented[r], augmented[col])]
    return [row_values[order_n:] for row_values in augmented]


def table_product(left, right):
    return [
        [sum((left[i][k] * right[k][j] for k in range(len(right)))) for j in range(len(right[0]))]
        for i in range(len(left))
    ]


def pair_add(first, second):
    return (first[0] + second[0], first[1] + second[1])


def pair_sub(first, second):
    return (first[0] - second[0], first[1] - second[1])


def pair_mul(first, second):
    return (
        first[0] * second[0] - first[1] * second[1],
        first[0] * second[1] + first[1] * second[0],
    )


def pair_div(first, second):
    scale_sq = second[0] * second[0] + second[1] * second[1]
    return (
        (first[0] * second[0] + first[1] * second[1]) / scale_sq,
        (first[1] * second[0] - first[0] * second[1]) / scale_sq,
    )


def quartic_value(point):
    return (((210.0 * point - 480.0) * point + 360.0) * point - 96.0) * point + 6.0


def bisect_root(lower, upper):
    for count in range(200):
        middle = 0.5 * (lower + upper)
        if (quartic_value(lower) < 0.0) == (quartic_value(middle) < 0.0):
            lower = middle
        else:
            upper = middle
    return 0.5 * (lower + upper)


def radau_tables():
    abscissae = []
    grid_steps = 4000
    for m in range(grid_steps):
        lower = 0.999 * m / grid_steps
        upper = 0.999 * (m + 1) / grid_steps
        if (quartic_value(lower) < 0.0) != (quartic_value(upper) < 0.0):
            abscissae.append(bisect_root(lower, upper))
    abscissae.append(1.0)
    vander = [[abscissae[j] ** k for k in range(4)] for j in range(4)]
    moments = [[abscissae[i] ** (k + 1) / (k + 1) for k in range(4)] for i in range(4)]
    tableau = table_product(moments, invert_table(vander))
    inverse = invert_table(tableau)
    running = [list(row_values) for row_values in inverse]
    coeffs = []
    for k in range(1, 5):
        trace_value = sum((running[i][i] for i in range(4)))
        coeffs.append(-trace_value / k)
        shifted_table = [
            [running[i][j] + (coeffs[-1] if i == j else 0.0) for j in range(4)] for i in range(4)
        ]
        running = table_product(inverse, shifted_table)
    start_point = (0.4, 0.9)
    estimates = [(1.0, 0.0)]
    for k in range(3):
        estimates.append(pair_mul(estimates[-1], start_point))
    for count in range(500):
        for i in range(4):
            value = (1.0, 0.0)
            for coef_value in coeffs:
                value = pair_add(pair_mul(value, estimates[i]), (coef_value, 0.0))
            denom = (1.0, 0.0)
            for j in range(4):
                if j != i:
                    denom = pair_mul(denom, pair_sub(estimates[i], estimates[j]))
            estimates[i] = pair_sub(estimates[i], pair_div(value, denom))
    chosen = [m for m in range(4) if estimates[m][1] > 0.0]
    ranking = sorted(chosen, key=lambda m: -estimates[m][1])
    columns = []
    pairs = []
    for m in ranking:
        eigen_pair = estimates[m]
        system = [
            [
                (
                    inverse[i][j] - (eigen_pair[0] if i == j else 0.0),
                    -(eigen_pair[1] if i == j else 0.0),
                )
                for j in range(4)
            ]
            for i in range(3)
        ]
        rows_left = [
            [system[i][j] for j in range(3)] + [(-system[i][3][0], -system[i][3][1])]
            for i in range(3)
        ]
        for col in range(3):
            pivot_row = max(
                range(col, 3), key=lambda r: rows_left[r][col][0] ** 2 + rows_left[r][col][1] ** 2
            )
            rows_left[col], rows_left[pivot_row] = (rows_left[pivot_row], rows_left[col])
            leading = rows_left[col][col]
            rows_left[col] = [pair_div(v, leading) for v in rows_left[col]]
            for r in range(3):
                if r != col:
                    factor = rows_left[r][col]
                    rows_left[r] = [
                        pair_sub(a, pair_mul(factor, b))
                        for a, b in zip(rows_left[r], rows_left[col])
                    ]
        vector = [rows_left[i][3] for i in range(3)] + [(1.0, 0.0)]
        columns.append([v[0] for v in vector])
        columns.append([v[1] for v in vector])
        pairs.append((eigen_pair[0], eigen_pair[1]))
    eigen_basis = [[columns[j][i] for j in range(4)] for i in range(4)]
    basis_inverse = invert_table(eigen_basis)
    return (tableau, inverse, eigen_basis, basis_inverse, pairs)


def constants():
    tableau, inverse, eigen_basis, basis_inverse, pairs = radau_tables()
    shift_table = table_product(basis_inverse, inverse)
    shift_rows = [[v / step_size for v in row_values] for row_values in shift_table]
    pairs = [(p[0] / step_size, p[1] / step_size) for p in pairs]
    return eigen_basis, basis_inverse, shift_rows, pairs


def lane_ids(rows):
    return lax.broadcasted_iota(jnp.int32, (rows, LANES), 1)


def turn(cells, amount):
    return pltpu.roll(cells, amount % LANES, cells.ndim - 1)


def left_half():
    return lax.rem(lax.axis_index("section") + lax.axis_index("sy"), 2) == 1


def half_mask(rows):
    return (lane_ids(rows) < LANES // 2) == left_half()


ORDER = (0, 1, 4, 5, 6, 2, 3)
TALL = 16
PARTS = 4


def border_start():
    return jnp.where(left_half(), LANES - EDGE, 0)


def leaving_start():
    return jnp.where(left_half(), 0, LANES - EDGE)


def on_even_row():
    return lax.rem(lax.axis_index("sx"), 2) == 0


def pack(border_ref, near_ref, far_ref, load, fields, first_slot, partial):
    nz = 2 * border_ref.shape[0]
    nx = border_ref.shape[1]
    lanes = lane_ids(nx)
    start = leaving_start()
    even = on_even_row()

    def plane_pair(plane):
        tile = partial(plane)
        for part in range(2):
            z = part * (nz // 2) + plane
            for slot, f in enumerate(fields, first_slot):
                cell = load(f, z)
                at = part * 64 + f * EDGE
                moved = pltpu.roll(cell, lax.rem(at + LANES - start, LANES), 1)
                tile = jnp.where((lanes >= at) & (lanes < at + EDGE), moved, tile)
                entry, row = divmod(8 * slot, TALL)
                last, ninth = divmod(56 + slot, TALL)
                near_ref[z * PARTS + entry, row : row + 8] = jnp.where(even, cell[nx - 8 : nx], cell[0:8])
                far_ref[z * PARTS + entry, row : row + 8] = jnp.where(even, cell[0:8], cell[nx - 8 : nx])
                near_ref[z * PARTS + last, ninth : ninth + 1] = jnp.where(even, cell[nx - 9 : nx - 8], cell[8:9])
                far_ref[z * PARTS + last, ninth : ninth + 1] = jnp.where(even, cell[8:9], cell[nx - 9 : nx - 8])
        border_ref[plane] = tile

    each_plane(nz // 2, 4, plane_pair)


def own_kernel(own_ref, prev_ref, diff_ref, react_ref, border_ref, near_ref, far_ref):
    nx = prev_ref.shape[1]
    refs = {4: prev_ref, 5: diff_ref, 6: react_ref}
    load = lambda f, z: own_ref[f, z] if f < 2 else refs[f][z]
    pack(border_ref, near_ref, far_ref, load, ORDER[:5], 0, lambda plane: jnp.zeros((nx, LANES), jnp.float32))


def other_kernel(other_ref, own_border_ref, own_near_ref, own_far_ref, border_ref, near_ref, far_ref):
    near_ref[...] = own_near_ref[...]
    far_ref[...] = own_far_ref[...]
    pack(border_ref, near_ref, far_ref, lambda f, z: other_ref[f - 2, z], ORDER[5:], 5, lambda plane: own_border_ref[plane])


ROWS = 48
FIRST, LAST = 8, 40
OWN = slice(16, 32)
WORK = slice(FIRST, LAST)
BEFORE = slice(FIRST - 1, LAST - 1)
AFTER = slice(FIRST + 1, LAST + 1)


def each_plane(count, unroll, work):
    def group(i, carry):
        for u in range(unroll):
            work(i * unroll + u)
        return carry

    lax.fori_loop(0, count // unroll, group, 0)


def main_kernel(consts, own_ref, other_ref, prev_ref, diff_ref, react_ref, border_ref, near_side_ref, far_side_ref, near_ref, far_ref, part_ref, sums_ref,
                val, kap, frozen, prv, rea, dif, fx, fy, fz, alpha, beta, vec, ya, yb, table):
    eigen_basis, basis_inverse, shift_rows, pairs = consts
    nz, nx = prev_ref.shape[0], prev_ref.shape[1]
    section = lax.axis_index("section")
    zero_plane = jnp.zeros((ROWS, LANES), jnp.float32)
    zero_rows = jnp.zeros((FIRST, LANES), jnp.float32)
    start = border_start()
    even = on_even_row()
    lanes = lane_ids(ROWS)
    edge = (lanes >= start) & (lanes < start + EDGE)
    tile = lambda t: jnp.broadcast_to(t, (8, LANES))

    for at in (0, nz + 1):
        frozen[at] = zero_plane
        for f in range(4):
            for ref in (val, kap, ya, yb):
                ref[f, at] = zero_plane

    def both(entry, row, count):
        near, far = near_ref[entry, row : row + count], far_ref[entry, row : row + count]
        return jnp.where(even, far, near), jnp.where(even, near, far)

    def assemble(plane):
        low = jnp.where(even, far_side_ref[plane], near_side_ref[plane])
        high = jnp.where(even, near_side_ref[plane], far_side_ref[plane])
        sides = jnp.concatenate([tile(low[nx - 9 : nx - 8]), low[nx - 8 : nx], border_ref[plane], high[0:8], tile(high[8:9])], 0)
        for part in range(2):
            z = part * (nz // 2) + plane

            def column(f):
                slot = ORDER.index(f)
                mid = (own_ref[0, z], own_ref[1, z], prev_ref[z], diff_ref[z], react_ref[z], other_ref[0, z], other_ref[1, z])[slot]
                entry, row = divmod(8 * slot, TALL)
                low, high = both(z * PARTS + entry, row, 8)
                entry, row = divmod(56 + slot, TALL)
                low_end, high_end = both(z * PARTS + entry, row, 1)
                cells = jnp.concatenate([tile(low_end), low, mid, high, tile(high_end)], 0)
                at = part * 64 + f * EDGE
                return jnp.where(edge, pltpu.roll(sides, lax.rem(start + LANES - at, LANES), 1), cells)

            diff, prev, react = column(5), column(4), column(6)
            frozen[z + 1] = diff * (0.5 + 0.25 * jnp.tanh(prev))
            prv[z] = prev[WORK]
            rea[z] = react[WORK]
            dif[z] = diff[WORK]
            for f in range(4):
                value = column(f)
                val[f, z + 1] = value
                kap[f, z + 1] = diff * (0.5 + 0.25 * jnp.tanh(value))
                for ref in (ya, yb):
                    ref[f, z + 1, 0:FIRST] = zero_rows
                    ref[f, z + 1, LAST:ROWS] = zero_rows

    each_plane(nz // 2, 1, assemble)

    def pick(matrix, m, j):
        return jnp.where(section == 0, jnp.float32(matrix[m][j]), jnp.float32(matrix[m][(j + 2) % 4]))

    q_rows = [[pick(basis_inverse, m, j) for j in range(4)] for m in range(4)]
    c_rows = [[pick(shift_rows, m, j) for j in range(4)] for m in range(4)]

    def prepare(z):
        mid = frozen[z + 1, WORK]
        faces = [
            mid + frozen[z + 1, BEFORE], mid + frozen[z + 1, AFTER], mid + turn(mid, 1), mid + turn(mid, -1),
            mid + frozen[z, WORK], mid + frozen[z + 2, WORK],
        ]
        for at, ref in enumerate((fx, fy, fz)):
            ref[0, z] = faces[2 * at]
            ref[1, z] = faces[2 * at + 1]
        prev, react = prv[z], rea[z]
        base = ((faces[0] + faces[1]) + (faces[2] + faces[3])) + (faces[4] + faces[5]) - react * (1.0 - 3.0 * prev * prev)
        inside = jnp.where(dif[z] > 0.0, 1.0, 0.0)
        scaled = []
        for b in range(2):
            real, imag = pairs[b]
            diag = base + real
            scale = inside / (diag * diag + imag * imag)
            scaled.append((diag * scale, imag * scale))
            alpha[b, z], beta[b, z] = scaled[b]
        rhs = [None] * 4
        for j in range(4):
            v = val[j, z + 1, WORK]
            k = kap[j, z + 1, WORK]
            flux = react * v * (1.0 - v * v)
            flux = flux + (k + kap[j, z + 1, BEFORE]) * (val[j, z + 1, BEFORE] - v)
            flux = flux + (k + kap[j, z + 1, AFTER]) * (val[j, z + 1, AFTER] - v)
            flux = flux + (k + turn(k, 1)) * (turn(v, 1) - v)
            flux = flux + (k + turn(k, -1)) * (turn(v, -1) - v)
            flux = flux + (k + kap[j, z, WORK]) * (val[j, z, WORK] - v)
            flux = flux + (k + kap[j, z + 2, WORK]) * (val[j, z + 2, WORK] - v)
            grown = v - prev
            for m in range(4):
                term = q_rows[m][j] * flux - c_rows[m][j] * grown
                rhs[m] = term if j == 0 else rhs[m] + term
        for m in range(4):
            vec[0, m, z] = rhs[m]
        for b in range(2):
            al, be = scaled[b]
            ya[2 * b, z + 1, WORK] = al * rhs[2 * b] - be * rhs[2 * b + 1]
            ya[2 * b + 1, z + 1, WORK] = be * rhs[2 * b] + al * rhs[2 * b + 1]

    each_plane(nz, PREPARE_UNROLL, prepare)

    def spread(ref, m, z, rows=WORK):
        lo, hi = rows.start, rows.stop
        cut = slice(lo - FIRST, hi - FIRST)
        mid = ref[m, z + 1, lo:hi]
        in_y = fy[0, z, cut] * turn(mid, 1) + fy[1, z, cut] * turn(mid, -1)
        in_x = fx[0, z, cut] * ref[m, z + 1, lo - 1 : hi - 1] + fx[1, z, cut] * ref[m, z + 1, lo + 1 : hi + 1]
        in_z = fz[0, z, cut] * ref[m, z, lo:hi] + fz[1, z, cut] * ref[m, z + 2, lo:hi]
        return (in_x + in_z) + in_y

    for j in range(ITERS):

        def odd(z, j=j):
            for b in range(2):
                t0 = spread(ya, 2 * b, z)
                t1 = spread(ya, 2 * b + 1, z)
                al, be = alpha[b, z], beta[b, z]
                y0 = al * t0 - be * t1
                y1 = be * t0 + al * t1
                yb[2 * b, z + 1, WORK] = y0
                yb[2 * b + 1, z + 1, WORK] = y1
                sums_ref[j, 2 * b, z] = ya[2 * b, z + 1, OWN] + y0[8:24]
                sums_ref[j, 2 * b + 1, z] = ya[2 * b + 1, z + 1, OWN] + y1[8:24]

        def even(z, j=j):
            last = j == ITERS - 1
            rows = OWN if last else WORK
            cut = slice(rows.start - FIRST, rows.stop - FIRST)
            for b in range(2):
                new = []
                for m in (2 * b, 2 * b + 1):
                    v = spread(yb, m, z, rows)
                    if SHIFTS[j]:
                        v = v - SHIFTS[j] * vec[j, m, z, cut]
                    vec[j + 1, m, z, cut] = v
                    new.append(v)
                if not last:
                    al, be = alpha[b, z], beta[b, z]
                    ya[2 * b, z + 1, WORK] = al * new[0] - be * new[1]
                    ya[2 * b + 1, z + 1, WORK] = be * new[0] + al * new[1]

        each_plane(nz, STEP_UNROLL, odd)
        each_plane(nz, STEP_UNROLL, even)

    table[...] = jnp.zeros((LANES, LANES), jnp.float32)
    mine = half_mask(8)
    for b in range(2):

        def dots(z, carry):
            out = list(carry)
            for m in (2 * b, 2 * b + 1):
                for r in (8, 16):
                    cells = [vec[i, m, z, r : r + 8] for i in range(SIZE)]
                    for at, (i, j) in enumerate(PAIRS):
                        out[at] = out[at] + cells[i] * cells[j]
            return tuple(out)

        zero = jnp.zeros((8, LANES), jnp.float32)
        out = lax.fori_loop(0, nz, dots, tuple(zero for _ in PAIRS))
        for at in range(len(PAIRS)):
            row = jnp.sum(jnp.where(mine, out[at], 0.0), axis=0, keepdims=True)
            table[b * len(PAIRS) + at : b * len(PAIRS) + at + 1] = row
    total = jnp.sum(table[...].T, axis=0, keepdims=True)
    part_ref[...] = jnp.broadcast_to(total, part_ref.shape)


def step_weights(gram):
    table = {}
    for at, (i, j) in enumerate(PAIRS):
        table[i, j] = table[j, i] = gram[at]
    coef = [jnp.ones_like(gram[0])]
    weight = []
    step = coef[0]
    for k in range(ITERS):
        moved = [SHIFTS[j] * coef[j] for j in range(k + 1)] + [jnp.zeros_like(step)]
        for j in range(k + 1):
            moved[j + 1] = moved[j + 1] + coef[j]
        coef = coef + [jnp.zeros_like(step)]
        image = [coef[j] - moved[j] for j in range(k + 2)]
        num, den, bound = 0.0, 0.0, 0.0
        for i in range(k + 2):
            row, size = 0.0, 0.0
            for j in range(k + 2):
                term = table[i, j] * image[j]
                row = row + term
                size = size + jnp.abs(term)
            num = num + row * coef[i]
            den = den + row * image[i]
            bound = bound + size * jnp.abs(image[i])
        step = jnp.where(den > bound * 6e-8, num / (jnp.maximum(den, 0.0) + tiny_value), step)
        weight = weight + [jnp.zeros_like(step)]
        for j in range(k + 1):
            weight[j] = weight[j] + step * coef[j]
        coef = [coef[j] - step * image[j] for j in range(k + 2)]
    return weight


def send_kernel(consts, total_ref, sums_ref, other_ref, send_ref, weight_ref):
    eigen_basis = consts[0]
    nz, nx = other_ref.shape[1], other_ref.shape[2]
    section = lax.axis_index("section")
    total = jnp.sum(total_ref[...], axis=0, keepdims=True)
    count = len(PAIRS)
    weights = []
    for b in range(2):
        gram = [jnp.broadcast_to(total[:, b * count + at : b * count + at + 1], (1, LANES)) for at in range(count)]
        weights.append(step_weights(gram))
    for b in range(2):
        for j in range(ITERS):
            weight_ref[b * ITERS + j : b * ITERS + j + 1] = weights[b][j]
    basis = [
        [jnp.where(section == 0, jnp.float32(eigen_basis[2 + r][m]), jnp.float32(eigen_basis[r][m])) for m in range(4)]
        for r in range(2)
    ]
    mine = half_mask(nx)

    def combine(z):
        outs = [other_ref[r, z] for r in range(2)]
        for m in range(4):
            field = weights[m // 2][0] * sums_ref[0, m, z]
            for j in range(1, ITERS):
                field = field + weights[m // 2][j] * sums_ref[j, m, z]
            outs = [outs[r] + basis[r][m] * field for r in range(2)]
        send_ref[z] = jnp.where(mine, outs[0], turn(outs[1], LANES // 2))

    each_plane(nz, 4, combine)


def mine_kernel(consts, weight_ref, sums_ref, own_ref, mine_ref):
    eigen_basis = consts[0]
    nz = own_ref.shape[1]
    section = lax.axis_index("section")
    weights = [[weight_ref[b * ITERS + j : b * ITERS + j + 1] for j in range(ITERS)] for b in range(2)]
    basis = [
        [jnp.where(section == 0, jnp.float32(eigen_basis[r][m]), jnp.float32(eigen_basis[2 + r][m])) for m in range(4)]
        for r in range(2)
    ]

    def combine(z):
        outs = [own_ref[r, z] for r in range(2)]
        for m in range(4):
            field = weights[m // 2][0] * sums_ref[0, m, z]
            for j in range(1, ITERS):
                field = field + weights[m // 2][j] * sums_ref[j, m, z]
            outs = [outs[r] + basis[r][m] * field for r in range(2)]
        mine_ref[0, z] = outs[0]
        mine_ref[1, z] = outs[1]

    each_plane(nz, 4, combine)


def join_kernel(mine_ref, other_ref, out_ref):
    nz, nx = mine_ref.shape[1], mine_ref.shape[2]
    mine = half_mask(nx)
    for z in range(nz):
        other = other_ref[z]
        out_ref[0, z] = jnp.where(mine, mine_ref[0, z], other)
        out_ref[1, z] = jnp.where(mine, mine_ref[1, z], turn(other, LANES // 2))


def call(kernel, outs, scratch=(), flops=1_000_000, name=None, limit=12):
    many = isinstance(outs, list)
    shapes = [jax.ShapeDtypeStruct(o, jnp.float32) for o in (outs if many else [outs])]

    def run(*args):
        moved = 4 * sum(int(a.size) for a in args) + 4 * sum(int(functools.reduce(lambda p, q: p * q, s.shape, 1)) for s in shapes)
        return pl.pallas_call(
            kernel,
            out_shape=shapes if many else shapes[0],
            in_specs=[pl.BlockSpec(memory_space=pltpu.VMEM)] * len(args),
            out_specs=[pl.BlockSpec(memory_space=pltpu.VMEM)] * len(shapes) if many else pl.BlockSpec(memory_space=pltpu.VMEM),
            scratch_shapes=[pltpu.VMEM(s, jnp.float32) for s in scratch],
            compiler_params=pltpu.CompilerParams(vmem_limit_bytes=limit * 1024 * 1024),
            cost_estimate=pl.CostEstimate(flops=flops, bytes_accessed=moved, transcendentals=0),
            name=name,
        )(*args)

    return run


def swaps(count, start):
    return [pair for i in range(start, count - 1, 2) for pair in ((i, i + 1), (i + 1, i))]


def body(previous, sections, diffusivity, reaction):
    consts = constants()
    nz, nx, ny = previous.shape
    columns, rows = lax.axis_size("sy"), lax.axis_size("sx")
    axes = ("section", "sx", "sy")
    partner = [(0, 1), (1, 0)]
    other = lax.ppermute(sections, "section", partner)
    shapes = [(nz // 2, nx, ny), (nz * PARTS, TALL, ny), (nz * PARTS, TALL, ny)]
    packed = call(own_kernel, shapes, name="own")(sections, previous, diffusivity, reaction)
    border, near, far = call(other_kernel, shapes, name="other")(other, *packed)
    on_chip, off_chip, stay = swaps(rows, 0), swaps(rows, 1), [(i, i) for i in range(rows)]

    def across(in_x):
        return [
            ((s * rows + a) * columns + c, (s * rows + b) * columns + d) for s in range(2) for a, b in in_x for c, d in swaps(columns, s)
        ]

    far = lax.ppermute(far, "sx", off_chip)
    near = lax.ppermute(near, "sx", on_chip)
    far_side = lax.ppermute(border, axes, across(off_chip))
    near_side = lax.ppermute(border, axes, across(on_chip))
    border = lax.ppermute(border, axes, across(stay))
    peers = 2 * columns * rows
    padded, work = (nz + 2, ROWS, ny), (nz, LAST - FIRST, ny)
    scratch = [
        (4,) + padded, (4,) + padded, padded, work, work, work, (2,) + work, (2,) + work, (2,) + work, (2,) + work, (2,) + work,
        (SIZE, 4) + work, (4,) + padded, (4,) + padded, (LANES, LANES),
    ]
    part, sums = call(
        functools.partial(main_kernel, consts), [(peers, LANES), (ITERS, 4, nz, nx, ny)], scratch, 50_000_000, "main", 26
    )(sections, other, previous, diffusivity, reaction, border, near_side, far_side, near, far)
    total = lax.all_to_all(part.reshape(peers, 1, LANES), axes, 0, 0).reshape(peers, LANES)
    half, weight = call(functools.partial(send_kernel, consts), [previous.shape, (2 * ITERS, LANES)], name="send")(total, sums, other)
    got = lax.ppermute(half, "section", partner)
    mine = call(functools.partial(mine_kernel, consts), sections.shape, name="mine")(weight, sums, sections)
    return call(join_kernel, sections.shape, name="join")(mine, got)


def solution(mesh):
    in_specs = (
        P(None, "sx", "sy"),
        P("section", None, "sx", "sy"),
        P(None, "sx", "sy"),
        P(None, "sx", "sy"),
    )
    out_specs = P("section", None, "sx", "sy")
    return jax.shard_map(body, mesh=mesh, in_specs=in_specs, out_specs=out_specs, check_vma=False)
```

```python
import functools

import jax
import jax.numpy as jnp
from jax import lax
from jax.experimental import pallas as pl
from jax.experimental.pallas import tpu as pltpu
from jax.sharding import PartitionSpec as P

ITERS = 4
SHIFTS = (0.0, 0.9, 0.45, 0.7)
EDGE = 9
LANES = 128
SIZE = ITERS + 1
PAIRS = [(i, j) for i in range(SIZE) for j in range(i, SIZE)]
PREPARE_UNROLL = 2
STEP_UNROLL = 8


step_size = 1.0
tiny_value = 1e-06


def invert_table(matrix):
    order_n = len(matrix)
    augmented = [
        list(matrix[r]) + [1.0 if c == r else 0.0 for c in range(order_n)] for r in range(order_n)
    ]
    for col in range(order_n):
        pivot_row = max(range(col, order_n), key=lambda r: abs(augmented[r][col]))
        augmented[col], augmented[pivot_row] = (augmented[pivot_row], augmented[col])
        leading = augmented[col][col]
        augmented[col] = [v / leading for v in augmented[col]]
        for r in range(order_n):
            if r != col:
                factor = augmented[r][col]
                augmented[r] = [a - factor * b for a, b in zip(augmented[r], augmented[col])]
    return [row_values[order_n:] for row_values in augmented]


def table_product(left, right):
    return [
        [sum((left[i][k] * right[k][j] for k in range(len(right)))) for j in range(len(right[0]))]
        for i in range(len(left))
    ]


def pair_add(first, second):
    return (first[0] + second[0], first[1] + second[1])


def pair_sub(first, second):
    return (first[0] - second[0], first[1] - second[1])


def pair_mul(first, second):
    return (
        first[0] * second[0] - first[1] * second[1],
        first[0] * second[1] + first[1] * second[0],
    )


def pair_div(first, second):
    scale_sq = second[0] * second[0] + second[1] * second[1]
    return (
        (first[0] * second[0] + first[1] * second[1]) / scale_sq,
        (first[1] * second[0] - first[0] * second[1]) / scale_sq,
    )


def quartic_value(point):
    return (((210.0 * point - 480.0) * point + 360.0) * point - 96.0) * point + 6.0


def bisect_root(lower, upper):
    for count in range(200):
        middle = 0.5 * (lower + upper)
        if (quartic_value(lower) < 0.0) == (quartic_value(middle) < 0.0):
            lower = middle
        else:
            upper = middle
    return 0.5 * (lower + upper)


def radau_tables():
    abscissae = []
    grid_steps = 4000
    for m in range(grid_steps):
        lower = 0.999 * m / grid_steps
        upper = 0.999 * (m + 1) / grid_steps
        if (quartic_value(lower) < 0.0) != (quartic_value(upper) < 0.0):
            abscissae.append(bisect_root(lower, upper))
    abscissae.append(1.0)
    vander = [[abscissae[j] ** k for k in range(4)] for j in range(4)]
    moments = [[abscissae[i] ** (k + 1) / (k + 1) for k in range(4)] for i in range(4)]
    tableau = table_product(moments, invert_table(vander))
    inverse = invert_table(tableau)
    running = [list(row_values) for row_values in inverse]
    coeffs = []
    for k in range(1, 5):
        trace_value = sum((running[i][i] for i in range(4)))
        coeffs.append(-trace_value / k)
        shifted_table = [
            [running[i][j] + (coeffs[-1] if i == j else 0.0) for j in range(4)] for i in range(4)
        ]
        running = table_product(inverse, shifted_table)
    start_point = (0.4, 0.9)
    estimates = [(1.0, 0.0)]
    for k in range(3):
        estimates.append(pair_mul(estimates[-1], start_point))
    for count in range(500):
        for i in range(4):
            value = (1.0, 0.0)
            for coef_value in coeffs:
                value = pair_add(pair_mul(value, estimates[i]), (coef_value, 0.0))
            denom = (1.0, 0.0)
            for j in range(4):
                if j != i:
                    denom = pair_mul(denom, pair_sub(estimates[i], estimates[j]))
            estimates[i] = pair_sub(estimates[i], pair_div(value, denom))
    chosen = [m for m in range(4) if estimates[m][1] > 0.0]
    ranking = sorted(chosen, key=lambda m: -estimates[m][1])
    columns = []
    pairs = []
    for m in ranking:
        eigen_pair = estimates[m]
        system = [
            [
                (
                    inverse[i][j] - (eigen_pair[0] if i == j else 0.0),
                    -(eigen_pair[1] if i == j else 0.0),
                )
                for j in range(4)
            ]
            for i in range(3)
        ]
        rows_left = [
            [system[i][j] for j in range(3)] + [(-system[i][3][0], -system[i][3][1])]
            for i in range(3)
        ]
        for col in range(3):
            pivot_row = max(
                range(col, 3), key=lambda r: rows_left[r][col][0] ** 2 + rows_left[r][col][1] ** 2
            )
            rows_left[col], rows_left[pivot_row] = (rows_left[pivot_row], rows_left[col])
            leading = rows_left[col][col]
            rows_left[col] = [pair_div(v, leading) for v in rows_left[col]]
            for r in range(3):
                if r != col:
                    factor = rows_left[r][col]
                    rows_left[r] = [
                        pair_sub(a, pair_mul(factor, b))
                        for a, b in zip(rows_left[r], rows_left[col])
                    ]
        vector = [rows_left[i][3] for i in range(3)] + [(1.0, 0.0)]
        columns.append([v[0] for v in vector])
        columns.append([v[1] for v in vector])
        pairs.append((eigen_pair[0], eigen_pair[1]))
    eigen_basis = [[columns[j][i] for j in range(4)] for i in range(4)]
    basis_inverse = invert_table(eigen_basis)
    return (tableau, inverse, eigen_basis, basis_inverse, pairs)


def constants():
    tableau, inverse, eigen_basis, basis_inverse, pairs = radau_tables()
    shift_table = table_product(basis_inverse, inverse)
    shift_rows = [[v / step_size for v in row_values] for row_values in shift_table]
    pairs = [(p[0] / step_size, p[1] / step_size) for p in pairs]
    return eigen_basis, basis_inverse, shift_rows, pairs


def lane_ids(rows):
    return lax.broadcasted_iota(jnp.int32, (rows, LANES), 1)


def turn(cells, amount):
    return pltpu.roll(cells, amount % LANES, cells.ndim - 1)


def left_half():
    return lax.rem(lax.axis_index("section") + lax.axis_index("sy"), 2) == 1


def half_mask(rows):
    return (lane_ids(rows) < LANES // 2) == left_half()


ORDER = (0, 1, 4, 5, 6, 2, 3)
TALL = 16
OWN_PARTS = 3


def border_start():
    return jnp.where(left_half(), LANES - EDGE, 0)


def leaving_start():
    return jnp.where(left_half(), 0, LANES - EDGE)


def on_even_row():
    return lax.rem(lax.axis_index("sx"), 2) == 0


def own_place(slot, z):
    entry, row = divmod(8 * slot, TALL)
    last, ninth = divmod(40 + slot, TALL)
    return z * OWN_PARTS + entry, row, z * OWN_PARTS + last, ninth


def other_place(slot, z, nz):
    return z, 8 * slot, nz + z // 8, 2 * lax.rem(z, 8) + slot


def pack(border_ref, near_ref, far_ref, load, fields, place, partial):
    nz = 2 * border_ref.shape[0]
    nx = border_ref.shape[1]
    lanes = lane_ids(nx)
    start = leaving_start()
    even = on_even_row()

    for plane in range(nz // 2):
        tile = partial(plane)
        for part in range(2):
            z = part * (nz // 2) + plane
            for slot, f in enumerate(fields):
                cell = load(f, z)
                at = part * 64 + f * EDGE
                moved = pltpu.roll(cell, lax.rem(at + LANES - start, LANES), 1)
                tile = jnp.where((lanes >= at) & (lanes < at + EDGE), moved, tile)
                entry, row, last, ninth = place(slot, z)
                near_ref[entry, row : row + 8] = jnp.where(even, cell[nx - 8 : nx], cell[0:8])
                far_ref[entry, row : row + 8] = jnp.where(even, cell[0:8], cell[nx - 8 : nx])
                near_ref[last, ninth : ninth + 1] = jnp.where(even, cell[nx - 9 : nx - 8], cell[8:9])
                far_ref[last, ninth : ninth + 1] = jnp.where(even, cell[8:9], cell[nx - 9 : nx - 8])
        border_ref[plane] = tile


def own_kernel(own_ref, prev_ref, diff_ref, react_ref, border_ref, near_ref, far_ref):
    nx = prev_ref.shape[1]
    refs = {4: prev_ref, 5: diff_ref, 6: react_ref}
    load = lambda f, z: own_ref[f, z] if f < 2 else refs[f][z]
    pack(border_ref, near_ref, far_ref, load, ORDER[:5], own_place, lambda plane: jnp.zeros((nx, LANES), jnp.float32))


def other_kernel(other_ref, own_border_ref, border_ref, near_ref, far_ref):
    nz = other_ref.shape[1]

    def place(slot, z):
        return z, 8 * slot, nz + z // 8, 2 * (z % 8) + slot

    pack(border_ref, near_ref, far_ref, lambda f, z: other_ref[f - 2, z], ORDER[5:], place, lambda plane: own_border_ref[plane])


ROWS = 48
FIRST, LAST = 8, 40
OWN = slice(16, 32)
WORK = slice(FIRST, LAST)
BEFORE = slice(FIRST - 1, LAST - 1)
AFTER = slice(FIRST + 1, LAST + 1)


def each_plane(count, unroll, work):
    def group(i, carry):
        for u in range(unroll):
            work(i * unroll + u)
        return carry

    lax.fori_loop(0, count // unroll, group, 0)


def main_kernel(consts, own_ref, other_ref, prev_ref, diff_ref, react_ref, border_ref, own_near_ref, own_far_ref, near_ref, far_ref, part_ref, sums_ref,
                val, kap, frozen, prv, rea, dif, fx, fy, fz, alpha, beta, vec, ya, yb, table):
    eigen_basis, basis_inverse, shift_rows, pairs = consts
    nz, nx = prev_ref.shape[0], prev_ref.shape[1]
    section = lax.axis_index("section")
    zero_plane = jnp.zeros((ROWS, LANES), jnp.float32)
    zero_rows = jnp.zeros((FIRST, LANES), jnp.float32)
    start = border_start()
    even = on_even_row()
    lanes = lane_ids(ROWS)
    edge = (lanes >= start) & (lanes < start + EDGE)
    tile = lambda t: jnp.broadcast_to(t, (8, LANES))

    for at in (0, nz + 1):
        frozen[at] = zero_plane
        for f in range(4):
            for ref in (val, kap, ya, yb):
                ref[f, at] = zero_plane

    def both(slot, entry, row, count):
        refs = (own_near_ref, own_far_ref) if slot < 5 else (near_ref, far_ref)
        near, far = [ref[entry, pl.ds(row, count)] for ref in refs]
        return jnp.where(even, far, near), jnp.where(even, near, far)

    def assemble(plane):
        at = nz + nz // 8 + plane
        low = jnp.where(even, far_ref[at], near_ref[at])
        high = jnp.where(even, near_ref[at], far_ref[at])
        sides = jnp.concatenate([tile(low[nx - 9 : nx - 8]), low[nx - 8 : nx], border_ref[plane], high[0:8], tile(high[8:9])], 0)
        for part in range(2):
            z = part * (nz // 2) + plane

            def column(f):
                slot = ORDER.index(f)
                mid = (own_ref[0, z], own_ref[1, z], prev_ref[z], diff_ref[z], react_ref[z], other_ref[0, z], other_ref[1, z])[slot]
                entry, row, last, ninth = own_place(slot, z) if slot < 5 else other_place(slot - 5, z, nz)
                low, high = both(slot, entry, row, 8)
                low_end, high_end = both(slot, last, ninth, 1)
                cells = jnp.concatenate([tile(low_end), low, mid, high, tile(high_end)], 0)
                at = part * 64 + f * EDGE
                return jnp.where(edge, pltpu.roll(sides, lax.rem(start + LANES - at, LANES), 1), cells)

            diff, prev, react = column(5), column(4), column(6)
            frozen[z + 1] = diff * (0.5 + 0.25 * jnp.tanh(prev))
            prv[z] = prev[WORK]
            rea[z] = react[WORK]
            dif[z] = diff[WORK]
            for f in range(4):
                value = column(f)
                val[f, z + 1] = value
                kap[f, z + 1] = diff * (0.5 + 0.25 * jnp.tanh(value))
                for ref in (ya, yb):
                    ref[f, z + 1, 0:FIRST] = zero_rows
                    ref[f, z + 1, LAST:ROWS] = zero_rows

    each_plane(nz // 2, 1, assemble)

    def pick(matrix, m, j):
        return jnp.where(section == 0, jnp.float32(matrix[m][j]), jnp.float32(matrix[m][(j + 2) % 4]))

    q_rows = [[pick(basis_inverse, m, j) for j in range(4)] for m in range(4)]
    c_rows = [[pick(shift_rows, m, j) for j in range(4)] for m in range(4)]

    def prepare(z):
        mid = frozen[z + 1, WORK]
        faces = [
            mid + frozen[z + 1, BEFORE], mid + frozen[z + 1, AFTER], mid + turn(mid, 1), mid + turn(mid, -1),
            mid + frozen[z, WORK], mid + frozen[z + 2, WORK],
        ]
        for at, ref in enumerate((fx, fy, fz)):
            ref[0, z] = faces[2 * at]
            ref[1, z] = faces[2 * at + 1]
        prev, react = prv[z], rea[z]
        base = ((faces[0] + faces[1]) + (faces[2] + faces[3])) + (faces[4] + faces[5]) - react * (1.0 - 3.0 * prev * prev)
        inside = jnp.where(dif[z] > 0.0, 1.0, 0.0)
        scaled = []
        for b in range(2):
            real, imag = pairs[b]
            diag = base + real
            scale = inside / (diag * diag + imag * imag)
            scaled.append((diag * scale, imag * scale))
            alpha[b, z], beta[b, z] = scaled[b]
        rhs = [None] * 4
        for j in range(4):
            v = val[j, z + 1, WORK]
            k = kap[j, z + 1, WORK]
            flux = react * v * (1.0 - v * v)
            flux = flux + (k + kap[j, z + 1, BEFORE]) * (val[j, z + 1, BEFORE] - v)
            flux = flux + (k + kap[j, z + 1, AFTER]) * (val[j, z + 1, AFTER] - v)
            flux = flux + (k + turn(k, 1)) * (turn(v, 1) - v)
            flux = flux + (k + turn(k, -1)) * (turn(v, -1) - v)
            flux = flux + (k + kap[j, z, WORK]) * (val[j, z, WORK] - v)
            flux = flux + (k + kap[j, z + 2, WORK]) * (val[j, z + 2, WORK] - v)
            grown = v - prev
            for m in range(4):
                term = q_rows[m][j] * flux - c_rows[m][j] * grown
                rhs[m] = term if j == 0 else rhs[m] + term
        for m in range(4):
            vec[0, m, z] = rhs[m]
        for b in range(2):
            al, be = scaled[b]
            ya[2 * b, z + 1, WORK] = al * rhs[2 * b] - be * rhs[2 * b + 1]
            ya[2 * b + 1, z + 1, WORK] = be * rhs[2 * b] + al * rhs[2 * b + 1]

    each_plane(nz, PREPARE_UNROLL, prepare)

    def spread(ref, m, z, rows=WORK):
        lo, hi = rows.start, rows.stop
        cut = slice(lo - FIRST, hi - FIRST)
        mid = ref[m, z + 1, lo:hi]
        in_y = fy[0, z, cut] * turn(mid, 1) + fy[1, z, cut] * turn(mid, -1)
        in_x = fx[0, z, cut] * ref[m, z + 1, lo - 1 : hi - 1] + fx[1, z, cut] * ref[m, z + 1, lo + 1 : hi + 1]
        in_z = fz[0, z, cut] * ref[m, z, lo:hi] + fz[1, z, cut] * ref[m, z + 2, lo:hi]
        return (in_x + in_z) + in_y

    for j in range(ITERS):

        def odd(z, j=j):
            for b in range(2):
                t0 = spread(ya, 2 * b, z)
                t1 = spread(ya, 2 * b + 1, z)
                al, be = alpha[b, z], beta[b, z]
                y0 = al * t0 - be * t1
                y1 = be * t0 + al * t1
                yb[2 * b, z + 1, WORK] = y0
                yb[2 * b + 1, z + 1, WORK] = y1
                sums_ref[j, 2 * b, z] = ya[2 * b, z + 1, OWN] + y0[8:24]
                sums_ref[j, 2 * b + 1, z] = ya[2 * b + 1, z + 1, OWN] + y1[8:24]

        def even(z, j=j):
            last = j == ITERS - 1
            rows = OWN if last else WORK
            cut = slice(rows.start - FIRST, rows.stop - FIRST)
            for b in range(2):
                new = []
                for m in (2 * b, 2 * b + 1):
                    v = spread(yb, m, z, rows)
                    if SHIFTS[j]:
                        v = v - SHIFTS[j] * vec[j, m, z, cut]
                    vec[j + 1, m, z, cut] = v
                    new.append(v)
                if not last:
                    al, be = alpha[b, z], beta[b, z]
                    ya[2 * b, z + 1, WORK] = al * new[0] - be * new[1]
                    ya[2 * b + 1, z + 1, WORK] = be * new[0] + al * new[1]

        each_plane(nz, STEP_UNROLL, odd)
        each_plane(nz, STEP_UNROLL, even)

    table[...] = jnp.zeros((LANES, LANES), jnp.float32)
    mine = half_mask(8)
    for b in range(2):

        def dots(z, carry):
            out = list(carry)
            for m in (2 * b, 2 * b + 1):
                for r in (8, 16):
                    cells = [vec[i, m, z, r : r + 8] for i in range(SIZE)]
                    for at, (i, j) in enumerate(PAIRS):
                        out[at] = out[at] + cells[i] * cells[j]
            return tuple(out)

        zero = jnp.zeros((8, LANES), jnp.float32)
        out = lax.fori_loop(0, nz, dots, tuple(zero for _ in PAIRS))
        for at in range(len(PAIRS)):
            row = jnp.sum(jnp.where(mine, out[at], 0.0), axis=0, keepdims=True)
            table[b * len(PAIRS) + at : b * len(PAIRS) + at + 1] = row
    total = jnp.sum(table[...].T, axis=0, keepdims=True)
    part_ref[...] = jnp.broadcast_to(total, part_ref.shape)


def step_weights(gram):
    table = {}
    for at, (i, j) in enumerate(PAIRS):
        table[i, j] = table[j, i] = gram[at]
    coef = [jnp.ones_like(gram[0])]
    weight = []
    step = coef[0]
    for k in range(ITERS):
        moved = [SHIFTS[j] * coef[j] for j in range(k + 1)] + [jnp.zeros_like(step)]
        for j in range(k + 1):
            moved[j + 1] = moved[j + 1] + coef[j]
        coef = coef + [jnp.zeros_like(step)]
        image = [coef[j] - moved[j] for j in range(k + 2)]
        num, den, bound = 0.0, 0.0, 0.0
        for i in range(k + 2):
            row, size = 0.0, 0.0
            for j in range(k + 2):
                term = table[i, j] * image[j]
                row = row + term
                size = size + jnp.abs(term)
            num = num + row * coef[i]
            den = den + row * image[i]
            bound = bound + size * jnp.abs(image[i])
        step = jnp.where(den > bound * 6e-8, num / (jnp.maximum(den, 0.0) + tiny_value), step)
        weight = weight + [jnp.zeros_like(step)]
        for j in range(k + 1):
            weight[j] = weight[j] + step * coef[j]
        coef = [coef[j] - step * image[j] for j in range(k + 2)]
    return weight


def send_kernel(consts, total_ref, sums_ref, other_ref, send_ref, weight_ref):
    eigen_basis = consts[0]
    nz, nx = other_ref.shape[1], other_ref.shape[2]
    section = lax.axis_index("section")
    total = jnp.sum(total_ref[...], axis=0, keepdims=True)
    count = len(PAIRS)
    weights = []
    for b in range(2):
        gram = [jnp.broadcast_to(total[:, b * count + at : b * count + at + 1], (1, LANES)) for at in range(count)]
        weights.append(step_weights(gram))
    for b in range(2):
        for j in range(ITERS):
            weight_ref[b * ITERS + j : b * ITERS + j + 1] = weights[b][j]
    basis = [
        [jnp.where(section == 0, jnp.float32(eigen_basis[2 + r][m]), jnp.float32(eigen_basis[r][m])) for m in range(4)]
        for r in range(2)
    ]
    mine = half_mask(nx)

    def combine(z):
        outs = [other_ref[r, z] for r in range(2)]
        for m in range(4):
            field = weights[m // 2][0] * sums_ref[0, m, z]
            for j in range(1, ITERS):
                field = field + weights[m // 2][j] * sums_ref[j, m, z]
            outs = [outs[r] + basis[r][m] * field for r in range(2)]
        send_ref[z] = jnp.where(mine, outs[0], turn(outs[1], LANES // 2))

    each_plane(nz, 4, combine)


def mine_kernel(consts, weight_ref, sums_ref, own_ref, mine_ref):
    eigen_basis = consts[0]
    nz = own_ref.shape[1]
    section = lax.axis_index("section")
    weights = [[weight_ref[b * ITERS + j : b * ITERS + j + 1] for j in range(ITERS)] for b in range(2)]
    basis = [
        [jnp.where(section == 0, jnp.float32(eigen_basis[r][m]), jnp.float32(eigen_basis[2 + r][m])) for m in range(4)]
        for r in range(2)
    ]

    def combine(z):
        outs = [own_ref[r, z] for r in range(2)]
        for m in range(4):
            field = weights[m // 2][0] * sums_ref[0, m, z]
            for j in range(1, ITERS):
                field = field + weights[m // 2][j] * sums_ref[j, m, z]
            outs = [outs[r] + basis[r][m] * field for r in range(2)]
        mine_ref[0, z] = outs[0]
        mine_ref[1, z] = outs[1]

    each_plane(nz, 4, combine)


def join_kernel(mine_ref, other_ref, out_ref):
    nz, nx = mine_ref.shape[1], mine_ref.shape[2]
    mine = half_mask(nx)
    for z in range(nz):
        other = other_ref[z]
        out_ref[0, z] = jnp.where(mine, mine_ref[0, z], other)
        out_ref[1, z] = jnp.where(mine, mine_ref[1, z], turn(other, LANES // 2))


def call(kernel, outs, scratch=(), flops=1_000_000, name=None, limit=12):
    many = isinstance(outs, list)
    shapes = [jax.ShapeDtypeStruct(o, jnp.float32) for o in (outs if many else [outs])]

    def run(*args):
        moved = 4 * sum(int(a.size) for a in args) + 4 * sum(int(functools.reduce(lambda p, q: p * q, s.shape, 1)) for s in shapes)
        return pl.pallas_call(
            kernel,
            out_shape=shapes if many else shapes[0],
            in_specs=[pl.BlockSpec(memory_space=pltpu.VMEM)] * len(args),
            out_specs=[pl.BlockSpec(memory_space=pltpu.VMEM)] * len(shapes) if many else pl.BlockSpec(memory_space=pltpu.VMEM),
            scratch_shapes=[pltpu.VMEM(s, jnp.float32) for s in scratch],
            compiler_params=pltpu.CompilerParams(vmem_limit_bytes=limit * 1024 * 1024),
            cost_estimate=pl.CostEstimate(flops=flops, bytes_accessed=moved, transcendentals=0),
            name=name,
        )(*args)

    return run


def swaps(count, start):
    return [pair for i in range(start, count - 1, 2) for pair in ((i, i + 1), (i + 1, i))]


def body(previous, sections, diffusivity, reaction):
    consts = constants()
    nz, nx, ny = previous.shape
    columns, rows = lax.axis_size("sy"), lax.axis_size("sx")
    axes = ("section", "sx", "sy")
    partner = [(0, 1), (1, 0)]
    other = lax.ppermute(sections, "section", partner)
    edge, rest = (nz // 2, nx, ny), nz + nz // 8
    own = (nz * OWN_PARTS, TALL, ny)
    border, own_near, own_far = call(own_kernel, [edge, own, own], name="own")(sections, previous, diffusivity, reaction)
    own_far = lax.ppermute(own_far, "sx", swaps(rows, 1))
    own_near = lax.ppermute(own_near, "sx", swaps(rows, 0))
    late = (rest + nz // 2, TALL, ny)
    border, near, far = call(other_kernel, [edge, late, late], name="other")(other, border)
    edges = [(s * columns + a, s * columns + b) for s in range(2) for a, b in swaps(columns, s)]
    border = lax.ppermute(border, ("section", "sy"), edges)
    near = lax.dynamic_update_slice(near, border, (rest, 0, 0))
    far = lax.dynamic_update_slice(far, border, (rest, 0, 0))
    far = lax.ppermute(far, "sx", swaps(rows, 1))
    near = lax.ppermute(near, "sx", swaps(rows, 0))
    peers = 2 * columns * rows
    padded, work = (nz + 2, ROWS, ny), (nz, LAST - FIRST, ny)
    scratch = [
        (4,) + padded, (4,) + padded, padded, work, work, work, (2,) + work, (2,) + work, (2,) + work, (2,) + work, (2,) + work,
        (SIZE, 4) + work, (4,) + padded, (4,) + padded, (LANES, LANES),
    ]
    part, sums = call(
        functools.partial(main_kernel, consts), [(peers, LANES), (ITERS, 4, nz, nx, ny)], scratch, 50_000_000, "main", 26
    )(sections, other, previous, diffusivity, reaction, border, own_near, own_far, near, far)
    total = lax.all_to_all(part.reshape(peers, 1, LANES), axes, 0, 0).reshape(peers, LANES)
    half, weight = call(functools.partial(send_kernel, consts), [previous.shape, (2 * ITERS, LANES)], name="send")(total, sums, other)
    got = lax.ppermute(half, "section", partner)
    mine = call(functools.partial(mine_kernel, consts), sections.shape, name="mine")(weight, sums, sections)
    return call(join_kernel, sections.shape, name="join")(mine, got)


def solution(mesh):
    in_specs = (
        P(None, "sx", "sy"),
        P("section", None, "sx", "sy"),
        P(None, "sx", "sy"),
        P(None, "sx", "sy"),
    )
    out_specs = P("section", None, "sx", "sy")
    return jax.shard_map(body, mesh=mesh, in_specs=in_specs, out_specs=out_specs, check_vma=False)
```

```python
import functools

import jax
import jax.numpy as jnp
from jax import lax
from jax.experimental import pallas as pl
from jax.experimental.pallas import tpu as pltpu
from jax.sharding import PartitionSpec as P

ITERS = 4
SHIFTS = (0.0, 0.9, 0.45, 0.7)
EDGE = 9
LANES = 128
SIZE = ITERS + 1
PAIRS = [(i, j) for i in range(SIZE) for j in range(i, SIZE)]
PREPARE_UNROLL = 2
STEP_UNROLL = 8


step_size = 1.0
tiny_value = 1e-06


def invert_table(matrix):
    order_n = len(matrix)
    augmented = [
        list(matrix[r]) + [1.0 if c == r else 0.0 for c in range(order_n)] for r in range(order_n)
    ]
    for col in range(order_n):
        pivot_row = max(range(col, order_n), key=lambda r: abs(augmented[r][col]))
        augmented[col], augmented[pivot_row] = (augmented[pivot_row], augmented[col])
        leading = augmented[col][col]
        augmented[col] = [v / leading for v in augmented[col]]
        for r in range(order_n):
            if r != col:
                factor = augmented[r][col]
                augmented[r] = [a - factor * b for a, b in zip(augmented[r], augmented[col])]
    return [row_values[order_n:] for row_values in augmented]


def table_product(left, right):
    return [
        [sum((left[i][k] * right[k][j] for k in range(len(right)))) for j in range(len(right[0]))]
        for i in range(len(left))
    ]


def pair_add(first, second):
    return (first[0] + second[0], first[1] + second[1])


def pair_sub(first, second):
    return (first[0] - second[0], first[1] - second[1])


def pair_mul(first, second):
    return (
        first[0] * second[0] - first[1] * second[1],
        first[0] * second[1] + first[1] * second[0],
    )


def pair_div(first, second):
    scale_sq = second[0] * second[0] + second[1] * second[1]
    return (
        (first[0] * second[0] + first[1] * second[1]) / scale_sq,
        (first[1] * second[0] - first[0] * second[1]) / scale_sq,
    )


def quartic_value(point):
    return (((210.0 * point - 480.0) * point + 360.0) * point - 96.0) * point + 6.0


def bisect_root(lower, upper):
    for count in range(200):
        middle = 0.5 * (lower + upper)
        if (quartic_value(lower) < 0.0) == (quartic_value(middle) < 0.0):
            lower = middle
        else:
            upper = middle
    return 0.5 * (lower + upper)


def radau_tables():
    abscissae = []
    grid_steps = 4000
    for m in range(grid_steps):
        lower = 0.999 * m / grid_steps
        upper = 0.999 * (m + 1) / grid_steps
        if (quartic_value(lower) < 0.0) != (quartic_value(upper) < 0.0):
            abscissae.append(bisect_root(lower, upper))
    abscissae.append(1.0)
    vander = [[abscissae[j] ** k for k in range(4)] for j in range(4)]
    moments = [[abscissae[i] ** (k + 1) / (k + 1) for k in range(4)] for i in range(4)]
    tableau = table_product(moments, invert_table(vander))
    inverse = invert_table(tableau)
    running = [list(row_values) for row_values in inverse]
    coeffs = []
    for k in range(1, 5):
        trace_value = sum((running[i][i] for i in range(4)))
        coeffs.append(-trace_value / k)
        shifted_table = [
            [running[i][j] + (coeffs[-1] if i == j else 0.0) for j in range(4)] for i in range(4)
        ]
        running = table_product(inverse, shifted_table)
    start_point = (0.4, 0.9)
    estimates = [(1.0, 0.0)]
    for k in range(3):
        estimates.append(pair_mul(estimates[-1], start_point))
    for count in range(500):
        for i in range(4):
            value = (1.0, 0.0)
            for coef_value in coeffs:
                value = pair_add(pair_mul(value, estimates[i]), (coef_value, 0.0))
            denom = (1.0, 0.0)
            for j in range(4):
                if j != i:
                    denom = pair_mul(denom, pair_sub(estimates[i], estimates[j]))
            estimates[i] = pair_sub(estimates[i], pair_div(value, denom))
    chosen = [m for m in range(4) if estimates[m][1] > 0.0]
    ranking = sorted(chosen, key=lambda m: -estimates[m][1])
    columns = []
    pairs = []
    for m in ranking:
        eigen_pair = estimates[m]
        system = [
            [
                (
                    inverse[i][j] - (eigen_pair[0] if i == j else 0.0),
                    -(eigen_pair[1] if i == j else 0.0),
                )
                for j in range(4)
            ]
            for i in range(3)
        ]
        rows_left = [
            [system[i][j] for j in range(3)] + [(-system[i][3][0], -system[i][3][1])]
            for i in range(3)
        ]
        for col in range(3):
            pivot_row = max(
                range(col, 3), key=lambda r: rows_left[r][col][0] ** 2 + rows_left[r][col][1] ** 2
            )
            rows_left[col], rows_left[pivot_row] = (rows_left[pivot_row], rows_left[col])
            leading = rows_left[col][col]
            rows_left[col] = [pair_div(v, leading) for v in rows_left[col]]
            for r in range(3):
                if r != col:
                    factor = rows_left[r][col]
                    rows_left[r] = [
                        pair_sub(a, pair_mul(factor, b))
                        for a, b in zip(rows_left[r], rows_left[col])
                    ]
        vector = [rows_left[i][3] for i in range(3)] + [(1.0, 0.0)]
        columns.append([v[0] for v in vector])
        columns.append([v[1] for v in vector])
        pairs.append((eigen_pair[0], eigen_pair[1]))
    eigen_basis = [[columns[j][i] for j in range(4)] for i in range(4)]
    basis_inverse = invert_table(eigen_basis)
    return (tableau, inverse, eigen_basis, basis_inverse, pairs)


def constants():
    tableau, inverse, eigen_basis, basis_inverse, pairs = radau_tables()
    shift_table = table_product(basis_inverse, inverse)
    shift_rows = [[v / step_size for v in row_values] for row_values in shift_table]
    pairs = [(p[0] / step_size, p[1] / step_size) for p in pairs]
    return eigen_basis, basis_inverse, shift_rows, pairs


def lane_ids(rows):
    return lax.broadcasted_iota(jnp.int32, (rows, LANES), 1)


def turn(cells, amount):
    return pltpu.roll(cells, amount % LANES, cells.ndim - 1)


def left_half():
    return lax.axis_index("section") == 0


def half_mask(rows):
    return (lane_ids(rows) < LANES // 2) == left_half()


ORDER = (0, 1, 4, 5, 6, 2, 3)
TALL = 16
OWN_PARTS = 3


def border_start():
    return jnp.where(left_half(), LANES - EDGE, 0)


def on_even_row():
    return lax.rem(lax.axis_index("sx"), 2) == 0


def own_place(slot, z):
    entry, row = divmod(8 * slot, TALL)
    last, ninth = divmod(40 + slot, TALL)
    return z * OWN_PARTS + entry, row, z * OWN_PARTS + last, ninth


def pack_rows(near_ref, far_ref, cell, place, even):
    nx = cell.shape[0]
    entry, row, last, ninth = place
    near_ref[entry, row : row + 8] = jnp.where(even, cell[nx - 8 : nx], cell[0:8])
    far_ref[entry, row : row + 8] = jnp.where(even, cell[0:8], cell[nx - 8 : nx])
    near_ref[last, ninth : ninth + 1] = jnp.where(even, cell[nx - 9 : nx - 8], cell[8:9])
    far_ref[last, ninth : ninth + 1] = jnp.where(even, cell[8:9], cell[nx - 9 : nx - 8])


def own_kernel(own_ref, prev_ref, diff_ref, react_ref, held_ref, same_ref, cross_ref, near_ref, far_ref):
    nz, nx = prev_ref.shape[0], prev_ref.shape[1]
    lanes = lane_ids(nx)
    even = on_even_row()
    incoming = border_start()
    outgoing = LANES - EDGE - incoming

    def put(tile, cell, at, start):
        moved = pltpu.roll(cell, lax.rem(at + LANES - start, LANES), 1)
        return jnp.where((lanes >= at) & (lanes < at + EDGE), moved, tile)

    for plane in range(nz // 2):
        same = jnp.zeros((nx, LANES), jnp.float32)
        cross = same
        for part in range(2):
            z = part * (nz // 2) + plane
            cells = [own_ref[0, z], own_ref[1, z], prev_ref[z], diff_ref[z], react_ref[z]]
            for slot, cell in enumerate(cells):
                held_ref[slot, z] = cell
                same = put(same, cell, part * 64 + ORDER[slot] * EDGE, incoming)
                if slot < 2:
                    cross = put(cross, cell, part * 64 + (2 + slot) * EDGE, outgoing)
                pack_rows(near_ref, far_ref, cell, own_place(slot, z), even)
        same_ref[plane] = same
        cross_ref[plane] = cross


def other_kernel(other_ref, same_ref, cross_ref, border_ref, near_ref, far_ref):
    nz = other_ref.shape[1]
    even = on_even_row()
    rest = nz + nz // 8
    for z in range(nz):
        for slot in range(2):
            pack_rows(near_ref, far_ref, other_ref[slot, z], (z, 8 * slot, nz + z // 8, 2 * (z % 8) + slot), even)
    for plane in range(nz // 2):
        border = same_ref[plane] + cross_ref[plane]
        border_ref[plane] = border
        near_ref[rest + plane] = border
        far_ref[rest + plane] = border


ROWS = 48
FIRST, LAST = 8, 40
OWN = slice(16, 32)
WORK = slice(FIRST, LAST)
BEFORE = slice(FIRST - 1, LAST - 1)
AFTER = slice(FIRST + 1, LAST + 1)


def each_plane(count, unroll, work):
    def group(i, carry):
        for u in range(unroll):
            work(i * unroll + u)
        return carry

    lax.fori_loop(0, count // unroll, group, 0)


def main_kernel(consts, held_ref, other_ref, border_ref, own_near_ref, own_far_ref, near_ref, far_ref, part_ref, sums_ref,
                val, kap, frozen, prv, rea, dif, fx, fy, fz, alpha, beta, vec, ya, yb, table):
    eigen_basis, basis_inverse, shift_rows, pairs = consts
    nz, nx = held_ref.shape[1], held_ref.shape[2]
    section = lax.axis_index("section")
    zero_plane = jnp.zeros((ROWS, LANES), jnp.float32)
    zero_rows = jnp.zeros((FIRST, LANES), jnp.float32)
    start = border_start()
    even = on_even_row()
    lanes = lane_ids(ROWS)
    edge = (lanes >= start) & (lanes < start + EDGE)
    tile = lambda t: jnp.broadcast_to(t, (8, LANES))

    for at in (0, nz + 1):
        frozen[at] = zero_plane
        for f in range(4):
            for ref in (val, kap, ya, yb):
                ref[f, at] = zero_plane

    def both(slot, entry, row, count):
        refs = (own_near_ref, own_far_ref) if slot < 5 else (near_ref, far_ref)
        near, far = [ref[entry, pl.ds(row, count)] for ref in refs]
        return jnp.where(even, far, near), jnp.where(even, near, far)

    def assemble(plane):
        at = nz + nz // 8 + plane
        low = jnp.where(even, far_ref[at], near_ref[at])
        high = jnp.where(even, near_ref[at], far_ref[at])
        sides = jnp.concatenate([tile(low[nx - 9 : nx - 8]), low[nx - 8 : nx], border_ref[plane], high[0:8], tile(high[8:9])], 0)
        for part in range(2):
            z = part * (nz // 2) + plane

            def column(f):
                slot = ORDER.index(f)
                mid = held_ref[slot, z] if slot < 5 else other_ref[slot - 5, z]
                entry, row, last, ninth = own_place(slot, z) if slot < 5 else (z, 8 * (slot - 5), nz + z // 8, 2 * lax.rem(z, 8) + slot - 5)
                low, high = both(slot, entry, row, 8)
                low_end, high_end = both(slot, last, ninth, 1)
                cells = jnp.concatenate([tile(low_end), low, mid, high, tile(high_end)], 0)
                at = part * 64 + f * EDGE
                return jnp.where(edge, pltpu.roll(sides, lax.rem(start + LANES - at, LANES), 1), cells)

            diff, prev, react = column(5), column(4), column(6)
            frozen[z + 1] = diff * (0.5 + 0.25 * jnp.tanh(prev))
            prv[z] = prev[WORK]
            rea[z] = react[WORK]
            dif[z] = diff[WORK]
            for f in range(4):
                value = column(f)
                val[f, z + 1] = value
                kap[f, z + 1] = diff * (0.5 + 0.25 * jnp.tanh(value))
                for ref in (ya, yb):
                    ref[f, z + 1, 0:FIRST] = zero_rows
                    ref[f, z + 1, LAST:ROWS] = zero_rows

    each_plane(nz // 2, 1, assemble)

    def pick(matrix, m, j):
        return jnp.where(section == 0, jnp.float32(matrix[m][j]), jnp.float32(matrix[m][(j + 2) % 4]))

    q_rows = [[pick(basis_inverse, m, j) for j in range(4)] for m in range(4)]
    c_rows = [[pick(shift_rows, m, j) for j in range(4)] for m in range(4)]

    def prepare(z):
        mid = frozen[z + 1, WORK]
        faces = [
            mid + frozen[z + 1, BEFORE], mid + frozen[z + 1, AFTER], mid + turn(mid, 1), mid + turn(mid, -1),
            mid + frozen[z, WORK], mid + frozen[z + 2, WORK],
        ]
        for at, ref in enumerate((fx, fy, fz)):
            ref[0, z] = faces[2 * at]
            ref[1, z] = faces[2 * at + 1]
        prev, react = prv[z], rea[z]
        base = ((faces[0] + faces[1]) + (faces[2] + faces[3])) + (faces[4] + faces[5]) - react * (1.0 - 3.0 * prev * prev)
        inside = jnp.where(dif[z] > 0.0, 1.0, 0.0)
        scaled = []
        for b in range(2):
            real, imag = pairs[b]
            diag = base + real
            scale = inside / (diag * diag + imag * imag)
            scaled.append((diag * scale, imag * scale))
            alpha[b, z], beta[b, z] = scaled[b]
        rhs = [None] * 4
        for j in range(4):
            v = val[j, z + 1, WORK]
            k = kap[j, z + 1, WORK]
            flux = react * v * (1.0 - v * v)
            flux = flux + (k + kap[j, z + 1, BEFORE]) * (val[j, z + 1, BEFORE] - v)
            flux = flux + (k + kap[j, z + 1, AFTER]) * (val[j, z + 1, AFTER] - v)
            flux = flux + (k + turn(k, 1)) * (turn(v, 1) - v)
            flux = flux + (k + turn(k, -1)) * (turn(v, -1) - v)
            flux = flux + (k + kap[j, z, WORK]) * (val[j, z, WORK] - v)
            flux = flux + (k + kap[j, z + 2, WORK]) * (val[j, z + 2, WORK] - v)
            grown = v - prev
            for m in range(4):
                term = q_rows[m][j] * flux - c_rows[m][j] * grown
                rhs[m] = term if j == 0 else rhs[m] + term
        for m in range(4):
            vec[0, m, z] = rhs[m]
        for b in range(2):
            al, be = scaled[b]
            ya[2 * b, z + 1, WORK] = al * rhs[2 * b] - be * rhs[2 * b + 1]
            ya[2 * b + 1, z + 1, WORK] = be * rhs[2 * b] + al * rhs[2 * b + 1]

    each_plane(nz, PREPARE_UNROLL, prepare)

    def spread(ref, m, z, rows=WORK):
        lo, hi = rows.start, rows.stop
        cut = slice(lo - FIRST, hi - FIRST)
        mid = ref[m, z + 1, lo:hi]
        in_y = fy[0, z, cut] * turn(mid, 1) + fy[1, z, cut] * turn(mid, -1)
        in_x = fx[0, z, cut] * ref[m, z + 1, lo - 1 : hi - 1] + fx[1, z, cut] * ref[m, z + 1, lo + 1 : hi + 1]
        in_z = fz[0, z, cut] * ref[m, z, lo:hi] + fz[1, z, cut] * ref[m, z + 2, lo:hi]
        return (in_x + in_z) + in_y

    for j in range(ITERS):

        def odd(z, j=j):
            for b in range(2):
                t0 = spread(ya, 2 * b, z)
                t1 = spread(ya, 2 * b + 1, z)
                al, be = alpha[b, z], beta[b, z]
                y0 = al * t0 - be * t1
                y1 = be * t0 + al * t1
                yb[2 * b, z + 1, WORK] = y0
                yb[2 * b + 1, z + 1, WORK] = y1
                sums_ref[j, 2 * b, z] = ya[2 * b, z + 1, OWN] + y0[8:24]
                sums_ref[j, 2 * b + 1, z] = ya[2 * b + 1, z + 1, OWN] + y1[8:24]

        def even(z, j=j):
            last = j == ITERS - 1
            rows = OWN if last else WORK
            cut = slice(rows.start - FIRST, rows.stop - FIRST)
            for b in range(2):
                new = []
                for m in (2 * b, 2 * b + 1):
                    v = spread(yb, m, z, rows)
                    if SHIFTS[j]:
                        v = v - SHIFTS[j] * vec[j, m, z, cut]
                    vec[j + 1, m, z, cut] = v
                    new.append(v)
                if not last:
                    al, be = alpha[b, z], beta[b, z]
                    ya[2 * b, z + 1, WORK] = al * new[0] - be * new[1]
                    ya[2 * b + 1, z + 1, WORK] = be * new[0] + al * new[1]

        each_plane(nz, STEP_UNROLL, odd)
        each_plane(nz, STEP_UNROLL, even)

    table[...] = jnp.zeros((LANES, LANES), jnp.float32)
    mine = half_mask(8)
    for b in range(2):

        def dots(z, carry):
            out = list(carry)
            for m in (2 * b, 2 * b + 1):
                for r in (8, 16):
                    cells = [vec[i, m, z, r : r + 8] for i in range(SIZE)]
                    for at, (i, j) in enumerate(PAIRS):
                        out[at] = out[at] + cells[i] * cells[j]
            return tuple(out)

        zero = jnp.zeros((8, LANES), jnp.float32)
        out = lax.fori_loop(0, nz, dots, tuple(zero for _ in PAIRS))
        for at in range(len(PAIRS)):
            row = jnp.sum(jnp.where(mine, out[at], 0.0), axis=0, keepdims=True)
            table[b * len(PAIRS) + at : b * len(PAIRS) + at + 1] = row
    total = jnp.sum(table[...].T, axis=0, keepdims=True)
    part_ref[...] = jnp.broadcast_to(total, part_ref.shape)


def step_weights(gram):
    table = {}
    for at, (i, j) in enumerate(PAIRS):
        table[i, j] = table[j, i] = gram[at]
    coef = [jnp.ones_like(gram[0])]
    weight = []
    step = coef[0]
    for k in range(ITERS):
        moved = [SHIFTS[j] * coef[j] for j in range(k + 1)] + [jnp.zeros_like(step)]
        for j in range(k + 1):
            moved[j + 1] = moved[j + 1] + coef[j]
        coef = coef + [jnp.zeros_like(step)]
        image = [coef[j] - moved[j] for j in range(k + 2)]
        num, den, bound = 0.0, 0.0, 0.0
        for i in range(k + 2):
            row, size = 0.0, 0.0
            for j in range(k + 2):
                term = table[i, j] * image[j]
                row = row + term
                size = size + jnp.abs(term)
            num = num + row * coef[i]
            den = den + row * image[i]
            bound = bound + size * jnp.abs(image[i])
        step = jnp.where(den > bound * 6e-8, num / (jnp.maximum(den, 0.0) + tiny_value), step)
        weight = weight + [jnp.zeros_like(step)]
        for j in range(k + 1):
            weight[j] = weight[j] + step * coef[j]
        coef = [coef[j] - step * image[j] for j in range(k + 2)]
    return weight


def send_kernel(consts, total_ref, sums_ref, other_ref, send_ref, weight_ref):
    eigen_basis = consts[0]
    nz, nx = other_ref.shape[1], other_ref.shape[2]
    section = lax.axis_index("section")
    total = jnp.sum(total_ref[...], axis=0, keepdims=True)
    count = len(PAIRS)
    weights = []
    for b in range(2):
        gram = [jnp.broadcast_to(total[:, b * count + at : b * count + at + 1], (1, LANES)) for at in range(count)]
        weights.append(step_weights(gram))
    for b in range(2):
        for j in range(ITERS):
            weight_ref[b * ITERS + j : b * ITERS + j + 1] = weights[b][j]
    basis = [
        [jnp.where(section == 0, jnp.float32(eigen_basis[2 + r][m]), jnp.float32(eigen_basis[r][m])) for m in range(4)]
        for r in range(2)
    ]
    mine = half_mask(nx)

    def combine(z):
        outs = [other_ref[r, z] for r in range(2)]
        for m in range(4):
            field = weights[m // 2][0] * sums_ref[0, m, z]
            for j in range(1, ITERS):
                field = field + weights[m // 2][j] * sums_ref[j, m, z]
            outs = [outs[r] + basis[r][m] * field for r in range(2)]
        send_ref[z] = jnp.where(mine, outs[0], turn(outs[1], LANES // 2))

    each_plane(nz, 4, combine)


def mine_kernel(consts, weight_ref, sums_ref, own_ref, mine_ref):
    eigen_basis = consts[0]
    nz = own_ref.shape[1]
    section = lax.axis_index("section")
    weights = [[weight_ref[b * ITERS + j : b * ITERS + j + 1] for j in range(ITERS)] for b in range(2)]
    basis = [
        [jnp.where(section == 0, jnp.float32(eigen_basis[r][m]), jnp.float32(eigen_basis[2 + r][m])) for m in range(4)]
        for r in range(2)
    ]

    def combine(z):
        outs = [own_ref[r, z] for r in range(2)]
        for m in range(4):
            field = weights[m // 2][0] * sums_ref[0, m, z]
            for j in range(1, ITERS):
                field = field + weights[m // 2][j] * sums_ref[j, m, z]
            outs = [outs[r] + basis[r][m] * field for r in range(2)]
        mine_ref[0, z] = outs[0]
        mine_ref[1, z] = outs[1]

    each_plane(nz, 4, combine)


def join_kernel(mine_ref, other_ref, out_ref):
    nz, nx = mine_ref.shape[1], mine_ref.shape[2]
    mine = half_mask(nx)
    for z in range(nz):
        other = other_ref[z]
        out_ref[0, z] = jnp.where(mine, mine_ref[0, z], other)
        out_ref[1, z] = jnp.where(mine, mine_ref[1, z], turn(other, LANES // 2))


def call(kernel, outs, scratch=(), flops=1_000_000, name=None, limit=12):
    many = isinstance(outs, list)
    shapes = [jax.ShapeDtypeStruct(o, jnp.float32) for o in (outs if many else [outs])]

    def run(*args):
        moved = 4 * sum(int(a.size) for a in args) + 4 * sum(int(functools.reduce(lambda p, q: p * q, s.shape, 1)) for s in shapes)
        return pl.pallas_call(
            kernel,
            out_shape=shapes if many else shapes[0],
            in_specs=[pl.BlockSpec(memory_space=pltpu.VMEM)] * len(args),
            out_specs=[pl.BlockSpec(memory_space=pltpu.VMEM)] * len(shapes) if many else pl.BlockSpec(memory_space=pltpu.VMEM),
            scratch_shapes=[pltpu.VMEM(s, jnp.float32) for s in scratch],
            compiler_params=pltpu.CompilerParams(vmem_limit_bytes=limit * 1024 * 1024),
            cost_estimate=pl.CostEstimate(flops=flops, bytes_accessed=moved, transcendentals=0),
            name=name,
        )(*args)

    return run


def swaps(count, start):
    return [pair for i in range(start, count - 1, 2) for pair in ((i, i + 1), (i + 1, i))]


def beside(count, cross):
    pairs = []
    for s in range(2):
        to = 1 - s if cross else s
        step = 1 if to == 0 else -1
        for i in range(count):
            if 0 <= i + step < count:
                pairs.append((s * count + i, to * count + i + step))
    return pairs


def body(previous, sections, diffusivity, reaction):
    consts = constants()
    nz, nx, ny = previous.shape
    columns, rows = lax.axis_size("sy"), lax.axis_size("sx")
    axes = ("section", "sx", "sy")
    partner = [(0, 1), (1, 0)]
    other = lax.ppermute(sections, "section", partner)
    edge, own, late = (nz // 2, nx, ny), (nz * OWN_PARTS, TALL, ny), (nz + nz // 8 + nz // 2, TALL, ny)
    held, same, cross, own_near, own_far = call(own_kernel, [(5, nz, nx, ny), edge, edge, own, own], name="own")(
        sections, previous, diffusivity, reaction
    )
    same = lax.ppermute(same, ("section", "sy"), beside(columns, False))
    cross = lax.ppermute(cross, ("section", "sy"), beside(columns, True))
    own_far = lax.ppermute(own_far, "sx", swaps(rows, 1))
    own_near = lax.ppermute(own_near, "sx", swaps(rows, 0))
    border, near, far = call(other_kernel, [edge, late, late], name="other")(other, same, cross)
    far = lax.ppermute(far, "sx", swaps(rows, 1))
    near = lax.ppermute(near, "sx", swaps(rows, 0))
    peers = 2 * columns * rows
    padded, work = (nz + 2, ROWS, ny), (nz, LAST - FIRST, ny)
    scratch = [
        (4,) + padded, (4,) + padded, padded, work, work, work, (2,) + work, (2,) + work, (2,) + work, (2,) + work, (2,) + work,
        (SIZE, 4) + work, (4,) + padded, (4,) + padded, (LANES, LANES),
    ]
    part, sums = call(
        functools.partial(main_kernel, consts), [(peers, LANES), (ITERS, 4, nz, nx, ny)], scratch, 50_000_000, "main", 26
    )(held, other, border, own_near, own_far, near, far)
    total = lax.all_to_all(part.reshape(peers, 1, LANES), axes, 0, 0).reshape(peers, LANES)
    half, weight = call(functools.partial(send_kernel, consts), [previous.shape, (2 * ITERS, LANES)], name="send")(total, sums, other)
    got = lax.ppermute(half, "section", partner)
    mine = call(functools.partial(mine_kernel, consts), sections.shape, name="mine")(weight, sums, held)
    return call(join_kernel, sections.shape, name="join")(mine, got)


def solution(mesh):
    in_specs = (
        P(None, "sx", "sy"),
        P("section", None, "sx", "sy"),
        P(None, "sx", "sy"),
        P(None, "sx", "sy"),
    )
    out_specs = P("section", None, "sx", "sy")
    return jax.shard_map(body, mesh=mesh, in_specs=in_specs, out_specs=out_specs, check_vma=False)
```

```python
import functools

import jax
import jax.numpy as jnp
from jax import lax
from jax.experimental import pallas as pl
from jax.experimental.pallas import tpu as pltpu
from jax.sharding import PartitionSpec as P

ITERS = 4
SHIFTS = (0.0, 0.9, 0.45, 0.7)
EDGE = 9
LANES = 128
SIZE = ITERS + 1
PAIRS = [(i, j) for i in range(SIZE) for j in range(i, SIZE)]
PREPARE_UNROLL = 2
STEP_UNROLL = 8


step_size = 1.0
tiny_value = 1e-06


def invert_table(matrix):
    order_n = len(matrix)
    augmented = [
        list(matrix[r]) + [1.0 if c == r else 0.0 for c in range(order_n)] for r in range(order_n)
    ]
    for col in range(order_n):
        pivot_row = max(range(col, order_n), key=lambda r: abs(augmented[r][col]))
        augmented[col], augmented[pivot_row] = (augmented[pivot_row], augmented[col])
        leading = augmented[col][col]
        augmented[col] = [v / leading for v in augmented[col]]
        for r in range(order_n):
            if r != col:
                factor = augmented[r][col]
                augmented[r] = [a - factor * b for a, b in zip(augmented[r], augmented[col])]
    return [row_values[order_n:] for row_values in augmented]


def table_product(left, right):
    return [
        [sum((left[i][k] * right[k][j] for k in range(len(right)))) for j in range(len(right[0]))]
        for i in range(len(left))
    ]


def pair_add(first, second):
    return (first[0] + second[0], first[1] + second[1])


def pair_sub(first, second):
    return (first[0] - second[0], first[1] - second[1])


def pair_mul(first, second):
    return (
        first[0] * second[0] - first[1] * second[1],
        first[0] * second[1] + first[1] * second[0],
    )


def pair_div(first, second):
    scale_sq = second[0] * second[0] + second[1] * second[1]
    return (
        (first[0] * second[0] + first[1] * second[1]) / scale_sq,
        (first[1] * second[0] - first[0] * second[1]) / scale_sq,
    )


def quartic_value(point):
    return (((210.0 * point - 480.0) * point + 360.0) * point - 96.0) * point + 6.0


def bisect_root(lower, upper):
    for count in range(200):
        middle = 0.5 * (lower + upper)
        if (quartic_value(lower) < 0.0) == (quartic_value(middle) < 0.0):
            lower = middle
        else:
            upper = middle
    return 0.5 * (lower + upper)


def radau_tables():
    abscissae = []
    grid_steps = 4000
    for m in range(grid_steps):
        lower = 0.999 * m / grid_steps
        upper = 0.999 * (m + 1) / grid_steps
        if (quartic_value(lower) < 0.0) != (quartic_value(upper) < 0.0):
            abscissae.append(bisect_root(lower, upper))
    abscissae.append(1.0)
    vander = [[abscissae[j] ** k for k in range(4)] for j in range(4)]
    moments = [[abscissae[i] ** (k + 1) / (k + 1) for k in range(4)] for i in range(4)]
    tableau = table_product(moments, invert_table(vander))
    inverse = invert_table(tableau)
    running = [list(row_values) for row_values in inverse]
    coeffs = []
    for k in range(1, 5):
        trace_value = sum((running[i][i] for i in range(4)))
        coeffs.append(-trace_value / k)
        shifted_table = [
            [running[i][j] + (coeffs[-1] if i == j else 0.0) for j in range(4)] for i in range(4)
        ]
        running = table_product(inverse, shifted_table)
    start_point = (0.4, 0.9)
    estimates = [(1.0, 0.0)]
    for k in range(3):
        estimates.append(pair_mul(estimates[-1], start_point))
    for count in range(500):
        for i in range(4):
            value = (1.0, 0.0)
            for coef_value in coeffs:
                value = pair_add(pair_mul(value, estimates[i]), (coef_value, 0.0))
            denom = (1.0, 0.0)
            for j in range(4):
                if j != i:
                    denom = pair_mul(denom, pair_sub(estimates[i], estimates[j]))
            estimates[i] = pair_sub(estimates[i], pair_div(value, denom))
    chosen = [m for m in range(4) if estimates[m][1] > 0.0]
    ranking = sorted(chosen, key=lambda m: -estimates[m][1])
    columns = []
    pairs = []
    for m in ranking:
        eigen_pair = estimates[m]
        system = [
            [
                (
                    inverse[i][j] - (eigen_pair[0] if i == j else 0.0),
                    -(eigen_pair[1] if i == j else 0.0),
                )
                for j in range(4)
            ]
            for i in range(3)
        ]
        rows_left = [
            [system[i][j] for j in range(3)] + [(-system[i][3][0], -system[i][3][1])]
            for i in range(3)
        ]
        for col in range(3):
            pivot_row = max(
                range(col, 3), key=lambda r: rows_left[r][col][0] ** 2 + rows_left[r][col][1] ** 2
            )
            rows_left[col], rows_left[pivot_row] = (rows_left[pivot_row], rows_left[col])
            leading = rows_left[col][col]
            rows_left[col] = [pair_div(v, leading) for v in rows_left[col]]
            for r in range(3):
                if r != col:
                    factor = rows_left[r][col]
                    rows_left[r] = [
                        pair_sub(a, pair_mul(factor, b))
                        for a, b in zip(rows_left[r], rows_left[col])
                    ]
        vector = [rows_left[i][3] for i in range(3)] + [(1.0, 0.0)]
        columns.append([v[0] for v in vector])
        columns.append([v[1] for v in vector])
        pairs.append((eigen_pair[0], eigen_pair[1]))
    eigen_basis = [[columns[j][i] for j in range(4)] for i in range(4)]
    basis_inverse = invert_table(eigen_basis)
    return (tableau, inverse, eigen_basis, basis_inverse, pairs)


def constants():
    tableau, inverse, eigen_basis, basis_inverse, pairs = radau_tables()
    shift_table = table_product(basis_inverse, inverse)
    shift_rows = [[v / step_size for v in row_values] for row_values in shift_table]
    pairs = [(p[0] / step_size, p[1] / step_size) for p in pairs]
    return eigen_basis, basis_inverse, shift_rows, pairs


def lane_ids(rows):
    return lax.broadcasted_iota(jnp.int32, (rows, LANES), 1)


def turn(cells, amount):
    return pltpu.roll(cells, amount % LANES, cells.ndim - 1)


def left_half():
    return lax.axis_index("section") == 0


def half_mask(rows):
    return (lane_ids(rows) < LANES // 2) == left_half()


ORDER = (0, 1, 4, 5, 6, 2, 3)
TALL = 16
PARTS = 4


def border_start():
    return jnp.where(left_half(), LANES - EDGE, 0)


def on_even_row():
    return lax.rem(lax.axis_index("sx"), 2) == 0


def place(slot, z):
    entry, row = divmod(8 * slot, TALL)
    last, ninth = divmod(56 + slot, TALL)
    return z * PARTS + entry, row, z * PARTS + last, ninth


def pack_rows(near_ref, far_ref, cell, slot, z, even):
    nx = cell.shape[0]
    entry, row, last, ninth = place(slot, z)
    near_ref[entry, row : row + 8] = jnp.where(even, cell[nx - 8 : nx], cell[0:8])
    far_ref[entry, row : row + 8] = jnp.where(even, cell[0:8], cell[nx - 8 : nx])
    near_ref[last, ninth : ninth + 1] = jnp.where(even, cell[nx - 9 : nx - 8], cell[8:9])
    far_ref[last, ninth : ninth + 1] = jnp.where(even, cell[8:9], cell[nx - 9 : nx - 8])


def own_kernel(held_ref, same_ref, cross_ref):
    nz, nx = held_ref.shape[1], held_ref.shape[2]
    lanes = lane_ids(nx)
    incoming = border_start()
    outgoing = LANES - EDGE - incoming

    def put(tile, cell, at, start):
        moved = pltpu.roll(cell, lax.rem(at + LANES - start, LANES), 1)
        return jnp.where((lanes >= at) & (lanes < at + EDGE), moved, tile)

    for plane in range(nz // 2):
        same = jnp.zeros((nx, LANES), jnp.float32)
        cross = same
        for part in range(2):
            z = part * (nz // 2) + plane
            for slot in range(5):
                cell = held_ref[slot, z]
                same = put(same, cell, part * 64 + ORDER[slot] * EDGE, incoming)
                if slot < 2:
                    cross = put(cross, cell, part * 64 + (2 + slot) * EDGE, outgoing)
        same_ref[plane] = same
        cross_ref[plane] = cross


def rows_kernel(held_ref, other_ref, same_ref, cross_ref, border_ref, near_ref, far_ref):
    nz = other_ref.shape[1]
    even = on_even_row()
    for z in range(nz):
        for slot in range(7):
            pack_rows(near_ref, far_ref, held_ref[slot, z] if slot < 5 else other_ref[slot - 5, z], slot, z, even)
    for plane in range(nz // 2):
        border = same_ref[plane] + cross_ref[plane]
        border_ref[plane] = border
        near_ref[nz * PARTS + plane] = border
        far_ref[nz * PARTS + plane] = border


ROWS = 48
FIRST, LAST = 8, 40
OWN = slice(16, 32)
WORK = slice(FIRST, LAST)
BEFORE = slice(FIRST - 1, LAST - 1)
AFTER = slice(FIRST + 1, LAST + 1)


def each_plane(count, unroll, work):
    def group(i, carry):
        for u in range(unroll):
            work(i * unroll + u)
        return carry

    lax.fori_loop(0, count // unroll, group, 0)


def main_kernel(consts, held_ref, other_ref, border_ref, near_ref, far_ref, part_ref, sums_ref,
                val, kap, frozen, prv, rea, dif, fx, fy, fz, alpha, beta, vec, ya, yb, table):
    eigen_basis, basis_inverse, shift_rows, pairs = consts
    nz, nx = held_ref.shape[1], held_ref.shape[2]
    section = lax.axis_index("section")
    zero_plane = jnp.zeros((ROWS, LANES), jnp.float32)
    zero_rows = jnp.zeros((FIRST, LANES), jnp.float32)
    start = border_start()
    even = on_even_row()
    lanes = lane_ids(ROWS)
    edge = (lanes >= start) & (lanes < start + EDGE)
    tile = lambda t: jnp.broadcast_to(t, (8, LANES))

    for at in (0, nz + 1):
        frozen[at] = zero_plane
        for f in range(4):
            for ref in (val, kap, ya, yb):
                ref[f, at] = zero_plane

    def both(entry, row, count):
        near, far = near_ref[entry, row : row + count], far_ref[entry, row : row + count]
        return jnp.where(even, far, near), jnp.where(even, near, far)

    def assemble(plane):
        at = nz * PARTS + plane
        low = jnp.where(even, far_ref[at], near_ref[at])
        high = jnp.where(even, near_ref[at], far_ref[at])
        sides = jnp.concatenate([tile(low[nx - 9 : nx - 8]), low[nx - 8 : nx], border_ref[plane], high[0:8], tile(high[8:9])], 0)
        for part in range(2):
            z = part * (nz // 2) + plane

            def column(f):
                slot = ORDER.index(f)
                mid = held_ref[slot, z] if slot < 5 else other_ref[slot - 5, z]
                entry, row, last, ninth = place(slot, z)
                low, high = both(entry, row, 8)
                low_end, high_end = both(last, ninth, 1)
                cells = jnp.concatenate([tile(low_end), low, mid, high, tile(high_end)], 0)
                at = part * 64 + f * EDGE
                return jnp.where(edge, pltpu.roll(sides, lax.rem(start + LANES - at, LANES), 1), cells)

            diff, prev, react = column(5), column(4), column(6)
            frozen[z + 1] = diff * (0.5 + 0.25 * jnp.tanh(prev))
            prv[z] = prev[WORK]
            rea[z] = react[WORK]
            dif[z] = diff[WORK]
            for f in range(4):
                value = column(f)
                val[f, z + 1] = value
                kap[f, z + 1] = diff * (0.5 + 0.25 * jnp.tanh(value))
                for ref in (ya, yb):
                    ref[f, z + 1, 0:FIRST] = zero_rows
                    ref[f, z + 1, LAST:ROWS] = zero_rows

    each_plane(nz // 2, 1, assemble)

    def pick(matrix, m, j):
        return jnp.where(section == 0, jnp.float32(matrix[m][j]), jnp.float32(matrix[m][(j + 2) % 4]))

    q_rows = [[pick(basis_inverse, m, j) for j in range(4)] for m in range(4)]
    c_rows = [[pick(shift_rows, m, j) for j in range(4)] for m in range(4)]

    def prepare(z):
        mid = frozen[z + 1, WORK]
        faces = [
            mid + frozen[z + 1, BEFORE], mid + frozen[z + 1, AFTER], mid + turn(mid, 1), mid + turn(mid, -1),
            mid + frozen[z, WORK], mid + frozen[z + 2, WORK],
        ]
        for at, ref in enumerate((fx, fy, fz)):
            ref[0, z] = faces[2 * at]
            ref[1, z] = faces[2 * at + 1]
        prev, react = prv[z], rea[z]
        base = ((faces[0] + faces[1]) + (faces[2] + faces[3])) + (faces[4] + faces[5]) - react * (1.0 - 3.0 * prev * prev)
        inside = jnp.where(dif[z] > 0.0, 1.0, 0.0)
        scaled = []
        for b in range(2):
            real, imag = pairs[b]
            diag = base + real
            scale = inside / (diag * diag + imag * imag)
            scaled.append((diag * scale, imag * scale))
            alpha[b, z], beta[b, z] = scaled[b]
        rhs = [None] * 4
        for j in range(4):
            v = val[j, z + 1, WORK]
            k = kap[j, z + 1, WORK]
            flux = react * v * (1.0 - v * v)
            flux = flux + (k + kap[j, z + 1, BEFORE]) * (val[j, z + 1, BEFORE] - v)
            flux = flux + (k + kap[j, z + 1, AFTER]) * (val[j, z + 1, AFTER] - v)
            flux = flux + (k + turn(k, 1)) * (turn(v, 1) - v)
            flux = flux + (k + turn(k, -1)) * (turn(v, -1) - v)
            flux = flux + (k + kap[j, z, WORK]) * (val[j, z, WORK] - v)
            flux = flux + (k + kap[j, z + 2, WORK]) * (val[j, z + 2, WORK] - v)
            grown = v - prev
            for m in range(4):
                term = q_rows[m][j] * flux - c_rows[m][j] * grown
                rhs[m] = term if j == 0 else rhs[m] + term
        for m in range(4):
            vec[0, m, z] = rhs[m]
        for b in range(2):
            al, be = scaled[b]
            ya[2 * b, z + 1, WORK] = al * rhs[2 * b] - be * rhs[2 * b + 1]
            ya[2 * b + 1, z + 1, WORK] = be * rhs[2 * b] + al * rhs[2 * b + 1]

    each_plane(nz, PREPARE_UNROLL, prepare)

    def spread(ref, m, z, rows=WORK):
        lo, hi = rows.start, rows.stop
        cut = slice(lo - FIRST, hi - FIRST)
        mid = ref[m, z + 1, lo:hi]
        in_y = fy[0, z, cut] * turn(mid, 1) + fy[1, z, cut] * turn(mid, -1)
        in_x = fx[0, z, cut] * ref[m, z + 1, lo - 1 : hi - 1] + fx[1, z, cut] * ref[m, z + 1, lo + 1 : hi + 1]
        in_z = fz[0, z, cut] * ref[m, z, lo:hi] + fz[1, z, cut] * ref[m, z + 2, lo:hi]
        return (in_x + in_z) + in_y

    for j in range(ITERS):

        def odd(z, j=j):
            for b in range(2):
                t0 = spread(ya, 2 * b, z)
                t1 = spread(ya, 2 * b + 1, z)
                al, be = alpha[b, z], beta[b, z]
                y0 = al * t0 - be * t1
                y1 = be * t0 + al * t1
                yb[2 * b, z + 1, WORK] = y0
                yb[2 * b + 1, z + 1, WORK] = y1
                sums_ref[j, 2 * b, z] = ya[2 * b, z + 1, OWN] + y0[8:24]
                sums_ref[j, 2 * b + 1, z] = ya[2 * b + 1, z + 1, OWN] + y1[8:24]

        def even(z, j=j):
            last = j == ITERS - 1
            rows = OWN if last else WORK
            cut = slice(rows.start - FIRST, rows.stop - FIRST)
            for b in range(2):
                new = []
                for m in (2 * b, 2 * b + 1):
                    v = spread(yb, m, z, rows)
                    if SHIFTS[j]:
                        v = v - SHIFTS[j] * vec[j, m, z, cut]
                    vec[j + 1, m, z, cut] = v
                    new.append(v)
                if not last:
                    al, be = alpha[b, z], beta[b, z]
                    ya[2 * b, z + 1, WORK] = al * new[0] - be * new[1]
                    ya[2 * b + 1, z + 1, WORK] = be * new[0] + al * new[1]

        each_plane(nz, STEP_UNROLL, odd)
        each_plane(nz, STEP_UNROLL, even)

    table[...] = jnp.zeros((LANES, LANES), jnp.float32)
    mine = half_mask(8)
    for b in range(2):

        def dots(z, carry):
            out = list(carry)
            for m in (2 * b, 2 * b + 1):
                for r in (8, 16):
                    cells = [vec[i, m, z, r : r + 8] for i in range(SIZE)]
                    for at, (i, j) in enumerate(PAIRS):
                        out[at] = out[at] + cells[i] * cells[j]
            return tuple(out)

        zero = jnp.zeros((8, LANES), jnp.float32)
        out = lax.fori_loop(0, nz, dots, tuple(zero for _ in PAIRS))
        for at in range(len(PAIRS)):
            row = jnp.sum(jnp.where(mine, out[at], 0.0), axis=0, keepdims=True)
            table[b * len(PAIRS) + at : b * len(PAIRS) + at + 1] = row
    total = jnp.sum(table[...].T, axis=0, keepdims=True)
    part_ref[...] = jnp.broadcast_to(total, part_ref.shape)


def step_weights(gram):
    table = {}
    for at, (i, j) in enumerate(PAIRS):
        table[i, j] = table[j, i] = gram[at]
    coef = [jnp.ones_like(gram[0])]
    weight = []
    step = coef[0]
    for k in range(ITERS):
        moved = [SHIFTS[j] * coef[j] for j in range(k + 1)] + [jnp.zeros_like(step)]
        for j in range(k + 1):
            moved[j + 1] = moved[j + 1] + coef[j]
        coef = coef + [jnp.zeros_like(step)]
        image = [coef[j] - moved[j] for j in range(k + 2)]
        num, den, bound = 0.0, 0.0, 0.0
        for i in range(k + 2):
            row, size = 0.0, 0.0
            for j in range(k + 2):
                term = table[i, j] * image[j]
                row = row + term
                size = size + jnp.abs(term)
            num = num + row * coef[i]
            den = den + row * image[i]
            bound = bound + size * jnp.abs(image[i])
        step = jnp.where(den > bound * 6e-8, num / (jnp.maximum(den, 0.0) + tiny_value), step)
        weight = weight + [jnp.zeros_like(step)]
        for j in range(k + 1):
            weight[j] = weight[j] + step * coef[j]
        coef = [coef[j] - step * image[j] for j in range(k + 2)]
    return weight


def send_kernel(consts, total_ref, sums_ref, other_ref, send_ref, weight_ref):
    eigen_basis = consts[0]
    nz, nx = other_ref.shape[1], other_ref.shape[2]
    section = lax.axis_index("section")
    total = jnp.sum(total_ref[...], axis=0, keepdims=True)
    count = len(PAIRS)
    weights = []
    for b in range(2):
        gram = [jnp.broadcast_to(total[:, b * count + at : b * count + at + 1], (1, LANES)) for at in range(count)]
        weights.append(step_weights(gram))
    for b in range(2):
        for j in range(ITERS):
            weight_ref[b * ITERS + j : b * ITERS + j + 1] = weights[b][j]
    basis = [
        [jnp.where(section == 0, jnp.float32(eigen_basis[2 + r][m]), jnp.float32(eigen_basis[r][m])) for m in range(4)]
        for r in range(2)
    ]
    mine = half_mask(nx)

    def combine(z):
        outs = [other_ref[r, z] for r in range(2)]
        for m in range(4):
            field = weights[m // 2][0] * sums_ref[0, m, z]
            for j in range(1, ITERS):
                field = field + weights[m // 2][j] * sums_ref[j, m, z]
            outs = [outs[r] + basis[r][m] * field for r in range(2)]
        send_ref[z] = jnp.where(mine, outs[0], turn(outs[1], LANES // 2))

    each_plane(nz, 4, combine)


def mine_kernel(consts, weight_ref, sums_ref, own_ref, mine_ref):
    eigen_basis = consts[0]
    nz = own_ref.shape[1]
    section = lax.axis_index("section")
    weights = [[weight_ref[b * ITERS + j : b * ITERS + j + 1] for j in range(ITERS)] for b in range(2)]
    basis = [
        [jnp.where(section == 0, jnp.float32(eigen_basis[r][m]), jnp.float32(eigen_basis[2 + r][m])) for m in range(4)]
        for r in range(2)
    ]

    def combine(z):
        outs = [own_ref[r, z] for r in range(2)]
        for m in range(4):
            field = weights[m // 2][0] * sums_ref[0, m, z]
            for j in range(1, ITERS):
                field = field + weights[m // 2][j] * sums_ref[j, m, z]
            outs = [outs[r] + basis[r][m] * field for r in range(2)]
        mine_ref[0, z] = outs[0]
        mine_ref[1, z] = outs[1]

    each_plane(nz, 4, combine)


def join_kernel(mine_ref, other_ref, out_ref):
    nz, nx = mine_ref.shape[1], mine_ref.shape[2]
    mine = half_mask(nx)
    for z in range(nz):
        other = other_ref[z]
        out_ref[0, z] = jnp.where(mine, mine_ref[0, z], other)
        out_ref[1, z] = jnp.where(mine, mine_ref[1, z], turn(other, LANES // 2))


def call(kernel, outs, scratch=(), flops=1_000_000, name=None, limit=12):
    many = isinstance(outs, list)
    shapes = [jax.ShapeDtypeStruct(o, jnp.float32) for o in (outs if many else [outs])]

    def run(*args):
        moved = 4 * sum(int(a.size) for a in args) + 4 * sum(int(functools.reduce(lambda p, q: p * q, s.shape, 1)) for s in shapes)
        return pl.pallas_call(
            kernel,
            out_shape=shapes if many else shapes[0],
            in_specs=[pl.BlockSpec(memory_space=pltpu.VMEM)] * len(args),
            out_specs=[pl.BlockSpec(memory_space=pltpu.VMEM)] * len(shapes) if many else pl.BlockSpec(memory_space=pltpu.VMEM),
            scratch_shapes=[pltpu.VMEM(s, jnp.float32) for s in scratch],
            compiler_params=pltpu.CompilerParams(vmem_limit_bytes=int(limit * 1024 * 1024)),
            cost_estimate=pl.CostEstimate(flops=flops, bytes_accessed=moved, transcendentals=0),
            name=name,
        )(*args)

    return run


def swaps(count, start):
    return [pair for i in range(start, count - 1, 2) for pair in ((i, i + 1), (i + 1, i))]


def beside(count, cross):
    pairs = []
    for s in range(2):
        to = 1 - s if cross else s
        step = 1 if to == 0 else -1
        for i in range(count):
            if 0 <= i + step < count:
                pairs.append((s * count + i, to * count + i + step))
    return pairs


def body(previous, sections, diffusivity, reaction):
    consts = constants()
    nz, nx, ny = previous.shape
    columns, rows = lax.axis_size("sy"), lax.axis_size("sx")
    axes = ("section", "sx", "sy")
    partner = [(0, 1), (1, 0)]
    other = lax.ppermute(sections, "section", partner)
    edge, line = (nz // 2, nx, ny), (nz * PARTS + nz // 2, TALL, ny)
    held = jnp.concatenate([sections, previous[None], diffusivity[None], reaction[None]], 0)
    same, cross = call(own_kernel, [edge, edge], name="own")(held)
    same = lax.ppermute(same, ("section", "sy"), beside(columns, False))
    cross = lax.ppermute(cross, ("section", "sy"), beside(columns, True))
    border, near, far = call(rows_kernel, [edge, line, line], name="rows")(held, other, same, cross)
    far = lax.ppermute(far, "sx", swaps(rows, 1))
    near = lax.ppermute(near, "sx", swaps(rows, 0))
    peers = 2 * columns * rows
    padded, work = (nz + 2, ROWS, ny), (nz, LAST - FIRST, ny)
    scratch = [
        (4,) + padded, (4,) + padded, padded, work, work, work, (2,) + work, (2,) + work, (2,) + work, (2,) + work, (2,) + work,
        (SIZE, 4) + work, (4,) + padded, (4,) + padded, (LANES, LANES),
    ]
    part, sums = call(
        functools.partial(main_kernel, consts), [(peers, LANES), (ITERS, 4, nz, nx, ny)], scratch, 50_000_000, "main", 26
    )(held, other, border, near, far)
    total = lax.all_to_all(part.reshape(peers, 1, LANES), axes, 0, 0).reshape(peers, LANES)
    half, weight = call(functools.partial(send_kernel, consts), [previous.shape, (2 * ITERS, LANES)], name="send")(total, sums, other)
    got = lax.ppermute(half, "section", partner)
    mine = call(functools.partial(mine_kernel, consts), sections.shape, name="mine")(weight, sums, held)
    return call(join_kernel, sections.shape, name="join")(mine, got)


def solution(mesh):
    in_specs = (
        P(None, "sx", "sy"),
        P("section", None, "sx", "sy"),
        P(None, "sx", "sy"),
        P(None, "sx", "sy"),
    )
    out_specs = P("section", None, "sx", "sy")
    return jax.shard_map(body, mesh=mesh, in_specs=in_specs, out_specs=out_specs, check_vma=False)
```

```python
import functools

import jax
import jax.numpy as jnp
from jax import lax
from jax.experimental import pallas as pl
from jax.experimental.pallas import tpu as pltpu
from jax.sharding import PartitionSpec as P

ITERS = 4
SHIFTS = (0.0, 0.9, 0.45, 0.7)
EDGE = 9
LANES = 128
SIZE = ITERS + 1
PAIRS = [(i, j) for i in range(SIZE) for j in range(i, SIZE)]
PREPARE_UNROLL = 2
STEP_UNROLL = 8


step_size = 1.0
tiny_value = 1e-06


def invert_table(matrix):
    order_n = len(matrix)
    augmented = [
        list(matrix[r]) + [1.0 if c == r else 0.0 for c in range(order_n)] for r in range(order_n)
    ]
    for col in range(order_n):
        pivot_row = max(range(col, order_n), key=lambda r: abs(augmented[r][col]))
        augmented[col], augmented[pivot_row] = (augmented[pivot_row], augmented[col])
        leading = augmented[col][col]
        augmented[col] = [v / leading for v in augmented[col]]
        for r in range(order_n):
            if r != col:
                factor = augmented[r][col]
                augmented[r] = [a - factor * b for a, b in zip(augmented[r], augmented[col])]
    return [row_values[order_n:] for row_values in augmented]


def table_product(left, right):
    return [
        [sum((left[i][k] * right[k][j] for k in range(len(right)))) for j in range(len(right[0]))]
        for i in range(len(left))
    ]


def pair_add(first, second):
    return (first[0] + second[0], first[1] + second[1])


def pair_sub(first, second):
    return (first[0] - second[0], first[1] - second[1])


def pair_mul(first, second):
    return (
        first[0] * second[0] - first[1] * second[1],
        first[0] * second[1] + first[1] * second[0],
    )


def pair_div(first, second):
    scale_sq = second[0] * second[0] + second[1] * second[1]
    return (
        (first[0] * second[0] + first[1] * second[1]) / scale_sq,
        (first[1] * second[0] - first[0] * second[1]) / scale_sq,
    )


def quartic_value(point):
    return (((210.0 * point - 480.0) * point + 360.0) * point - 96.0) * point + 6.0


def bisect_root(lower, upper):
    for count in range(200):
        middle = 0.5 * (lower + upper)
        if (quartic_value(lower) < 0.0) == (quartic_value(middle) < 0.0):
            lower = middle
        else:
            upper = middle
    return 0.5 * (lower + upper)


def radau_tables():
    abscissae = []
    grid_steps = 4000
    for m in range(grid_steps):
        lower = 0.999 * m / grid_steps
        upper = 0.999 * (m + 1) / grid_steps
        if (quartic_value(lower) < 0.0) != (quartic_value(upper) < 0.0):
            abscissae.append(bisect_root(lower, upper))
    abscissae.append(1.0)
    vander = [[abscissae[j] ** k for k in range(4)] for j in range(4)]
    moments = [[abscissae[i] ** (k + 1) / (k + 1) for k in range(4)] for i in range(4)]
    tableau = table_product(moments, invert_table(vander))
    inverse = invert_table(tableau)
    running = [list(row_values) for row_values in inverse]
    coeffs = []
    for k in range(1, 5):
        trace_value = sum((running[i][i] for i in range(4)))
        coeffs.append(-trace_value / k)
        shifted_table = [
            [running[i][j] + (coeffs[-1] if i == j else 0.0) for j in range(4)] for i in range(4)
        ]
        running = table_product(inverse, shifted_table)
    start_point = (0.4, 0.9)
    estimates = [(1.0, 0.0)]
    for k in range(3):
        estimates.append(pair_mul(estimates[-1], start_point))
    for count in range(500):
        for i in range(4):
            value = (1.0, 0.0)
            for coef_value in coeffs:
                value = pair_add(pair_mul(value, estimates[i]), (coef_value, 0.0))
            denom = (1.0, 0.0)
            for j in range(4):
                if j != i:
                    denom = pair_mul(denom, pair_sub(estimates[i], estimates[j]))
            estimates[i] = pair_sub(estimates[i], pair_div(value, denom))
    chosen = [m for m in range(4) if estimates[m][1] > 0.0]
    ranking = sorted(chosen, key=lambda m: -estimates[m][1])
    columns = []
    pairs = []
    for m in ranking:
        eigen_pair = estimates[m]
        system = [
            [
                (
                    inverse[i][j] - (eigen_pair[0] if i == j else 0.0),
                    -(eigen_pair[1] if i == j else 0.0),
                )
                for j in range(4)
            ]
            for i in range(3)
        ]
        rows_left = [
            [system[i][j] for j in range(3)] + [(-system[i][3][0], -system[i][3][1])]
            for i in range(3)
        ]
        for col in range(3):
            pivot_row = max(
                range(col, 3), key=lambda r: rows_left[r][col][0] ** 2 + rows_left[r][col][1] ** 2
            )
            rows_left[col], rows_left[pivot_row] = (rows_left[pivot_row], rows_left[col])
            leading = rows_left[col][col]
            rows_left[col] = [pair_div(v, leading) for v in rows_left[col]]
            for r in range(3):
                if r != col:
                    factor = rows_left[r][col]
                    rows_left[r] = [
                        pair_sub(a, pair_mul(factor, b))
                        for a, b in zip(rows_left[r], rows_left[col])
                    ]
        vector = [rows_left[i][3] for i in range(3)] + [(1.0, 0.0)]
        columns.append([v[0] for v in vector])
        columns.append([v[1] for v in vector])
        pairs.append((eigen_pair[0], eigen_pair[1]))
    eigen_basis = [[columns[j][i] for j in range(4)] for i in range(4)]
    basis_inverse = invert_table(eigen_basis)
    return (tableau, inverse, eigen_basis, basis_inverse, pairs)


def constants():
    tableau, inverse, eigen_basis, basis_inverse, pairs = radau_tables()
    shift_table = table_product(basis_inverse, inverse)
    shift_rows = [[v / step_size for v in row_values] for row_values in shift_table]
    pairs = [(p[0] / step_size, p[1] / step_size) for p in pairs]
    return eigen_basis, basis_inverse, shift_rows, pairs


def lane_ids(rows):
    return lax.broadcasted_iota(jnp.int32, (rows, LANES), 1)


def turn(cells, amount):
    return pltpu.roll(cells, amount % LANES, cells.ndim - 1)


def left_half():
    return lax.axis_index("section") == 0


def half_mask(rows):
    return (lane_ids(rows) < LANES // 2) == left_half()


ORDER = (0, 1, 4, 5, 6, 2, 3)
TALL = 16
PARTS = 4


def border_start():
    return jnp.where(left_half(), LANES - EDGE, 0)


def on_even_row():
    return lax.rem(lax.axis_index("sx"), 2) == 0


def place(slot, z):
    entry, row = divmod(8 * slot, TALL)
    last, ninth = divmod(56 + slot, TALL)
    return z * PARTS + entry, row, z * PARTS + last, ninth


def pack_rows(near_ref, far_ref, cell, slot, z, even):
    nx = cell.shape[0]
    entry, row, last, ninth = place(slot, z)
    near_ref[entry, row : row + 8] = jnp.where(even, cell[nx - 8 : nx], cell[0:8])
    far_ref[entry, row : row + 8] = jnp.where(even, cell[0:8], cell[nx - 8 : nx])
    near_ref[last, ninth : ninth + 1] = jnp.where(even, cell[nx - 9 : nx - 8], cell[8:9])
    far_ref[last, ninth : ninth + 1] = jnp.where(even, cell[8:9], cell[nx - 9 : nx - 8])


def own_kernel(held_ref, same_ref, cross_ref):
    nz, nx = held_ref.shape[1], held_ref.shape[2]
    lanes = lane_ids(nx)
    incoming = border_start()
    outgoing = LANES - EDGE - incoming

    def put(tile, cell, at, start):
        moved = pltpu.roll(cell, lax.rem(at + LANES - start, LANES), 1)
        return jnp.where((lanes >= at) & (lanes < at + EDGE), moved, tile)

    for plane in range(nz // 2):
        same = jnp.zeros((nx, LANES), jnp.float32)
        cross = same
        for part in range(2):
            z = part * (nz // 2) + plane
            for slot in range(5):
                cell = held_ref[slot, z]
                same = put(same, cell, part * 64 + ORDER[slot] * EDGE, incoming)
                if slot < 2:
                    cross = put(cross, cell, part * 64 + (2 + slot) * EDGE, outgoing)
        same_ref[plane] = same
        cross_ref[plane] = cross


def rows_kernel(held_ref, other_ref, same_ref, cross_ref, border_ref, near_ref, far_ref):
    nz = other_ref.shape[1]
    even = on_even_row()
    for z in range(nz):
        for slot in range(7):
            pack_rows(near_ref, far_ref, held_ref[slot, z] if slot < 5 else other_ref[slot - 5, z], slot, z, even)
    for plane in range(nz // 2):
        border = same_ref[plane] + cross_ref[plane]
        border_ref[plane] = border
        near_ref[nz * PARTS + plane] = border
        far_ref[nz * PARTS + plane] = border


ROWS = 48
FIRST, LAST = 8, 40
OWN = slice(16, 32)
WORK = slice(FIRST, LAST)
BEFORE = slice(FIRST - 1, LAST - 1)
AFTER = slice(FIRST + 1, LAST + 1)


def each_plane(count, unroll, work):
    def group(i, carry):
        for u in range(unroll):
            work(i * unroll + u)
        return carry

    lax.fori_loop(0, count // unroll, group, 0)


def main_kernel(consts, held_ref, other_ref, border_ref, far_ref, near_ref, part_ref, sums_ref,
                val, kap, frozen, prv, rea, dif, fx, fy, fz, alpha, beta, vec, ya, yb, table):
    eigen_basis, basis_inverse, shift_rows, pairs = consts
    nz, nx = held_ref.shape[1], held_ref.shape[2]
    section = lax.axis_index("section")
    zero_plane = jnp.zeros((ROWS, LANES), jnp.float32)
    zero_rows = jnp.zeros((FIRST, LANES), jnp.float32)
    start = border_start()
    even = on_even_row()
    lanes = lane_ids(ROWS)
    edge = (lanes >= start) & (lanes < start + EDGE)
    tile = lambda t: jnp.broadcast_to(t, (8, LANES))

    for at in (0, nz + 1):
        frozen[at] = zero_plane
        for f in range(4):
            for ref in (val, kap, ya, yb):
                ref[f, at] = zero_plane

    def both(entry, row, count):
        near, far = near_ref[entry, row : row + count], far_ref[entry, row : row + count]
        return jnp.where(even, far, near), jnp.where(even, near, far)

    def assemble(plane):
        at = nz * PARTS + plane
        low = jnp.where(even, far_ref[at], near_ref[at])
        high = jnp.where(even, near_ref[at], far_ref[at])
        sides = jnp.concatenate([tile(low[nx - 9 : nx - 8]), low[nx - 8 : nx], border_ref[plane], high[0:8], tile(high[8:9])], 0)
        for part in range(2):
            z = part * (nz // 2) + plane

            def column(f):
                slot = ORDER.index(f)
                mid = held_ref[slot, z] if slot < 5 else other_ref[slot - 5, z]
                entry, row, last, ninth = place(slot, z)
                low, high = both(entry, row, 8)
                low_end, high_end = both(last, ninth, 1)
                cells = jnp.concatenate([tile(low_end), low, mid, high, tile(high_end)], 0)
                at = part * 64 + f * EDGE
                return jnp.where(edge, pltpu.roll(sides, lax.rem(start + LANES - at, LANES), 1), cells)

            diff, prev, react = column(5), column(4), column(6)
            frozen[z + 1] = diff * (0.5 + 0.25 * jnp.tanh(prev))
            prv[z] = prev[WORK]
            rea[z] = react[WORK]
            dif[z] = diff[WORK]
            for f in range(4):
                value = column(f)
                val[f, z + 1] = value
                kap[f, z + 1] = diff * (0.5 + 0.25 * jnp.tanh(value))
                for ref in (ya, yb):
                    ref[f, z + 1, 0:FIRST] = zero_rows
                    ref[f, z + 1, LAST:ROWS] = zero_rows

    each_plane(nz // 2, 1, assemble)

    def pick(matrix, m, j):
        return jnp.where(section == 0, jnp.float32(matrix[m][j]), jnp.float32(matrix[m][(j + 2) % 4]))

    q_rows = [[pick(basis_inverse, m, j) for j in range(4)] for m in range(4)]
    c_rows = [[pick(shift_rows, m, j) for j in range(4)] for m in range(4)]

    def prepare(z):
        mid = frozen[z + 1, WORK]
        faces = [
            mid + frozen[z + 1, BEFORE], mid + frozen[z + 1, AFTER], mid + turn(mid, 1), mid + turn(mid, -1),
            mid + frozen[z, WORK], mid + frozen[z + 2, WORK],
        ]
        for at, ref in enumerate((fx, fy, fz)):
            ref[0, z] = faces[2 * at]
            ref[1, z] = faces[2 * at + 1]
        prev, react = prv[z], rea[z]
        base = ((faces[0] + faces[1]) + (faces[2] + faces[3])) + (faces[4] + faces[5]) - react * (1.0 - 3.0 * prev * prev)
        inside = jnp.where(dif[z] > 0.0, 1.0, 0.0)
        scaled = []
        for b in range(2):
            real, imag = pairs[b]
            diag = base + real
            scale = inside / (diag * diag + imag * imag)
            scaled.append((diag * scale, imag * scale))
            alpha[b, z], beta[b, z] = scaled[b]
        rhs = [None] * 4
        for j in range(4):
            v = val[j, z + 1, WORK]
            k = kap[j, z + 1, WORK]
            flux = react * v * (1.0 - v * v)
            flux = flux + (k + kap[j, z + 1, BEFORE]) * (val[j, z + 1, BEFORE] - v)
            flux = flux + (k + kap[j, z + 1, AFTER]) * (val[j, z + 1, AFTER] - v)
            flux = flux + (k + turn(k, 1)) * (turn(v, 1) - v)
            flux = flux + (k + turn(k, -1)) * (turn(v, -1) - v)
            flux = flux + (k + kap[j, z, WORK]) * (val[j, z, WORK] - v)
            flux = flux + (k + kap[j, z + 2, WORK]) * (val[j, z + 2, WORK] - v)
            grown = v - prev
            for m in range(4):
                term = q_rows[m][j] * flux - c_rows[m][j] * grown
                rhs[m] = term if j == 0 else rhs[m] + term
        for m in range(4):
            vec[0, m, z] = rhs[m]
        for b in range(2):
            al, be = scaled[b]
            ya[2 * b, z + 1, WORK] = al * rhs[2 * b] - be * rhs[2 * b + 1]
            ya[2 * b + 1, z + 1, WORK] = be * rhs[2 * b] + al * rhs[2 * b + 1]

    each_plane(nz, PREPARE_UNROLL, prepare)

    def spread(ref, m, z, rows=WORK):
        lo, hi = rows.start, rows.stop
        cut = slice(lo - FIRST, hi - FIRST)
        mid = ref[m, z + 1, lo:hi]
        in_y = fy[0, z, cut] * turn(mid, 1) + fy[1, z, cut] * turn(mid, -1)
        in_x = fx[0, z, cut] * ref[m, z + 1, lo - 1 : hi - 1] + fx[1, z, cut] * ref[m, z + 1, lo + 1 : hi + 1]
        in_z = fz[0, z, cut] * ref[m, z, lo:hi] + fz[1, z, cut] * ref[m, z + 2, lo:hi]
        return (in_x + in_z) + in_y

    for j in range(ITERS):

        def odd(z, j=j):
            for b in range(2):
                t0 = spread(ya, 2 * b, z)
                t1 = spread(ya, 2 * b + 1, z)
                al, be = alpha[b, z], beta[b, z]
                y0 = al * t0 - be * t1
                y1 = be * t0 + al * t1
                yb[2 * b, z + 1, WORK] = y0
                yb[2 * b + 1, z + 1, WORK] = y1
                sums_ref[j, 2 * b, z] = ya[2 * b, z + 1, OWN] + y0[8:24]
                sums_ref[j, 2 * b + 1, z] = ya[2 * b + 1, z + 1, OWN] + y1[8:24]

        def even(z, j=j):
            last = j == ITERS - 1
            rows = OWN if last else WORK
            cut = slice(rows.start - FIRST, rows.stop - FIRST)
            for b in range(2):
                new = []
                for m in (2 * b, 2 * b + 1):
                    v = spread(yb, m, z, rows)
                    if SHIFTS[j]:
                        v = v - SHIFTS[j] * vec[j, m, z, cut]
                    vec[j + 1, m, z, cut] = v
                    new.append(v)
                if not last:
                    al, be = alpha[b, z], beta[b, z]
                    ya[2 * b, z + 1, WORK] = al * new[0] - be * new[1]
                    ya[2 * b + 1, z + 1, WORK] = be * new[0] + al * new[1]

        each_plane(nz, STEP_UNROLL, odd)
        each_plane(nz, STEP_UNROLL, even)

    table[...] = jnp.zeros((LANES, LANES), jnp.float32)
    mine = half_mask(8)
    for b in range(2):

        def dots(z, carry):
            out = list(carry)
            for m in (2 * b, 2 * b + 1):
                for r in (8, 16):
                    cells = [vec[i, m, z, r : r + 8] for i in range(SIZE)]
                    for at, (i, j) in enumerate(PAIRS):
                        out[at] = out[at] + cells[i] * cells[j]
            return tuple(out)

        zero = jnp.zeros((8, LANES), jnp.float32)
        out = lax.fori_loop(0, nz, dots, tuple(zero for _ in PAIRS))
        for at in range(len(PAIRS)):
            row = jnp.sum(jnp.where(mine, out[at], 0.0), axis=0, keepdims=True)
            table[b * len(PAIRS) + at : b * len(PAIRS) + at + 1] = row
    total = jnp.sum(table[...].T, axis=0, keepdims=True)
    part_ref[...] = jnp.broadcast_to(total, part_ref.shape)


def step_weights(gram):
    table = {}
    for at, (i, j) in enumerate(PAIRS):
        table[i, j] = table[j, i] = gram[at]
    coef = [jnp.ones_like(gram[0])]
    weight = []
    step = coef[0]
    for k in range(ITERS):
        moved = [SHIFTS[j] * coef[j] for j in range(k + 1)] + [jnp.zeros_like(step)]
        for j in range(k + 1):
            moved[j + 1] = moved[j + 1] + coef[j]
        coef = coef + [jnp.zeros_like(step)]
        image = [coef[j] - moved[j] for j in range(k + 2)]
        num, den, bound = 0.0, 0.0, 0.0
        for i in range(k + 2):
            row, size = 0.0, 0.0
            for j in range(k + 2):
                term = table[i, j] * image[j]
                row = row + term
                size = size + jnp.abs(term)
            num = num + row * coef[i]
            den = den + row * image[i]
            bound = bound + size * jnp.abs(image[i])
        step = jnp.where(den > bound * 6e-8, num / (jnp.maximum(den, 0.0) + tiny_value), step)
        weight = weight + [jnp.zeros_like(step)]
        for j in range(k + 1):
            weight[j] = weight[j] + step * coef[j]
        coef = [coef[j] - step * image[j] for j in range(k + 2)]
    return weight


def send_kernel(consts, total_ref, sums_ref, other_ref, send_ref, weight_ref):
    eigen_basis = consts[0]
    nz, nx = other_ref.shape[1], other_ref.shape[2]
    section = lax.axis_index("section")
    total = jnp.sum(total_ref[...], axis=0, keepdims=True)
    count = len(PAIRS)
    weights = []
    for b in range(2):
        gram = [jnp.broadcast_to(total[:, b * count + at : b * count + at + 1], (1, LANES)) for at in range(count)]
        weights.append(step_weights(gram))
    for b in range(2):
        for j in range(ITERS):
            weight_ref[b * ITERS + j : b * ITERS + j + 1] = weights[b][j]
    basis = [
        [jnp.where(section == 0, jnp.float32(eigen_basis[2 + r][m]), jnp.float32(eigen_basis[r][m])) for m in range(4)]
        for r in range(2)
    ]
    mine = half_mask(nx)

    def combine(z):
        outs = [other_ref[r, z] for r in range(2)]
        for m in range(4):
            field = weights[m // 2][0] * sums_ref[0, m, z]
            for j in range(1, ITERS):
                field = field + weights[m // 2][j] * sums_ref[j, m, z]
            outs = [outs[r] + basis[r][m] * field for r in range(2)]
        send_ref[z] = jnp.where(mine, outs[0], turn(outs[1], LANES // 2))

    each_plane(nz, 4, combine)


def mine_kernel(consts, weight_ref, sums_ref, own_ref, mine_ref):
    eigen_basis = consts[0]
    nz = own_ref.shape[1]
    section = lax.axis_index("section")
    weights = [[weight_ref[b * ITERS + j : b * ITERS + j + 1] for j in range(ITERS)] for b in range(2)]
    basis = [
        [jnp.where(section == 0, jnp.float32(eigen_basis[r][m]), jnp.float32(eigen_basis[2 + r][m])) for m in range(4)]
        for r in range(2)
    ]

    def combine(z):
        outs = [own_ref[r, z] for r in range(2)]
        for m in range(4):
            field = weights[m // 2][0] * sums_ref[0, m, z]
            for j in range(1, ITERS):
                field = field + weights[m // 2][j] * sums_ref[j, m, z]
            outs = [outs[r] + basis[r][m] * field for r in range(2)]
        mine_ref[0, z] = outs[0]
        mine_ref[1, z] = outs[1]

    each_plane(nz, 4, combine)


def join_kernel(mine_ref, other_ref, out_ref):
    nz, nx = mine_ref.shape[1], mine_ref.shape[2]
    mine = half_mask(nx)
    for z in range(nz):
        other = other_ref[z]
        out_ref[0, z] = jnp.where(mine, mine_ref[0, z], other)
        out_ref[1, z] = jnp.where(mine, mine_ref[1, z], turn(other, LANES // 2))


def call(kernel, outs, scratch=(), flops=1_000_000, name=None, limit=12):
    many = isinstance(outs, list)
    shapes = [jax.ShapeDtypeStruct(o, jnp.float32) for o in (outs if many else [outs])]

    def run(*args):
        moved = 4 * sum(int(a.size) for a in args) + 4 * sum(int(functools.reduce(lambda p, q: p * q, s.shape, 1)) for s in shapes)
        return pl.pallas_call(
            kernel,
            out_shape=shapes if many else shapes[0],
            in_specs=[pl.BlockSpec(memory_space=pltpu.VMEM)] * len(args),
            out_specs=[pl.BlockSpec(memory_space=pltpu.VMEM)] * len(shapes) if many else pl.BlockSpec(memory_space=pltpu.VMEM),
            scratch_shapes=[pltpu.VMEM(s, jnp.float32) for s in scratch],
            compiler_params=pltpu.CompilerParams(vmem_limit_bytes=int(limit * 1024 * 1024)),
            cost_estimate=pl.CostEstimate(flops=flops, bytes_accessed=moved, transcendentals=0),
            name=name,
        )(*args)

    return run


def swaps(count, start):
    return [pair for i in range(start, count - 1, 2) for pair in ((i, i + 1), (i + 1, i))]


def beside(count, cross):
    pairs = []
    for s in range(2):
        to = 1 - s if cross else s
        step = 1 if to == 0 else -1
        for i in range(count):
            if 0 <= i + step < count:
                pairs.append((s * count + i, to * count + i + step))
    return pairs


def body(previous, sections, diffusivity, reaction):
    consts = constants()
    nz, nx, ny = previous.shape
    columns, rows = lax.axis_size("sy"), lax.axis_size("sx")
    axes = ("section", "sx", "sy")
    partner = [(0, 1), (1, 0)]
    other = lax.ppermute(sections, "section", partner)
    edge, line = (nz // 2, nx, ny), (nz * PARTS + nz // 2, TALL, ny)
    held = jnp.concatenate([sections, previous[None], diffusivity[None], reaction[None]], 0)
    same, cross = call(own_kernel, [edge, edge], name="own")(held)
    same = lax.ppermute(same, ("section", "sy"), beside(columns, False))
    cross = lax.ppermute(cross, ("section", "sy"), beside(columns, True))
    border, near, far = call(rows_kernel, [edge, line, line], name="rows")(held, other, same, cross)
    far = lax.ppermute(far, "sx", swaps(rows, 1))
    near = lax.ppermute(near, "sx", swaps(rows, 0))
    peers = 2 * columns * rows
    padded, work = (nz + 2, ROWS, ny), (nz, LAST - FIRST, ny)
    scratch = [
        (4,) + padded, (4,) + padded, padded, work, work, work, (2,) + work, (2,) + work, (2,) + work, (2,) + work, (2,) + work,
        (SIZE, 4) + work, (4,) + padded, (4,) + padded, (LANES, LANES),
    ]
    part, sums = call(
        functools.partial(main_kernel, consts), [(peers, LANES), (ITERS, 4, nz, nx, ny)], scratch, 50_000_000, "main", 26
    )(held, other, border, far, near)
    total = lax.all_to_all(part.reshape(peers, 1, LANES), axes, 0, 0).reshape(peers, LANES)
    half, weight = call(functools.partial(send_kernel, consts), [previous.shape, (2 * ITERS, LANES)], name="send")(total, sums, other)
    got = lax.ppermute(half, "section", partner)
    mine = call(functools.partial(mine_kernel, consts), sections.shape, name="mine")(weight, sums, held)
    return call(join_kernel, sections.shape, name="join")(mine, got)


def solution(mesh):
    in_specs = (
        P(None, "sx", "sy"),
        P("section", None, "sx", "sy"),
        P(None, "sx", "sy"),
        P(None, "sx", "sy"),
    )
    out_specs = P("section", None, "sx", "sy")
    return jax.shard_map(body, mesh=mesh, in_specs=in_specs, out_specs=out_specs, check_vma=False)
```

```python
import functools

import jax
import jax.numpy as jnp
from jax import lax
from jax.experimental import pallas as pl
from jax.experimental.pallas import tpu as pltpu
from jax.sharding import PartitionSpec as P

ITERS = 4
SHIFTS = (0.0, 0.9, 0.45, 0.7)
EDGE = 9
LANES = 128
SIZE = ITERS + 1
PAIRS = [(i, j) for i in range(SIZE) for j in range(i, SIZE)]
PREPARE_UNROLL = 2
STEP_UNROLL = 8


step_size = 1.0
tiny_value = 1e-06


def invert_table(matrix):
    order_n = len(matrix)
    augmented = [
        list(matrix[r]) + [1.0 if c == r else 0.0 for c in range(order_n)] for r in range(order_n)
    ]
    for col in range(order_n):
        pivot_row = max(range(col, order_n), key=lambda r: abs(augmented[r][col]))
        augmented[col], augmented[pivot_row] = (augmented[pivot_row], augmented[col])
        leading = augmented[col][col]
        augmented[col] = [v / leading for v in augmented[col]]
        for r in range(order_n):
            if r != col:
                factor = augmented[r][col]
                augmented[r] = [a - factor * b for a, b in zip(augmented[r], augmented[col])]
    return [row_values[order_n:] for row_values in augmented]


def table_product(left, right):
    return [
        [sum((left[i][k] * right[k][j] for k in range(len(right)))) for j in range(len(right[0]))]
        for i in range(len(left))
    ]


def pair_add(first, second):
    return (first[0] + second[0], first[1] + second[1])


def pair_sub(first, second):
    return (first[0] - second[0], first[1] - second[1])


def pair_mul(first, second):
    return (
        first[0] * second[0] - first[1] * second[1],
        first[0] * second[1] + first[1] * second[0],
    )


def pair_div(first, second):
    scale_sq = second[0] * second[0] + second[1] * second[1]
    return (
        (first[0] * second[0] + first[1] * second[1]) / scale_sq,
        (first[1] * second[0] - first[0] * second[1]) / scale_sq,
    )


def quartic_value(point):
    return (((210.0 * point - 480.0) * point + 360.0) * point - 96.0) * point + 6.0


def bisect_root(lower, upper):
    for count in range(200):
        middle = 0.5 * (lower + upper)
        if (quartic_value(lower) < 0.0) == (quartic_value(middle) < 0.0):
            lower = middle
        else:
            upper = middle
    return 0.5 * (lower + upper)


def radau_tables():
    abscissae = []
    grid_steps = 4000
    for m in range(grid_steps):
        lower = 0.999 * m / grid_steps
        upper = 0.999 * (m + 1) / grid_steps
        if (quartic_value(lower) < 0.0) != (quartic_value(upper) < 0.0):
            abscissae.append(bisect_root(lower, upper))
    abscissae.append(1.0)
    vander = [[abscissae[j] ** k for k in range(4)] for j in range(4)]
    moments = [[abscissae[i] ** (k + 1) / (k + 1) for k in range(4)] for i in range(4)]
    tableau = table_product(moments, invert_table(vander))
    inverse = invert_table(tableau)
    running = [list(row_values) for row_values in inverse]
    coeffs = []
    for k in range(1, 5):
        trace_value = sum((running[i][i] for i in range(4)))
        coeffs.append(-trace_value / k)
        shifted_table = [
            [running[i][j] + (coeffs[-1] if i == j else 0.0) for j in range(4)] for i in range(4)
        ]
        running = table_product(inverse, shifted_table)
    start_point = (0.4, 0.9)
    estimates = [(1.0, 0.0)]
    for k in range(3):
        estimates.append(pair_mul(estimates[-1], start_point))
    for count in range(500):
        for i in range(4):
            value = (1.0, 0.0)
            for coef_value in coeffs:
                value = pair_add(pair_mul(value, estimates[i]), (coef_value, 0.0))
            denom = (1.0, 0.0)
            for j in range(4):
                if j != i:
                    denom = pair_mul(denom, pair_sub(estimates[i], estimates[j]))
            estimates[i] = pair_sub(estimates[i], pair_div(value, denom))
    chosen = [m for m in range(4) if estimates[m][1] > 0.0]
    ranking = sorted(chosen, key=lambda m: -estimates[m][1])
    columns = []
    pairs = []
    for m in ranking:
        eigen_pair = estimates[m]
        system = [
            [
                (
                    inverse[i][j] - (eigen_pair[0] if i == j else 0.0),
                    -(eigen_pair[1] if i == j else 0.0),
                )
                for j in range(4)
            ]
            for i in range(3)
        ]
        rows_left = [
            [system[i][j] for j in range(3)] + [(-system[i][3][0], -system[i][3][1])]
            for i in range(3)
        ]
        for col in range(3):
            pivot_row = max(
                range(col, 3), key=lambda r: rows_left[r][col][0] ** 2 + rows_left[r][col][1] ** 2
            )
            rows_left[col], rows_left[pivot_row] = (rows_left[pivot_row], rows_left[col])
            leading = rows_left[col][col]
            rows_left[col] = [pair_div(v, leading) for v in rows_left[col]]
            for r in range(3):
                if r != col:
                    factor = rows_left[r][col]
                    rows_left[r] = [
                        pair_sub(a, pair_mul(factor, b))
                        for a, b in zip(rows_left[r], rows_left[col])
                    ]
        vector = [rows_left[i][3] for i in range(3)] + [(1.0, 0.0)]
        columns.append([v[0] for v in vector])
        columns.append([v[1] for v in vector])
        pairs.append((eigen_pair[0], eigen_pair[1]))
    eigen_basis = [[columns[j][i] for j in range(4)] for i in range(4)]
    basis_inverse = invert_table(eigen_basis)
    return (tableau, inverse, eigen_basis, basis_inverse, pairs)


def constants():
    tableau, inverse, eigen_basis, basis_inverse, pairs = radau_tables()
    shift_table = table_product(basis_inverse, inverse)
    shift_rows = [[v / step_size for v in row_values] for row_values in shift_table]
    pairs = [(p[0] / step_size, p[1] / step_size) for p in pairs]
    return eigen_basis, basis_inverse, shift_rows, pairs


def lane_ids(rows):
    return lax.broadcasted_iota(jnp.int32, (rows, LANES), 1)


def turn(cells, amount):
    return pltpu.roll(cells, amount % LANES, cells.ndim - 1)


def left_half():
    return lax.axis_index("section") == 0


def half_mask(rows):
    return (lane_ids(rows) < LANES // 2) == left_half()


ORDER = (0, 1, 4, 5, 6, 2, 3)
TALL = 16
PARTS = 4


def border_start():
    return jnp.where(left_half(), LANES - EDGE, 0)


def on_even_row():
    return lax.rem(lax.axis_index("sx"), 2) == 0


def place(slot, z):
    entry, row = divmod(8 * slot, TALL)
    last, ninth = divmod(56 + slot, TALL)
    return z * PARTS + entry, row, z * PARTS + last, ninth


def put(tile, cell, at, start, lanes):
    moved = pltpu.roll(cell, lax.rem(at + LANES - start, LANES), 1)
    return jnp.where((lanes >= at) & (lanes < at + EDGE), moved, tile)


def inner_start():
    return jnp.where(left_half(), LANES // 2, LANES // 2 - EDGE)


def own_kernel(held_ref, same_ref, cross_ref):
    nz, nx = held_ref.shape[1], held_ref.shape[2]
    lanes = lane_ids(nx)
    incoming = border_start()
    outgoing = LANES - EDGE - incoming

    for plane in range(nz // 2):
        same = jnp.zeros((nx, LANES), jnp.float32)
        cross = same
        for part in range(2):
            z = part * (nz // 2) + plane
            for slot in range(5):
                cell = held_ref[slot, z]
                same = put(same, cell, part * 64 + ORDER[slot] * EDGE, incoming, lanes)
                if slot < 2:
                    cross = put(cross, cell, part * 64 + (2 + slot) * EDGE, outgoing, lanes)
        same_ref[plane] = same
        cross_ref[plane] = cross


def rows_kernel(held_ref, other_ref, same_ref, cross_ref, border_ref, near_ref, far_ref):
    nz, nx = other_ref.shape[1], other_ref.shape[2]
    even = on_even_row()
    inner = inner_start()
    half = nz // 2
    for plane in range(half):
        inner_rows, inner_ninth = jnp.zeros((8, LANES), jnp.float32), jnp.zeros((1, LANES), jnp.float32)
        for part in range(2):
            z = part * half + plane
            rows, ninths = [], []
            for slot, f in enumerate(ORDER):
                cell = held_ref[slot, z] if slot < 5 else other_ref[slot - 5, z]
                entry, row, last, ninth = place(slot, z)
                near_ref[entry, row : row + 8] = jnp.where(even, cell[nx - 8 : nx], cell[0:8])
                near_ref[last, ninth : ninth + 1] = jnp.where(even, cell[nx - 9 : nx - 8], cell[8:9])
                rows.append(jnp.where(even, cell[0:8], cell[nx - 8 : nx]))
                ninths.append(jnp.where(even, cell[8:9], cell[nx - 9 : nx - 8]))
                at = part * 64 + f * EDGE
                inner_rows = put(inner_rows, rows[-1], at, inner, lane_ids(8))
                inner_ninth = put(inner_ninth, ninths[-1], at, inner, lane_ids(1))
            for pair in range(4):
                first, second = 2 * pair, min(2 * pair + 1, 6)
                top = 8 * (pair % 2)
                far_ref[2 * z + pair // 2, top : top + 8] = jnp.where(half_mask(8), rows[first], turn(rows[second], LANES // 2))
                row = 4 * part + pair
                far_ref[2 * nz + plane, row : row + 1] = jnp.where(half_mask(1), ninths[first], turn(ninths[second], LANES // 2))
        border = same_ref[plane] + cross_ref[plane]
        border_ref[plane] = border
        near_ref[nz * PARTS + plane] = border
        far_ref[2 * nz + plane, 8:9] = jnp.where(even, border[8:9], border[nx - 9 : nx - 8])
        far_ref[2 * nz + plane, 9:10] = inner_ninth
        far_ref[2 * nz + half + plane, 0:8] = jnp.where(even, border[0:8], border[nx - 8 : nx])
        far_ref[2 * nz + half + plane, 8:16] = inner_rows


ROWS = 48
FIRST, LAST = 8, 40
OWN = slice(16, 32)
WORK = slice(FIRST, LAST)
BEFORE = slice(FIRST - 1, LAST - 1)
AFTER = slice(FIRST + 1, LAST + 1)


def each_plane(count, unroll, work):
    def group(i, carry):
        for u in range(unroll):
            work(i * unroll + u)
        return carry

    lax.fori_loop(0, count // unroll, group, 0)


def main_kernel(consts, held_ref, other_ref, border_ref, far_ref, near_ref, part_ref, sums_ref,
                val, kap, frozen, prv, rea, dif, fx, fy, fz, alpha, beta, vec, ya, yb, table):
    eigen_basis, basis_inverse, shift_rows, pairs = consts
    nz, nx = held_ref.shape[1], held_ref.shape[2]
    section = lax.axis_index("section")
    zero_plane = jnp.zeros((ROWS, LANES), jnp.float32)
    zero_rows = jnp.zeros((FIRST, LANES), jnp.float32)
    start = border_start()
    even = on_even_row()
    lanes = lane_ids(ROWS)
    edge = (lanes >= start) & (lanes < start + EDGE)
    tile = lambda t: jnp.broadcast_to(t, (8, LANES))

    for at in (0, nz + 1):
        frozen[at] = zero_plane
        for f in range(4):
            for ref in (val, kap, ya, yb):
                ref[f, at] = zero_plane

    inner = inner_start()

    def unpack(cells, window, second, at):
        count = cells.shape[0]
        ids = lane_ids(count)
        cells = turn(cells, LANES // 2) if second else cells
        window = pltpu.roll(window, lax.rem(inner + LANES - at, LANES), 1)
        return jnp.where(half_mask(count), cells, jnp.where((ids >= inner) & (ids < inner + EDGE), window, 0.0))

    def assemble(plane):
        near_side = near_ref[nz * PARTS + plane]
        ends, window = 2 * nz + plane, 2 * nz + nz // 2 + plane
        far_side, far_end = far_ref[window, 0:8], far_ref[ends, 8:9]
        sides = jnp.concatenate(
            [
                tile(jnp.where(even, far_end, near_side[nx - 9 : nx - 8])), jnp.where(even, far_side, near_side[nx - 8 : nx]),
                border_ref[plane],
                jnp.where(even, near_side[0:8], far_side), tile(jnp.where(even, near_side[8:9], far_end)),
            ],
            0,
        )
        for part in range(2):
            z = part * (nz // 2) + plane

            def column(f):
                slot = ORDER.index(f)
                mid = held_ref[slot, z] if slot < 5 else other_ref[slot - 5, z]
                at = part * 64 + f * EDGE
                entry, row, last, ninth = place(slot, z)
                near, near_end = near_ref[entry, row : row + 8], near_ref[last, ninth : ninth + 1]
                pair, second = divmod(slot, 2)
                top, end = 8 * (pair % 2), 4 * part + pair
                far = unpack(far_ref[2 * z + pair // 2, top : top + 8], far_ref[window, 8:16], second, at)
                far_end = unpack(far_ref[ends, end : end + 1], far_ref[ends, 9:10], second, at)
                low, high = jnp.where(even, far, near), jnp.where(even, near, far)
                low_end, high_end = jnp.where(even, far_end, near_end), jnp.where(even, near_end, far_end)
                cells = jnp.concatenate([tile(low_end), low, mid, high, tile(high_end)], 0)
                return jnp.where(edge, pltpu.roll(sides, lax.rem(start + LANES - at, LANES), 1), cells)

            diff, prev, react = column(5), column(4), column(6)
            frozen[z + 1] = diff * (0.5 + 0.25 * jnp.tanh(prev))
            prv[z] = prev[WORK]
            rea[z] = react[WORK]
            dif[z] = diff[WORK]
            for f in range(4):
                value = column(f)
                val[f, z + 1] = value
                kap[f, z + 1] = diff * (0.5 + 0.25 * jnp.tanh(value))
                for ref in (ya, yb):
                    ref[f, z + 1, 0:FIRST] = zero_rows
                    ref[f, z + 1, LAST:ROWS] = zero_rows

    each_plane(nz // 2, 1, assemble)

    def pick(matrix, m, j):
        return jnp.where(section == 0, jnp.float32(matrix[m][j]), jnp.float32(matrix[m][(j + 2) % 4]))

    q_rows = [[pick(basis_inverse, m, j) for j in range(4)] for m in range(4)]
    c_rows = [[pick(shift_rows, m, j) for j in range(4)] for m in range(4)]

    def prepare(z):
        mid = frozen[z + 1, WORK]
        faces = [
            mid + frozen[z + 1, BEFORE], mid + frozen[z + 1, AFTER], mid + turn(mid, 1), mid + turn(mid, -1),
            mid + frozen[z, WORK], mid + frozen[z + 2, WORK],
        ]
        for at, ref in enumerate((fx, fy, fz)):
            ref[0, z] = faces[2 * at]
            ref[1, z] = faces[2 * at + 1]
        prev, react = prv[z], rea[z]
        base = ((faces[0] + faces[1]) + (faces[2] + faces[3])) + (faces[4] + faces[5]) - react * (1.0 - 3.0 * prev * prev)
        inside = jnp.where(dif[z] > 0.0, 1.0, 0.0)
        scaled = []
        for b in range(2):
            real, imag = pairs[b]
            diag = base + real
            scale = inside / (diag * diag + imag * imag)
            scaled.append((diag * scale, imag * scale))
            alpha[b, z], beta[b, z] = scaled[b]
        rhs = [None] * 4
        for j in range(4):
            v = val[j, z + 1, WORK]
            k = kap[j, z + 1, WORK]
            flux = react * v * (1.0 - v * v)
            flux = flux + (k + kap[j, z + 1, BEFORE]) * (val[j, z + 1, BEFORE] - v)
            flux = flux + (k + kap[j, z + 1, AFTER]) * (val[j, z + 1, AFTER] - v)
            flux = flux + (k + turn(k, 1)) * (turn(v, 1) - v)
            flux = flux + (k + turn(k, -1)) * (turn(v, -1) - v)
            flux = flux + (k + kap[j, z, WORK]) * (val[j, z, WORK] - v)
            flux = flux + (k + kap[j, z + 2, WORK]) * (val[j, z + 2, WORK] - v)
            grown = v - prev
            for m in range(4):
                term = q_rows[m][j] * flux - c_rows[m][j] * grown
                rhs[m] = term if j == 0 else rhs[m] + term
        for m in range(4):
            vec[0, m, z] = rhs[m]
        for b in range(2):
            al, be = scaled[b]
            ya[2 * b, z + 1, WORK] = al * rhs[2 * b] - be * rhs[2 * b + 1]
            ya[2 * b + 1, z + 1, WORK] = be * rhs[2 * b] + al * rhs[2 * b + 1]

    each_plane(nz, PREPARE_UNROLL, prepare)

    def spread(ref, m, z, rows=WORK):
        lo, hi = rows.start, rows.stop
        cut = slice(lo - FIRST, hi - FIRST)
        mid = ref[m, z + 1, lo:hi]
        in_y = fy[0, z, cut] * turn(mid, 1) + fy[1, z, cut] * turn(mid, -1)
        in_x = fx[0, z, cut] * ref[m, z + 1, lo - 1 : hi - 1] + fx[1, z, cut] * ref[m, z + 1, lo + 1 : hi + 1]
        in_z = fz[0, z, cut] * ref[m, z, lo:hi] + fz[1, z, cut] * ref[m, z + 2, lo:hi]
        return (in_x + in_z) + in_y

    for j in range(ITERS):

        def odd(z, j=j):
            for b in range(2):
                t0 = spread(ya, 2 * b, z)
                t1 = spread(ya, 2 * b + 1, z)
                al, be = alpha[b, z], beta[b, z]
                y0 = al * t0 - be * t1
                y1 = be * t0 + al * t1
                yb[2 * b, z + 1, WORK] = y0
                yb[2 * b + 1, z + 1, WORK] = y1
                sums_ref[j, 2 * b, z] = ya[2 * b, z + 1, OWN] + y0[8:24]
                sums_ref[j, 2 * b + 1, z] = ya[2 * b + 1, z + 1, OWN] + y1[8:24]

        def even(z, j=j):
            last = j == ITERS - 1
            rows = OWN if last else WORK
            cut = slice(rows.start - FIRST, rows.stop - FIRST)
            for b in range(2):
                new = []
                for m in (2 * b, 2 * b + 1):
                    v = spread(yb, m, z, rows)
                    if SHIFTS[j]:
                        v = v - SHIFTS[j] * vec[j, m, z, cut]
                    vec[j + 1, m, z, cut] = v
                    new.append(v)
                if not last:
                    al, be = alpha[b, z], beta[b, z]
                    ya[2 * b, z + 1, WORK] = al * new[0] - be * new[1]
                    ya[2 * b + 1, z + 1, WORK] = be * new[0] + al * new[1]

        each_plane(nz, STEP_UNROLL, odd)
        each_plane(nz, STEP_UNROLL, even)

    table[...] = jnp.zeros((LANES, LANES), jnp.float32)
    mine = half_mask(8)
    for b in range(2):

        def dots(z, carry):
            out = list(carry)
            for m in (2 * b, 2 * b + 1):
                for r in (8, 16):
                    cells = [vec[i, m, z, r : r + 8] for i in range(SIZE)]
                    for at, (i, j) in enumerate(PAIRS):
                        out[at] = out[at] + cells[i] * cells[j]
            return tuple(out)

        zero = jnp.zeros((8, LANES), jnp.float32)
        out = lax.fori_loop(0, nz, dots, tuple(zero for _ in PAIRS))
        for at in range(len(PAIRS)):
            row = jnp.sum(jnp.where(mine, out[at], 0.0), axis=0, keepdims=True)
            table[b * len(PAIRS) + at : b * len(PAIRS) + at + 1] = row
    total = jnp.sum(table[...].T, axis=0, keepdims=True)
    part_ref[...] = jnp.broadcast_to(total, part_ref.shape)


def step_weights(gram):
    table = {}
    for at, (i, j) in enumerate(PAIRS):
        table[i, j] = table[j, i] = gram[at]
    coef = [jnp.ones_like(gram[0])]
    weight = []
    step = coef[0]
    for k in range(ITERS):
        moved = [SHIFTS[j] * coef[j] for j in range(k + 1)] + [jnp.zeros_like(step)]
        for j in range(k + 1):
            moved[j + 1] = moved[j + 1] + coef[j]
        coef = coef + [jnp.zeros_like(step)]
        image = [coef[j] - moved[j] for j in range(k + 2)]
        num, den, bound = 0.0, 0.0, 0.0
        for i in range(k + 2):
            row, size = 0.0, 0.0
            for j in range(k + 2):
                term = table[i, j] * image[j]
                row = row + term
                size = size + jnp.abs(term)
            num = num + row * coef[i]
            den = den + row * image[i]
            bound = bound + size * jnp.abs(image[i])
        step = jnp.where(den > bound * 6e-8, num / (jnp.maximum(den, 0.0) + tiny_value), step)
        weight = weight + [jnp.zeros_like(step)]
        for j in range(k + 1):
            weight[j] = weight[j] + step * coef[j]
        coef = [coef[j] - step * image[j] for j in range(k + 2)]
    return weight


def send_kernel(consts, total_ref, sums_ref, other_ref, send_ref, weight_ref):
    eigen_basis = consts[0]
    nz, nx = other_ref.shape[1], other_ref.shape[2]
    section = lax.axis_index("section")
    total = jnp.sum(total_ref[...], axis=0, keepdims=True)
    count = len(PAIRS)
    weights = []
    for b in range(2):
        gram = [jnp.broadcast_to(total[:, b * count + at : b * count + at + 1], (1, LANES)) for at in range(count)]
        weights.append(step_weights(gram))
    for b in range(2):
        for j in range(ITERS):
            weight_ref[b * ITERS + j : b * ITERS + j + 1] = weights[b][j]
    basis = [
        [jnp.where(section == 0, jnp.float32(eigen_basis[2 + r][m]), jnp.float32(eigen_basis[r][m])) for m in range(4)]
        for r in range(2)
    ]
    mine = half_mask(nx)

    def combine(z):
        outs = [other_ref[r, z] for r in range(2)]
        for m in range(4):
            field = weights[m // 2][0] * sums_ref[0, m, z]
            for j in range(1, ITERS):
                field = field + weights[m // 2][j] * sums_ref[j, m, z]
            outs = [outs[r] + basis[r][m] * field for r in range(2)]
        send_ref[z] = jnp.where(mine, outs[0], turn(outs[1], LANES // 2))

    each_plane(nz, 4, combine)


def mine_kernel(consts, weight_ref, sums_ref, own_ref, mine_ref):
    eigen_basis = consts[0]
    nz = own_ref.shape[1]
    section = lax.axis_index("section")
    weights = [[weight_ref[b * ITERS + j : b * ITERS + j + 1] for j in range(ITERS)] for b in range(2)]
    basis = [
        [jnp.where(section == 0, jnp.float32(eigen_basis[r][m]), jnp.float32(eigen_basis[2 + r][m])) for m in range(4)]
        for r in range(2)
    ]

    def combine(z):
        outs = [own_ref[r, z] for r in range(2)]
        for m in range(4):
            field = weights[m // 2][0] * sums_ref[0, m, z]
            for j in range(1, ITERS):
                field = field + weights[m // 2][j] * sums_ref[j, m, z]
            outs = [outs[r] + basis[r][m] * field for r in range(2)]
        mine_ref[0, z] = outs[0]
        mine_ref[1, z] = outs[1]

    each_plane(nz, 4, combine)


def join_kernel(mine_ref, other_ref, out_ref):
    nz, nx = mine_ref.shape[1], mine_ref.shape[2]
    mine = half_mask(nx)
    for z in range(nz):
        other = other_ref[z]
        out_ref[0, z] = jnp.where(mine, mine_ref[0, z], other)
        out_ref[1, z] = jnp.where(mine, mine_ref[1, z], turn(other, LANES // 2))


def call(kernel, outs, scratch=(), flops=1_000_000, name=None, limit=12):
    many = isinstance(outs, list)
    shapes = [jax.ShapeDtypeStruct(o, jnp.float32) for o in (outs if many else [outs])]

    def run(*args):
        moved = 4 * sum(int(a.size) for a in args) + 4 * sum(int(functools.reduce(lambda p, q: p * q, s.shape, 1)) for s in shapes)
        return pl.pallas_call(
            kernel,
            out_shape=shapes if many else shapes[0],
            in_specs=[pl.BlockSpec(memory_space=pltpu.VMEM)] * len(args),
            out_specs=[pl.BlockSpec(memory_space=pltpu.VMEM)] * len(shapes) if many else pl.BlockSpec(memory_space=pltpu.VMEM),
            scratch_shapes=[pltpu.VMEM(s, jnp.float32) for s in scratch],
            compiler_params=pltpu.CompilerParams(vmem_limit_bytes=int(limit * 1024 * 1024)),
            cost_estimate=pl.CostEstimate(flops=flops, bytes_accessed=moved, transcendentals=0),
            name=name,
        )(*args)

    return run


def swaps(count, start):
    return [pair for i in range(start, count - 1, 2) for pair in ((i, i + 1), (i + 1, i))]


def beside(count, cross):
    pairs = []
    for s in range(2):
        to = 1 - s if cross else s
        step = 1 if to == 0 else -1
        for i in range(count):
            if 0 <= i + step < count:
                pairs.append((s * count + i, to * count + i + step))
    return pairs


def body(previous, sections, diffusivity, reaction):
    consts = constants()
    nz, nx, ny = previous.shape
    columns, rows = lax.axis_size("sy"), lax.axis_size("sx")
    axes = ("section", "sx", "sy")
    partner = [(0, 1), (1, 0)]
    other = lax.ppermute(sections, "section", partner)
    edge, whole, thin = (nz // 2, nx, ny), (nz * PARTS + nz // 2, TALL, ny), (3 * nz, TALL, ny)
    held = jnp.concatenate([sections, previous[None], diffusivity[None], reaction[None]], 0)
    same, cross = call(own_kernel, [edge, edge], name="own")(held)
    same = lax.ppermute(same, ("section", "sy"), beside(columns, False))
    cross = lax.ppermute(cross, ("section", "sy"), beside(columns, True))
    border, near, far = call(rows_kernel, [edge, whole, thin], name="rows")(held, other, same, cross)
    far = lax.ppermute(far, "sx", swaps(rows, 1))
    near = lax.ppermute(near, "sx", swaps(rows, 0))
    peers = 2 * columns * rows
    padded, work = (nz + 2, ROWS, ny), (nz, LAST - FIRST, ny)
    scratch = [
        (4,) + padded, (4,) + padded, padded, work, work, work, (2,) + work, (2,) + work, (2,) + work, (2,) + work, (2,) + work,
        (SIZE, 4) + work, (4,) + padded, (4,) + padded, (LANES, LANES),
    ]
    part, sums = call(
        functools.partial(main_kernel, consts), [(peers, LANES), (ITERS, 4, nz, nx, ny)], scratch, 50_000_000, "main", 26
    )(held, other, border, far, near)
    total = lax.all_to_all(part.reshape(peers, 1, LANES), axes, 0, 0).reshape(peers, LANES)
    half, weight = call(functools.partial(send_kernel, consts), [previous.shape, (2 * ITERS, LANES)], name="send")(total, sums, other)
    got = lax.ppermute(half, "section", partner)
    mine = call(functools.partial(mine_kernel, consts), sections.shape, name="mine")(weight, sums, held)
    return call(join_kernel, sections.shape, name="join")(mine, got)


def solution(mesh):
    in_specs = (
        P(None, "sx", "sy"),
        P("section", None, "sx", "sy"),
        P(None, "sx", "sy"),
        P(None, "sx", "sy"),
    )
    out_specs = P("section", None, "sx", "sy")
    return jax.shard_map(body, mesh=mesh, in_specs=in_specs, out_specs=out_specs, check_vma=False)
```

```python
import functools

import jax
import jax.numpy as jnp
from jax import lax
from jax.experimental import pallas as pl
from jax.experimental.pallas import tpu as pltpu
from jax.sharding import PartitionSpec as P

ITERS = 4
SHIFTS = (0.0, 0.9, 0.45, 0.7)
EDGE = 9
LANES = 128
SIZE = ITERS + 1
PAIRS = [(i, j) for i in range(SIZE) for j in range(i, SIZE)]
PREPARE_UNROLL = 2
STEP_UNROLL = 8


step_size = 1.0
tiny_value = 1e-06


def invert_table(matrix):
    order_n = len(matrix)
    augmented = [
        list(matrix[r]) + [1.0 if c == r else 0.0 for c in range(order_n)] for r in range(order_n)
    ]
    for col in range(order_n):
        pivot_row = max(range(col, order_n), key=lambda r: abs(augmented[r][col]))
        augmented[col], augmented[pivot_row] = (augmented[pivot_row], augmented[col])
        leading = augmented[col][col]
        augmented[col] = [v / leading for v in augmented[col]]
        for r in range(order_n):
            if r != col:
                factor = augmented[r][col]
                augmented[r] = [a - factor * b for a, b in zip(augmented[r], augmented[col])]
    return [row_values[order_n:] for row_values in augmented]


def table_product(left, right):
    return [
        [sum((left[i][k] * right[k][j] for k in range(len(right)))) for j in range(len(right[0]))]
        for i in range(len(left))
    ]


def pair_add(first, second):
    return (first[0] + second[0], first[1] + second[1])


def pair_sub(first, second):
    return (first[0] - second[0], first[1] - second[1])


def pair_mul(first, second):
    return (
        first[0] * second[0] - first[1] * second[1],
        first[0] * second[1] + first[1] * second[0],
    )


def pair_div(first, second):
    scale_sq = second[0] * second[0] + second[1] * second[1]
    return (
        (first[0] * second[0] + first[1] * second[1]) / scale_sq,
        (first[1] * second[0] - first[0] * second[1]) / scale_sq,
    )


def quartic_value(point):
    return (((210.0 * point - 480.0) * point + 360.0) * point - 96.0) * point + 6.0


def bisect_root(lower, upper):
    for count in range(200):
        middle = 0.5 * (lower + upper)
        if (quartic_value(lower) < 0.0) == (quartic_value(middle) < 0.0):
            lower = middle
        else:
            upper = middle
    return 0.5 * (lower + upper)


def radau_tables():
    abscissae = []
    grid_steps = 4000
    for m in range(grid_steps):
        lower = 0.999 * m / grid_steps
        upper = 0.999 * (m + 1) / grid_steps
        if (quartic_value(lower) < 0.0) != (quartic_value(upper) < 0.0):
            abscissae.append(bisect_root(lower, upper))
    abscissae.append(1.0)
    vander = [[abscissae[j] ** k for k in range(4)] for j in range(4)]
    moments = [[abscissae[i] ** (k + 1) / (k + 1) for k in range(4)] for i in range(4)]
    tableau = table_product(moments, invert_table(vander))
    inverse = invert_table(tableau)
    running = [list(row_values) for row_values in inverse]
    coeffs = []
    for k in range(1, 5):
        trace_value = sum((running[i][i] for i in range(4)))
        coeffs.append(-trace_value / k)
        shifted_table = [
            [running[i][j] + (coeffs[-1] if i == j else 0.0) for j in range(4)] for i in range(4)
        ]
        running = table_product(inverse, shifted_table)
    start_point = (0.4, 0.9)
    estimates = [(1.0, 0.0)]
    for k in range(3):
        estimates.append(pair_mul(estimates[-1], start_point))
    for count in range(500):
        for i in range(4):
            value = (1.0, 0.0)
            for coef_value in coeffs:
                value = pair_add(pair_mul(value, estimates[i]), (coef_value, 0.0))
            denom = (1.0, 0.0)
            for j in range(4):
                if j != i:
                    denom = pair_mul(denom, pair_sub(estimates[i], estimates[j]))
            estimates[i] = pair_sub(estimates[i], pair_div(value, denom))
    chosen = [m for m in range(4) if estimates[m][1] > 0.0]
    ranking = sorted(chosen, key=lambda m: -estimates[m][1])
    columns = []
    pairs = []
    for m in ranking:
        eigen_pair = estimates[m]
        system = [
            [
                (
                    inverse[i][j] - (eigen_pair[0] if i == j else 0.0),
                    -(eigen_pair[1] if i == j else 0.0),
                )
                for j in range(4)
            ]
            for i in range(3)
        ]
        rows_left = [
            [system[i][j] for j in range(3)] + [(-system[i][3][0], -system[i][3][1])]
            for i in range(3)
        ]
        for col in range(3):
            pivot_row = max(
                range(col, 3), key=lambda r: rows_left[r][col][0] ** 2 + rows_left[r][col][1] ** 2
            )
            rows_left[col], rows_left[pivot_row] = (rows_left[pivot_row], rows_left[col])
            leading = rows_left[col][col]
            rows_left[col] = [pair_div(v, leading) for v in rows_left[col]]
            for r in range(3):
                if r != col:
                    factor = rows_left[r][col]
                    rows_left[r] = [
                        pair_sub(a, pair_mul(factor, b))
                        for a, b in zip(rows_left[r], rows_left[col])
                    ]
        vector = [rows_left[i][3] for i in range(3)] + [(1.0, 0.0)]
        columns.append([v[0] for v in vector])
        columns.append([v[1] for v in vector])
        pairs.append((eigen_pair[0], eigen_pair[1]))
    eigen_basis = [[columns[j][i] for j in range(4)] for i in range(4)]
    basis_inverse = invert_table(eigen_basis)
    return (tableau, inverse, eigen_basis, basis_inverse, pairs)


def constants():
    tableau, inverse, eigen_basis, basis_inverse, pairs = radau_tables()
    shift_table = table_product(basis_inverse, inverse)
    shift_rows = [[v / step_size for v in row_values] for row_values in shift_table]
    pairs = [(p[0] / step_size, p[1] / step_size) for p in pairs]
    return eigen_basis, basis_inverse, shift_rows, pairs


def lane_ids(rows):
    return lax.broadcasted_iota(jnp.int32, (rows, LANES), 1)


def turn(cells, amount):
    return pltpu.roll(cells, amount % LANES, cells.ndim - 1)


def left_half():
    return lax.axis_index("section") == 0


def half_mask(rows):
    return (lane_ids(rows) < LANES // 2) == left_half()


ORDER = (0, 1, 4, 5, 6, 2, 3)
TALL = 16
PARTS = 4


def border_start():
    return jnp.where(left_half(), LANES - EDGE, 0)


def on_even_row():
    return lax.rem(lax.axis_index("sx"), 2) == 0


def place(slot, z):
    entry, row = divmod(8 * slot, TALL)
    last, ninth = divmod(56 + slot, TALL)
    return z * PARTS + entry, row, z * PARTS + last, ninth


def put(tile, cell, at, start, lanes):
    moved = pltpu.roll(cell, lax.rem(at + LANES - start, LANES), 1)
    return jnp.where((lanes >= at) & (lanes < at + EDGE), moved, tile)


def inner_start():
    return jnp.where(left_half(), LANES // 2, LANES // 2 - EDGE)


def own_kernel(held_ref, same_ref, cross_ref):
    nz, nx = held_ref.shape[1], held_ref.shape[2]
    lanes = lane_ids(nx)
    incoming = border_start()
    outgoing = LANES - EDGE - incoming

    for plane in range(nz // 2):
        same = jnp.zeros((nx, LANES), jnp.float32)
        cross = same
        for part in range(2):
            z = part * (nz // 2) + plane
            for slot in range(5):
                cell = held_ref[slot, z]
                same = put(same, cell, part * 64 + ORDER[slot] * EDGE, incoming, lanes)
                if slot < 2:
                    cross = put(cross, cell, part * 64 + (2 + slot) * EDGE, outgoing, lanes)
        same_ref[plane] = same
        cross_ref[plane] = cross


def rows_kernel(held_ref, other_ref, same_ref, cross_ref, border_ref, near_ref, far_ref):
    nz, nx = other_ref.shape[1], other_ref.shape[2]
    even = on_even_row()
    inner = inner_start()
    half = nz // 2
    for plane in range(half):
        inner_rows, inner_ninth = jnp.zeros((8, LANES), jnp.float32), jnp.zeros((1, LANES), jnp.float32)
        for part in range(2):
            z = part * half + plane
            rows, ninths = [], []
            for slot, f in enumerate(ORDER):
                cell = held_ref[slot, z] if slot < 5 else other_ref[slot - 5, z]
                entry, row, last, ninth = place(slot, z)
                near_ref[entry, row : row + 8] = jnp.where(even, cell[nx - 8 : nx], cell[0:8])
                near_ref[last, ninth : ninth + 1] = jnp.where(even, cell[nx - 9 : nx - 8], cell[8:9])
                rows.append(jnp.where(even, cell[0:8], cell[nx - 8 : nx]))
                ninths.append(jnp.where(even, cell[8:9], cell[nx - 9 : nx - 8]))
                at = part * 64 + f * EDGE
                inner_rows = put(inner_rows, rows[-1], at, inner, lane_ids(8))
                inner_ninth = put(inner_ninth, ninths[-1], at, inner, lane_ids(1))
            for pair in range(4):
                first, second = 2 * pair, min(2 * pair + 1, 6)
                top = 8 * (pair % 2)
                far_ref[2 * z + pair // 2, top : top + 8] = jnp.where(half_mask(8), rows[first], turn(rows[second], LANES // 2))
                row = 4 * part + pair
                far_ref[2 * nz + plane, row : row + 1] = jnp.where(half_mask(1), ninths[first], turn(ninths[second], LANES // 2))
        border = same_ref[plane] + cross_ref[plane]
        border_ref[plane] = border
        near_ref[nz * PARTS + plane] = border
        far_ref[2 * nz + plane, 8:9] = jnp.where(even, border[8:9], border[nx - 9 : nx - 8])
        far_ref[2 * nz + plane, 9:10] = inner_ninth
        far_ref[2 * nz + half + plane, 0:8] = jnp.where(even, border[0:8], border[nx - 8 : nx])
        far_ref[2 * nz + half + plane, 8:16] = inner_rows


ROWS = 48
FIRST, LAST = 8, 40
OWN = slice(16, 32)
WORK = slice(FIRST, LAST)
NARROW = slice(12, 36)
BEFORE = slice(FIRST - 1, LAST - 1)
AFTER = slice(FIRST + 1, LAST + 1)


def each_plane(count, unroll, work):
    def group(i, carry):
        for u in range(unroll):
            work(i * unroll + u)
        return carry

    lax.fori_loop(0, count // unroll, group, 0)


def main_kernel(consts, held_ref, other_ref, border_ref, far_ref, near_ref, part_ref, sums_ref,
                val, kap, frozen, prv, rea, dif, fx, fy, fz, alpha, beta, vec, ya, yb, table):
    eigen_basis, basis_inverse, shift_rows, pairs = consts
    nz, nx = held_ref.shape[1], held_ref.shape[2]
    section = lax.axis_index("section")
    zero_plane = jnp.zeros((ROWS, LANES), jnp.float32)
    zero_rows = jnp.zeros((FIRST, LANES), jnp.float32)
    start = border_start()
    even = on_even_row()
    lanes = lane_ids(ROWS)
    edge = (lanes >= start) & (lanes < start + EDGE)
    tile = lambda t: jnp.broadcast_to(t, (8, LANES))

    for at in (0, nz + 1):
        frozen[at] = zero_plane
        for f in range(4):
            for ref in (val, kap, ya, yb):
                ref[f, at] = zero_plane

    inner = inner_start()

    def unpack(cells, window, second, at):
        count = cells.shape[0]
        ids = lane_ids(count)
        cells = turn(cells, LANES // 2) if second else cells
        window = pltpu.roll(window, lax.rem(inner + LANES - at, LANES), 1)
        return jnp.where(half_mask(count), cells, jnp.where((ids >= inner) & (ids < inner + EDGE), window, 0.0))

    def assemble(plane):
        near_side = near_ref[nz * PARTS + plane]
        ends, window = 2 * nz + plane, 2 * nz + nz // 2 + plane
        far_side, far_end = far_ref[window, 0:8], far_ref[ends, 8:9]
        sides = jnp.concatenate(
            [
                tile(jnp.where(even, far_end, near_side[nx - 9 : nx - 8])), jnp.where(even, far_side, near_side[nx - 8 : nx]),
                border_ref[plane],
                jnp.where(even, near_side[0:8], far_side), tile(jnp.where(even, near_side[8:9], far_end)),
            ],
            0,
        )
        for part in range(2):
            z = part * (nz // 2) + plane

            def column(f):
                slot = ORDER.index(f)
                mid = held_ref[slot, z] if slot < 5 else other_ref[slot - 5, z]
                at = part * 64 + f * EDGE
                entry, row, last, ninth = place(slot, z)
                near, near_end = near_ref[entry, row : row + 8], near_ref[last, ninth : ninth + 1]
                pair, second = divmod(slot, 2)
                top, end = 8 * (pair % 2), 4 * part + pair
                far = unpack(far_ref[2 * z + pair // 2, top : top + 8], far_ref[window, 8:16], second, at)
                far_end = unpack(far_ref[ends, end : end + 1], far_ref[ends, 9:10], second, at)
                low, high = jnp.where(even, far, near), jnp.where(even, near, far)
                low_end, high_end = jnp.where(even, far_end, near_end), jnp.where(even, near_end, far_end)
                cells = jnp.concatenate([tile(low_end), low, mid, high, tile(high_end)], 0)
                return jnp.where(edge, pltpu.roll(sides, lax.rem(start + LANES - at, LANES), 1), cells)

            diff, prev, react = column(5), column(4), column(6)
            frozen[z + 1] = diff * (0.5 + 0.25 * jnp.tanh(prev))
            prv[z] = prev[WORK]
            rea[z] = react[WORK]
            dif[z] = diff[WORK]
            for f in range(4):
                value = column(f)
                val[f, z + 1] = value
                kap[f, z + 1] = diff * (0.5 + 0.25 * jnp.tanh(value))
                for ref in (ya, yb):
                    ref[f, z + 1, 0:FIRST] = zero_rows
                    ref[f, z + 1, LAST:ROWS] = zero_rows

    each_plane(nz // 2, 1, assemble)

    def pick(matrix, m, j):
        return jnp.where(section == 0, jnp.float32(matrix[m][j]), jnp.float32(matrix[m][(j + 2) % 4]))

    q_rows = [[pick(basis_inverse, m, j) for j in range(4)] for m in range(4)]
    c_rows = [[pick(shift_rows, m, j) for j in range(4)] for m in range(4)]

    def prepare(z):
        mid = frozen[z + 1, WORK]
        faces = [
            mid + frozen[z + 1, BEFORE], mid + frozen[z + 1, AFTER], mid + turn(mid, 1), mid + turn(mid, -1),
            mid + frozen[z, WORK], mid + frozen[z + 2, WORK],
        ]
        for at, ref in enumerate((fx, fy, fz)):
            ref[0, z] = faces[2 * at]
            ref[1, z] = faces[2 * at + 1]
        prev, react = prv[z], rea[z]
        base = ((faces[0] + faces[1]) + (faces[2] + faces[3])) + (faces[4] + faces[5]) - react * (1.0 - 3.0 * prev * prev)
        inside = jnp.where(dif[z] > 0.0, 1.0, 0.0)
        scaled = []
        for b in range(2):
            real, imag = pairs[b]
            diag = base + real
            scale = inside / (diag * diag + imag * imag)
            scaled.append((diag * scale, imag * scale))
            alpha[b, z], beta[b, z] = scaled[b]
        rhs = [None] * 4
        for j in range(4):
            v = val[j, z + 1, WORK]
            k = kap[j, z + 1, WORK]
            flux = react * v * (1.0 - v * v)
            flux = flux + (k + kap[j, z + 1, BEFORE]) * (val[j, z + 1, BEFORE] - v)
            flux = flux + (k + kap[j, z + 1, AFTER]) * (val[j, z + 1, AFTER] - v)
            flux = flux + (k + turn(k, 1)) * (turn(v, 1) - v)
            flux = flux + (k + turn(k, -1)) * (turn(v, -1) - v)
            flux = flux + (k + kap[j, z, WORK]) * (val[j, z, WORK] - v)
            flux = flux + (k + kap[j, z + 2, WORK]) * (val[j, z + 2, WORK] - v)
            grown = v - prev
            for m in range(4):
                term = q_rows[m][j] * flux - c_rows[m][j] * grown
                rhs[m] = term if j == 0 else rhs[m] + term
        for m in range(4):
            vec[0, m, z] = rhs[m]
        for b in range(2):
            al, be = scaled[b]
            ya[2 * b, z + 1, WORK] = al * rhs[2 * b] - be * rhs[2 * b + 1]
            ya[2 * b + 1, z + 1, WORK] = be * rhs[2 * b] + al * rhs[2 * b + 1]

    each_plane(nz, PREPARE_UNROLL, prepare)

    def spread(ref, m, z, rows=WORK):
        lo, hi = rows.start, rows.stop
        cut = slice(lo - FIRST, hi - FIRST)
        mid = ref[m, z + 1, lo:hi]
        in_y = fy[0, z, cut] * turn(mid, 1) + fy[1, z, cut] * turn(mid, -1)
        in_x = fx[0, z, cut] * ref[m, z + 1, lo - 1 : hi - 1] + fx[1, z, cut] * ref[m, z + 1, lo + 1 : hi + 1]
        in_z = fz[0, z, cut] * ref[m, z, lo:hi] + fz[1, z, cut] * ref[m, z + 2, lo:hi]
        return (in_x + in_z) + in_y

    def window(done):
        reach = 2 * ITERS - done
        return OWN if reach == 0 else NARROW if reach <= 4 else WORK

    for j in range(ITERS):

        def odd(z, j=j):
            rows = window(2 * j + 1)
            cut = slice(rows.start - FIRST, rows.stop - FIRST)
            for b in range(2):
                t0 = spread(ya, 2 * b, z, rows)
                t1 = spread(ya, 2 * b + 1, z, rows)
                al, be = alpha[b, z, cut], beta[b, z, cut]
                for m, y in ((2 * b, al * t0 - be * t1), (2 * b + 1, be * t0 + al * t1)):
                    yb[m, z + 1, rows] = y
                    if rows == WORK:
                        sums_ref[j, m, z, 4:20] = ya[m, z + 1, OWN] + y[8:24]
                    else:
                        sums_ref[j, m, z] = ya[m, z + 1, rows] + y

        def even(z, j=j):
            last = j == ITERS - 1
            rows = window(2 * j + 2)
            cut = slice(rows.start - FIRST, rows.stop - FIRST)
            for b in range(2):
                new = []
                for m in (2 * b, 2 * b + 1):
                    v = spread(yb, m, z, rows)
                    if SHIFTS[j]:
                        v = v - SHIFTS[j] * vec[j, m, z, cut]
                    vec[j + 1, m, z, cut] = v
                    new.append(v)
                if not last:
                    al, be = alpha[b, z, cut], beta[b, z, cut]
                    ya[2 * b, z + 1, rows] = al * new[0] - be * new[1]
                    ya[2 * b + 1, z + 1, rows] = be * new[0] + al * new[1]

        each_plane(nz, STEP_UNROLL, odd)
        each_plane(nz, STEP_UNROLL, even)

    table[...] = jnp.zeros((LANES, LANES), jnp.float32)
    mine = half_mask(8)
    for b in range(2):

        def dots(i, carry):
            out = list(carry)
            for z, m in [(4 * i + u, m) for u in range(4) for m in (2 * b, 2 * b + 1)]:
                cells = [jnp.where(mine, vec[k, m, z, 8:16], turn(vec[k, m, z, 16:24], LANES // 2)) for k in range(SIZE)]
                for at, (k, j) in enumerate(PAIRS):
                    out[at] = out[at] + cells[k] * cells[j]
            return tuple(out)

        zero = jnp.zeros((8, LANES), jnp.float32)
        out = lax.fori_loop(0, nz // 4, dots, tuple(zero for _ in PAIRS))
        for at in range(len(PAIRS)):
            row = jnp.sum(out[at], axis=0, keepdims=True)
            table[b * len(PAIRS) + at : b * len(PAIRS) + at + 1] = row
    total = jnp.sum(table[...].T, axis=0, keepdims=True)
    part_ref[...] = jnp.broadcast_to(total, part_ref.shape)


def step_weights(gram):
    table = {}
    for at, (i, j) in enumerate(PAIRS):
        table[i, j] = table[j, i] = gram[at]
    coef = [jnp.ones_like(gram[0])]
    weight = []
    step = coef[0]
    for k in range(ITERS):
        moved = [SHIFTS[j] * coef[j] for j in range(k + 1)] + [jnp.zeros_like(step)]
        for j in range(k + 1):
            moved[j + 1] = moved[j + 1] + coef[j]
        coef = coef + [jnp.zeros_like(step)]
        image = [coef[j] - moved[j] for j in range(k + 2)]
        num, den, bound = 0.0, 0.0, 0.0
        for i in range(k + 2):
            row, size = 0.0, 0.0
            for j in range(k + 2):
                term = table[i, j] * image[j]
                row = row + term
                size = size + jnp.abs(term)
            num = num + row * coef[i]
            den = den + row * image[i]
            bound = bound + size * jnp.abs(image[i])
        step = jnp.where(den > bound * 6e-8, num / (jnp.maximum(den, 0.0) + tiny_value), step)
        weight = weight + [jnp.zeros_like(step)]
        for j in range(k + 1):
            weight[j] = weight[j] + step * coef[j]
        coef = [coef[j] - step * image[j] for j in range(k + 2)]
    return weight


def send_kernel(consts, total_ref, sums_ref, other_ref, send_ref, weight_ref):
    eigen_basis = consts[0]
    nz, nx = other_ref.shape[1], other_ref.shape[2]
    section = lax.axis_index("section")
    total = jnp.sum(total_ref[...], axis=0, keepdims=True)
    count = len(PAIRS)
    weights = []
    for b in range(2):
        gram = [jnp.broadcast_to(total[:, b * count + at : b * count + at + 1], (1, LANES)) for at in range(count)]
        weights.append(step_weights(gram))
    for b in range(2):
        for j in range(ITERS):
            weight_ref[b * ITERS + j : b * ITERS + j + 1] = weights[b][j]
    basis = [
        [jnp.where(section == 0, jnp.float32(eigen_basis[2 + r][m]), jnp.float32(eigen_basis[r][m])) for m in range(4)]
        for r in range(2)
    ]
    mine = half_mask(nx)

    def combine(z):
        outs = [other_ref[r, z] for r in range(2)]
        for m in range(4):
            field = weights[m // 2][0] * sums_ref[0, m, z, 4:20]
            for j in range(1, ITERS):
                field = field + weights[m // 2][j] * sums_ref[j, m, z, 4:20]
            outs = [outs[r] + basis[r][m] * field for r in range(2)]
        send_ref[z] = jnp.where(mine, outs[0], turn(outs[1], LANES // 2))

    each_plane(nz, 4, combine)


def mine_kernel(consts, weight_ref, sums_ref, own_ref, mine_ref):
    eigen_basis = consts[0]
    nz = own_ref.shape[1]
    section = lax.axis_index("section")
    weights = [[weight_ref[b * ITERS + j : b * ITERS + j + 1] for j in range(ITERS)] for b in range(2)]
    basis = [
        [jnp.where(section == 0, jnp.float32(eigen_basis[r][m]), jnp.float32(eigen_basis[2 + r][m])) for m in range(4)]
        for r in range(2)
    ]

    def combine(z):
        outs = [own_ref[r, z] for r in range(2)]
        for m in range(4):
            field = weights[m // 2][0] * sums_ref[0, m, z, 4:20]
            for j in range(1, ITERS):
                field = field + weights[m // 2][j] * sums_ref[j, m, z, 4:20]
            outs = [outs[r] + basis[r][m] * field for r in range(2)]
        mine_ref[0, z] = outs[0]
        mine_ref[1, z] = outs[1]

    each_plane(nz, 4, combine)


def join_kernel(mine_ref, other_ref, out_ref):
    nz, nx = mine_ref.shape[1], mine_ref.shape[2]
    mine = half_mask(nx)
    for z in range(nz):
        other = other_ref[z]
        out_ref[0, z] = jnp.where(mine, mine_ref[0, z], other)
        out_ref[1, z] = jnp.where(mine, mine_ref[1, z], turn(other, LANES // 2))


def call(kernel, outs, scratch=(), flops=1_000_000, name=None, limit=12):
    many = isinstance(outs, list)
    shapes = [jax.ShapeDtypeStruct(o, jnp.float32) for o in (outs if many else [outs])]

    def run(*args):
        moved = 4 * sum(int(a.size) for a in args) + 4 * sum(int(functools.reduce(lambda p, q: p * q, s.shape, 1)) for s in shapes)
        return pl.pallas_call(
            kernel,
            out_shape=shapes if many else shapes[0],
            in_specs=[pl.BlockSpec(memory_space=pltpu.VMEM)] * len(args),
            out_specs=[pl.BlockSpec(memory_space=pltpu.VMEM)] * len(shapes) if many else pl.BlockSpec(memory_space=pltpu.VMEM),
            scratch_shapes=[pltpu.VMEM(s, jnp.float32) for s in scratch],
            compiler_params=pltpu.CompilerParams(vmem_limit_bytes=int(limit * 1024 * 1024)),
            cost_estimate=pl.CostEstimate(flops=flops, bytes_accessed=moved, transcendentals=0),
            name=name,
        )(*args)

    return run


def swaps(count, start):
    return [pair for i in range(start, count - 1, 2) for pair in ((i, i + 1), (i + 1, i))]


def beside(count, cross):
    pairs = []
    for s in range(2):
        to = 1 - s if cross else s
        step = 1 if to == 0 else -1
        for i in range(count):
            if 0 <= i + step < count:
                pairs.append((s * count + i, to * count + i + step))
    return pairs


def body(previous, sections, diffusivity, reaction):
    consts = constants()
    nz, nx, ny = previous.shape
    columns, rows = lax.axis_size("sy"), lax.axis_size("sx")
    axes = ("section", "sx", "sy")
    partner = [(0, 1), (1, 0)]
    other = lax.ppermute(sections, "section", partner)
    edge, whole, thin = (nz // 2, nx, ny), (nz * PARTS + nz // 2, TALL, ny), (3 * nz, TALL, ny)
    held = jnp.concatenate([sections, previous[None], diffusivity[None], reaction[None]], 0)
    same, cross = call(own_kernel, [edge, edge], name="own")(held)
    same = lax.ppermute(same, ("section", "sy"), beside(columns, False))
    cross = lax.ppermute(cross, ("section", "sy"), beside(columns, True))
    border, near, far = call(rows_kernel, [edge, whole, thin], name="rows")(held, other, same, cross)
    far = lax.ppermute(far, "sx", swaps(rows, 1))
    near = lax.ppermute(near, "sx", swaps(rows, 0))
    peers = 2 * columns * rows
    padded, work = (nz + 2, ROWS, ny), (nz, LAST - FIRST, ny)
    scratch = [
        (4,) + padded, (4,) + padded, padded, work, work, work, (2,) + work, (2,) + work, (2,) + work, (2,) + work, (2,) + work,
        (SIZE, 4) + work, (4,) + padded, (4,) + padded, (LANES, LANES),
    ]
    part, sums = call(
        functools.partial(main_kernel, consts), [(peers, LANES), (ITERS, 4, nz, nx + 8, ny)], scratch, 50_000_000, "main", 26
    )(held, other, border, far, near)
    total = lax.all_to_all(part.reshape(peers, 1, LANES), axes, 0, 0).reshape(peers, LANES)
    half, weight = call(functools.partial(send_kernel, consts), [previous.shape, (2 * ITERS, LANES)], name="send")(total, sums, other)
    got = lax.ppermute(half, "section", partner)
    mine = call(functools.partial(mine_kernel, consts), sections.shape, name="mine")(weight, sums, held)
    return call(join_kernel, sections.shape, name="join")(mine, got)


def solution(mesh):
    in_specs = (
        P(None, "sx", "sy"),
        P("section", None, "sx", "sy"),
        P(None, "sx", "sy"),
        P(None, "sx", "sy"),
    )
    out_specs = P("section", None, "sx", "sy")
    return jax.shard_map(body, mesh=mesh, in_specs=in_specs, out_specs=out_specs, check_vma=False)
```

```python
import functools

import jax
import jax.numpy as jnp
from jax import lax
from jax.experimental import pallas as pl
from jax.experimental.pallas import tpu as pltpu
from jax.sharding import PartitionSpec as P

ITERS = 4
SHIFTS = (0.0, 0.9, 0.45, 0.7)
EDGE = 9
LANES = 128
SIZE = ITERS + 1
PAIRS = [(i, j) for i in range(SIZE) for j in range(i, SIZE)]
PREPARE_UNROLL = 2
STEP_UNROLL = 8


step_size = 1.0
tiny_value = 1e-06


def invert_table(matrix):
    order_n = len(matrix)
    augmented = [
        list(matrix[r]) + [1.0 if c == r else 0.0 for c in range(order_n)] for r in range(order_n)
    ]
    for col in range(order_n):
        pivot_row = max(range(col, order_n), key=lambda r: abs(augmented[r][col]))
        augmented[col], augmented[pivot_row] = (augmented[pivot_row], augmented[col])
        leading = augmented[col][col]
        augmented[col] = [v / leading for v in augmented[col]]
        for r in range(order_n):
            if r != col:
                factor = augmented[r][col]
                augmented[r] = [a - factor * b for a, b in zip(augmented[r], augmented[col])]
    return [row_values[order_n:] for row_values in augmented]


def table_product(left, right):
    return [
        [sum((left[i][k] * right[k][j] for k in range(len(right)))) for j in range(len(right[0]))]
        for i in range(len(left))
    ]


def pair_add(first, second):
    return (first[0] + second[0], first[1] + second[1])


def pair_sub(first, second):
    return (first[0] - second[0], first[1] - second[1])


def pair_mul(first, second):
    return (
        first[0] * second[0] - first[1] * second[1],
        first[0] * second[1] + first[1] * second[0],
    )


def pair_div(first, second):
    scale_sq = second[0] * second[0] + second[1] * second[1]
    return (
        (first[0] * second[0] + first[1] * second[1]) / scale_sq,
        (first[1] * second[0] - first[0] * second[1]) / scale_sq,
    )


def quartic_value(point):
    return (((210.0 * point - 480.0) * point + 360.0) * point - 96.0) * point + 6.0


def bisect_root(lower, upper):
    for count in range(200):
        middle = 0.5 * (lower + upper)
        if (quartic_value(lower) < 0.0) == (quartic_value(middle) < 0.0):
            lower = middle
        else:
            upper = middle
    return 0.5 * (lower + upper)


def radau_tables():
    abscissae = []
    grid_steps = 4000
    for m in range(grid_steps):
        lower = 0.999 * m / grid_steps
        upper = 0.999 * (m + 1) / grid_steps
        if (quartic_value(lower) < 0.0) != (quartic_value(upper) < 0.0):
            abscissae.append(bisect_root(lower, upper))
    abscissae.append(1.0)
    vander = [[abscissae[j] ** k for k in range(4)] for j in range(4)]
    moments = [[abscissae[i] ** (k + 1) / (k + 1) for k in range(4)] for i in range(4)]
    tableau = table_product(moments, invert_table(vander))
    inverse = invert_table(tableau)
    running = [list(row_values) for row_values in inverse]
    coeffs = []
    for k in range(1, 5):
        trace_value = sum((running[i][i] for i in range(4)))
        coeffs.append(-trace_value / k)
        shifted_table = [
            [running[i][j] + (coeffs[-1] if i == j else 0.0) for j in range(4)] for i in range(4)
        ]
        running = table_product(inverse, shifted_table)
    start_point = (0.4, 0.9)
    estimates = [(1.0, 0.0)]
    for k in range(3):
        estimates.append(pair_mul(estimates[-1], start_point))
    for count in range(500):
        for i in range(4):
            value = (1.0, 0.0)
            for coef_value in coeffs:
                value = pair_add(pair_mul(value, estimates[i]), (coef_value, 0.0))
            denom = (1.0, 0.0)
            for j in range(4):
                if j != i:
                    denom = pair_mul(denom, pair_sub(estimates[i], estimates[j]))
            estimates[i] = pair_sub(estimates[i], pair_div(value, denom))
    chosen = [m for m in range(4) if estimates[m][1] > 0.0]
    ranking = sorted(chosen, key=lambda m: -estimates[m][1])
    columns = []
    pairs = []
    for m in ranking:
        eigen_pair = estimates[m]
        system = [
            [
                (
                    inverse[i][j] - (eigen_pair[0] if i == j else 0.0),
                    -(eigen_pair[1] if i == j else 0.0),
                )
                for j in range(4)
            ]
            for i in range(3)
        ]
        rows_left = [
            [system[i][j] for j in range(3)] + [(-system[i][3][0], -system[i][3][1])]
            for i in range(3)
        ]
        for col in range(3):
            pivot_row = max(
                range(col, 3), key=lambda r: rows_left[r][col][0] ** 2 + rows_left[r][col][1] ** 2
            )
            rows_left[col], rows_left[pivot_row] = (rows_left[pivot_row], rows_left[col])
            leading = rows_left[col][col]
            rows_left[col] = [pair_div(v, leading) for v in rows_left[col]]
            for r in range(3):
                if r != col:
                    factor = rows_left[r][col]
                    rows_left[r] = [
                        pair_sub(a, pair_mul(factor, b))
                        for a, b in zip(rows_left[r], rows_left[col])
                    ]
        vector = [rows_left[i][3] for i in range(3)] + [(1.0, 0.0)]
        columns.append([v[0] for v in vector])
        columns.append([v[1] for v in vector])
        pairs.append((eigen_pair[0], eigen_pair[1]))
    eigen_basis = [[columns[j][i] for j in range(4)] for i in range(4)]
    basis_inverse = invert_table(eigen_basis)
    return (tableau, inverse, eigen_basis, basis_inverse, pairs)


def constants():
    tableau, inverse, eigen_basis, basis_inverse, pairs = radau_tables()
    shift_table = table_product(basis_inverse, inverse)
    shift_rows = [[v / step_size for v in row_values] for row_values in shift_table]
    pairs = [(p[0] / step_size, p[1] / step_size) for p in pairs]
    return eigen_basis, basis_inverse, shift_rows, pairs


def lane_ids(rows):
    return lax.broadcasted_iota(jnp.int32, (rows, LANES), 1)


def turn(cells, amount):
    return pltpu.roll(cells, amount % LANES, cells.ndim - 1)


def left_half():
    return lax.axis_index("section") == 0


def half_mask(rows):
    return (lane_ids(rows) < LANES // 2) == left_half()


ORDER = (0, 1, 4, 5, 6, 2, 3)
TALL = 16
PARTS = 4


def border_start():
    return jnp.where(left_half(), LANES - EDGE, 0)


def on_even_row():
    return lax.rem(lax.axis_index("sx"), 2) == 0


def place(slot, z):
    entry, row = divmod(8 * slot, TALL)
    last, ninth = divmod(56 + slot, TALL)
    return z * PARTS + entry, row, z * PARTS + last, ninth


def put(tile, cell, at, start, lanes):
    moved = pltpu.roll(cell, lax.rem(at + LANES - start, LANES), 1)
    return jnp.where((lanes >= at) & (lanes < at + EDGE), moved, tile)


def inner_start():
    return jnp.where(left_half(), LANES // 2, LANES // 2 - EDGE)


def pack_far(far_ref, load, fields, base, plane, nz):
    even = on_even_row()
    half = nz // 2
    pairs = (len(fields) + 1) // 2
    window, end = jnp.zeros((8, LANES), jnp.float32), jnp.zeros((1, LANES), jnp.float32)
    for part in range(2):
        z = part * half + plane
        rows, ninths = [], []
        for slot, f in enumerate(fields):
            cell = load(slot, z)
            nx = cell.shape[0]
            rows.append(jnp.where(even, cell[0:8], cell[nx - 8 : nx]))
            ninths.append(jnp.where(even, cell[8:9], cell[nx - 9 : nx - 8]))
            at = part * 64 + f * EDGE
            window = put(window, rows[-1], at, inner_start(), lane_ids(8))
            end = put(end, ninths[-1], at, inner_start(), lane_ids(1))
        for pair in range(pairs):
            first, second = 2 * pair, min(2 * pair + 1, len(fields) - 1)
            far_ref[pairs * z + pair] = jnp.where(half_mask(8), rows[first], turn(rows[second], LANES // 2))
            row = part * pairs + pair
            far_ref[base + plane, row : row + 1] = jnp.where(half_mask(1), ninths[first], turn(ninths[second], LANES // 2))
    far_ref[base + plane, 7:8] = end
    far_ref[base + half + plane] = window


def own_kernel(held_ref, same_ref, cross_ref, far_ref):
    nz, nx = held_ref.shape[1], held_ref.shape[2]
    load = lambda slot, z: held_ref[slot, z]
    for plane in range(nz // 2):
        pack_far(far_ref, load, ORDER[:5], 3 * nz, plane, nz)
    lanes = lane_ids(nx)
    incoming = border_start()
    outgoing = LANES - EDGE - incoming

    for plane in range(nz // 2):
        same = jnp.zeros((nx, LANES), jnp.float32)
        cross = same
        for part in range(2):
            z = part * (nz // 2) + plane
            for slot in range(5):
                cell = held_ref[slot, z]
                same = put(same, cell, part * 64 + ORDER[slot] * EDGE, incoming, lanes)
                if slot < 2:
                    cross = put(cross, cell, part * 64 + (2 + slot) * EDGE, outgoing, lanes)
        same_ref[plane] = same
        cross_ref[plane] = cross


def rows_kernel(held_ref, other_ref, same_ref, cross_ref, border_ref, near_ref, far_ref):
    nz, nx = other_ref.shape[1], other_ref.shape[2]
    even = on_even_row()
    for z in range(nz):
        for slot in range(7):
            cell = held_ref[slot, z] if slot < 5 else other_ref[slot - 5, z]
            entry, row, last, ninth = place(slot, z)
            near_ref[entry, row : row + 8] = jnp.where(even, cell[nx - 8 : nx], cell[0:8])
            near_ref[last, ninth : ninth + 1] = jnp.where(even, cell[nx - 9 : nx - 8], cell[8:9])
    load = lambda slot, z: other_ref[slot, z]
    for plane in range(nz // 2):
        pack_far(far_ref, load, ORDER[5:], nz, plane, nz)
        border = same_ref[plane] + cross_ref[plane]
        border_ref[plane] = border
        near_ref[nz * PARTS + plane] = border
        far_ref[nz + plane, 6:7] = jnp.where(even, border[8:9], border[nx - 9 : nx - 8])
        far_ref[2 * nz + plane] = jnp.where(even, border[0:8], border[nx - 8 : nx])


ROWS = 48
FIRST, LAST = 8, 40
OWN = slice(16, 32)
WORK = slice(FIRST, LAST)
NARROW = slice(12, 36)
BEFORE = slice(FIRST - 1, LAST - 1)
AFTER = slice(FIRST + 1, LAST + 1)


def each_plane(count, unroll, work):
    def group(i, carry):
        for u in range(unroll):
            work(i * unroll + u)
        return carry

    lax.fori_loop(0, count // unroll, group, 0)


def main_kernel(consts, held_ref, other_ref, border_ref, own_far_ref, far_ref, near_ref, part_ref, sums_ref,
                val, kap, frozen, prv, rea, dif, fx, fy, fz, alpha, beta, vec, ya, yb, table):
    eigen_basis, basis_inverse, shift_rows, pairs = consts
    nz, nx = held_ref.shape[1], held_ref.shape[2]
    section = lax.axis_index("section")
    zero_plane = jnp.zeros((ROWS, LANES), jnp.float32)
    zero_rows = jnp.zeros((FIRST, LANES), jnp.float32)
    start = border_start()
    even = on_even_row()
    lanes = lane_ids(ROWS)
    edge = (lanes >= start) & (lanes < start + EDGE)
    tile = lambda t: jnp.broadcast_to(t, (8, LANES))

    for at in (0, nz + 1):
        frozen[at] = zero_plane
        for f in range(4):
            for ref in (val, kap, ya, yb):
                ref[f, at] = zero_plane

    inner = inner_start()

    def unpack(cells, window, second, at):
        count = cells.shape[0]
        ids = lane_ids(count)
        cells = turn(cells, LANES // 2) if second else cells
        window = pltpu.roll(window, lax.rem(inner + LANES - at, LANES), 1)
        return jnp.where(half_mask(count), cells, jnp.where((ids >= inner) & (ids < inner + EDGE), window, 0.0))

    def assemble(plane):
        near_side = near_ref[nz * PARTS + plane]
        far_side, far_end = far_ref[2 * nz + plane], far_ref[nz + plane, 6:7]
        sides = jnp.concatenate(
            [
                tile(jnp.where(even, far_end, near_side[nx - 9 : nx - 8])), jnp.where(even, far_side, near_side[nx - 8 : nx]),
                border_ref[plane],
                jnp.where(even, near_side[0:8], far_side), tile(jnp.where(even, near_side[8:9], far_end)),
            ],
            0,
        )
        for part in range(2):
            z = part * (nz // 2) + plane

            def column(f):
                slot = ORDER.index(f)
                mid = held_ref[slot, z] if slot < 5 else other_ref[slot - 5, z]
                at = part * 64 + f * EDGE
                entry, row, last, ninth = place(slot, z)
                near, near_end = near_ref[entry, row : row + 8], near_ref[last, ninth : ninth + 1]
                if slot < 5:
                    ref, pairs, base, (pair, second) = own_far_ref, 3, 3 * nz, divmod(slot, 2)
                else:
                    ref, pairs, base, pair, second = far_ref, 1, nz, 0, slot - 5
                end = part * pairs + pair
                far = unpack(ref[pairs * z + pair], ref[base + nz // 2 + plane], second, at)
                far_end = unpack(ref[base + plane, end : end + 1], ref[base + plane, 7:8], second, at)
                low, high = jnp.where(even, far, near), jnp.where(even, near, far)
                low_end, high_end = jnp.where(even, far_end, near_end), jnp.where(even, near_end, far_end)
                cells = jnp.concatenate([tile(low_end), low, mid, high, tile(high_end)], 0)
                return jnp.where(edge, pltpu.roll(sides, lax.rem(start + LANES - at, LANES), 1), cells)

            diff, prev, react = column(5), column(4), column(6)
            frozen[z + 1] = diff * (0.5 + 0.25 * jnp.tanh(prev))
            prv[z] = prev[WORK]
            rea[z] = react[WORK]
            dif[z] = diff[WORK]
            for f in range(4):
                value = column(f)
                val[f, z + 1] = value
                kap[f, z + 1] = diff * (0.5 + 0.25 * jnp.tanh(value))
                for ref in (ya, yb):
                    ref[f, z + 1, 0:FIRST] = zero_rows
                    ref[f, z + 1, LAST:ROWS] = zero_rows

    each_plane(nz // 2, 1, assemble)

    def pick(matrix, m, j):
        return jnp.where(section == 0, jnp.float32(matrix[m][j]), jnp.float32(matrix[m][(j + 2) % 4]))

    q_rows = [[pick(basis_inverse, m, j) for j in range(4)] for m in range(4)]
    c_rows = [[pick(shift_rows, m, j) for j in range(4)] for m in range(4)]

    def prepare(z):
        mid = frozen[z + 1, WORK]
        faces = [
            mid + frozen[z + 1, BEFORE], mid + frozen[z + 1, AFTER], mid + turn(mid, 1), mid + turn(mid, -1),
            mid + frozen[z, WORK], mid + frozen[z + 2, WORK],
        ]
        for at, ref in enumerate((fx, fy, fz)):
            ref[0, z] = faces[2 * at]
            ref[1, z] = faces[2 * at + 1]
        prev, react = prv[z], rea[z]
        base = ((faces[0] + faces[1]) + (faces[2] + faces[3])) + (faces[4] + faces[5]) - react * (1.0 - 3.0 * prev * prev)
        inside = jnp.where(dif[z] > 0.0, 1.0, 0.0)
        scaled = []
        for b in range(2):
            real, imag = pairs[b]
            diag = base + real
            scale = inside / (diag * diag + imag * imag)
            scaled.append((diag * scale, imag * scale))
            alpha[b, z], beta[b, z] = scaled[b]
        rhs = [None] * 4
        for j in range(4):
            v = val[j, z + 1, WORK]
            k = kap[j, z + 1, WORK]
            flux = react * v * (1.0 - v * v)
            flux = flux + (k + kap[j, z + 1, BEFORE]) * (val[j, z + 1, BEFORE] - v)
            flux = flux + (k + kap[j, z + 1, AFTER]) * (val[j, z + 1, AFTER] - v)
            flux = flux + (k + turn(k, 1)) * (turn(v, 1) - v)
            flux = flux + (k + turn(k, -1)) * (turn(v, -1) - v)
            flux = flux + (k + kap[j, z, WORK]) * (val[j, z, WORK] - v)
            flux = flux + (k + kap[j, z + 2, WORK]) * (val[j, z + 2, WORK] - v)
            grown = v - prev
            for m in range(4):
                term = q_rows[m][j] * flux - c_rows[m][j] * grown
                rhs[m] = term if j == 0 else rhs[m] + term
        for m in range(4):
            vec[0, m, z] = rhs[m]
        for b in range(2):
            al, be = scaled[b]
            ya[2 * b, z + 1, WORK] = al * rhs[2 * b] - be * rhs[2 * b + 1]
            ya[2 * b + 1, z + 1, WORK] = be * rhs[2 * b] + al * rhs[2 * b + 1]

    each_plane(nz, PREPARE_UNROLL, prepare)

    def spread(ref, m, z, rows=WORK):
        lo, hi = rows.start, rows.stop
        cut = slice(lo - FIRST, hi - FIRST)
        mid = ref[m, z + 1, lo:hi]
        in_y = fy[0, z, cut] * turn(mid, 1) + fy[1, z, cut] * turn(mid, -1)
        in_x = fx[0, z, cut] * ref[m, z + 1, lo - 1 : hi - 1] + fx[1, z, cut] * ref[m, z + 1, lo + 1 : hi + 1]
        in_z = fz[0, z, cut] * ref[m, z, lo:hi] + fz[1, z, cut] * ref[m, z + 2, lo:hi]
        return (in_x + in_z) + in_y

    def window(done):
        reach = 2 * ITERS - done
        return OWN if reach == 0 else NARROW if reach <= 4 else WORK

    for j in range(ITERS):

        def odd(z, j=j):
            rows = window(2 * j + 1)
            cut = slice(rows.start - FIRST, rows.stop - FIRST)
            for b in range(2):
                t0 = spread(ya, 2 * b, z, rows)
                t1 = spread(ya, 2 * b + 1, z, rows)
                al, be = alpha[b, z, cut], beta[b, z, cut]
                for m, y in ((2 * b, al * t0 - be * t1), (2 * b + 1, be * t0 + al * t1)):
                    yb[m, z + 1, rows] = y
                    if rows == WORK:
                        sums_ref[j, m, z, 4:20] = ya[m, z + 1, OWN] + y[8:24]
                    else:
                        sums_ref[j, m, z] = ya[m, z + 1, rows] + y

        def even(z, j=j):
            last = j == ITERS - 1
            rows = window(2 * j + 2)
            cut = slice(rows.start - FIRST, rows.stop - FIRST)
            for b in range(2):
                new = []
                for m in (2 * b, 2 * b + 1):
                    v = spread(yb, m, z, rows)
                    if SHIFTS[j]:
                        v = v - SHIFTS[j] * vec[j, m, z, cut]
                    vec[j + 1, m, z, cut] = v
                    new.append(v)
                if not last:
                    al, be = alpha[b, z, cut], beta[b, z, cut]
                    ya[2 * b, z + 1, rows] = al * new[0] - be * new[1]
                    ya[2 * b + 1, z + 1, rows] = be * new[0] + al * new[1]

        each_plane(nz, STEP_UNROLL, odd)
        each_plane(nz, STEP_UNROLL, even)

    table[...] = jnp.zeros((LANES, LANES), jnp.float32)
    mine = half_mask(8)
    for b in range(2):

        def dots(i, carry):
            out = list(carry)
            for z, m in [(4 * i + u, m) for u in range(4) for m in (2 * b, 2 * b + 1)]:
                cells = [jnp.where(mine, vec[k, m, z, 8:16], turn(vec[k, m, z, 16:24], LANES // 2)) for k in range(SIZE)]
                for at, (k, j) in enumerate(PAIRS):
                    out[at] = out[at] + cells[k] * cells[j]
            return tuple(out)

        zero = jnp.zeros((8, LANES), jnp.float32)
        out = lax.fori_loop(0, nz // 4, dots, tuple(zero for _ in PAIRS))
        for at in range(len(PAIRS)):
            row = jnp.sum(out[at], axis=0, keepdims=True)
            table[b * len(PAIRS) + at : b * len(PAIRS) + at + 1] = row
    total = jnp.sum(table[...].T, axis=0, keepdims=True)
    part_ref[...] = jnp.broadcast_to(total, part_ref.shape)


def step_weights(gram):
    table = {}
    for at, (i, j) in enumerate(PAIRS):
        table[i, j] = table[j, i] = gram[at]
    coef = [jnp.ones_like(gram[0])]
    weight = []
    step = coef[0]
    for k in range(ITERS):
        moved = [SHIFTS[j] * coef[j] for j in range(k + 1)] + [jnp.zeros_like(step)]
        for j in range(k + 1):
            moved[j + 1] = moved[j + 1] + coef[j]
        coef = coef + [jnp.zeros_like(step)]
        image = [coef[j] - moved[j] for j in range(k + 2)]
        num, den, bound = 0.0, 0.0, 0.0
        for i in range(k + 2):
            row, size = 0.0, 0.0
            for j in range(k + 2):
                term = table[i, j] * image[j]
                row = row + term
                size = size + jnp.abs(term)
            num = num + row * coef[i]
            den = den + row * image[i]
            bound = bound + size * jnp.abs(image[i])
        step = jnp.where(den > bound * 6e-8, num / (jnp.maximum(den, 0.0) + tiny_value), step)
        weight = weight + [jnp.zeros_like(step)]
        for j in range(k + 1):
            weight[j] = weight[j] + step * coef[j]
        coef = [coef[j] - step * image[j] for j in range(k + 2)]
    return weight


def send_kernel(consts, total_ref, sums_ref, other_ref, send_ref, weight_ref):
    eigen_basis = consts[0]
    nz, nx = other_ref.shape[1], other_ref.shape[2]
    section = lax.axis_index("section")
    total = jnp.sum(total_ref[...], axis=0, keepdims=True)
    count = len(PAIRS)
    weights = []
    for b in range(2):
        gram = [jnp.broadcast_to(total[:, b * count + at : b * count + at + 1], (1, LANES)) for at in range(count)]
        weights.append(step_weights(gram))
    for b in range(2):
        for j in range(ITERS):
            weight_ref[b * ITERS + j : b * ITERS + j + 1] = weights[b][j]
    basis = [
        [jnp.where(section == 0, jnp.float32(eigen_basis[2 + r][m]), jnp.float32(eigen_basis[r][m])) for m in range(4)]
        for r in range(2)
    ]
    mine = half_mask(nx)

    def combine(z):
        outs = [other_ref[r, z] for r in range(2)]
        for m in range(4):
            field = weights[m // 2][0] * sums_ref[0, m, z, 4:20]
            for j in range(1, ITERS):
                field = field + weights[m // 2][j] * sums_ref[j, m, z, 4:20]
            outs = [outs[r] + basis[r][m] * field for r in range(2)]
        send_ref[z] = jnp.where(mine, outs[0], turn(outs[1], LANES // 2))

    each_plane(nz, 4, combine)


def mine_kernel(consts, weight_ref, sums_ref, own_ref, mine_ref):
    eigen_basis = consts[0]
    nz = own_ref.shape[1]
    section = lax.axis_index("section")
    weights = [[weight_ref[b * ITERS + j : b * ITERS + j + 1] for j in range(ITERS)] for b in range(2)]
    basis = [
        [jnp.where(section == 0, jnp.float32(eigen_basis[r][m]), jnp.float32(eigen_basis[2 + r][m])) for m in range(4)]
        for r in range(2)
    ]

    def combine(z):
        outs = [own_ref[r, z] for r in range(2)]
        for m in range(4):
            field = weights[m // 2][0] * sums_ref[0, m, z, 4:20]
            for j in range(1, ITERS):
                field = field + weights[m // 2][j] * sums_ref[j, m, z, 4:20]
            outs = [outs[r] + basis[r][m] * field for r in range(2)]
        mine_ref[0, z] = outs[0]
        mine_ref[1, z] = outs[1]

    each_plane(nz, 4, combine)


def join_kernel(mine_ref, other_ref, out_ref):
    nz, nx = mine_ref.shape[1], mine_ref.shape[2]
    mine = half_mask(nx)
    for z in range(nz):
        other = other_ref[z]
        out_ref[0, z] = jnp.where(mine, mine_ref[0, z], other)
        out_ref[1, z] = jnp.where(mine, mine_ref[1, z], turn(other, LANES // 2))


def call(kernel, outs, scratch=(), flops=1_000_000, name=None, limit=12):
    many = isinstance(outs, list)
    shapes = [jax.ShapeDtypeStruct(o, jnp.float32) for o in (outs if many else [outs])]

    def run(*args):
        moved = 4 * sum(int(a.size) for a in args) + 4 * sum(int(functools.reduce(lambda p, q: p * q, s.shape, 1)) for s in shapes)
        return pl.pallas_call(
            kernel,
            out_shape=shapes if many else shapes[0],
            in_specs=[pl.BlockSpec(memory_space=pltpu.VMEM)] * len(args),
            out_specs=[pl.BlockSpec(memory_space=pltpu.VMEM)] * len(shapes) if many else pl.BlockSpec(memory_space=pltpu.VMEM),
            scratch_shapes=[pltpu.VMEM(s, jnp.float32) for s in scratch],
            compiler_params=pltpu.CompilerParams(vmem_limit_bytes=int(limit * 1024 * 1024)),
            cost_estimate=pl.CostEstimate(flops=flops, bytes_accessed=moved, transcendentals=0),
            name=name,
        )(*args)

    return run


def swaps(count, start):
    return [pair for i in range(start, count - 1, 2) for pair in ((i, i + 1), (i + 1, i))]


def beside(count, cross):
    pairs = []
    for s in range(2):
        to = 1 - s if cross else s
        step = 1 if to == 0 else -1
        for i in range(count):
            if 0 <= i + step < count:
                pairs.append((s * count + i, to * count + i + step))
    return pairs


def body(previous, sections, diffusivity, reaction):
    consts = constants()
    nz, nx, ny = previous.shape
    columns, rows = lax.axis_size("sy"), lax.axis_size("sx")
    axes = ("section", "sx", "sy")
    partner = [(0, 1), (1, 0)]
    other = lax.ppermute(sections, "section", partner)
    edge, whole, early, late = (nz // 2, nx, ny), (nz * PARTS + nz // 2, TALL, ny), (4 * nz, 8, ny), (2 * nz + nz // 2, 8, ny)
    held = jnp.concatenate([sections, previous[None], diffusivity[None], reaction[None]], 0)
    same, cross, own_far = call(own_kernel, [edge, edge, early], name="own")(held)
    own_far = lax.ppermute(own_far, "sx", swaps(rows, 1))
    same = lax.ppermute(same, ("section", "sy"), beside(columns, False))
    cross = lax.ppermute(cross, ("section", "sy"), beside(columns, True))
    cross, own_far = lax.optimization_barrier((cross, own_far))
    border, near, far = call(rows_kernel, [edge, whole, late], name="rows")(held, other, same, cross)
    far = lax.ppermute(far, "sx", swaps(rows, 1))
    near = lax.ppermute(near, "sx", swaps(rows, 0))
    peers = 2 * columns * rows
    padded, work = (nz + 2, ROWS, ny), (nz, LAST - FIRST, ny)
    scratch = [
        (4,) + padded, (4,) + padded, padded, work, work, work, (2,) + work, (2,) + work, (2,) + work, (2,) + work, (2,) + work,
        (SIZE, 4) + work, (4,) + padded, (4,) + padded, (LANES, LANES),
    ]
    part, sums = call(
        functools.partial(main_kernel, consts), [(peers, LANES), (ITERS, 4, nz, nx + 8, ny)], scratch, 50_000_000, "main", 26
    )(held, other, border, own_far, far, near)
    total = lax.all_to_all(part.reshape(peers, 1, LANES), axes, 0, 0).reshape(peers, LANES)
    half, weight = call(functools.partial(send_kernel, consts), [previous.shape, (2 * ITERS, LANES)], name="send")(total, sums, other)
    got = lax.ppermute(half, "section", partner)
    mine = call(functools.partial(mine_kernel, consts), sections.shape, name="mine")(weight, sums, held)
    return call(join_kernel, sections.shape, name="join")(mine, got)


def solution(mesh):
    in_specs = (
        P(None, "sx", "sy"),
        P("section", None, "sx", "sy"),
        P(None, "sx", "sy"),
        P(None, "sx", "sy"),
    )
    out_specs = P("section", None, "sx", "sy")
    return jax.shard_map(body, mesh=mesh, in_specs=in_specs, out_specs=out_specs, check_vma=False)
```

```python
import functools

import jax
import jax.numpy as jnp
from jax import lax
from jax.experimental import pallas as pl
from jax.experimental.pallas import tpu as pltpu
from jax.sharding import PartitionSpec as P

ITERS = 4
SHIFTS = (0.0, 0.9, 0.45, 0.7)
EDGE = 9
LANES = 128
SIZE = ITERS + 1
PAIRS = [(i, j) for i in range(SIZE) for j in range(i, SIZE)]
PREPARE_UNROLL = 2
STEP_UNROLL = 8


step_size = 1.0
tiny_value = 1e-06


def invert_table(matrix):
    order_n = len(matrix)
    augmented = [
        list(matrix[r]) + [1.0 if c == r else 0.0 for c in range(order_n)] for r in range(order_n)
    ]
    for col in range(order_n):
        pivot_row = max(range(col, order_n), key=lambda r: abs(augmented[r][col]))
        augmented[col], augmented[pivot_row] = (augmented[pivot_row], augmented[col])
        leading = augmented[col][col]
        augmented[col] = [v / leading for v in augmented[col]]
        for r in range(order_n):
            if r != col:
                factor = augmented[r][col]
                augmented[r] = [a - factor * b for a, b in zip(augmented[r], augmented[col])]
    return [row_values[order_n:] for row_values in augmented]


def table_product(left, right):
    return [
        [sum((left[i][k] * right[k][j] for k in range(len(right)))) for j in range(len(right[0]))]
        for i in range(len(left))
    ]


def pair_add(first, second):
    return (first[0] + second[0], first[1] + second[1])


def pair_sub(first, second):
    return (first[0] - second[0], first[1] - second[1])


def pair_mul(first, second):
    return (
        first[0] * second[0] - first[1] * second[1],
        first[0] * second[1] + first[1] * second[0],
    )


def pair_div(first, second):
    scale_sq = second[0] * second[0] + second[1] * second[1]
    return (
        (first[0] * second[0] + first[1] * second[1]) / scale_sq,
        (first[1] * second[0] - first[0] * second[1]) / scale_sq,
    )


def quartic_value(point):
    return (((210.0 * point - 480.0) * point + 360.0) * point - 96.0) * point + 6.0


def bisect_root(lower, upper):
    for count in range(200):
        middle = 0.5 * (lower + upper)
        if (quartic_value(lower) < 0.0) == (quartic_value(middle) < 0.0):
            lower = middle
        else:
            upper = middle
    return 0.5 * (lower + upper)


def radau_tables():
    abscissae = []
    grid_steps = 4000
    for m in range(grid_steps):
        lower = 0.999 * m / grid_steps
        upper = 0.999 * (m + 1) / grid_steps
        if (quartic_value(lower) < 0.0) != (quartic_value(upper) < 0.0):
            abscissae.append(bisect_root(lower, upper))
    abscissae.append(1.0)
    vander = [[abscissae[j] ** k for k in range(4)] for j in range(4)]
    moments = [[abscissae[i] ** (k + 1) / (k + 1) for k in range(4)] for i in range(4)]
    tableau = table_product(moments, invert_table(vander))
    inverse = invert_table(tableau)
    running = [list(row_values) for row_values in inverse]
    coeffs = []
    for k in range(1, 5):
        trace_value = sum((running[i][i] for i in range(4)))
        coeffs.append(-trace_value / k)
        shifted_table = [
            [running[i][j] + (coeffs[-1] if i == j else 0.0) for j in range(4)] for i in range(4)
        ]
        running = table_product(inverse, shifted_table)
    start_point = (0.4, 0.9)
    estimates = [(1.0, 0.0)]
    for k in range(3):
        estimates.append(pair_mul(estimates[-1], start_point))
    for count in range(500):
        for i in range(4):
            value = (1.0, 0.0)
            for coef_value in coeffs:
                value = pair_add(pair_mul(value, estimates[i]), (coef_value, 0.0))
            denom = (1.0, 0.0)
            for j in range(4):
                if j != i:
                    denom = pair_mul(denom, pair_sub(estimates[i], estimates[j]))
            estimates[i] = pair_sub(estimates[i], pair_div(value, denom))
    chosen = [m for m in range(4) if estimates[m][1] > 0.0]
    ranking = sorted(chosen, key=lambda m: -estimates[m][1])
    columns = []
    pairs = []
    for m in ranking:
        eigen_pair = estimates[m]
        system = [
            [
                (
                    inverse[i][j] - (eigen_pair[0] if i == j else 0.0),
                    -(eigen_pair[1] if i == j else 0.0),
                )
                for j in range(4)
            ]
            for i in range(3)
        ]
        rows_left = [
            [system[i][j] for j in range(3)] + [(-system[i][3][0], -system[i][3][1])]
            for i in range(3)
        ]
        for col in range(3):
            pivot_row = max(
                range(col, 3), key=lambda r: rows_left[r][col][0] ** 2 + rows_left[r][col][1] ** 2
            )
            rows_left[col], rows_left[pivot_row] = (rows_left[pivot_row], rows_left[col])
            leading = rows_left[col][col]
            rows_left[col] = [pair_div(v, leading) for v in rows_left[col]]
            for r in range(3):
                if r != col:
                    factor = rows_left[r][col]
                    rows_left[r] = [
                        pair_sub(a, pair_mul(factor, b))
                        for a, b in zip(rows_left[r], rows_left[col])
                    ]
        vector = [rows_left[i][3] for i in range(3)] + [(1.0, 0.0)]
        columns.append([v[0] for v in vector])
        columns.append([v[1] for v in vector])
        pairs.append((eigen_pair[0], eigen_pair[1]))
    eigen_basis = [[columns[j][i] for j in range(4)] for i in range(4)]
    basis_inverse = invert_table(eigen_basis)
    return (tableau, inverse, eigen_basis, basis_inverse, pairs)


def constants():
    tableau, inverse, eigen_basis, basis_inverse, pairs = radau_tables()
    shift_table = table_product(basis_inverse, inverse)
    shift_rows = [[v / step_size for v in row_values] for row_values in shift_table]
    pairs = [(p[0] / step_size, p[1] / step_size) for p in pairs]
    return eigen_basis, basis_inverse, shift_rows, pairs


def lane_ids(rows):
    return lax.broadcasted_iota(jnp.int32, (rows, LANES), 1)


def turn(cells, amount):
    return pltpu.roll(cells, amount % LANES, cells.ndim - 1)


def left_half():
    return lax.axis_index("section") == 0


def half_mask(rows):
    return (lane_ids(rows) < LANES // 2) == left_half()


ORDER = (0, 1, 4, 5, 6, 2, 3)
TALL = 16
PARTS = 4


def border_start():
    return jnp.where(left_half(), LANES - EDGE, 0)


def on_even_row():
    return lax.rem(lax.axis_index("sx"), 2) == 0


def place(slot, z):
    entry, row = divmod(8 * slot, TALL)
    last, ninth = divmod(56 + slot, TALL)
    return z * PARTS + entry, row, z * PARTS + last, ninth


def put(tile, cell, at, start, lanes):
    moved = pltpu.roll(cell, lax.rem(at + LANES - start, LANES), 1)
    return jnp.where((lanes >= at) & (lanes < at + EDGE), moved, tile)


def inner_start():
    return jnp.where(left_half(), LANES // 2, LANES // 2 - EDGE)


def unpack(cells, window, second, at):
    count = cells.shape[0]
    inner = inner_start()
    ids = lane_ids(count)
    cells = turn(cells, LANES // 2) if second else cells
    window = pltpu.roll(window, lax.rem(inner + LANES - at, LANES), 1)
    return jnp.where(half_mask(count), cells, jnp.where((ids >= inner) & (ids < inner + EDGE), window, 0.0))


def pack_far(far_ref, load, fields, base, plane, nz):
    even = on_even_row()
    half = nz // 2
    pairs = (len(fields) + 1) // 2
    window, end = jnp.zeros((8, LANES), jnp.float32), jnp.zeros((1, LANES), jnp.float32)
    for part in range(2):
        z = part * half + plane
        rows, ninths = [], []
        for slot, f in enumerate(fields):
            cell = load(slot, z)
            nx = cell.shape[0]
            rows.append(jnp.where(even, cell[0:8], cell[nx - 8 : nx]))
            ninths.append(jnp.where(even, cell[8:9], cell[nx - 9 : nx - 8]))
            at = part * 64 + f * EDGE
            window = put(window, rows[-1], at, inner_start(), lane_ids(8))
            end = put(end, ninths[-1], at, inner_start(), lane_ids(1))
        for pair in range(pairs):
            first, second = 2 * pair, min(2 * pair + 1, len(fields) - 1)
            far_ref[pairs * z + pair] = jnp.where(half_mask(8), rows[first], turn(rows[second], LANES // 2))
            row = part * pairs + pair
            far_ref[base + plane, row : row + 1] = jnp.where(half_mask(1), ninths[first], turn(ninths[second], LANES // 2))
    far_ref[base + plane, 7:8] = end
    far_ref[base + half + plane] = window


def own_kernel(held_ref, same_ref, cross_ref, far_ref, swap_ref):
    nz, nx = held_ref.shape[1], held_ref.shape[2]
    load = lambda slot, z: held_ref[slot, z]
    for plane in range(nz // 2):
        pack_far(far_ref, load, ORDER[:5], 3 * nz, plane, nz)
    quarter = nz // 4
    theirs = LANES - EDGE - inner_start()
    for plane in range(quarter):
        window = jnp.zeros((nx, LANES), jnp.float32)
        for part in range(4):
            z = part * quarter + plane
            swap_ref[z] = jnp.where(half_mask(nx), turn(held_ref[1, z], LANES // 2), held_ref[0, z])
            for slot in range(2):
                window = put(window, held_ref[slot, z], part * 32 + slot * EDGE, theirs, lane_ids(nx))
        swap_ref[nz + plane] = window
    lanes = lane_ids(nx)
    incoming = border_start()
    outgoing = LANES - EDGE - incoming

    for plane in range(nz // 2):
        same = jnp.zeros((nx, LANES), jnp.float32)
        cross = same
        for part in range(2):
            z = part * (nz // 2) + plane
            for slot in range(5):
                cell = held_ref[slot, z]
                same = put(same, cell, part * 64 + ORDER[slot] * EDGE, incoming, lanes)
                if slot < 2:
                    cross = put(cross, cell, part * 64 + (2 + slot) * EDGE, outgoing, lanes)
        same_ref[plane] = same
        cross_ref[plane] = cross


def rows_kernel(held_ref, got_ref, same_ref, cross_ref, other_ref, border_ref, near_ref, far_ref):
    nz, nx = other_ref.shape[1], other_ref.shape[2]
    even = on_even_row()
    quarter = nz // 4
    for z in range(nz):
        part, plane = divmod(z, quarter)
        fresh = [
            unpack(got_ref[z], got_ref[nz + plane], slot == 1, part * 32 + slot * EDGE) for slot in range(2)
        ]
        for slot in range(7):
            cell = held_ref[slot, z] if slot < 5 else fresh[slot - 5]
            entry, row, last, ninth = place(slot, z)
            near_ref[entry, row : row + 8] = jnp.where(even, cell[nx - 8 : nx], cell[0:8])
            near_ref[last, ninth : ninth + 1] = jnp.where(even, cell[nx - 9 : nx - 8], cell[8:9])
        other_ref[0, z] = fresh[0]
        other_ref[1, z] = fresh[1]
    load = lambda slot, z: other_ref[slot, z]
    for plane in range(nz // 2):
        pack_far(far_ref, load, ORDER[5:], nz, plane, nz)
        border = same_ref[plane] + cross_ref[plane]
        border_ref[plane] = border
        near_ref[nz * PARTS + plane] = border
        far_ref[nz + plane, 6:7] = jnp.where(even, border[8:9], border[nx - 9 : nx - 8])
        far_ref[2 * nz + plane] = jnp.where(even, border[0:8], border[nx - 8 : nx])


ROWS = 48
FIRST, LAST = 8, 40
OWN = slice(16, 32)
WORK = slice(FIRST, LAST)
NARROW = slice(12, 36)
BEFORE = slice(FIRST - 1, LAST - 1)
AFTER = slice(FIRST + 1, LAST + 1)


def each_plane(count, unroll, work):
    def group(i, carry):
        for u in range(unroll):
            work(i * unroll + u)
        return carry

    lax.fori_loop(0, count // unroll, group, 0)


def main_kernel(consts, held_ref, other_ref, border_ref, own_far_ref, far_ref, near_ref, part_ref, sums_ref,
                val, kap, frozen, prv, rea, dif, fx, fy, fz, alpha, beta, vec, ya, yb, table):
    eigen_basis, basis_inverse, shift_rows, pairs = consts
    nz, nx = held_ref.shape[1], held_ref.shape[2]
    section = lax.axis_index("section")
    zero_plane = jnp.zeros((ROWS, LANES), jnp.float32)
    zero_rows = jnp.zeros((FIRST, LANES), jnp.float32)
    start = border_start()
    even = on_even_row()
    lanes = lane_ids(ROWS)
    edge = (lanes >= start) & (lanes < start + EDGE)
    tile = lambda t: jnp.broadcast_to(t, (8, LANES))

    for at in (0, nz + 1):
        frozen[at] = zero_plane
        for f in range(4):
            for ref in (val, kap, ya, yb):
                ref[f, at] = zero_plane

    def assemble(plane):
        near_side = near_ref[nz * PARTS + plane]
        far_side, far_end = far_ref[2 * nz + plane], far_ref[nz + plane, 6:7]
        sides = jnp.concatenate(
            [
                tile(jnp.where(even, far_end, near_side[nx - 9 : nx - 8])), jnp.where(even, far_side, near_side[nx - 8 : nx]),
                border_ref[plane],
                jnp.where(even, near_side[0:8], far_side), tile(jnp.where(even, near_side[8:9], far_end)),
            ],
            0,
        )
        for part in range(2):
            z = part * (nz // 2) + plane

            def column(f):
                slot = ORDER.index(f)
                mid = held_ref[slot, z] if slot < 5 else other_ref[slot - 5, z]
                at = part * 64 + f * EDGE
                entry, row, last, ninth = place(slot, z)
                near, near_end = near_ref[entry, row : row + 8], near_ref[last, ninth : ninth + 1]
                if slot < 5:
                    ref, pairs, base, (pair, second) = own_far_ref, 3, 3 * nz, divmod(slot, 2)
                else:
                    ref, pairs, base, pair, second = far_ref, 1, nz, 0, slot - 5
                end = part * pairs + pair
                far = unpack(ref[pairs * z + pair], ref[base + nz // 2 + plane], second, at)
                far_end = unpack(ref[base + plane, end : end + 1], ref[base + plane, 7:8], second, at)
                low, high = jnp.where(even, far, near), jnp.where(even, near, far)
                low_end, high_end = jnp.where(even, far_end, near_end), jnp.where(even, near_end, far_end)
                cells = jnp.concatenate([tile(low_end), low, mid, high, tile(high_end)], 0)
                return jnp.where(edge, pltpu.roll(sides, lax.rem(start + LANES - at, LANES), 1), cells)

            diff, prev, react = column(5), column(4), column(6)
            frozen[z + 1] = diff * (0.5 + 0.25 * jnp.tanh(prev))
            prv[z] = prev[WORK]
            rea[z] = react[WORK]
            dif[z] = diff[WORK]
            for f in range(4):
                value = column(f)
                val[f, z + 1] = value
                kap[f, z + 1] = diff * (0.5 + 0.25 * jnp.tanh(value))
                for ref in (ya, yb):
                    ref[f, z + 1, 0:FIRST] = zero_rows
                    ref[f, z + 1, LAST:ROWS] = zero_rows

    each_plane(nz // 2, 1, assemble)

    def pick(matrix, m, j):
        return jnp.where(section == 0, jnp.float32(matrix[m][j]), jnp.float32(matrix[m][(j + 2) % 4]))

    q_rows = [[pick(basis_inverse, m, j) for j in range(4)] for m in range(4)]
    c_rows = [[pick(shift_rows, m, j) for j in range(4)] for m in range(4)]

    def prepare(z):
        mid = frozen[z + 1, WORK]
        faces = [
            mid + frozen[z + 1, BEFORE], mid + frozen[z + 1, AFTER], mid + turn(mid, 1), mid + turn(mid, -1),
            mid + frozen[z, WORK], mid + frozen[z + 2, WORK],
        ]
        for at, ref in enumerate((fx, fy, fz)):
            ref[0, z] = faces[2 * at]
            ref[1, z] = faces[2 * at + 1]
        prev, react = prv[z], rea[z]
        base = ((faces[0] + faces[1]) + (faces[2] + faces[3])) + (faces[4] + faces[5]) - react * (1.0 - 3.0 * prev * prev)
        inside = jnp.where(dif[z] > 0.0, 1.0, 0.0)
        scaled = []
        for b in range(2):
            real, imag = pairs[b]
            diag = base + real
            scale = inside / (diag * diag + imag * imag)
            scaled.append((diag * scale, imag * scale))
            alpha[b, z], beta[b, z] = scaled[b]
        rhs = [None] * 4
        for j in range(4):
            v = val[j, z + 1, WORK]
            k = kap[j, z + 1, WORK]
            flux = react * v * (1.0 - v * v)
            flux = flux + (k + kap[j, z + 1, BEFORE]) * (val[j, z + 1, BEFORE] - v)
            flux = flux + (k + kap[j, z + 1, AFTER]) * (val[j, z + 1, AFTER] - v)
            flux = flux + (k + turn(k, 1)) * (turn(v, 1) - v)
            flux = flux + (k + turn(k, -1)) * (turn(v, -1) - v)
            flux = flux + (k + kap[j, z, WORK]) * (val[j, z, WORK] - v)
            flux = flux + (k + kap[j, z + 2, WORK]) * (val[j, z + 2, WORK] - v)
            grown = v - prev
            for m in range(4):
                term = q_rows[m][j] * flux - c_rows[m][j] * grown
                rhs[m] = term if j == 0 else rhs[m] + term
        for m in range(4):
            vec[0, m, z] = rhs[m]
        for b in range(2):
            al, be = scaled[b]
            ya[2 * b, z + 1, WORK] = al * rhs[2 * b] - be * rhs[2 * b + 1]
            ya[2 * b + 1, z + 1, WORK] = be * rhs[2 * b] + al * rhs[2 * b + 1]

    each_plane(nz, PREPARE_UNROLL, prepare)

    def spread(ref, m, z, rows=WORK):
        lo, hi = rows.start, rows.stop
        cut = slice(lo - FIRST, hi - FIRST)
        mid = ref[m, z + 1, lo:hi]
        in_y = fy[0, z, cut] * turn(mid, 1) + fy[1, z, cut] * turn(mid, -1)
        in_x = fx[0, z, cut] * ref[m, z + 1, lo - 1 : hi - 1] + fx[1, z, cut] * ref[m, z + 1, lo + 1 : hi + 1]
        in_z = fz[0, z, cut] * ref[m, z, lo:hi] + fz[1, z, cut] * ref[m, z + 2, lo:hi]
        return (in_x + in_z) + in_y

    def window(done):
        reach = 2 * ITERS - done
        return OWN if reach == 0 else NARROW if reach <= 4 else WORK

    for j in range(ITERS):

        def odd(z, j=j):
            rows = window(2 * j + 1)
            cut = slice(rows.start - FIRST, rows.stop - FIRST)
            for b in range(2):
                t0 = spread(ya, 2 * b, z, rows)
                t1 = spread(ya, 2 * b + 1, z, rows)
                al, be = alpha[b, z, cut], beta[b, z, cut]
                for m, y in ((2 * b, al * t0 - be * t1), (2 * b + 1, be * t0 + al * t1)):
                    yb[m, z + 1, rows] = y
                    if rows == WORK:
                        sums_ref[j, m, z, 4:20] = ya[m, z + 1, OWN] + y[8:24]
                    else:
                        sums_ref[j, m, z] = ya[m, z + 1, rows] + y

        def even(z, j=j):
            last = j == ITERS - 1
            rows = window(2 * j + 2)
            cut = slice(rows.start - FIRST, rows.stop - FIRST)
            for b in range(2):
                new = []
                for m in (2 * b, 2 * b + 1):
                    v = spread(yb, m, z, rows)
                    if SHIFTS[j]:
                        v = v - SHIFTS[j] * vec[j, m, z, cut]
                    vec[j + 1, m, z, cut] = v
                    new.append(v)
                if not last:
                    al, be = alpha[b, z, cut], beta[b, z, cut]
                    ya[2 * b, z + 1, rows] = al * new[0] - be * new[1]
                    ya[2 * b + 1, z + 1, rows] = be * new[0] + al * new[1]

        each_plane(nz, STEP_UNROLL, odd)
        each_plane(nz, STEP_UNROLL, even)

    table[...] = jnp.zeros((LANES, LANES), jnp.float32)
    mine = half_mask(8)
    for b in range(2):

        def dots(i, carry):
            out = list(carry)
            for z, m in [(4 * i + u, m) for u in range(4) for m in (2 * b, 2 * b + 1)]:
                cells = [jnp.where(mine, vec[k, m, z, 8:16], turn(vec[k, m, z, 16:24], LANES // 2)) for k in range(SIZE)]
                for at, (k, j) in enumerate(PAIRS):
                    out[at] = out[at] + cells[k] * cells[j]
            return tuple(out)

        zero = jnp.zeros((8, LANES), jnp.float32)
        out = lax.fori_loop(0, nz // 4, dots, tuple(zero for _ in PAIRS))
        for at in range(len(PAIRS)):
            row = jnp.sum(out[at], axis=0, keepdims=True)
            table[b * len(PAIRS) + at : b * len(PAIRS) + at + 1] = row
    total = jnp.sum(table[...].T, axis=0, keepdims=True)
    part_ref[...] = jnp.broadcast_to(total, part_ref.shape)


def step_weights(gram):
    table = {}
    for at, (i, j) in enumerate(PAIRS):
        table[i, j] = table[j, i] = gram[at]
    coef = [jnp.ones_like(gram[0])]
    weight = []
    step = coef[0]
    for k in range(ITERS):
        moved = [SHIFTS[j] * coef[j] for j in range(k + 1)] + [jnp.zeros_like(step)]
        for j in range(k + 1):
            moved[j + 1] = moved[j + 1] + coef[j]
        coef = coef + [jnp.zeros_like(step)]
        image = [coef[j] - moved[j] for j in range(k + 2)]
        num, den, bound = 0.0, 0.0, 0.0
        for i in range(k + 2):
            row, size = 0.0, 0.0
            for j in range(k + 2):
                term = table[i, j] * image[j]
                row = row + term
                size = size + jnp.abs(term)
            num = num + row * coef[i]
            den = den + row * image[i]
            bound = bound + size * jnp.abs(image[i])
        step = jnp.where(den > bound * 6e-8, num / (jnp.maximum(den, 0.0) + tiny_value), step)
        weight = weight + [jnp.zeros_like(step)]
        for j in range(k + 1):
            weight[j] = weight[j] + step * coef[j]
        coef = [coef[j] - step * image[j] for j in range(k + 2)]
    return weight


def send_kernel(consts, total_ref, sums_ref, other_ref, send_ref, weight_ref):
    eigen_basis = consts[0]
    nz, nx = other_ref.shape[1], other_ref.shape[2]
    section = lax.axis_index("section")
    total = jnp.sum(total_ref[...], axis=0, keepdims=True)
    count = len(PAIRS)
    weights = []
    for b in range(2):
        gram = [jnp.broadcast_to(total[:, b * count + at : b * count + at + 1], (1, LANES)) for at in range(count)]
        weights.append(step_weights(gram))
    for b in range(2):
        for j in range(ITERS):
            weight_ref[b * ITERS + j : b * ITERS + j + 1] = weights[b][j]
    basis = [
        [jnp.where(section == 0, jnp.float32(eigen_basis[2 + r][m]), jnp.float32(eigen_basis[r][m])) for m in range(4)]
        for r in range(2)
    ]
    mine = half_mask(nx)

    def combine(z):
        outs = [other_ref[r, z] for r in range(2)]
        for m in range(4):
            field = weights[m // 2][0] * sums_ref[0, m, z, 4:20]
            for j in range(1, ITERS):
                field = field + weights[m // 2][j] * sums_ref[j, m, z, 4:20]
            outs = [outs[r] + basis[r][m] * field for r in range(2)]
        send_ref[z] = jnp.where(mine, outs[0], turn(outs[1], LANES // 2))

    each_plane(nz, 4, combine)


def mine_kernel(consts, weight_ref, sums_ref, own_ref, mine_ref):
    eigen_basis = consts[0]
    nz = own_ref.shape[1]
    section = lax.axis_index("section")
    weights = [[weight_ref[b * ITERS + j : b * ITERS + j + 1] for j in range(ITERS)] for b in range(2)]
    basis = [
        [jnp.where(section == 0, jnp.float32(eigen_basis[r][m]), jnp.float32(eigen_basis[2 + r][m])) for m in range(4)]
        for r in range(2)
    ]

    def combine(z):
        outs = [own_ref[r, z] for r in range(2)]
        for m in range(4):
            field = weights[m // 2][0] * sums_ref[0, m, z, 4:20]
            for j in range(1, ITERS):
                field = field + weights[m // 2][j] * sums_ref[j, m, z, 4:20]
            outs = [outs[r] + basis[r][m] * field for r in range(2)]
        mine_ref[0, z] = outs[0]
        mine_ref[1, z] = outs[1]

    each_plane(nz, 4, combine)


def join_kernel(mine_ref, other_ref, out_ref):
    nz, nx = mine_ref.shape[1], mine_ref.shape[2]
    mine = half_mask(nx)
    for z in range(nz):
        other = other_ref[z]
        out_ref[0, z] = jnp.where(mine, mine_ref[0, z], other)
        out_ref[1, z] = jnp.where(mine, mine_ref[1, z], turn(other, LANES // 2))


def call(kernel, outs, scratch=(), flops=1_000_000, name=None, limit=12):
    many = isinstance(outs, list)
    shapes = [jax.ShapeDtypeStruct(o, jnp.float32) for o in (outs if many else [outs])]

    def run(*args):
        moved = 4 * sum(int(a.size) for a in args) + 4 * sum(int(functools.reduce(lambda p, q: p * q, s.shape, 1)) for s in shapes)
        return pl.pallas_call(
            kernel,
            out_shape=shapes if many else shapes[0],
            in_specs=[pl.BlockSpec(memory_space=pltpu.VMEM)] * len(args),
            out_specs=[pl.BlockSpec(memory_space=pltpu.VMEM)] * len(shapes) if many else pl.BlockSpec(memory_space=pltpu.VMEM),
            scratch_shapes=[pltpu.VMEM(s, jnp.float32) for s in scratch],
            compiler_params=pltpu.CompilerParams(vmem_limit_bytes=int(limit * 1024 * 1024)),
            cost_estimate=pl.CostEstimate(flops=flops, bytes_accessed=moved, transcendentals=0),
            name=name,
        )(*args)

    return run


def swaps(count, start):
    return [pair for i in range(start, count - 1, 2) for pair in ((i, i + 1), (i + 1, i))]


def beside(count, cross):
    pairs = []
    for s in range(2):
        to = 1 - s if cross else s
        step = 1 if to == 0 else -1
        for i in range(count):
            if 0 <= i + step < count:
                pairs.append((s * count + i, to * count + i + step))
    return pairs


def body(previous, sections, diffusivity, reaction):
    consts = constants()
    nz, nx, ny = previous.shape
    columns, rows = lax.axis_size("sy"), lax.axis_size("sx")
    axes = ("section", "sx", "sy")
    partner = [(0, 1), (1, 0)]
    edge, whole, early, late = (nz // 2, nx, ny), (nz * PARTS + nz // 2, TALL, ny), (4 * nz, 8, ny), (2 * nz + nz // 2, 8, ny)
    held = jnp.concatenate([sections, previous[None], diffusivity[None], reaction[None]], 0)
    same, cross, own_far, half = call(own_kernel, [edge, edge, early, (nz + nz // 4, nx, ny)], name="own")(held)
    half = lax.ppermute(half, "section", partner)
    own_far = lax.ppermute(own_far, "sx", swaps(rows, 1))
    same = lax.ppermute(same, ("section", "sy"), beside(columns, False))
    cross = lax.ppermute(cross, ("section", "sy"), beside(columns, True))
    cross, own_far = lax.optimization_barrier((cross, own_far))
    other, border, near, far = call(rows_kernel, [sections.shape, edge, whole, late], name="rows")(held, half, same, cross)
    far = lax.ppermute(far, "sx", swaps(rows, 1))
    near = lax.ppermute(near, "sx", swaps(rows, 0))
    peers = 2 * columns * rows
    padded, work = (nz + 2, ROWS, ny), (nz, LAST - FIRST, ny)
    scratch = [
        (4,) + padded, (4,) + padded, padded, work, work, work, (2,) + work, (2,) + work, (2,) + work, (2,) + work, (2,) + work,
        (SIZE, 4) + work, (4,) + padded, (4,) + padded, (LANES, LANES),
    ]
    part, sums = call(
        functools.partial(main_kernel, consts), [(peers, LANES), (ITERS, 4, nz, nx + 8, ny)], scratch, 50_000_000, "main", 26
    )(held, other, border, own_far, far, near)
    total = lax.all_to_all(part.reshape(peers, 1, LANES), axes, 0, 0).reshape(peers, LANES)
    half, weight = call(functools.partial(send_kernel, consts), [previous.shape, (2 * ITERS, LANES)], name="send")(total, sums, other)
    got = lax.ppermute(half, "section", partner)
    mine = call(functools.partial(mine_kernel, consts), sections.shape, name="mine")(weight, sums, held)
    return call(join_kernel, sections.shape, name="join")(mine, got)


def solution(mesh):
    in_specs = (
        P(None, "sx", "sy"),
        P("section", None, "sx", "sy"),
        P(None, "sx", "sy"),
        P(None, "sx", "sy"),
    )
    out_specs = P("section", None, "sx", "sy")
    return jax.shard_map(body, mesh=mesh, in_specs=in_specs, out_specs=out_specs, check_vma=False)
```

```python
import functools

import jax
import jax.numpy as jnp
from jax import lax
from jax.experimental import pallas as pl
from jax.experimental.pallas import tpu as pltpu
from jax.sharding import PartitionSpec as P

ITERS = 4
SHIFTS = (0.0, 0.9, 0.45, 0.7)
EDGE = 9
LANES = 128
SIZE = ITERS + 1
PAIRS = [(i, j) for i in range(SIZE) for j in range(i, SIZE)]
PREPARE_UNROLL = 4
STEP_UNROLL = 16


step_size = 1.0
tiny_value = 1e-06


def invert_table(matrix):
    order_n = len(matrix)
    augmented = [
        list(matrix[r]) + [1.0 if c == r else 0.0 for c in range(order_n)] for r in range(order_n)
    ]
    for col in range(order_n):
        pivot_row = max(range(col, order_n), key=lambda r: abs(augmented[r][col]))
        augmented[col], augmented[pivot_row] = (augmented[pivot_row], augmented[col])
        leading = augmented[col][col]
        augmented[col] = [v / leading for v in augmented[col]]
        for r in range(order_n):
            if r != col:
                factor = augmented[r][col]
                augmented[r] = [a - factor * b for a, b in zip(augmented[r], augmented[col])]
    return [row_values[order_n:] for row_values in augmented]


def table_product(left, right):
    return [
        [sum((left[i][k] * right[k][j] for k in range(len(right)))) for j in range(len(right[0]))]
        for i in range(len(left))
    ]


def pair_add(first, second):
    return (first[0] + second[0], first[1] + second[1])


def pair_sub(first, second):
    return (first[0] - second[0], first[1] - second[1])


def pair_mul(first, second):
    return (
        first[0] * second[0] - first[1] * second[1],
        first[0] * second[1] + first[1] * second[0],
    )


def pair_div(first, second):
    scale_sq = second[0] * second[0] + second[1] * second[1]
    return (
        (first[0] * second[0] + first[1] * second[1]) / scale_sq,
        (first[1] * second[0] - first[0] * second[1]) / scale_sq,
    )


def quartic_value(point):
    return (((210.0 * point - 480.0) * point + 360.0) * point - 96.0) * point + 6.0


def bisect_root(lower, upper):
    for count in range(200):
        middle = 0.5 * (lower + upper)
        if (quartic_value(lower) < 0.0) == (quartic_value(middle) < 0.0):
            lower = middle
        else:
            upper = middle
    return 0.5 * (lower + upper)


def radau_tables():
    abscissae = []
    grid_steps = 4000
    for m in range(grid_steps):
        lower = 0.999 * m / grid_steps
        upper = 0.999 * (m + 1) / grid_steps
        if (quartic_value(lower) < 0.0) != (quartic_value(upper) < 0.0):
            abscissae.append(bisect_root(lower, upper))
    abscissae.append(1.0)
    vander = [[abscissae[j] ** k for k in range(4)] for j in range(4)]
    moments = [[abscissae[i] ** (k + 1) / (k + 1) for k in range(4)] for i in range(4)]
    tableau = table_product(moments, invert_table(vander))
    inverse = invert_table(tableau)
    running = [list(row_values) for row_values in inverse]
    coeffs = []
    for k in range(1, 5):
        trace_value = sum((running[i][i] for i in range(4)))
        coeffs.append(-trace_value / k)
        shifted_table = [
            [running[i][j] + (coeffs[-1] if i == j else 0.0) for j in range(4)] for i in range(4)
        ]
        running = table_product(inverse, shifted_table)
    start_point = (0.4, 0.9)
    estimates = [(1.0, 0.0)]
    for k in range(3):
        estimates.append(pair_mul(estimates[-1], start_point))
    for count in range(500):
        for i in range(4):
            value = (1.0, 0.0)
            for coef_value in coeffs:
                value = pair_add(pair_mul(value, estimates[i]), (coef_value, 0.0))
            denom = (1.0, 0.0)
            for j in range(4):
                if j != i:
                    denom = pair_mul(denom, pair_sub(estimates[i], estimates[j]))
            estimates[i] = pair_sub(estimates[i], pair_div(value, denom))
    chosen = [m for m in range(4) if estimates[m][1] > 0.0]
    ranking = sorted(chosen, key=lambda m: -estimates[m][1])
    columns = []
    pairs = []
    for m in ranking:
        eigen_pair = estimates[m]
        system = [
            [
                (
                    inverse[i][j] - (eigen_pair[0] if i == j else 0.0),
                    -(eigen_pair[1] if i == j else 0.0),
                )
                for j in range(4)
            ]
            for i in range(3)
        ]
        rows_left = [
            [system[i][j] for j in range(3)] + [(-system[i][3][0], -system[i][3][1])]
            for i in range(3)
        ]
        for col in range(3):
            pivot_row = max(
                range(col, 3), key=lambda r: rows_left[r][col][0] ** 2 + rows_left[r][col][1] ** 2
            )
            rows_left[col], rows_left[pivot_row] = (rows_left[pivot_row], rows_left[col])
            leading = rows_left[col][col]
            rows_left[col] = [pair_div(v, leading) for v in rows_left[col]]
            for r in range(3):
                if r != col:
                    factor = rows_left[r][col]
                    rows_left[r] = [
                        pair_sub(a, pair_mul(factor, b))
                        for a, b in zip(rows_left[r], rows_left[col])
                    ]
        vector = [rows_left[i][3] for i in range(3)] + [(1.0, 0.0)]
        columns.append([v[0] for v in vector])
        columns.append([v[1] for v in vector])
        pairs.append((eigen_pair[0], eigen_pair[1]))
    eigen_basis = [[columns[j][i] for j in range(4)] for i in range(4)]
    basis_inverse = invert_table(eigen_basis)
    return (tableau, inverse, eigen_basis, basis_inverse, pairs)


def constants():
    tableau, inverse, eigen_basis, basis_inverse, pairs = radau_tables()
    shift_table = table_product(basis_inverse, inverse)
    shift_rows = [[v / step_size for v in row_values] for row_values in shift_table]
    pairs = [(p[0] / step_size, p[1] / step_size) for p in pairs]
    return eigen_basis, basis_inverse, shift_rows, pairs


def lane_ids(rows):
    return lax.broadcasted_iota(jnp.int32, (rows, LANES), 1)


def turn(cells, amount):
    return pltpu.roll(cells, amount % LANES, cells.ndim - 1)


def left_half():
    return lax.axis_index("section") == 0


def half_mask(rows):
    return (lane_ids(rows) < LANES // 2) == left_half()


ORDER = (0, 1, 4, 5, 6, 2, 3)
TALL = 16
PARTS = 4


def border_start():
    return jnp.where(left_half(), LANES - EDGE, 0)


def on_even_row():
    return lax.rem(lax.axis_index("sx"), 2) == 0


def place(slot, z):
    entry, row = divmod(8 * slot, TALL)
    last, ninth = divmod(56 + slot, TALL)
    return z * PARTS + entry, row, z * PARTS + last, ninth


def put(tile, cell, at, start, lanes):
    moved = pltpu.roll(cell, lax.rem(at + LANES - start, LANES), 1)
    return jnp.where((lanes >= at) & (lanes < at + EDGE), moved, tile)


def inner_start():
    return jnp.where(left_half(), LANES // 2, LANES // 2 - EDGE)


def pack_far(far_ref, load, fields, base, plane, nz):
    even = on_even_row()
    half = nz // 2
    pairs = (len(fields) + 1) // 2
    window, end = jnp.zeros((8, LANES), jnp.float32), jnp.zeros((1, LANES), jnp.float32)
    for part in range(2):
        z = part * half + plane
        rows, ninths = [], []
        for slot, f in enumerate(fields):
            cell = load(slot, z)
            nx = cell.shape[0]
            rows.append(jnp.where(even, cell[0:8], cell[nx - 8 : nx]))
            ninths.append(jnp.where(even, cell[8:9], cell[nx - 9 : nx - 8]))
            at = part * 64 + f * EDGE
            window = put(window, rows[-1], at, inner_start(), lane_ids(8))
            end = put(end, ninths[-1], at, inner_start(), lane_ids(1))
        for pair in range(pairs):
            first, second = 2 * pair, min(2 * pair + 1, len(fields) - 1)
            far_ref[pairs * z + pair] = jnp.where(half_mask(8), rows[first], turn(rows[second], LANES // 2))
            row = part * pairs + pair
            far_ref[base + plane, row : row + 1] = jnp.where(half_mask(1), ninths[first], turn(ninths[second], LANES // 2))
    far_ref[base + plane, 7:8] = end
    far_ref[base + half + plane] = window


def own_kernel(held_ref, same_ref, cross_ref, far_ref):
    nz, nx = held_ref.shape[1], held_ref.shape[2]
    load = lambda slot, z: held_ref[slot, z]
    for plane in range(nz // 2):
        pack_far(far_ref, load, ORDER[:5], 3 * nz, plane, nz)
    lanes = lane_ids(nx)
    incoming = border_start()
    outgoing = LANES - EDGE - incoming

    for plane in range(nz // 2):
        same = jnp.zeros((nx, LANES), jnp.float32)
        cross = same
        for part in range(2):
            z = part * (nz // 2) + plane
            for slot in range(5):
                cell = held_ref[slot, z]
                same = put(same, cell, part * 64 + ORDER[slot] * EDGE, incoming, lanes)
                if slot < 2:
                    cross = put(cross, cell, part * 64 + (2 + slot) * EDGE, outgoing, lanes)
        same_ref[plane] = same
        cross_ref[plane] = cross


def rows_kernel(held_ref, other_ref, same_ref, cross_ref, border_ref, near_ref, far_ref):
    nz, nx = other_ref.shape[1], other_ref.shape[2]
    even = on_even_row()
    for z in range(nz):
        for slot in range(7):
            cell = held_ref[slot, z] if slot < 5 else other_ref[slot - 5, z]
            entry, row, last, ninth = place(slot, z)
            near_ref[entry, row : row + 8] = jnp.where(even, cell[nx - 8 : nx], cell[0:8])
            near_ref[last, ninth : ninth + 1] = jnp.where(even, cell[nx - 9 : nx - 8], cell[8:9])
    load = lambda slot, z: other_ref[slot, z]
    for plane in range(nz // 2):
        pack_far(far_ref, load, ORDER[5:], nz, plane, nz)
        border = same_ref[plane] + cross_ref[plane]
        border_ref[plane] = border
        near_ref[nz * PARTS + plane] = border
        far_ref[nz + plane, 6:7] = jnp.where(even, border[8:9], border[nx - 9 : nx - 8])
        far_ref[2 * nz + plane] = jnp.where(even, border[0:8], border[nx - 8 : nx])


ROWS = 48
FIRST, LAST = 8, 40
OWN = slice(16, 32)
WORK = slice(FIRST, LAST)
NARROW = slice(12, 36)
BEFORE = slice(FIRST - 1, LAST - 1)
AFTER = slice(FIRST + 1, LAST + 1)


def each_plane(count, unroll, work):
    def group(i, carry):
        for u in range(unroll):
            work(i * unroll + u)
        return carry

    lax.fori_loop(0, count // unroll, group, 0)


def main_kernel(consts, held_ref, other_ref, border_ref, own_far_ref, far_ref, near_ref, part_ref, sums_ref,
                val, kap, frozen, prv, rea, dif, fx, fy, fz, alpha, beta, vec, ya, yb, table):
    eigen_basis, basis_inverse, shift_rows, pairs = consts
    nz, nx = held_ref.shape[1], held_ref.shape[2]
    section = lax.axis_index("section")
    zero_plane = jnp.zeros((ROWS, LANES), jnp.float32)
    zero_rows = jnp.zeros((FIRST, LANES), jnp.float32)
    start = border_start()
    even = on_even_row()
    lanes = lane_ids(ROWS)
    edge = (lanes >= start) & (lanes < start + EDGE)
    tile = lambda t: jnp.broadcast_to(t, (8, LANES))

    for at in (0, nz + 1):
        frozen[at] = zero_plane
        for f in range(4):
            for ref in (val, kap, ya, yb):
                ref[f, at] = zero_plane

    inner = inner_start()

    def unpack(cells, window, second, at):
        count = cells.shape[0]
        ids = lane_ids(count)
        cells = turn(cells, LANES // 2) if second else cells
        window = pltpu.roll(window, lax.rem(inner + LANES - at, LANES), 1)
        return jnp.where(half_mask(count), cells, jnp.where((ids >= inner) & (ids < inner + EDGE), window, 0.0))

    def assemble(plane):
        near_side = near_ref[nz * PARTS + plane]
        far_side, far_end = far_ref[2 * nz + plane], far_ref[nz + plane, 6:7]
        sides = jnp.concatenate(
            [
                tile(jnp.where(even, far_end, near_side[nx - 9 : nx - 8])), jnp.where(even, far_side, near_side[nx - 8 : nx]),
                border_ref[plane],
                jnp.where(even, near_side[0:8], far_side), tile(jnp.where(even, near_side[8:9], far_end)),
            ],
            0,
        )
        for part in range(2):
            z = part * (nz // 2) + plane

            def column(f):
                slot = ORDER.index(f)
                mid = held_ref[slot, z] if slot < 5 else other_ref[slot - 5, z]
                at = part * 64 + f * EDGE
                entry, row, last, ninth = place(slot, z)
                near, near_end = near_ref[entry, row : row + 8], near_ref[last, ninth : ninth + 1]
                if slot < 5:
                    ref, pairs, base, (pair, second) = own_far_ref, 3, 3 * nz, divmod(slot, 2)
                else:
                    ref, pairs, base, pair, second = far_ref, 1, nz, 0, slot - 5
                end = part * pairs + pair
                far = unpack(ref[pairs * z + pair], ref[base + nz // 2 + plane], second, at)
                far_end = unpack(ref[base + plane, end : end + 1], ref[base + plane, 7:8], second, at)
                low, high = jnp.where(even, far, near), jnp.where(even, near, far)
                low_end, high_end = jnp.where(even, far_end, near_end), jnp.where(even, near_end, far_end)
                cells = jnp.concatenate([tile(low_end), low, mid, high, tile(high_end)], 0)
                return jnp.where(edge, pltpu.roll(sides, lax.rem(start + LANES - at, LANES), 1), cells)

            diff, prev, react = column(5), column(4), column(6)
            frozen[z + 1] = diff * (0.5 + 0.25 * jnp.tanh(prev))
            prv[z] = prev[WORK]
            rea[z] = react[WORK]
            dif[z] = diff[WORK]
            for f in range(4):
                value = column(f)
                val[f, z + 1] = value
                kap[f, z + 1] = diff * (0.5 + 0.25 * jnp.tanh(value))
                for ref in (ya, yb):
                    ref[f, z + 1, 0:FIRST] = zero_rows
                    ref[f, z + 1, LAST:ROWS] = zero_rows

    each_plane(nz // 2, 1, assemble)

    def pick(matrix, m, j):
        return jnp.where(section == 0, jnp.float32(matrix[m][j]), jnp.float32(matrix[m][(j + 2) % 4]))

    q_rows = [[pick(basis_inverse, m, j) for j in range(4)] for m in range(4)]
    c_rows = [[pick(shift_rows, m, j) for j in range(4)] for m in range(4)]

    def prepare(z):
        mid = frozen[z + 1, WORK]
        faces = [
            mid + frozen[z + 1, BEFORE], mid + frozen[z + 1, AFTER], mid + turn(mid, 1), mid + turn(mid, -1),
            mid + frozen[z, WORK], mid + frozen[z + 2, WORK],
        ]
        for at, ref in enumerate((fx, fy, fz)):
            ref[0, z] = faces[2 * at]
            ref[1, z] = faces[2 * at + 1]
        prev, react = prv[z], rea[z]
        base = ((faces[0] + faces[1]) + (faces[2] + faces[3])) + (faces[4] + faces[5]) - react * (1.0 - 3.0 * prev * prev)
        inside = jnp.where(dif[z] > 0.0, 1.0, 0.0)
        scaled = []
        for b in range(2):
            real, imag = pairs[b]
            diag = base + real
            scale = inside / (diag * diag + imag * imag)
            scaled.append((diag * scale, imag * scale))
            alpha[b, z], beta[b, z] = scaled[b]
        rhs = [None] * 4
        for j in range(4):
            v = val[j, z + 1, WORK]
            k = kap[j, z + 1, WORK]
            flux = react * v * (1.0 - v * v)
            flux = flux + (k + kap[j, z + 1, BEFORE]) * (val[j, z + 1, BEFORE] - v)
            flux = flux + (k + kap[j, z + 1, AFTER]) * (val[j, z + 1, AFTER] - v)
            flux = flux + (k + turn(k, 1)) * (turn(v, 1) - v)
            flux = flux + (k + turn(k, -1)) * (turn(v, -1) - v)
            flux = flux + (k + kap[j, z, WORK]) * (val[j, z, WORK] - v)
            flux = flux + (k + kap[j, z + 2, WORK]) * (val[j, z + 2, WORK] - v)
            grown = v - prev
            for m in range(4):
                term = q_rows[m][j] * flux - c_rows[m][j] * grown
                rhs[m] = term if j == 0 else rhs[m] + term
        for m in range(4):
            vec[0, m, z] = rhs[m]
        for b in range(2):
            al, be = scaled[b]
            ya[2 * b, z + 1, WORK] = al * rhs[2 * b] - be * rhs[2 * b + 1]
            ya[2 * b + 1, z + 1, WORK] = be * rhs[2 * b] + al * rhs[2 * b + 1]

    each_plane(nz, PREPARE_UNROLL, prepare)

    def spread(ref, m, z, rows=WORK):
        lo, hi = rows.start, rows.stop
        cut = slice(lo - FIRST, hi - FIRST)
        mid = ref[m, z + 1, lo:hi]
        in_y = fy[0, z, cut] * turn(mid, 1) + fy[1, z, cut] * turn(mid, -1)
        in_x = fx[0, z, cut] * ref[m, z + 1, lo - 1 : hi - 1] + fx[1, z, cut] * ref[m, z + 1, lo + 1 : hi + 1]
        in_z = fz[0, z, cut] * ref[m, z, lo:hi] + fz[1, z, cut] * ref[m, z + 2, lo:hi]
        return (in_x + in_z) + in_y

    def window(done):
        reach = 2 * ITERS - done
        return OWN if reach == 0 else NARROW if reach <= 4 else WORK

    for j in range(ITERS):

        def odd(z, j=j):
            rows = window(2 * j + 1)
            cut = slice(rows.start - FIRST, rows.stop - FIRST)
            for b in range(2):
                t0 = spread(ya, 2 * b, z, rows)
                t1 = spread(ya, 2 * b + 1, z, rows)
                al, be = alpha[b, z, cut], beta[b, z, cut]
                for m, y in ((2 * b, al * t0 - be * t1), (2 * b + 1, be * t0 + al * t1)):
                    yb[m, z + 1, rows] = y
                    if rows == WORK:
                        sums_ref[j, m, z, 4:20] = ya[m, z + 1, OWN] + y[8:24]
                    else:
                        sums_ref[j, m, z] = ya[m, z + 1, rows] + y

        def even(z, j=j):
            last = j == ITERS - 1
            rows = window(2 * j + 2)
            cut = slice(rows.start - FIRST, rows.stop - FIRST)
            for b in range(2):
                new = []
                for m in (2 * b, 2 * b + 1):
                    v = spread(yb, m, z, rows)
                    if SHIFTS[j]:
                        v = v - SHIFTS[j] * vec[j, m, z, cut]
                    vec[j + 1, m, z, cut] = v
                    new.append(v)
                if not last:
                    al, be = alpha[b, z, cut], beta[b, z, cut]
                    ya[2 * b, z + 1, rows] = al * new[0] - be * new[1]
                    ya[2 * b + 1, z + 1, rows] = be * new[0] + al * new[1]

        each_plane(nz, STEP_UNROLL, odd)
        each_plane(nz, STEP_UNROLL, even)

    table[...] = jnp.zeros((LANES, LANES), jnp.float32)
    mine = half_mask(8)
    for b in range(2):

        def dots(i, carry):
            out = list(carry)
            for z, m in [(4 * i + u, m) for u in range(4) for m in (2 * b, 2 * b + 1)]:
                cells = [jnp.where(mine, vec[k, m, z, 8:16], turn(vec[k, m, z, 16:24], LANES // 2)) for k in range(SIZE)]
                for at, (k, j) in enumerate(PAIRS):
                    out[at] = out[at] + cells[k] * cells[j]
            return tuple(out)

        zero = jnp.zeros((8, LANES), jnp.float32)
        out = lax.fori_loop(0, nz // 4, dots, tuple(zero for _ in PAIRS))
        for at in range(len(PAIRS)):
            row = jnp.sum(out[at], axis=0, keepdims=True)
            table[b * len(PAIRS) + at : b * len(PAIRS) + at + 1] = row
    total = jnp.sum(table[...].T, axis=0, keepdims=True)
    part_ref[...] = jnp.broadcast_to(total, part_ref.shape)


def step_weights(gram):
    table = {}
    for at, (i, j) in enumerate(PAIRS):
        table[i, j] = table[j, i] = gram[at]
    coef = [jnp.ones_like(gram[0])]
    weight = []
    step = coef[0]
    for k in range(ITERS):
        moved = [SHIFTS[j] * coef[j] for j in range(k + 1)] + [jnp.zeros_like(step)]
        for j in range(k + 1):
            moved[j + 1] = moved[j + 1] + coef[j]
        coef = coef + [jnp.zeros_like(step)]
        image = [coef[j] - moved[j] for j in range(k + 2)]
        num, den, bound = 0.0, 0.0, 0.0
        for i in range(k + 2):
            row, size = 0.0, 0.0
            for j in range(k + 2):
                term = table[i, j] * image[j]
                row = row + term
                size = size + jnp.abs(term)
            num = num + row * coef[i]
            den = den + row * image[i]
            bound = bound + size * jnp.abs(image[i])
        step = jnp.where(den > bound * 6e-8, num / (jnp.maximum(den, 0.0) + tiny_value), step)
        weight = weight + [jnp.zeros_like(step)]
        for j in range(k + 1):
            weight[j] = weight[j] + step * coef[j]
        coef = [coef[j] - step * image[j] for j in range(k + 2)]
    return weight


def send_kernel(consts, total_ref, sums_ref, other_ref, send_ref, weight_ref):
    eigen_basis = consts[0]
    nz, nx = other_ref.shape[1], other_ref.shape[2]
    section = lax.axis_index("section")
    total = jnp.sum(total_ref[...], axis=0, keepdims=True)
    count = len(PAIRS)
    weights = []
    for b in range(2):
        gram = [jnp.broadcast_to(total[:, b * count + at : b * count + at + 1], (1, LANES)) for at in range(count)]
        weights.append(step_weights(gram))
    for b in range(2):
        for j in range(ITERS):
            weight_ref[b * ITERS + j : b * ITERS + j + 1] = weights[b][j]
    basis = [
        [jnp.where(section == 0, jnp.float32(eigen_basis[2 + r][m]), jnp.float32(eigen_basis[r][m])) for m in range(4)]
        for r in range(2)
    ]
    mine = half_mask(nx)

    def combine(z):
        outs = [other_ref[r, z] for r in range(2)]
        for m in range(4):
            field = weights[m // 2][0] * sums_ref[0, m, z, 4:20]
            for j in range(1, ITERS):
                field = field + weights[m // 2][j] * sums_ref[j, m, z, 4:20]
            outs = [outs[r] + basis[r][m] * field for r in range(2)]
        send_ref[z] = jnp.where(mine, outs[0], turn(outs[1], LANES // 2))

    each_plane(nz, 4, combine)


def mine_kernel(consts, weight_ref, sums_ref, own_ref, mine_ref):
    eigen_basis = consts[0]
    nz = own_ref.shape[1]
    section = lax.axis_index("section")
    weights = [[weight_ref[b * ITERS + j : b * ITERS + j + 1] for j in range(ITERS)] for b in range(2)]
    basis = [
        [jnp.where(section == 0, jnp.float32(eigen_basis[r][m]), jnp.float32(eigen_basis[2 + r][m])) for m in range(4)]
        for r in range(2)
    ]

    def combine(z):
        outs = [own_ref[r, z] for r in range(2)]
        for m in range(4):
            field = weights[m // 2][0] * sums_ref[0, m, z, 4:20]
            for j in range(1, ITERS):
                field = field + weights[m // 2][j] * sums_ref[j, m, z, 4:20]
            outs = [outs[r] + basis[r][m] * field for r in range(2)]
        mine_ref[0, z] = outs[0]
        mine_ref[1, z] = outs[1]

    each_plane(nz, 4, combine)


def join_kernel(mine_ref, other_ref, out_ref):
    nz, nx = mine_ref.shape[1], mine_ref.shape[2]
    mine = half_mask(nx)
    for z in range(nz):
        other = other_ref[z]
        out_ref[0, z] = jnp.where(mine, mine_ref[0, z], other)
        out_ref[1, z] = jnp.where(mine, mine_ref[1, z], turn(other, LANES // 2))


def call(kernel, outs, scratch=(), flops=1_000_000, name=None, limit=12):
    many = isinstance(outs, list)
    shapes = [jax.ShapeDtypeStruct(o, jnp.float32) for o in (outs if many else [outs])]

    def run(*args):
        moved = 4 * sum(int(a.size) for a in args) + 4 * sum(int(functools.reduce(lambda p, q: p * q, s.shape, 1)) for s in shapes)
        return pl.pallas_call(
            kernel,
            out_shape=shapes if many else shapes[0],
            in_specs=[pl.BlockSpec(memory_space=pltpu.VMEM)] * len(args),
            out_specs=[pl.BlockSpec(memory_space=pltpu.VMEM)] * len(shapes) if many else pl.BlockSpec(memory_space=pltpu.VMEM),
            scratch_shapes=[pltpu.VMEM(s, jnp.float32) for s in scratch],
            compiler_params=pltpu.CompilerParams(vmem_limit_bytes=int(limit * 1024 * 1024)),
            cost_estimate=pl.CostEstimate(flops=flops, bytes_accessed=moved, transcendentals=0),
            name=name,
        )(*args)

    return run


def swaps(count, start):
    return [pair for i in range(start, count - 1, 2) for pair in ((i, i + 1), (i + 1, i))]


def beside(count, cross):
    pairs = []
    for s in range(2):
        to = 1 - s if cross else s
        step = 1 if to == 0 else -1
        for i in range(count):
            if 0 <= i + step < count:
                pairs.append((s * count + i, to * count + i + step))
    return pairs


def body(previous, sections, diffusivity, reaction):
    consts = constants()
    nz, nx, ny = previous.shape
    columns, rows = lax.axis_size("sy"), lax.axis_size("sx")
    axes = ("section", "sx", "sy")
    partner = [(0, 1), (1, 0)]
    other = lax.ppermute(sections, "section", partner)
    edge, whole, early, late = (nz // 2, nx, ny), (nz * PARTS + nz // 2, TALL, ny), (4 * nz, 8, ny), (2 * nz + nz // 2, 8, ny)
    held = jnp.concatenate([sections, previous[None], diffusivity[None], reaction[None]], 0)
    same, cross, own_far = call(own_kernel, [edge, edge, early], name="own")(held)
    own_far = lax.ppermute(own_far, "sx", swaps(rows, 1))
    same = lax.ppermute(same, ("section", "sy"), beside(columns, False))
    cross = lax.ppermute(cross, ("section", "sy"), beside(columns, True))
    cross, own_far = lax.optimization_barrier((cross, own_far))
    border, near, far = call(rows_kernel, [edge, whole, late], name="rows")(held, other, same, cross)
    far = lax.ppermute(far, "sx", swaps(rows, 1))
    near = lax.ppermute(near, "sx", swaps(rows, 0))
    peers = 2 * columns * rows
    padded, work = (nz + 2, ROWS, ny), (nz, LAST - FIRST, ny)
    scratch = [
        (4,) + padded, (4,) + padded, padded, work, work, work, (2,) + work, (2,) + work, (2,) + work, (2,) + work, (2,) + work,
        (SIZE, 4) + work, (4,) + padded, (4,) + padded, (LANES, LANES),
    ]
    part, sums = call(
        functools.partial(main_kernel, consts), [(peers, LANES), (ITERS, 4, nz, nx + 8, ny)], scratch, 50_000_000, "main", 26
    )(held, other, border, own_far, far, near)
    total = lax.all_to_all(part.reshape(peers, 1, LANES), axes, 0, 0).reshape(peers, LANES)
    half, weight = call(functools.partial(send_kernel, consts), [previous.shape, (2 * ITERS, LANES)], name="send")(total, sums, other)
    got = lax.ppermute(half, "section", partner)
    mine = call(functools.partial(mine_kernel, consts), sections.shape, name="mine")(weight, sums, held)
    return call(join_kernel, sections.shape, name="join")(mine, got)


def solution(mesh):
    in_specs = (
        P(None, "sx", "sy"),
        P("section", None, "sx", "sy"),
        P(None, "sx", "sy"),
        P(None, "sx", "sy"),
    )
    out_specs = P("section", None, "sx", "sy")
    return jax.shard_map(body, mesh=mesh, in_specs=in_specs, out_specs=out_specs, check_vma=False)
```

```python
import functools

import jax
import jax.numpy as jnp
from jax import lax
from jax.experimental import pallas as pl
from jax.experimental.pallas import tpu as pltpu
from jax.sharding import PartitionSpec as P

ITERS = 4
SHIFTS = (0.0, 0.9, 0.45, 0.7)
EDGE = 9
LANES = 128
SIZE = ITERS + 1
PAIRS = [(i, j) for i in range(SIZE) for j in range(i, SIZE)]
PREPARE_UNROLL = 4
STEP_UNROLL = 16


step_size = 1.0
tiny_value = 1e-06


def invert_table(matrix):
    order_n = len(matrix)
    augmented = [
        list(matrix[r]) + [1.0 if c == r else 0.0 for c in range(order_n)] for r in range(order_n)
    ]
    for col in range(order_n):
        pivot_row = max(range(col, order_n), key=lambda r: abs(augmented[r][col]))
        augmented[col], augmented[pivot_row] = (augmented[pivot_row], augmented[col])
        leading = augmented[col][col]
        augmented[col] = [v / leading for v in augmented[col]]
        for r in range(order_n):
            if r != col:
                factor = augmented[r][col]
                augmented[r] = [a - factor * b for a, b in zip(augmented[r], augmented[col])]
    return [row_values[order_n:] for row_values in augmented]


def table_product(left, right):
    return [
        [sum((left[i][k] * right[k][j] for k in range(len(right)))) for j in range(len(right[0]))]
        for i in range(len(left))
    ]


def pair_add(first, second):
    return (first[0] + second[0], first[1] + second[1])


def pair_sub(first, second):
    return (first[0] - second[0], first[1] - second[1])


def pair_mul(first, second):
    return (
        first[0] * second[0] - first[1] * second[1],
        first[0] * second[1] + first[1] * second[0],
    )


def pair_div(first, second):
    scale_sq = second[0] * second[0] + second[1] * second[1]
    return (
        (first[0] * second[0] + first[1] * second[1]) / scale_sq,
        (first[1] * second[0] - first[0] * second[1]) / scale_sq,
    )


def quartic_value(point):
    return (((210.0 * point - 480.0) * point + 360.0) * point - 96.0) * point + 6.0


def bisect_root(lower, upper):
    for count in range(200):
        middle = 0.5 * (lower + upper)
        if (quartic_value(lower) < 0.0) == (quartic_value(middle) < 0.0):
            lower = middle
        else:
            upper = middle
    return 0.5 * (lower + upper)


def radau_tables():
    abscissae = []
    grid_steps = 4000
    for m in range(grid_steps):
        lower = 0.999 * m / grid_steps
        upper = 0.999 * (m + 1) / grid_steps
        if (quartic_value(lower) < 0.0) != (quartic_value(upper) < 0.0):
            abscissae.append(bisect_root(lower, upper))
    abscissae.append(1.0)
    vander = [[abscissae[j] ** k for k in range(4)] for j in range(4)]
    moments = [[abscissae[i] ** (k + 1) / (k + 1) for k in range(4)] for i in range(4)]
    tableau = table_product(moments, invert_table(vander))
    inverse = invert_table(tableau)
    running = [list(row_values) for row_values in inverse]
    coeffs = []
    for k in range(1, 5):
        trace_value = sum((running[i][i] for i in range(4)))
        coeffs.append(-trace_value / k)
        shifted_table = [
            [running[i][j] + (coeffs[-1] if i == j else 0.0) for j in range(4)] for i in range(4)
        ]
        running = table_product(inverse, shifted_table)
    start_point = (0.4, 0.9)
    estimates = [(1.0, 0.0)]
    for k in range(3):
        estimates.append(pair_mul(estimates[-1], start_point))
    for count in range(500):
        for i in range(4):
            value = (1.0, 0.0)
            for coef_value in coeffs:
                value = pair_add(pair_mul(value, estimates[i]), (coef_value, 0.0))
            denom = (1.0, 0.0)
            for j in range(4):
                if j != i:
                    denom = pair_mul(denom, pair_sub(estimates[i], estimates[j]))
            estimates[i] = pair_sub(estimates[i], pair_div(value, denom))
    chosen = [m for m in range(4) if estimates[m][1] > 0.0]
    ranking = sorted(chosen, key=lambda m: -estimates[m][1])
    columns = []
    pairs = []
    for m in ranking:
        eigen_pair = estimates[m]
        system = [
            [
                (
                    inverse[i][j] - (eigen_pair[0] if i == j else 0.0),
                    -(eigen_pair[1] if i == j else 0.0),
                )
                for j in range(4)
            ]
            for i in range(3)
        ]
        rows_left = [
            [system[i][j] for j in range(3)] + [(-system[i][3][0], -system[i][3][1])]
            for i in range(3)
        ]
        for col in range(3):
            pivot_row = max(
                range(col, 3), key=lambda r: rows_left[r][col][0] ** 2 + rows_left[r][col][1] ** 2
            )
            rows_left[col], rows_left[pivot_row] = (rows_left[pivot_row], rows_left[col])
            leading = rows_left[col][col]
            rows_left[col] = [pair_div(v, leading) for v in rows_left[col]]
            for r in range(3):
                if r != col:
                    factor = rows_left[r][col]
                    rows_left[r] = [
                        pair_sub(a, pair_mul(factor, b))
                        for a, b in zip(rows_left[r], rows_left[col])
                    ]
        vector = [rows_left[i][3] for i in range(3)] + [(1.0, 0.0)]
        columns.append([v[0] for v in vector])
        columns.append([v[1] for v in vector])
        pairs.append((eigen_pair[0], eigen_pair[1]))
    eigen_basis = [[columns[j][i] for j in range(4)] for i in range(4)]
    basis_inverse = invert_table(eigen_basis)
    return (tableau, inverse, eigen_basis, basis_inverse, pairs)


def constants():
    tableau, inverse, eigen_basis, basis_inverse, pairs = radau_tables()
    shift_table = table_product(basis_inverse, inverse)
    shift_rows = [[v / step_size for v in row_values] for row_values in shift_table]
    pairs = [(p[0] / step_size, p[1] / step_size) for p in pairs]
    return eigen_basis, basis_inverse, shift_rows, pairs


def lane_ids(rows):
    return lax.broadcasted_iota(jnp.int32, (rows, LANES), 1)


def turn(cells, amount):
    return pltpu.roll(cells, amount % LANES, cells.ndim - 1)


def left_half():
    return lax.axis_index("section") == 0


def half_mask(rows):
    return (lane_ids(rows) < LANES // 2) == left_half()


ORDER = (0, 1, 4, 5, 6, 2, 3)
TALL = 16
PARTS = 4


def border_start():
    return jnp.where(left_half(), LANES - EDGE, 0)


def on_even_row():
    return lax.rem(lax.axis_index("sx"), 2) == 0


def place(slot, z):
    entry, row = divmod(8 * slot, TALL)
    last, ninth = divmod(56 + slot, TALL)
    return z * PARTS + entry, row, z * PARTS + last, ninth


def put(tile, cell, at, start, lanes):
    moved = pltpu.roll(cell, lax.rem(at + LANES - start, LANES), 1)
    return jnp.where((lanes >= at) & (lanes < at + EDGE), moved, tile)


def inner_start():
    return jnp.where(left_half(), LANES // 2, LANES // 2 - EDGE)


def pack_far(far_ref, load, fields, base, plane, nz):
    even = on_even_row()
    half = nz // 2
    pairs = (len(fields) + 1) // 2
    window, end = jnp.zeros((8, LANES), jnp.float32), jnp.zeros((1, LANES), jnp.float32)
    for part in range(2):
        z = part * half + plane
        rows, ninths = [], []
        for slot, f in enumerate(fields):
            cell = load(slot, z)
            nx = cell.shape[0]
            rows.append(jnp.where(even, cell[0:8], cell[nx - 8 : nx]))
            ninths.append(jnp.where(even, cell[8:9], cell[nx - 9 : nx - 8]))
            at = part * 64 + f * EDGE
            window = put(window, rows[-1], at, inner_start(), lane_ids(8))
            end = put(end, ninths[-1], at, inner_start(), lane_ids(1))
        for pair in range(pairs):
            first, second = 2 * pair, min(2 * pair + 1, len(fields) - 1)
            far_ref[pairs * z + pair] = jnp.where(half_mask(8), rows[first], turn(rows[second], LANES // 2))
            row = part * pairs + pair
            far_ref[base + plane, row : row + 1] = jnp.where(half_mask(1), ninths[first], turn(ninths[second], LANES // 2))
    far_ref[base + plane, 7:8] = end
    far_ref[base + half + plane] = window


def own_kernel(held_ref, same_ref, cross_ref, far_ref):
    nz, nx = held_ref.shape[1], held_ref.shape[2]
    load = lambda slot, z: held_ref[slot, z]
    for plane in range(nz // 2):
        pack_far(far_ref, load, ORDER[:5], 3 * nz, plane, nz)
    lanes = lane_ids(nx)
    incoming = border_start()
    outgoing = LANES - EDGE - incoming

    for plane in range(nz // 2):
        same = jnp.zeros((nx, LANES), jnp.float32)
        cross = same
        for part in range(2):
            z = part * (nz // 2) + plane
            for slot in range(5):
                cell = held_ref[slot, z]
                same = put(same, cell, part * 64 + ORDER[slot] * EDGE, incoming, lanes)
                if slot < 2:
                    cross = put(cross, cell, part * 64 + (2 + slot) * EDGE, outgoing, lanes)
        same_ref[plane] = same
        cross_ref[plane] = cross


def rows_kernel(held_ref, other_ref, same_ref, cross_ref, border_ref, near_ref, far_ref):
    nz, nx = other_ref.shape[1], other_ref.shape[2]
    even = on_even_row()
    for z in range(nz):
        for slot in range(7):
            cell = held_ref[slot, z] if slot < 5 else other_ref[slot - 5, z]
            entry, row, last, ninth = place(slot, z)
            near_ref[entry, row : row + 8] = jnp.where(even, cell[nx - 8 : nx], cell[0:8])
            near_ref[last, ninth : ninth + 1] = jnp.where(even, cell[nx - 9 : nx - 8], cell[8:9])
    load = lambda slot, z: other_ref[slot, z]
    for plane in range(nz // 2):
        pack_far(far_ref, load, ORDER[5:], nz, plane, nz)
        border = same_ref[plane] + cross_ref[plane]
        border_ref[plane] = border
        near_ref[nz * PARTS + plane] = border
        far_ref[nz + plane, 6:7] = jnp.where(even, border[8:9], border[nx - 9 : nx - 8])
        far_ref[2 * nz + plane] = jnp.where(even, border[0:8], border[nx - 8 : nx])


ROWS = 48
FIRST, LAST = 8, 40
OWN = slice(16, 32)
WORK = slice(FIRST, LAST)
NARROW = slice(12, 36)
BEFORE = slice(FIRST - 1, LAST - 1)
AFTER = slice(FIRST + 1, LAST + 1)


def each_plane(count, unroll, work):
    def group(i, carry):
        for u in range(unroll):
            work(i * unroll + u)
        return carry

    lax.fori_loop(0, count // unroll, group, 0)


def main_kernel(consts, held_ref, other_ref, border_ref, own_far_ref, far_ref, near_ref, part_ref, sums_ref,
                val, kap, frozen, prv, rea, dif, fx, fy, fz, alpha, beta, vec, ya, yb, table):
    eigen_basis, basis_inverse, shift_rows, pairs = consts
    nz, nx = held_ref.shape[1], held_ref.shape[2]
    section = lax.axis_index("section")
    zero_plane = jnp.zeros((ROWS, LANES), jnp.float32)
    zero_rows = jnp.zeros((FIRST, LANES), jnp.float32)
    start = border_start()
    even = on_even_row()
    lanes = lane_ids(ROWS)
    edge = (lanes >= start) & (lanes < start + EDGE)
    tile = lambda t: jnp.broadcast_to(t, (8, LANES))

    for at in (0, nz + 1):
        frozen[at] = zero_plane
        for f in range(4):
            for ref in (val, kap, ya, yb):
                ref[f, at] = zero_plane

    inner = inner_start()

    def unpack(cells, window, second, at):
        count = cells.shape[0]
        ids = lane_ids(count)
        cells = turn(cells, LANES // 2) if second else cells
        window = pltpu.roll(window, lax.rem(inner + LANES - at, LANES), 1)
        return jnp.where(half_mask(count), cells, jnp.where((ids >= inner) & (ids < inner + EDGE), window, 0.0))

    def assemble(plane):
        near_side = near_ref[nz * PARTS + plane]
        far_side, far_end = far_ref[2 * nz + plane], far_ref[nz + plane, 6:7]
        sides = jnp.concatenate(
            [
                tile(jnp.where(even, far_end, near_side[nx - 9 : nx - 8])), jnp.where(even, far_side, near_side[nx - 8 : nx]),
                border_ref[plane],
                jnp.where(even, near_side[0:8], far_side), tile(jnp.where(even, near_side[8:9], far_end)),
            ],
            0,
        )
        for part in range(2):
            z = part * (nz // 2) + plane

            def column(f):
                slot = ORDER.index(f)
                mid = held_ref[slot, z] if slot < 5 else other_ref[slot - 5, z]
                at = part * 64 + f * EDGE
                entry, row, last, ninth = place(slot, z)
                near, near_end = near_ref[entry, row : row + 8], near_ref[last, ninth : ninth + 1]
                if slot < 5:
                    ref, pairs, base, (pair, second) = own_far_ref, 3, 3 * nz, divmod(slot, 2)
                else:
                    ref, pairs, base, pair, second = far_ref, 1, nz, 0, slot - 5
                end = part * pairs + pair
                far = unpack(ref[pairs * z + pair], ref[base + nz // 2 + plane], second, at)
                far_end = unpack(ref[base + plane, end : end + 1], ref[base + plane, 7:8], second, at)
                low, high = jnp.where(even, far, near), jnp.where(even, near, far)
                low_end, high_end = jnp.where(even, far_end, near_end), jnp.where(even, near_end, far_end)
                cells = jnp.concatenate([tile(low_end), low, mid, high, tile(high_end)], 0)
                return jnp.where(edge, pltpu.roll(sides, lax.rem(start + LANES - at, LANES), 1), cells)

            diff, prev, react = column(5), column(4), column(6)
            frozen[z + 1] = diff * (0.5 + 0.25 * jnp.tanh(prev))
            prv[z] = prev[WORK]
            rea[z] = react[WORK]
            dif[z] = diff[WORK]
            for f in range(4):
                value = column(f)
                val[f, z + 1] = value
                kap[f, z + 1] = diff * (0.5 + 0.25 * jnp.tanh(value))
                for ref in (ya, yb):
                    ref[f, z + 1, 0:FIRST] = zero_rows
                    ref[f, z + 1, LAST:ROWS] = zero_rows

    each_plane(nz // 2, 2, assemble)

    def pick(matrix, m, j):
        return jnp.where(section == 0, jnp.float32(matrix[m][j]), jnp.float32(matrix[m][(j + 2) % 4]))

    q_rows = [[pick(basis_inverse, m, j) for j in range(4)] for m in range(4)]
    c_rows = [[pick(shift_rows, m, j) for j in range(4)] for m in range(4)]

    def prepare(z):
        mid = frozen[z + 1, WORK]
        faces = [
            mid + frozen[z + 1, BEFORE], mid + frozen[z + 1, AFTER], mid + turn(mid, 1), mid + turn(mid, -1),
            mid + frozen[z, WORK], mid + frozen[z + 2, WORK],
        ]
        for at, ref in enumerate((fx, fy, fz)):
            ref[0, z] = faces[2 * at]
            ref[1, z] = faces[2 * at + 1]
        prev, react = prv[z], rea[z]
        base = ((faces[0] + faces[1]) + (faces[2] + faces[3])) + (faces[4] + faces[5]) - react * (1.0 - 3.0 * prev * prev)
        inside = jnp.where(dif[z] > 0.0, 1.0, 0.0)
        scaled = []
        for b in range(2):
            real, imag = pairs[b]
            diag = base + real
            scale = inside / (diag * diag + imag * imag)
            scaled.append((diag * scale, imag * scale))
            alpha[b, z], beta[b, z] = scaled[b]
        rhs = [None] * 4
        for j in range(4):
            v = val[j, z + 1, WORK]
            k = kap[j, z + 1, WORK]
            flux = react * v * (1.0 - v * v)
            flux = flux + (k + kap[j, z + 1, BEFORE]) * (val[j, z + 1, BEFORE] - v)
            flux = flux + (k + kap[j, z + 1, AFTER]) * (val[j, z + 1, AFTER] - v)
            flux = flux + (k + turn(k, 1)) * (turn(v, 1) - v)
            flux = flux + (k + turn(k, -1)) * (turn(v, -1) - v)
            flux = flux + (k + kap[j, z, WORK]) * (val[j, z, WORK] - v)
            flux = flux + (k + kap[j, z + 2, WORK]) * (val[j, z + 2, WORK] - v)
            grown = v - prev
            for m in range(4):
                term = q_rows[m][j] * flux - c_rows[m][j] * grown
                rhs[m] = term if j == 0 else rhs[m] + term
        for m in range(4):
            vec[0, m, z] = rhs[m]
        for b in range(2):
            al, be = scaled[b]
            ya[2 * b, z + 1, WORK] = al * rhs[2 * b] - be * rhs[2 * b + 1]
            ya[2 * b + 1, z + 1, WORK] = be * rhs[2 * b] + al * rhs[2 * b + 1]

    each_plane(nz, PREPARE_UNROLL, prepare)

    def spread(ref, m, z, rows=WORK):
        lo, hi = rows.start, rows.stop
        cut = slice(lo - FIRST, hi - FIRST)
        mid = ref[m, z + 1, lo:hi]
        in_y = fy[0, z, cut] * turn(mid, 1) + fy[1, z, cut] * turn(mid, -1)
        in_x = fx[0, z, cut] * ref[m, z + 1, lo - 1 : hi - 1] + fx[1, z, cut] * ref[m, z + 1, lo + 1 : hi + 1]
        in_z = fz[0, z, cut] * ref[m, z, lo:hi] + fz[1, z, cut] * ref[m, z + 2, lo:hi]
        return (in_x + in_z) + in_y

    def window(done):
        reach = 2 * ITERS - done
        return OWN if reach == 0 else NARROW if reach <= 4 else WORK

    for j in range(ITERS):

        def odd(z, j=j):
            rows = window(2 * j + 1)
            cut = slice(rows.start - FIRST, rows.stop - FIRST)
            for b in range(2):
                t0 = spread(ya, 2 * b, z, rows)
                t1 = spread(ya, 2 * b + 1, z, rows)
                al, be = alpha[b, z, cut], beta[b, z, cut]
                for m, y in ((2 * b, al * t0 - be * t1), (2 * b + 1, be * t0 + al * t1)):
                    yb[m, z + 1, rows] = y
                    if rows == WORK:
                        sums_ref[j, m, z, 4:20] = ya[m, z + 1, OWN] + y[8:24]
                    else:
                        sums_ref[j, m, z] = ya[m, z + 1, rows] + y

        def even(z, j=j):
            last = j == ITERS - 1
            rows = window(2 * j + 2)
            cut = slice(rows.start - FIRST, rows.stop - FIRST)
            for b in range(2):
                new = []
                for m in (2 * b, 2 * b + 1):
                    v = spread(yb, m, z, rows)
                    if SHIFTS[j]:
                        v = v - SHIFTS[j] * vec[j, m, z, cut]
                    vec[j + 1, m, z, cut] = v
                    new.append(v)
                if not last:
                    al, be = alpha[b, z, cut], beta[b, z, cut]
                    ya[2 * b, z + 1, rows] = al * new[0] - be * new[1]
                    ya[2 * b + 1, z + 1, rows] = be * new[0] + al * new[1]

        each_plane(nz, STEP_UNROLL, odd)
        each_plane(nz, STEP_UNROLL, even)

    table[...] = jnp.zeros((LANES, LANES), jnp.float32)
    mine = half_mask(8)
    for b in range(2):

        def dots(i, carry):
            out = list(carry)
            for z, m in [(4 * i + u, m) for u in range(4) for m in (2 * b, 2 * b + 1)]:
                cells = [jnp.where(mine, vec[k, m, z, 8:16], turn(vec[k, m, z, 16:24], LANES // 2)) for k in range(SIZE)]
                for at, (k, j) in enumerate(PAIRS):
                    out[at] = out[at] + cells[k] * cells[j]
            return tuple(out)

        zero = jnp.zeros((8, LANES), jnp.float32)
        out = lax.fori_loop(0, nz // 4, dots, tuple(zero for _ in PAIRS))
        for at in range(len(PAIRS)):
            row = jnp.sum(out[at], axis=0, keepdims=True)
            table[b * len(PAIRS) + at : b * len(PAIRS) + at + 1] = row
    total = jnp.sum(table[...].T, axis=0, keepdims=True)
    part_ref[...] = jnp.broadcast_to(total, part_ref.shape)


def step_weights(gram):
    table = {}
    for at, (i, j) in enumerate(PAIRS):
        table[i, j] = table[j, i] = gram[at]
    coef = [jnp.ones_like(gram[0])]
    weight = []
    step = coef[0]
    for k in range(ITERS):
        moved = [SHIFTS[j] * coef[j] for j in range(k + 1)] + [jnp.zeros_like(step)]
        for j in range(k + 1):
            moved[j + 1] = moved[j + 1] + coef[j]
        coef = coef + [jnp.zeros_like(step)]
        image = [coef[j] - moved[j] for j in range(k + 2)]
        num, den, bound = 0.0, 0.0, 0.0
        for i in range(k + 2):
            row, size = 0.0, 0.0
            for j in range(k + 2):
                term = table[i, j] * image[j]
                row = row + term
                size = size + jnp.abs(term)
            num = num + row * coef[i]
            den = den + row * image[i]
            bound = bound + size * jnp.abs(image[i])
        step = jnp.where(den > bound * 6e-8, num / (jnp.maximum(den, 0.0) + tiny_value), step)
        weight = weight + [jnp.zeros_like(step)]
        for j in range(k + 1):
            weight[j] = weight[j] + step * coef[j]
        coef = [coef[j] - step * image[j] for j in range(k + 2)]
    return weight


def send_kernel(consts, total_ref, sums_ref, other_ref, send_ref, weight_ref):
    eigen_basis = consts[0]
    nz, nx = other_ref.shape[1], other_ref.shape[2]
    section = lax.axis_index("section")
    total = jnp.sum(total_ref[...], axis=0, keepdims=True)
    count = len(PAIRS)
    weights = []
    for b in range(2):
        gram = [jnp.broadcast_to(total[:, b * count + at : b * count + at + 1], (1, LANES)) for at in range(count)]
        weights.append(step_weights(gram))
    for b in range(2):
        for j in range(ITERS):
            weight_ref[b * ITERS + j : b * ITERS + j + 1] = weights[b][j]
    basis = [
        [jnp.where(section == 0, jnp.float32(eigen_basis[2 + r][m]), jnp.float32(eigen_basis[r][m])) for m in range(4)]
        for r in range(2)
    ]
    mine = half_mask(nx)

    def combine(z):
        outs = [other_ref[r, z] for r in range(2)]
        for m in range(4):
            field = weights[m // 2][0] * sums_ref[0, m, z, 4:20]
            for j in range(1, ITERS):
                field = field + weights[m // 2][j] * sums_ref[j, m, z, 4:20]
            outs = [outs[r] + basis[r][m] * field for r in range(2)]
        send_ref[z] = jnp.where(mine, outs[0], turn(outs[1], LANES // 2))

    each_plane(nz, 4, combine)


def mine_kernel(consts, weight_ref, sums_ref, own_ref, mine_ref):
    eigen_basis = consts[0]
    nz = own_ref.shape[1]
    section = lax.axis_index("section")
    weights = [[weight_ref[b * ITERS + j : b * ITERS + j + 1] for j in range(ITERS)] for b in range(2)]
    basis = [
        [jnp.where(section == 0, jnp.float32(eigen_basis[r][m]), jnp.float32(eigen_basis[2 + r][m])) for m in range(4)]
        for r in range(2)
    ]

    def combine(z):
        outs = [own_ref[r, z] for r in range(2)]
        for m in range(4):
            field = weights[m // 2][0] * sums_ref[0, m, z, 4:20]
            for j in range(1, ITERS):
                field = field + weights[m // 2][j] * sums_ref[j, m, z, 4:20]
            outs = [outs[r] + basis[r][m] * field for r in range(2)]
        mine_ref[0, z] = outs[0]
        mine_ref[1, z] = outs[1]

    each_plane(nz, 4, combine)


def join_kernel(mine_ref, other_ref, out_ref):
    nz, nx = mine_ref.shape[1], mine_ref.shape[2]
    mine = half_mask(nx)
    for z in range(nz):
        other = other_ref[z]
        out_ref[0, z] = jnp.where(mine, mine_ref[0, z], other)
        out_ref[1, z] = jnp.where(mine, mine_ref[1, z], turn(other, LANES // 2))


def call(kernel, outs, scratch=(), flops=1_000_000, name=None, limit=12):
    many = isinstance(outs, list)
    shapes = [jax.ShapeDtypeStruct(o, jnp.float32) for o in (outs if many else [outs])]

    def run(*args):
        moved = 4 * sum(int(a.size) for a in args) + 4 * sum(int(functools.reduce(lambda p, q: p * q, s.shape, 1)) for s in shapes)
        return pl.pallas_call(
            kernel,
            out_shape=shapes if many else shapes[0],
            in_specs=[pl.BlockSpec(memory_space=pltpu.VMEM)] * len(args),
            out_specs=[pl.BlockSpec(memory_space=pltpu.VMEM)] * len(shapes) if many else pl.BlockSpec(memory_space=pltpu.VMEM),
            scratch_shapes=[pltpu.VMEM(s, jnp.float32) for s in scratch],
            compiler_params=pltpu.CompilerParams(vmem_limit_bytes=int(limit * 1024 * 1024)),
            cost_estimate=pl.CostEstimate(flops=flops, bytes_accessed=moved, transcendentals=0),
            name=name,
        )(*args)

    return run


def swaps(count, start):
    return [pair for i in range(start, count - 1, 2) for pair in ((i, i + 1), (i + 1, i))]


def beside(count, cross):
    pairs = []
    for s in range(2):
        to = 1 - s if cross else s
        step = 1 if to == 0 else -1
        for i in range(count):
            if 0 <= i + step < count:
                pairs.append((s * count + i, to * count + i + step))
    return pairs


def body(previous, sections, diffusivity, reaction):
    consts = constants()
    nz, nx, ny = previous.shape
    columns, rows = lax.axis_size("sy"), lax.axis_size("sx")
    axes = ("section", "sx", "sy")
    partner = [(0, 1), (1, 0)]
    other = lax.ppermute(sections, "section", partner)
    edge, whole, early, late = (nz // 2, nx, ny), (nz * PARTS + nz // 2, TALL, ny), (4 * nz, 8, ny), (2 * nz + nz // 2, 8, ny)
    held = jnp.concatenate([sections, previous[None], diffusivity[None], reaction[None]], 0)
    same, cross, own_far = call(own_kernel, [edge, edge, early], name="own")(held)
    own_far = lax.ppermute(own_far, "sx", swaps(rows, 1))
    same = lax.ppermute(same, ("section", "sy"), beside(columns, False))
    cross = lax.ppermute(cross, ("section", "sy"), beside(columns, True))
    cross, own_far = lax.optimization_barrier((cross, own_far))
    border, near, far = call(rows_kernel, [edge, whole, late], name="rows")(held, other, same, cross)
    far = lax.ppermute(far, "sx", swaps(rows, 1))
    near = lax.ppermute(near, "sx", swaps(rows, 0))
    peers = 2 * columns * rows
    padded, work = (nz + 2, ROWS, ny), (nz, LAST - FIRST, ny)
    scratch = [
        (4,) + padded, (4,) + padded, padded, work, work, work, (2,) + work, (2,) + work, (2,) + work, (2,) + work, (2,) + work,
        (SIZE, 4) + work, (4,) + padded, (4,) + padded, (LANES, LANES),
    ]
    part, sums = call(
        functools.partial(main_kernel, consts), [(peers, LANES), (ITERS, 4, nz, nx + 8, ny)], scratch, 50_000_000, "main", 26
    )(held, other, border, own_far, far, near)
    total = lax.all_to_all(part.reshape(peers, 1, LANES), axes, 0, 0).reshape(peers, LANES)
    half, weight = call(functools.partial(send_kernel, consts), [previous.shape, (2 * ITERS, LANES)], name="send")(total, sums, other)
    got = lax.ppermute(half, "section", partner)
    mine = call(functools.partial(mine_kernel, consts), sections.shape, name="mine")(weight, sums, held)
    return call(join_kernel, sections.shape, name="join")(mine, got)


def solution(mesh):
    in_specs = (
        P(None, "sx", "sy"),
        P("section", None, "sx", "sy"),
        P(None, "sx", "sy"),
        P(None, "sx", "sy"),
    )
    out_specs = P("section", None, "sx", "sy")
    return jax.shard_map(body, mesh=mesh, in_specs=in_specs, out_specs=out_specs, check_vma=False)
```
